32 devices in a mesh: dp: 8 (over z, y), tensor: 4 (over x, core).
Axes of the slice: x: 2, y: 2, z: 4, core: 2. Of those that a mesh axis runs over, the one named last changes fastest.
Arguments:
- inputs: bfloat16 [4096, 2048], P('dp'), may hold values from -6 to 6
- targets: int32 [4096], P('dp'), may hold values from 0 to 25599
- doc_lengths: int32 [8, 4], P('dp'), may hold values from 1 to 384, 512 in all within a row
- desirable: int32 [8, 4], P('dp'), may hold values 0 or 1
- head_weight: bfloat16 [2048, 25600], P(None, 'tensor'), may hold values from -0.21213203 to 0.21213203, as said below
- qkv_master: float32 [2048, 6144], P('dp', 'tensor'), may hold values from -0.125 to 0.125
- out_master: float32 [2048, 2048], P('tensor', 'dp'), may hold values from -0.5 to 0.5
- up_master: float32 [2048, 8192], P('dp', 'tensor'), may hold values from -0.125 to 0.125
- down_master: float32 [8192, 2048], P('tensor', 'dp'), may hold values from -0.0625 to 0.0625
- vectors: float32 [6, 2048], replicated, may hold values from -0.525 to 2.125, as said below
- hidden_bias: float32 [14336], P('tensor'), may hold values from -1.5 to 1.5
- qkv_mean: float32 [2048, 6144], P('dp', 'tensor'), may hold values from -2.3841858e-06 to 2.3841858e-06
- out_mean: float32 [2048, 2048], P('tensor', 'dp'), may hold values from -2.3841858e-06 to 2.3841858e-06
- up_mean: float32 [2048, 8192], P('dp', 'tensor'), may hold values from -2.3841858e-06 to 2.3841858e-06
- down_mean: float32 [8192, 2048], P('tensor', 'dp'), may hold values from -2.3841858e-06 to 2.3841858e-06
- vectors_mean: float32 [6, 2048], replicated, may hold values from -9.536743e-06 to 9.536743e-06
- hidden_mean: float32 [14336], P('tensor'), may hold values from -9.536743e-06 to 9.536743e-06
- qkv_square: float32 [2048, 6144], P('dp', 'tensor'), may hold values from 9.928856e-16 to 1.5886169e-14
- out_square: float32 [2048, 2048], P('tensor', 'dp'), may hold values from 9.928856e-16 to 1.5886169e-14
- up_square: float32 [2048, 8192], P('dp', 'tensor'), may hold values from 9.928856e-16 to 1.5886169e-14
- down_square: float32 [8192, 2048], P('tensor', 'dp'), may hold values from 9.928856e-16 to 1.5886169e-14
- vectors_square: float32 [6, 2048], replicated, may hold values from 1.5886169e-14 to 2.541787e-13
- hidden_square: float32 [14336], P('tensor'), may hold values from 1.5886169e-14 to 2.541787e-13
- qkv_frozen: bfloat16 [2048, 6144], P('dp', 'tensor'), may hold values from -0.125 to 0.125
- out_frozen: bfloat16 [2048, 2048], P('tensor', 'dp'), may hold values from -0.5 to 0.5
- up_frozen: bfloat16 [2048, 8192], P('dp', 'tensor'), may hold values from -0.125 to 0.125
- down_frozen: bfloat16 [8192, 2048], P('tensor', 'dp'), may hold values from -0.0625 to 0.0625
- vectors_frozen: float32 [6, 2048], replicated, may hold values from -0.525 to 2.125
- hidden_frozen: float32 [14336], P('tensor'), may hold values from -1.5 to 1.5
Outputs:
- block_out: bfloat16 [4096, 2048], P('dp')
- input_grad: float32 [4096, 2048], P('dp')
- grad_norm: float32 [], replicated
- qkv_mean_new: float32 [2048, 6144], P('dp', 'tensor')
- qkv_square_new: float32 [2048, 6144], P('dp', 'tensor')
- qkv_master_new: float32 [2048, 6144], P('dp', 'tensor')
- out_mean_new: float32 [2048, 2048], P('tensor', 'dp')
- out_square_new: float32 [2048, 2048], P('tensor', 'dp')
- out_master_new: float32 [2048, 2048], P('tensor', 'dp')
- up_mean_new: float32 [2048, 8192], P('dp', 'tensor')
- up_square_new: float32 [2048, 8192], P('dp', 'tensor')
- up_master_new: float32 [2048, 8192], P('dp', 'tensor')
- down_mean_new: float32 [8192, 2048], P('tensor', 'dp')
- down_square_new: float32 [8192, 2048], P('tensor', 'dp')
- down_master_new: float32 [8192, 2048], P('tensor', 'dp')
- vectors_mean_new: float32 [6, 2048], replicated
- vectors_square_new: float32 [6, 2048], replicated
- vectors_new: float32 [6, 2048], replicated
- hidden_mean_new: float32 [14336], P('tensor')
- hidden_square_new: float32 [14336], P('tensor')
- hidden_bias_new: float32 [14336], P('tensor')
The draws below stay inside these ranges and needn't reach their ends.
Inputs may be any that keep to these rules, and one draw needn't show every extreme that they name: `doc_lengths`: each row sums to 512. `vectors`: rows 0 and 2 are gains, the other rows shifts and biases. `head_weight`: frozen head weights of order one over the root of 2048.
All inputs are finite; a program needn't handle non-finite values. No bound on the sum of `desirable` on one device may be relied on, other than what follows from the above.
Results may differ from the reference program's by a relative error of at most 0.015.
Values may be sent and summed in bfloat16 or wider, within the bound.
A program may use at most 256 MiB of HBM per device.

```python
import math
import jax
import jax.numpy as jnp
import numpy as np
from jax import lax

D = 2048
H = 16
HD = 128
ROT = 32
FF = 8192
V = 25600
TOK_DEV = 512
SEGS = 4
STEP = 3
TOKENS = 4096
PARAMS = 50358272
N_DP = 8
N_TENSOR = 4


def rising(count, start_value, end_value):
    steps_along = jnp.arange(count, dtype=jnp.float32) / (count - 1)
    return start_value + (end_value - start_value) * steps_along


def feature_profile():
    return rising(D, 0.4, 1.4)


def shared_rows(key):
    noise = jnp.clip(jax.random.normal(key, (6, D), jnp.float32), -3.5, 3.5)
    profile = feature_profile()
    zero_row = jnp.zeros((D,), jnp.float32)
    base = jnp.stack([profile, zero_row, profile, zero_row, zero_row, zero_row])
    return base + 0.15 * noise


def draw_vectors(key, part):
    return shared_rows(jax.random.fold_in(key, 11))


def draw_vectors_frozen(key, part):
    return shared_rows(jax.random.fold_in(key, 23))


def draw_head_weight(key, part):
    own_key = jax.random.fold_in(key, 37)
    noise = jnp.clip(jax.random.normal(own_key, (D, V), jnp.float32), -6.0, 6.0)
    profile = feature_profile()
    return (noise * profile[:, None] * D ** (-0.5)).astype(jnp.bfloat16)


def set_ends(entries, stream_key, least, high):
    spot = [jax.random.randint(jax.random.fold_in(stream_key, axis), (), 0, length) for axis, length in enumerate(entries.shape)]
    longest = entries.shape.index(max(entries.shape))
    beside = spot[:longest] + [(spot[longest] + 1) % entries.shape[longest]] + spot[longest + 1:]
    return entries.at[tuple(spot)].set(least).at[tuple(beside)].set(high)


def level_of(stream_key, shape, cuts, low, high):
    gain, own = 1.0, jax.random.fold_in(stream_key, 6)
    for dim, shards_of in cuts:
        heights = jnp.exp(jax.random.uniform(jax.random.fold_in(own, dim), (shards_of,), jnp.float32, low / len(cuts), high / len(cuts)))
        gain = gain * jnp.repeat(heights, shape[dim] // shards_of).reshape([-1 if axis == dim else 1 for axis in range(len(shape))])
    return gain


def split_up(count, total, reach, slope):
    portions = [(1 << 20) // math.isqrt(rank ** slope) + 1 for rank in range(2, count + 1)]
    surplus, given = total - reach - (count - 1), [1] * (count - 1)
    while surplus > 0:
        candidates = [i for i in range(count - 1) if given[i] < reach]
        pool, remaining = sum([portions[i] for i in candidates]), surplus
        for i in candidates:
            extra = min(reach - given[i], max(1, remaining * portions[i] // pool), surplus)
            given[i] = given[i] + extra
            surplus = surplus - extra
    return np.array([reach] + given)


def uneven_parts(stream_key, number_of, total, most, lean):
    if number_of == 2:
        one = jax.random.randint(stream_key, (), max(1, total - most), min(most, total - 1) + 1)
        return jnp.stack([one, total - one])
    sizes = jnp.asarray(split_up(number_of, total, most, lean), jnp.int32)
    pairs = (number_of - 1) // 2
    source_of, taker = sizes[1:1 + 2 * pairs:2], sizes[2:2 + 2 * pairs:2]
    slack = jnp.minimum(source_of - 1, most - taker)
    shifted = jax.random.randint(jax.random.fold_in(stream_key, 1), (pairs,), 0, 1 << 20) % (slack + 1)
    sizes = sizes.at[1:1 + 2 * pairs:2].set(source_of - shifted).at[2:2 + 2 * pairs:2].set(taker + shifted)
    return sizes[jax.random.permutation(jax.random.fold_in(stream_key, 2), number_of)]


def scatter_about(stream_key, extent, deviation, most, split=(), held_as=jnp.bfloat16):
    array = jax.random.normal(stream_key, extent, jnp.float32) * deviation
    if len(split) > 0:
        array = level_of(stream_key, extent, split, -0.22, 0.18) * array
    return jnp.clip(array, min=-most, max=most).astype(held_as)


def setup_inputs(seed: int = 0) -> dict:
    key_of = jax.random.split(jax.random.key(seed), 30)
    inputs = scatter_about(key_of[0], (TOKENS, D), 1.0, 6.0, ((0, 8),))
    targets = set_ends(jax.random.randint(key_of[1], (TOKENS,), 0, V), jax.random.fold_in(key_of[1], 1), 0, V - 1).astype(jnp.int32)
    doc_lengths = jax.vmap(lambda own: uneven_parts(own, SEGS, TOK_DEV, 3 * TOK_DEV // 4, 2))(jax.random.split(key_of[2], N_DP)).reshape((N_DP, SEGS)).astype(jnp.int32)
    desirable = set_ends((jax.random.randint(key_of[3], (N_DP, SEGS), 0, 2) < 1).astype(jnp.int32), jax.random.fold_in(key_of[3], 1), 0, 1)
    head_weight = draw_head_weight(jax.random.fold_in(key_of[29], 71), 0)
    qkv_master = scatter_about(key_of[5], (D, 3 * D), D ** -0.5, 0.125, ((0, 8), (1, 4)), jnp.float32)
    out_master = scatter_about(key_of[6], (D, D), (D // 16) ** -0.5, 0.5, ((0, 4), (1, 8)), jnp.float32)
    up_master = scatter_about(key_of[7], (D, FF), D ** -0.5, 0.125, ((0, 8), (1, 4)), jnp.float32)
    down_master = scatter_about(key_of[8], (FF, D), FF ** -0.5, 0.0625, ((0, 4), (1, 8)), jnp.float32)
    vectors = draw_vectors(jax.random.fold_in(key_of[29], 71), 0)
    hidden_bias = scatter_about(key_of[10], (3 * D + FF,), 0.1, 1.5, ((0, 4),), jnp.float32)
    qkv_mean = scatter_about(key_of[11], (D, 3 * D), (0.00111 / PARAMS ** 0.5), 2.384185791015625e-06, ((0, 8), (1, 4)), jnp.float32)
    out_mean = scatter_about(key_of[12], (D, D), (0.00111 / PARAMS ** 0.5), 2.384185791015625e-06, ((0, 4), (1, 8)), jnp.float32)
    up_mean = scatter_about(key_of[13], (D, FF), (0.00111 / PARAMS ** 0.5), 2.384185791015625e-06, ((0, 8), (1, 4)), jnp.float32)
    down_mean = scatter_about(key_of[14], (FF, D), (0.00111 / PARAMS ** 0.5), 2.384185791015625e-06, ((0, 4), (1, 8)), jnp.float32)
    vectors_mean = scatter_about(key_of[15], (6, D), (0.0044 / PARAMS ** 0.5), 9.5367431640625e-06, (), jnp.float32)
    hidden_mean = scatter_about(key_of[16], (3 * D + FF,), (0.0044 / PARAMS ** 0.5), 9.5367431640625e-06, ((0, 4),), jnp.float32)
    qkv_square = jnp.clip(jnp.exp(math.log(1.588616899432429e-14) - 2.7725887 * jax.random.uniform(key_of[17], (D, 3 * D), jnp.float32) ** level_of(key_of[17], (D, 3 * D), ((0, 8), (1, 4)), -0.2, 0.2)), 9.92885562145268e-16, 1.588616899432429e-14)
    out_square = jnp.clip(jnp.exp(math.log(1.588616899432429e-14) - 2.7725887 * jax.random.uniform(key_of[18], (D, D), jnp.float32) ** level_of(key_of[18], (D, D), ((0, 4), (1, 8)), -0.2, 0.2)), 9.92885562145268e-16, 1.588616899432429e-14)
    up_square = jnp.clip(jnp.exp(math.log(1.588616899432429e-14) - 2.7725887 * jax.random.uniform(key_of[19], (D, FF), jnp.float32) ** level_of(key_of[19], (D, FF), ((0, 8), (1, 4)), -0.2, 0.2)), 9.92885562145268e-16, 1.588616899432429e-14)
    down_square = jnp.clip(jnp.exp(math.log(1.588616899432429e-14) - 2.7725887 * jax.random.uniform(key_of[20], (FF, D), jnp.float32) ** level_of(key_of[20], (FF, D), ((0, 4), (1, 8)), -0.2, 0.2)), 9.92885562145268e-16, 1.588616899432429e-14)
    vectors_square = jnp.clip(jnp.exp(jax.random.uniform(key_of[21], (6, D), jnp.float32, math.log(1.588616899432429e-14), math.log(2.541787039091886e-13))), 1.588616899432429e-14, 2.541787039091886e-13)
    hidden_square = jnp.clip(jnp.exp(math.log(2.541787039091886e-13) - 2.7725887 * jax.random.uniform(key_of[22], (3 * D + FF,), jnp.float32) ** level_of(key_of[22], (3 * D + FF,), ((0, 4),), -0.2, 0.2)), 1.588616899432429e-14, 2.541787039091886e-13)
    qkv_frozen = scatter_about(key_of[23], (D, 3 * D), D ** -0.5, 0.125, ((0, 8), (1, 4)))
    out_frozen = scatter_about(key_of[24], (D, D), (D // 16) ** -0.5, 0.5, ((0, 4), (1, 8)))
    up_frozen = scatter_about(key_of[25], (D, FF), D ** -0.5, 0.125, ((0, 8), (1, 4)))
    down_frozen = scatter_about(key_of[26], (FF, D), FF ** -0.5, 0.0625, ((0, 4), (1, 8)))
    vectors_frozen = draw_vectors_frozen(jax.random.fold_in(key_of[29], 71), 0)
    hidden_frozen = scatter_about(key_of[28], (3 * D + FF,), 0.1, 1.5, ((0, 4),), jnp.float32)
    return dict(inputs=inputs, targets=targets, doc_lengths=doc_lengths, desirable=desirable, head_weight=head_weight, qkv_master=qkv_master, out_master=out_master, up_master=up_master, down_master=down_master, vectors=vectors, hidden_bias=hidden_bias, qkv_mean=qkv_mean, out_mean=out_mean, up_mean=up_mean, down_mean=down_mean, vectors_mean=vectors_mean, hidden_mean=hidden_mean, qkv_square=qkv_square, out_square=out_square, up_square=up_square, down_square=down_square, vectors_square=vectors_square, hidden_square=hidden_square, qkv_frozen=qkv_frozen, out_frozen=out_frozen, up_frozen=up_frozen, down_frozen=down_frozen, vectors_frozen=vectors_frozen, hidden_frozen=hidden_frozen)


@jax.custom_vjp
def low(v):
    return lax.optimization_barrier(v.astype(jnp.bfloat16)).astype(jnp.float32)

@jax.custom_vjp
def low_back(v):
    return v

def low_keep(v):
    return (low(v), None)

def low_pass(kept, grad):
    return (grad,)

def back_keep(v):
    return (v, None)

def back_low(kept, grad):
    return (low(grad),)
low.defvjp(low_keep, low_pass)
low_back.defvjp(back_keep, back_low)
EPS_NORM = 1e-05
BETA_KTO = 0.1
CLIP_NORM = 0.01
LEARN_RATE = 0.02
VECTOR_RATE = 0.2
BETA_FIRST = 0.9
BETA_SECOND = 0.999
ADAM_EPS = 1e-08
WEIGHT_DECAY = 0.01
MASKED = -1e+30
HIGH = lax.Precision.HIGHEST

def layer_norm(values, gain_row, shift_row):
    centre = values - lax.optimization_barrier(jnp.mean(values, axis=-1, keepdims=True))
    spread = lax.optimization_barrier(jnp.mean(centre * centre, axis=-1, keepdims=True))
    return centre * lax.rsqrt(spread + EPS_NORM) * gain_row + shift_row

def rotate(values, positions, direction):
    half_rot = ROT // 2
    frequency = 10000.0 ** (-2.0 * jnp.arange(half_rot, dtype=jnp.float32) / ROT)
    angles = positions.astype(jnp.float32)[:, None] * frequency[None, :]
    cosine = jnp.cos(angles)[:, None, :]
    sine_part = direction * jnp.sin(angles)[:, None, :]
    first_half = values[..., :half_rot]
    second_half = values[..., half_rot:ROT]
    return jnp.concatenate([first_half * cosine - second_half * sine_part, second_half * cosine + first_half * sine_part, values[..., ROT:]], axis=-1)

def doc_layout(lengths_row, row_count):
    lengths_row = lengths_row.astype(jnp.int32)
    doc_ends = jnp.cumsum(lengths_row).astype(jnp.int32)
    starts = (doc_ends - lengths_row).astype(jnp.int32)
    index_rows = jnp.arange(row_count, dtype=jnp.int32)
    member = (index_rows[:, None] >= starts[None, :]) & (index_rows[:, None] < doc_ends[None, :])
    doc_ids = jnp.arange(lengths_row.shape[0], dtype=jnp.int32)
    doc_of = lax.optimization_barrier(jnp.sum(jnp.where(member, doc_ids[None, :], 0), axis=1)).astype(jnp.int32)
    positions = (index_rows - lax.optimization_barrier(jnp.sum(jnp.where(member, starts[None, :], 0), axis=1))).astype(jnp.int32)
    allowed = (doc_of[:, None] == doc_of[None, :]) & (index_rows[:, None] >= index_rows[None, :])
    return (member, positions, allowed)

def split_hidden(bias_all):
    grouped = bias_all.reshape(N_TENSOR, -1)
    cut_at = 3 * D // N_TENSOR
    return (grouped[:, :cut_at].reshape(-1), grouped[:, cut_at:].reshape(-1))

def block_forward(param_set, block_in, block_targets, block_lengths, head_full):
    qkv_weight, out_weight, up_weight, down_weight, vector_rows, bias_all = param_set
    row_count = block_in.shape[0]
    member, positions, allowed = doc_layout(block_lengths, row_count)
    qkv_bias, up_bias = split_hidden(bias_all)
    normed_one = layer_norm(block_in, vector_rows[0], vector_rows[1])
    normed_two = layer_norm(block_in, vector_rows[2], vector_rows[3])
    mixed_proj = jnp.dot(low(normed_one), low(qkv_weight), precision=HIGH) + qkv_bias
    mixed_proj = low_back(mixed_proj).reshape(row_count, H, 3, HD)
    query_low = low(rotate(mixed_proj[:, :, 0], positions, 1.0))
    key_low = low(rotate(mixed_proj[:, :, 1], positions, 1.0))
    value_low = low(mixed_proj[:, :, 2])
    scores = jnp.einsum('qhd,khd->hqk', query_low, key_low, precision=HIGH)
    scores = low_back(scores * HD ** (-0.5))
    scores = jnp.where(allowed[None], scores, MASKED)
    probs_low = low(jax.nn.softmax(scores, axis=-1))
    attended = jnp.einsum('hqk,khd->qhd', probs_low, value_low, precision=HIGH).reshape(row_count, D)
    attended = low(low_back(attended))
    hidden = low_back(jnp.dot(low(normed_two), low(up_weight), precision=HIGH) + up_bias)
    active = low(jax.nn.gelu(hidden, approximate=False))
    branch = jnp.dot(attended, low(out_weight), precision=HIGH) + jnp.dot(active, low(down_weight), precision=HIGH)
    branch = low_back(branch + vector_rows[4] + vector_rows[5])
    final_out = block_in + branch
    logits = low_back(jnp.dot(low(final_out), head_full, precision=HIGH))
    log_total = jax.nn.logsumexp(logits, axis=-1)
    picked = jnp.take_along_axis(logits, block_targets[:, None].astype(jnp.int32), axis=1)[:, 0]
    doc_sums = lax.optimization_barrier(jnp.sum(jnp.where(member, (picked - log_total)[:, None], 0.0), axis=0))
    return (final_out, doc_sums)

def forward_all(param_set, inputs_f32, targets, doc_lengths, head_full):

    def one_block(params_in, carried):
        block_in, block_targets, block_lengths = carried
        return block_forward(params_in, block_in, block_targets, block_lengths, head_full)
    checked = jax.checkpoint(one_block)

    def mapped(carried):
        return checked(param_set, carried)
    finals, doc_sums = lax.map(mapped, (inputs_f32.reshape(N_DP, TOK_DEV, D), targets.reshape(N_DP, TOK_DEV), doc_lengths))
    return (finals.reshape(N_DP * TOK_DEV, D), doc_sums)

def kto_loss(policy_docs, frozen_docs, desirable, reward_shift):
    reward = policy_docs - frozen_docs
    labels = desirable.astype(reward.dtype)
    good_term = 1.0 - jax.nn.sigmoid(BETA_KTO * (reward - reward_shift))
    bad_term = 1.0 - jax.nn.sigmoid(BETA_KTO * (reward_shift - reward))
    return jnp.mean(labels * good_term + (1.0 - labels) * bad_term)

def adam_step(master, mean_old, square_old, gradient, factor, rate, decay_rate):
    clipped = gradient * factor
    mean_new = BETA_FIRST * mean_old + (1.0 - BETA_FIRST) * clipped
    square_new = BETA_SECOND * square_old + (1.0 - BETA_SECOND) * clipped * clipped
    mean_hat = mean_new / (1.0 - BETA_FIRST ** STEP)
    square_hat = square_new / (1.0 - BETA_SECOND ** STEP)
    master_new = master - rate * (mean_hat / (jnp.sqrt(square_hat) + ADAM_EPS) + decay_rate * master)
    return (mean_new, square_new, master_new)

def reference(inputs, targets, doc_lengths, desirable, head_weight, qkv_master, out_master, up_master, down_master, vectors, hidden_bias, qkv_mean, out_mean, up_mean, down_mean, vectors_mean, hidden_mean, qkv_square, out_square, up_square, down_square, vectors_square, hidden_square, qkv_frozen, out_frozen, up_frozen, down_frozen, vectors_frozen, hidden_frozen):
    head_full = head_weight.astype(jnp.float32)
    inputs_f32 = inputs.astype(jnp.float32)
    params = (qkv_master, out_master, up_master, down_master, vectors, hidden_bias)
    frozen = (qkv_frozen.astype(jnp.float32), out_frozen.astype(jnp.float32), up_frozen.astype(jnp.float32), down_frozen.astype(jnp.float32), vectors_frozen, hidden_frozen)

    def policy_pass(param_set, layer_in):
        return forward_all(param_set, layer_in, targets, doc_lengths, head_full)
    (finals, policy_docs), pull_back = jax.vjp(policy_pass, params, inputs_f32)
    unused, frozen_docs = forward_all(frozen, inputs_f32, targets, doc_lengths, head_full)
    reward_shift = jnp.mean(policy_docs - frozen_docs)
    doc_grad = jax.grad(kto_loss)(policy_docs, frozen_docs, desirable, reward_shift)
    param_grads, input_grad = pull_back((jnp.zeros_like(finals), doc_grad))
    total_square = jnp.sum(param_grads[0] * param_grads[0]) + jnp.sum(param_grads[1] * param_grads[1]) + jnp.sum(param_grads[2] * param_grads[2]) + jnp.sum(param_grads[3] * param_grads[3]) + jnp.sum(param_grads[4] * param_grads[4]) + jnp.sum(param_grads[5] * param_grads[5])
    grad_norm = jnp.sqrt(total_square)
    factor = jnp.minimum(1.0, CLIP_NORM / (grad_norm + 1e-06))
    qkv_state = adam_step(qkv_master, qkv_mean, qkv_square, param_grads[0], factor, LEARN_RATE, WEIGHT_DECAY)
    out_state = adam_step(out_master, out_mean, out_square, param_grads[1], factor, LEARN_RATE, WEIGHT_DECAY)
    up_state = adam_step(up_master, up_mean, up_square, param_grads[2], factor, LEARN_RATE, WEIGHT_DECAY)
    down_state = adam_step(down_master, down_mean, down_square, param_grads[3], factor, LEARN_RATE, WEIGHT_DECAY)
    vector_state = adam_step(vectors, vectors_mean, vectors_square, param_grads[4], factor, VECTOR_RATE, 0.0)
    hidden_state = adam_step(hidden_bias, hidden_mean, hidden_square, param_grads[5], factor, VECTOR_RATE, 0.0)
    return (finals.astype(jnp.bfloat16), input_grad, grad_norm, qkv_state[0], qkv_state[1], qkv_state[2], out_state[0], out_state[1], out_state[2], up_state[0], up_state[1], up_state[2], down_state[0], down_state[1], down_state[2], vector_state[0], vector_state[1], vector_state[2], hidden_state[0], hidden_state[1], hidden_state[2])
```

```python
import functools

import jax
import jax.numpy as jnp
from jax import lax
from jax.experimental import pallas as pl
from jax.experimental.pallas import tpu as pltpu
from jax.sharding import PartitionSpec as P

HD = 128
ROT = 32
SEGS = 4
STEP = 3
SPLIT = 4
QUARTERS = 4


EPS_NORM = 1e-05
BETA_KTO = 0.1
CLIP_NORM = 0.01
LEARN_RATE = 0.02
VECTOR_RATE = 0.2
BETA_FIRST = 0.9
BETA_SECOND = 0.999
ADAM_EPS = 1e-08
WEIGHT_DECAY = 0.01
MASKED = -1e30

MESH = pl.DeviceIdType.MESH
BF16 = jnp.bfloat16
F32 = jnp.float32
ANY_SPEC = pl.BlockSpec(memory_space=pltpu.HBM)
VMEM_SPEC = pl.BlockSpec(memory_space=pltpu.VMEM)


class Place:
    def __init__(self, inner):
        self.inner = inner
        self.dp = lax.axis_index("dp")
        self.t = lax.axis_index("tensor")
        self.o = self.dp // inner
        self.i = self.dp % inner
        self.near = self.t + 1 - 2 * (self.t % 2)
        self.far = (self.t + 2) % QUARTERS

    def outer_peer(self, shift):
        return (((self.o + shift) % SPLIT) * self.inner + self.i, self.t)

    def inner_peer(self, shift):
        return (self.o * self.inner + (self.i + shift) % self.inner, self.t)

    def near_peer(self):
        return (self.dp, self.near)

    def far_peer(self):
        return (self.dp, self.far)


def aligned(shard):
    return shard % 128 == 0


def greet(peers):
    barrier = pltpu.get_barrier_semaphore()
    for peer in peers:
        pl.semaphore_signal(barrier, inc=1, device_id=peer, device_id_type=MESH)
    pl.semaphore_wait(barrier, len(peers))


def remote(src, dst, send_sem, recv_sem, peer):
    copy = pltpu.make_async_remote_copy(
        src_ref=src,
        dst_ref=dst,
        send_sem=send_sem,
        recv_sem=recv_sem,
        device_id=peer,
        device_id_type=MESH,
    )
    copy.start()
    return copy


def spread_weights_kernel(inner, with_tokens, *refs):
    here = Place(inner)
    if with_tokens:
        (qkv, out, up, down, tokens, lengths, qkv_all, up_all, low_all, tokens_all, lengths_all,
         send_o, recv_o, send_i, recv_i, local, send_t, recv_t, send_l, recv_l) = refs
    else:
        qkv, out, up, down, qkv_all, up_all, low_all, send_o, recv_o, send_i, recv_i, local = refs
    shard = qkv.shape[0]
    width_qkv, width_up = qkv.shape[1] // SPLIT, up.shape[1] // SPLIT
    width_out, width_down = out.shape[0] // SPLIT, down.shape[0] // SPLIT

    def src(m, part):
        if m == 0:
            return qkv.at[:, pl.ds(part * width_qkv, width_qkv)]
        if m == 1:
            return up.at[:, pl.ds(part * width_up, width_up)]
        if m == 2:
            return out.at[pl.ds(part * width_out, width_out), :]
        return down.at[pl.ds(part * width_down, width_down), :]

    def dst(m, index):
        where = pl.ds(index * shard, shard)
        if m == 0:
            return qkv_all.at[where, :]
        if m == 1:
            return up_all.at[where, :]
        rows = pl.ds(0, width_out) if m == 2 else pl.ds(width_out, width_down)
        return low_all.at[rows, where] if aligned(shard) else low_all.at[index, rows, :]

    peers = [here.outer_peer(s) for s in range(1, SPLIT)]
    peers += [here.inner_peer(r) for r in range(1, inner)]
    if with_tokens:
        peers += [here.far_peer(), here.near_peer()]
    greet(peers)

    waits = []
    token_copies = []
    if with_tokens:
        rows = tokens.shape[0] // QUARTERS

        def piece(part, quarter):
            return tokens_all.at[pl.ds((part * QUARTERS + quarter) * rows, rows), :]

        for s in range(1, SPLIT):
            token_copies.append(
                remote(
                    tokens.at[pl.ds(here.t * rows, rows), :],
                    piece(here.o, here.t),
                    send_t.at[0, s - 1],
                    recv_t.at[0, s - 1],
                    here.outer_peer(s),
                )
            )
        for s in range(1, SPLIT):
            waits.append(
                remote(
                    lengths,
                    lengths_all.at[here.o],
                    send_l.at[s - 1],
                    recv_l.at[s - 1],
                    here.outer_peer(s),
                )
            )
    first = {}
    for m in range(4):
        for s in range(1, SPLIT):
            first[m, s] = remote(
                src(m, (here.o + s) % SPLIT),
                dst(m, here.dp),
                send_o.at[m, s - 1],
                recv_o.at[m, s - 1],
                here.outer_peer(s),
            )
    own = []
    for m in range(4):
        own.append(pltpu.make_async_copy(src(m, here.o), dst(m, here.dp), local.at[m]))
    if with_tokens:
        block = tokens.shape[0]
        own.append(
            pltpu.make_async_copy(
                tokens, tokens_all.at[pl.ds(here.o * block, block), :], local.at[4]
            )
        )
        own.append(pltpu.make_async_copy(lengths, lengths_all.at[here.o], local.at[5]))
    for copy in own:
        copy.start()
    for m in range(4):
        for r in range(1, inner):
            waits.append(
                remote(
                    src(m, here.o),
                    dst(m, here.dp),
                    send_i.at[m, 0, r - 1],
                    recv_i.at[m, 0, r - 1],
                    here.inner_peer(r),
                )
            )
    across = {}
    if with_tokens:
        for s in range(1, SPLIT):
            token_copies[s - 1].wait_recv()
            part = (here.o + SPLIT - s) % SPLIT
            across[s] = remote(
                piece(part, here.t),
                piece(part, here.t),
                send_t.at[1, s - 1],
                recv_t.at[1, s - 1],
                here.far_peer(),
            )
            waits.append(
                remote(
                    piece(part, here.t),
                    piece(part, here.t),
                    send_t.at[2, s - 1],
                    recv_t.at[2, s - 1],
                    here.near_peer(),
                )
            )
    for m in range(4):
        for s in range(1, SPLIT):
            first[m, s].wait_recv()
            index = ((here.o + SPLIT - s) % SPLIT) * inner + here.i
            for r in range(1, inner):
                waits.append(
                    remote(
                        dst(m, index),
                        dst(m, index),
                        send_i.at[m, s, r - 1],
                        recv_i.at[m, s, r - 1],
                        here.inner_peer(r),
                    )
                )
    if with_tokens:
        for s in range(1, SPLIT):
            across[s].wait_recv()
            part = (here.o + SPLIT - s) % SPLIT
            waits.append(
                remote(
                    piece(part, here.far),
                    piece(part, here.far),
                    send_t.at[3, s - 1],
                    recv_t.at[3, s - 1],
                    here.near_peer(),
                )
            )
        for copy in token_copies:
            copy.wait_send()
        for copy in across.values():
            copy.wait_send()
    for copy in first.values():
        copy.wait_send()
    for copy in own:
        copy.wait()
    for copy in waits:
        copy.wait()


def spread_weights(shards, inner, tokens, lengths, number):
    qkv, out, up, down = shards
    d_model = out.shape[1] * SPLIT * inner
    width = out.shape[0] // SPLIT + down.shape[0] // SPLIT
    shapes = [
        jax.ShapeDtypeStruct((d_model, qkv.shape[1] // SPLIT), BF16),
        jax.ShapeDtypeStruct((d_model, up.shape[1] // SPLIT), BF16),
        jax.ShapeDtypeStruct(
            (width, d_model) if aligned(out.shape[1]) else (SPLIT * inner, width, out.shape[1]),
            BF16,
        ),
    ]
    dma = pltpu.SemaphoreType.DMA
    scratch = [
        dma((4, SPLIT - 1)),
        dma((4, SPLIT - 1)),
        dma((4, SPLIT, max(inner - 1, 1))),
        dma((4, SPLIT, max(inner - 1, 1))),
        dma((6,)),
    ]
    operands = [qkv, out, up, down]
    if tokens is not None:
        operands += [tokens, lengths]
        shapes += [
            jax.ShapeDtypeStruct((tokens.shape[0] * SPLIT, tokens.shape[1]), BF16),
            jax.ShapeDtypeStruct((SPLIT, *lengths.shape), lengths.dtype),
        ]
        scratch += [
            dma((4, SPLIT - 1)),
            dma((4, SPLIT - 1)),
            dma((SPLIT - 1,)),
            dma((SPLIT - 1,)),
        ]
    qkv_all, up_all, low_all, *gathered = pl.pallas_call(
        functools.partial(spread_weights_kernel, inner, tokens is not None),
        out_shape=shapes,
        in_specs=[ANY_SPEC] * len(operands),
        out_specs=[ANY_SPEC] * len(shapes),
        scratch_shapes=scratch,
        compiler_params=pltpu.CompilerParams(collective_id=number, has_side_effects=True),
    )(*operands)
    if low_all.ndim == 3:
        low_all = jnp.swapaxes(low_all, 0, 1).reshape(width, d_model)
    return (qkv_all, up_all, low_all, *gathered)


def f32(value):
    return value.astype(F32)


def reduce_rows(here, part_ref, near_in, far_in, far_out, outer_in, outer_out, sems, last):
    rows = far_out.shape[1]
    near_send, near_recv, far_send, far_recv, outer_send, outer_recv = sems

    def rows_of(step, quarter):
        block = (here.o + 1 + step) % SPLIT
        return pl.ds((block * QUARTERS + quarter) * rows, rows)

    near = {}
    for step in range(SPLIT):
        for side, quarter in enumerate(((here.near + 2) % QUARTERS, here.near)):
            near[step, side] = remote(
                part_ref.at[rows_of(step, quarter), :],
                near_in.at[step, side],
                near_send.at[step, side],
                near_recv.at[step, side],
                here.near_peer(),
            )
    far = []
    for step in range(SPLIT):
        near[step, 0].wait_recv()
        far_out[step] = (f32(part_ref[rows_of(step, here.far), :]) + f32(near_in[step, 0])).astype(
            BF16
        )
        far.append(
            remote(
                far_out.at[step],
                far_in.at[step],
                far_send.at[step],
                far_recv.at[step],
                here.far_peer(),
            )
        )
    outer = []
    for step in range(SPLIT):
        near[step, 1].wait_recv()
        far[step].wait_recv()
        total = (
            f32(part_ref[rows_of(step, here.t), :]) + f32(near_in[step, 1]) + f32(far_in[step])
        )
        if step < SPLIT - 1:
            outer_out[step] = total.astype(BF16)
            outer.append(
                remote(
                    outer_out.at[step],
                    outer_in.at[step],
                    outer_send.at[step],
                    outer_recv.at[step],
                    here.outer_peer(step + 1),
                )
            )
        else:
            last(total)
    for copy in outer:
        copy.wait_recv()
    for copy in list(near.values()) + far + outer:
        copy.wait_send()


def gather_quarters(here, ref, rows, send, recv):
    def piece(quarter):
        return ref.at[pl.ds(quarter * rows, rows), :]

    far = remote(piece(here.t), piece(here.t), send.at[0], recv.at[0], here.far_peer())
    near = remote(piece(here.t), piece(here.t), send.at[1], recv.at[1], here.near_peer())
    far.wait_recv()
    passed = remote(piece(here.far), piece(here.far), send.at[2], recv.at[2], here.near_peer())
    near.wait_recv()
    passed.wait_recv()
    for copy in (far, near, passed):
        copy.wait_send()


def reduce_peers(here):
    return [here.outer_peer(s) for s in range(1, SPLIT)] + [here.far_peer(), here.near_peer()]


def branch_kernel(inner, part_ref, tokens_ref, rows_ref, final_ref, total, *scratch):
    here = Place(inner)
    buffers, sems, (send, recv) = scratch[:5], scratch[5:11], scratch[11:]
    rows = total.shape[0]
    greet(reduce_peers(here))
    mine = pl.ds(here.t * rows, rows)

    def last(value):
        total[...] = value

    reduce_rows(here, part_ref, *buffers, sems, last)
    outer_in = buffers[3]
    branch = total[...]
    for step in range(SPLIT - 1):
        branch = branch + f32(outer_in[step])
    branch = branch + rows_ref[0:1, :] + rows_ref[1:2, :]
    final_ref[mine, :] = (f32(tokens_ref[mine, :]) + branch).astype(BF16)
    gather_quarters(here, final_ref, rows, send, recv)


def input_kernel(inner, part_ref, tokens_ref, final_grad_ref, grad_ref, total, *scratch):
    here = Place(inner)
    buffers, sems, (send, recv) = scratch[:5], scratch[5:11], scratch[11:]
    rows = total.shape[0]
    greet(reduce_peers(here))
    mine = pl.ds(here.t * rows, rows)

    def last(value):
        total[...] = value

    reduce_rows(here, part_ref, *buffers, sems, last)
    outer_in = buffers[3]
    scaled = total[...]
    for step in range(SPLIT - 1):
        scaled = scaled + f32(outer_in[step])
    values = f32(tokens_ref[mine, :])
    centre = values - jnp.mean(values, axis=1, keepdims=True)
    spread = jnp.mean(centre * centre, axis=1, keepdims=True)
    scale = lax.rsqrt(spread + EPS_NORM)
    normed = centre * scale
    along = jnp.mean(scaled * normed, axis=1, keepdims=True)
    change = scale * (scaled - jnp.mean(scaled, axis=1, keepdims=True) - normed * along)
    grad_ref[mine, :] = (final_grad_ref[...] + change).astype(BF16)
    gather_quarters(here, grad_ref, rows, send, recv)


def reduce_scratch(rows, width):
    dma = pltpu.SemaphoreType.DMA
    return [
        pltpu.VMEM((rows, width), F32),
        pltpu.VMEM((SPLIT, 2, rows, width), BF16),
        pltpu.VMEM((SPLIT, rows, width), BF16),
        pltpu.VMEM((SPLIT, rows, width), BF16),
        pltpu.VMEM((SPLIT - 1, rows, width), BF16),
        pltpu.VMEM((SPLIT - 1, rows, width), BF16),
        dma((SPLIT, 2)),
        dma((SPLIT, 2)),
        dma((SPLIT,)),
        dma((SPLIT,)),
        dma((SPLIT - 1,)),
        dma((SPLIT - 1,)),
        dma((3,)),
        dma((3,)),
    ]


def reduce_call(body, inner, part, tokens, extra, number):
    block, width = tokens.shape
    return pl.pallas_call(
        functools.partial(body, inner),
        out_shape=jax.ShapeDtypeStruct((block, width), BF16),
        in_specs=[VMEM_SPEC] * 3,
        out_specs=VMEM_SPEC,
        scratch_shapes=reduce_scratch(block // QUARTERS, width),
        compiler_params=pltpu.CompilerParams(
            collective_id=number, has_side_effects=True, vmem_limit_bytes=56 * 1024 * 1024
        ),
    )(part, tokens, extra)


def final_grad_kernel(
    inner, part_ref, quarter_ref, branch_all, near_in, far_in, far_out, low, near_out,
    near_send, near_recv, far_send, far_recv, send, recv, local,
):
    here = Place(inner)
    rows = quarter_ref.shape[0]
    greet(reduce_peers(here))

    def rows_of(quarter):
        return pl.ds(quarter * rows, rows)

    near = []
    for side, quarter in enumerate(((here.near + 2) % QUARTERS, here.near)):
        near_out[side] = part_ref[rows_of(quarter), :].astype(BF16)
        near.append(
            remote(
                near_out.at[side],
                near_in.at[side],
                near_send.at[side],
                near_recv.at[side],
                here.near_peer(),
            )
        )
    near[0].wait_recv()
    far_out[...] = (part_ref[rows_of(here.far), :] + f32(near_in[0])).astype(BF16)
    far = remote(far_out, far_in, far_send, far_recv, here.far_peer())
    near[1].wait_recv()
    far.wait_recv()
    quarter_ref[...] = part_ref[rows_of(here.t), :] + f32(near_in[1]) + f32(far_in[...])
    low[...] = quarter_ref[...].astype(BF16)
    for copy in near + [far]:
        copy.wait_send()

    def piece(part, quarter):
        return branch_all.at[pl.ds((part * QUARTERS + quarter) * rows, rows), :]

    outer = [
        remote(
            low, piece(here.o, here.t), send.at[0, s], recv.at[0, s], here.outer_peer(s)
        )
        for s in range(1, SPLIT)
    ]
    own = pltpu.make_async_copy(low, piece(here.o, here.t), local)
    own.start()
    across, beside = [], []
    for s in range(SPLIT):
        part = (here.o + SPLIT - s) % SPLIT
        if s:
            outer[s - 1].wait_recv()
        source = piece(part, here.t) if s else low
        across.append(
            remote(source, piece(part, here.t), send.at[1, s], recv.at[1, s], here.far_peer())
        )
        beside.append(
            remote(source, piece(part, here.t), send.at[2, s], recv.at[2, s], here.near_peer())
        )
    for s in range(SPLIT):
        part = (here.o + SPLIT - s) % SPLIT
        across[s].wait_recv()
        beside.append(
            remote(
                piece(part, here.far),
                piece(part, here.far),
                send.at[3, s],
                recv.at[3, s],
                here.near_peer(),
            )
        )
    for copy in beside:
        copy.wait_recv()
    for copy in outer + across + beside:
        copy.wait_send()
    own.wait()


def final_grad_call(part, inner, number):
    block, width = part.shape
    rows = block // QUARTERS
    dma = pltpu.SemaphoreType.DMA
    return pl.pallas_call(
        functools.partial(final_grad_kernel, inner),
        out_shape=[
            jax.ShapeDtypeStruct((rows, width), F32),
            jax.ShapeDtypeStruct((SPLIT * block, width), BF16),
        ],
        in_specs=[VMEM_SPEC],
        out_specs=[VMEM_SPEC, ANY_SPEC],
        scratch_shapes=[
            pltpu.VMEM((2, rows, width), BF16),
            pltpu.VMEM((rows, width), BF16),
            pltpu.VMEM((rows, width), BF16),
            pltpu.VMEM((rows, width), BF16),
            pltpu.VMEM((2, rows, width), BF16),
            dma((2,)),
            dma((2,)),
            dma,
            dma,
            dma((4, SPLIT)),
            dma((4, SPLIT)),
            dma,
        ],
        compiler_params=pltpu.CompilerParams(
            collective_id=number, has_side_effects=True, vmem_limit_bytes=48 * 1024 * 1024
        ),
    )(part)


def weight_grads_kernel(inner, qkv, up, low, *refs):
    here = Place(inner)
    outs, inputs, sends = refs[:4], refs[4:8], refs[8:12]
    send_i, recv_i, send_o, recv_o, local = refs[12:]
    shard = outs[0].shape[0]
    width_out = outs[2].shape[0] // SPLIT
    width_down = outs[3].shape[0] // SPLIT

    def src(m, index):
        where = pl.ds(index * shard, shard)
        if m == 0:
            return qkv.at[where, :]
        if m == 1:
            return up.at[where, :]
        rows = pl.ds(0, width_out) if m == 2 else pl.ds(width_out, width_down)
        return low.at[rows, where] if aligned(shard) else low.at[index, rows, :]

    def dst(m):
        if m < 2:
            width = outs[m].shape[1] // SPLIT
            return outs[m].at[:, pl.ds(here.o * width, width)]
        width = outs[m].shape[0] // SPLIT
        return outs[m].at[pl.ds(here.o * width, width), :]

    peers = [here.outer_peer(s) for s in range(1, SPLIT)]
    peers += [here.inner_peer(r) for r in range(1, inner)]
    greet(peers)
    order = (2, 3, 1, 0)
    first = {}
    for m in order:
        for s in range(SPLIT):
            part = (here.o + s) % SPLIT
            for r in range(1, inner):
                first[m, s, r] = remote(
                    src(m, part * inner + (here.i + r) % inner),
                    inputs[m].at[s, r - 1],
                    send_i.at[m, s, r - 1],
                    recv_i.at[m, s, r - 1],
                    here.inner_peer(r),
                )
    last, own = [], []
    for m in order:
        for s in range(SPLIT):
            part = (here.o + s) % SPLIT
            total = f32(src(m, part * inner + here.i)[...])
            for r in range(1, inner):
                first[m, s, r].wait_recv()
                total = total + f32(inputs[m][s, r - 1])
            sends[m][s] = total.astype(BF16)
            if s:
                last.append(
                    remote(
                        sends[m].at[s],
                        dst(m),
                        send_o.at[m, s - 1],
                        recv_o.at[m, s - 1],
                        here.outer_peer(s),
                    )
                )
            else:
                copy = pltpu.make_async_copy(sends[m].at[0], dst(m), local.at[m])
                copy.start()
                own.append(copy)
    for copy in last:
        copy.wait()
    for copy in own:
        copy.wait()
    for copy in first.values():
        copy.wait_send()


def weight_grads_call(grads, shards, inner, number):
    dma = pltpu.SemaphoreType.DMA
    qkv, out, up, down = shards
    ordered = (qkv, up, out, down)
    if not aligned(out[1]):
        low = grads[2].reshape(grads[2].shape[0], SPLIT * inner, out[1])
        grads = (*grads[:2], jnp.swapaxes(low, 0, 1))
    pieces = [
        (qkv[0], qkv[1] // SPLIT),
        (up[0], up[1] // SPLIT),
        (out[0] // SPLIT, out[1]),
        (down[0] // SPLIT, down[1]),
    ]
    peers = max(inner - 1, 1)
    return pl.pallas_call(
        functools.partial(weight_grads_kernel, inner),
        out_shape=[jax.ShapeDtypeStruct(shape, BF16) for shape in ordered],
        in_specs=[VMEM_SPEC] * 3,
        out_specs=[ANY_SPEC] * 4,
        scratch_shapes=[pltpu.VMEM((SPLIT, peers, *piece), BF16) for piece in pieces]
        + [pltpu.VMEM((SPLIT, *piece), BF16) for piece in pieces]
        + [
            dma((4, SPLIT, peers)),
            dma((4, SPLIT, peers)),
            dma((4, SPLIT - 1)),
            dma((4, SPLIT - 1)),
            dma((4,)),
        ],
        compiler_params=pltpu.CompilerParams(
            collective_id=number, has_side_effects=True, vmem_limit_bytes=48 * 1024 * 1024
        ),
    )(*grads)


def combined_all(value, axis, join):
    pieces = jax.tree.map(lambda part: lax.all_gather(part, axis), value)
    head = jax.tree.map(lambda part: part[0], pieces)
    tail = jax.tree.map(lambda part: part[1:], pieces)
    total, _ = lax.scan(lambda total, section: (join(total, section), None), head, tail)
    return total


def rotate(values, positions, direction):
    half_rot = ROT // 2
    frequency = 10000.0 ** (-2.0 * jnp.arange(half_rot, dtype=F32) / ROT)
    angles = positions.astype(F32)[..., None] * frequency
    cosine = jnp.cos(angles)[..., None, :]
    sine_part = direction * jnp.sin(angles)[..., None, :]
    first_half = values[..., :half_rot]
    second_half = values[..., half_rot:ROT]
    return jnp.concatenate(
        [
            first_half * cosine - second_half * sine_part,
            second_half * cosine + first_half * sine_part,
            values[..., ROT:],
        ],
        axis=-1,
    )


def doc_layout(lengths_row, row_count):
    ends, run = [], 0
    for segment in range(lengths_row.shape[0]):
        run = run + lengths_row[segment]
        ends.append(run)
    doc_ends = jnp.stack(ends)
    starts = doc_ends - lengths_row
    index_rows = jnp.arange(row_count, dtype=jnp.int32)
    member = (index_rows[:, None] >= starts[None, :]) & (index_rows[:, None] < doc_ends[None, :])
    doc_ids = jnp.arange(lengths_row.shape[0], dtype=jnp.int32)
    doc_of = jnp.sum(jnp.where(member, doc_ids[None, :], 0), axis=1)
    positions = index_rows - jnp.sum(jnp.where(member, starts[None, :], 0), axis=1)
    return (member, positions, doc_of)


def allowed_keys(doc_of):
    index_rows = jnp.arange(doc_of.shape[-1], dtype=jnp.int32)
    return (doc_of[..., :, None] == doc_of[..., None, :]) & (
        index_rows[:, None] >= index_rows[None, :]
    )


def contract_rows(left_rows, right_rows):
    return lax.dot_general(
        left_rows, right_rows, (((0,), (0,)), ((), ())), preferred_element_type=F32
    )


def contract_cols(left_rows, right_rows):
    return lax.dot_general(
        left_rows, right_rows, (((1,), (1,)), ((), ())), preferred_element_type=F32
    )


def normed_rows(normed, gain_row, shift_row):
    return (normed * gain_row + shift_row).astype(BF16)


def attention_mlp(one_low, two_low, qkv_bias, up_bias, weight_set, positions, allowed):
    qkv_all, up_all, low_all = weight_set
    blocks, block = positions.shape
    heads_local = qkv_bias.shape[0] // (3 * HD)
    mixed_proj = jnp.dot(one_low, qkv_all, preferred_element_type=F32) + qkv_bias
    mixed_proj = mixed_proj.reshape(blocks, block, heads_local, 3, HD)
    query_low = rotate(mixed_proj[:, :, :, 0], positions, 1.0).astype(BF16)
    key_low = rotate(mixed_proj[:, :, :, 1], positions, 1.0).astype(BF16)
    value_low = mixed_proj[:, :, :, 2].astype(BF16)
    scores = jnp.einsum(
        "bqhd,bkhd->bhqk", query_low, key_low, preferred_element_type=F32
    ) * HD ** (-0.5)
    scores = jnp.where(allowed[:, None], scores, MASKED)
    highest = jnp.max(scores, axis=3, keepdims=True)
    log_total = highest + jnp.log(jnp.sum(jnp.exp(scores - highest), axis=3, keepdims=True))
    probs_low = jnp.exp(scores - log_total).astype(BF16)
    attended = jnp.einsum("bhqk,bkhd->bqhd", probs_low, value_low, preferred_element_type=F32)
    attended = attended.reshape(blocks * block, heads_local * HD).astype(BF16)
    hidden = jnp.dot(two_low, up_all, preferred_element_type=F32) + up_bias
    active = jax.nn.gelu(hidden, approximate=False).astype(BF16)
    joined = jnp.concatenate([attended, active], axis=1)
    branch_part = jnp.dot(joined, low_all, preferred_element_type=F32).astype(BF16)
    kept_values = (query_low, key_low, value_low, log_total, hidden, joined)
    return (branch_part, kept_values)


def layer_backward(branch_low, kept_values, weight_set, positions, allowed):
    qkv_all, up_all, low_all = weight_set
    query_low, key_low, value_low, log_total, hidden, joined = kept_values
    blocks, block, heads_local, _ = query_low.shape
    cut = heads_local * HD
    joined_grad = contract_cols(branch_low, low_all)
    active_grad = joined_grad[:, cut:]
    cumulative = 0.5 * (1.0 + lax.erf(hidden * 0.7071067811865476))
    density = jnp.exp(-0.5 * hidden * hidden) * 0.3989422804014327
    hidden_low = (active_grad * (cumulative + hidden * density)).astype(BF16)
    attended_grad = joined_grad[:, :cut].reshape(blocks, block, heads_local, HD).astype(BF16)
    score_scale = HD ** (-0.5)
    scores = (
        jnp.einsum("bqhd,bkhd->bhqk", query_low, key_low, preferred_element_type=F32) * score_scale
    )
    scores = jnp.where(allowed[:, None], scores, MASKED)
    probs = jnp.exp(scores - log_total)
    prob_grad = jnp.einsum("bqhd,bkhd->bhqk", attended_grad, value_low, preferred_element_type=F32)
    value_grad = jnp.einsum(
        "bhqk,bqhd->bkhd", probs.astype(BF16), attended_grad, preferred_element_type=F32
    )
    score_grad = (probs * (prob_grad - jnp.sum(probs * prob_grad, axis=3, keepdims=True))).astype(
        BF16
    )
    query_grad = (
        jnp.einsum("bhqk,bkhd->bqhd", score_grad, key_low, preferred_element_type=F32) * score_scale
    )
    key_grad = (
        jnp.einsum("bhqk,bqhd->bkhd", score_grad, query_low, preferred_element_type=F32)
        * score_scale
    )
    mixed_grad = jnp.stack(
        [rotate(query_grad, positions, -1.0), rotate(key_grad, positions, -1.0), value_grad], axis=3
    )
    mixed_grad = mixed_grad.reshape(blocks * block, heads_local * 3 * HD).astype(BF16)
    one_part = contract_cols(mixed_grad, qkv_all)
    two_part = contract_cols(hidden_low, up_all)
    return (one_part, two_part, mixed_grad, hidden_low)


def vocab_stats(final_low, head_weight, targets, vocab_start):
    logits = jnp.dot(final_low, head_weight, preferred_element_type=F32)
    highest = jnp.max(logits, axis=1)
    log_total = highest + jnp.log(jnp.sum(jnp.exp(logits - highest[:, None]), axis=1))
    column = vocab_start + lax.broadcasted_iota(jnp.int32, logits.shape, 1)
    chosen = column == targets[:, None]
    picked = jnp.sum(jnp.where(chosen, logits, 0.0), axis=1)
    return (logits, log_total, picked, chosen)


def combine_totals(first_set, second_set):
    return (
        jnp.logaddexp(first_set[0], second_set[0]),
        first_set[1] + second_set[1],
        jnp.logaddexp(first_set[2], second_set[2]),
        first_set[3] + second_set[3],
    )


def adam_step(master, mean_old, square_old, gradient, factor, rate, decay_rate):
    clipped = f32(gradient) * factor
    mean_new = BETA_FIRST * mean_old + (1.0 - BETA_FIRST) * clipped
    square_new = BETA_SECOND * square_old + (1.0 - BETA_SECOND) * clipped * clipped
    mean_hat = mean_new / (1.0 - BETA_FIRST**STEP)
    square_hat = square_new / (1.0 - BETA_SECOND**STEP)
    master_new = master - rate * (
        mean_hat / (jnp.sqrt(square_hat) + ADAM_EPS) + decay_rate * master
    )
    return (mean_new, square_new, master_new)


def on_device(
    inputs,
    targets,
    doc_lengths,
    desirable,
    head_weight,
    qkv_master,
    out_master,
    up_master,
    down_master,
    vectors,
    hidden_bias,
    qkv_mean,
    out_mean,
    up_mean,
    down_mean,
    vectors_mean,
    hidden_mean,
    qkv_square,
    out_square,
    up_square,
    down_square,
    vectors_square,
    hidden_square,
    qkv_frozen,
    out_frozen,
    up_frozen,
    down_frozen,
    vectors_frozen,
    hidden_frozen,
):
    dp_size = lax.axis_size("dp")
    tensor_size = lax.axis_size("tensor")
    inner = dp_size // SPLIT
    outer_index = lax.axis_index("dp") // inner
    block = inputs.shape[0]
    lengths_tile = jnp.zeros((8, 128), jnp.int32).at[0, :SEGS].set(doc_lengths[0])
    masters = tuple(w.astype(BF16) for w in (qkv_master, out_master, up_master, down_master))
    *policy_set, tokens_all, lengths_all = spread_weights(masters, inner, inputs, lengths_tile, 0)
    frozen_set = spread_weights(
        (qkv_frozen, out_frozen, up_frozen, down_frozen), inner, None, None, 1
    )
    member, _, _ = doc_layout(doc_lengths[0], block)
    _, positions, doc_of = jax.vmap(lambda row: doc_layout(row, block))(lengths_all[:, 0, :SEGS])
    allowed = allowed_keys(doc_of)

    cut = qkv_master.shape[1]
    width_qkv, width_up = cut // SPLIT, up_master.shape[1] // SPLIT

    def own_bias(bias):
        return (
            lax.dynamic_slice(bias, (outer_index * width_qkv,), (width_qkv,)),
            lax.dynamic_slice(bias, (cut + outer_index * width_up,), (width_up,)),
        )

    values = f32(tokens_all)
    centre = values - jnp.mean(values, axis=1, keepdims=True)
    scale = lax.rsqrt(jnp.mean(centre * centre, axis=1, keepdims=True) + EPS_NORM)
    normed = centre * scale
    one_low = normed_rows(normed, vectors[0], vectors[1])
    two_low = normed_rows(normed, vectors[2], vectors[3])
    policy_part, kept_values = attention_mlp(
        one_low, two_low, *own_bias(hidden_bias), policy_set, positions, allowed
    )
    final_low = reduce_call(branch_kernel, inner, policy_part, inputs, vectors[4:6], 2)
    frozen_part, _ = attention_mlp(
        normed_rows(normed, vectors_frozen[0], vectors_frozen[1]),
        normed_rows(normed, vectors_frozen[2], vectors_frozen[3]),
        *own_bias(hidden_frozen),
        frozen_set,
        positions,
        allowed,
    )
    frozen_low = reduce_call(branch_kernel, inner, frozen_part, inputs, vectors_frozen[4:6], 3)
    vocab_start = lax.axis_index("tensor") * head_weight.shape[1]
    policy_logits, policy_total, policy_pick, chosen = vocab_stats(
        final_low, head_weight, targets, vocab_start
    )
    _, frozen_total, frozen_pick, _ = vocab_stats(frozen_low, head_weight, targets, vocab_start)
    policy_total, policy_pick, frozen_total, frozen_pick = combined_all(
        (policy_total, policy_pick, frozen_total, frozen_pick), "tensor", combine_totals
    )
    doc_weights = member.astype(F32)
    policy_docs = jnp.sum(doc_weights * (policy_pick - policy_total)[:, None], axis=0)
    frozen_docs = jnp.sum(doc_weights * (frozen_pick - frozen_total)[:, None], axis=0)
    reward = policy_docs - frozen_docs
    seq_count = dp_size * SEGS
    reward_shift = lax.psum(jnp.sum(reward), "dp") / seq_count
    sigmoid_value = jax.nn.sigmoid(BETA_KTO * (reward - reward_shift))
    labels = desirable[0].astype(F32)
    doc_grad = BETA_KTO * sigmoid_value * (1.0 - sigmoid_value) * (1.0 - 2.0 * labels) / seq_count
    token_grad = jnp.sum(doc_weights * doc_grad[None, :], axis=1)
    logit_grad = (
        token_grad[:, None]
        * (chosen.astype(F32) - jnp.exp(policy_logits - policy_total[:, None]))
    ).astype(BF16)
    final_part = contract_cols(logit_grad, head_weight)
    final_quarter, branch_low = final_grad_call(final_part, inner, 4)
    joined = kept_values[5]
    one_part, two_part, mixed_grad, hidden_low = layer_backward(
        branch_low, kept_values, policy_set, positions, allowed
    )
    scaled_part = (one_part * vectors[0] + two_part * vectors[2]).astype(BF16)
    input_grad = f32(reduce_call(input_kernel, inner, scaled_part, inputs, final_quarter, 5))
    shards = tuple(w.shape for w in masters)
    grads = (
        contract_rows(one_low, mixed_grad).astype(BF16),
        contract_rows(two_low, hidden_low).astype(BF16),
        contract_rows(joined, branch_low).astype(BF16),
    )
    qkv_grad, up_grad, out_grad, down_grad = weight_grads_call(grads, shards, inner, 6)
    branch_bias = jnp.sum(f32(final_quarter.astype(BF16)), axis=0)
    vector_grad = jnp.stack(
        [
            jnp.sum(one_part * normed, axis=0),
            jnp.sum(one_part, axis=0),
            jnp.sum(two_part * normed, axis=0),
            jnp.sum(two_part, axis=0),
            branch_bias,
            branch_bias,
        ]
    )
    bias_grad = jnp.concatenate(
        [
            lax.dynamic_update_slice(
                jnp.zeros((cut,), F32),
                jnp.sum(mixed_grad, axis=0, dtype=F32),
                (outer_index * width_qkv,),
            ),
            lax.dynamic_update_slice(
                jnp.zeros((up_master.shape[1],), F32),
                jnp.sum(hidden_low, axis=0, dtype=F32),
                (outer_index * width_up,),
            ),
        ]
    )
    vector_grad, hidden_grad = (
        f32(lax.psum(vector_grad.astype(BF16), ("dp", "tensor"))),
        f32(lax.psum(bias_grad.astype(BF16), "dp")),
    )
    local_square = sum(jnp.sum(f32(g) * f32(g)) for g in (qkv_grad, out_grad, up_grad, down_grad))
    local_square = (
        local_square
        + jnp.sum(vector_grad * vector_grad) / (dp_size * tensor_size)
        + jnp.sum(hidden_grad * hidden_grad) / dp_size
    )
    grad_norm = jnp.sqrt(lax.psum(local_square, ("dp", "tensor")))
    factor = jnp.minimum(1.0, CLIP_NORM / (grad_norm + 1e-06))
    qkv_state = adam_step(
        qkv_master, qkv_mean, qkv_square, qkv_grad, factor, LEARN_RATE, WEIGHT_DECAY
    )
    out_state = adam_step(
        out_master, out_mean, out_square, out_grad, factor, LEARN_RATE, WEIGHT_DECAY
    )
    up_state = adam_step(up_master, up_mean, up_square, up_grad, factor, LEARN_RATE, WEIGHT_DECAY)
    down_state = adam_step(
        down_master, down_mean, down_square, down_grad, factor, LEARN_RATE, WEIGHT_DECAY
    )
    vector_state = adam_step(
        vectors, vectors_mean, vectors_square, vector_grad, factor, VECTOR_RATE, 0.0
    )
    hidden_state = adam_step(
        hidden_bias, hidden_mean, hidden_square, hidden_grad, factor, VECTOR_RATE, 0.0
    )
    return (
        final_low,
        input_grad,
        grad_norm,
        *qkv_state,
        *out_state,
        *up_state,
        *down_state,
        *vector_state,
        *hidden_state,
    )


def solution(mesh):
    rows, cols = P("dp", "tensor"), P("tensor", "dp")
    matrices = (rows, cols, rows, cols)
    placed = (
        P("dp", None),
        P("dp"),
        P("dp", None),
        P("dp", None),
        P(None, "tensor"),
        *matrices,
        P(),
        P("tensor"),
        *matrices,
        P(),
        P("tensor"),
        *matrices,
        P(),
        P("tensor"),
        *matrices,
        P(),
        P("tensor"),
    )
    return jax.shard_map(
        on_device,
        mesh=mesh,
        in_specs=placed,
        out_specs=(
            P("dp", None),
            P("dp", None),
            P(),
            *(spec for spec in matrices for _ in range(3)),
            P(),
            P(),
            P(),
            P("tensor"),
            P("tensor"),
            P("tensor"),
        ),
        check_vma=False,
    )
```

```python
import functools

import jax
import jax.numpy as jnp
from jax import lax
from jax.experimental import pallas as pl
from jax.experimental.pallas import tpu as pltpu
from jax.sharding import PartitionSpec as P

HD = 128
ROT = 32
SEGS = 4
STEP = 3
SPLIT = 4
QUARTERS = 4
AHEAD = 3


EPS_NORM = 1e-05
BETA_KTO = 0.1
CLIP_NORM = 0.01
LEARN_RATE = 0.02
VECTOR_RATE = 0.2
BETA_FIRST = 0.9
BETA_SECOND = 0.999
ADAM_EPS = 1e-08
WEIGHT_DECAY = 0.01
MASKED = -1e30

MESH = pl.DeviceIdType.MESH
BF16 = jnp.bfloat16
F32 = jnp.float32
ANY_SPEC = pl.BlockSpec(memory_space=pltpu.HBM)
VMEM_SPEC = pl.BlockSpec(memory_space=pltpu.VMEM)


class Place:
    def __init__(self, inner):
        self.inner = inner
        self.dp = lax.axis_index("dp")
        self.t = lax.axis_index("tensor")
        self.o = self.dp // inner
        self.i = self.dp % inner
        self.near = self.t + 1 - 2 * (self.t % 2)
        self.far = (self.t + 2) % QUARTERS

    def outer_peer(self, shift):
        return (((self.o + shift) % SPLIT) * self.inner + self.i, self.t)

    def inner_peer(self, shift):
        return (self.o * self.inner + (self.i + shift) % self.inner, self.t)

    def near_peer(self):
        return (self.dp, self.near)

    def far_peer(self):
        return (self.dp, self.far)


def aligned(shard):
    return shard % 128 == 0


def greet(peers):
    barrier = pltpu.get_barrier_semaphore()
    for peer in peers:
        pl.semaphore_signal(barrier, inc=1, device_id=peer, device_id_type=MESH)
    pl.semaphore_wait(barrier, len(peers))


def remote(src, dst, send_sem, recv_sem, peer):
    copy = pltpu.make_async_remote_copy(
        src_ref=src,
        dst_ref=dst,
        send_sem=send_sem,
        recv_sem=recv_sem,
        device_id=peer,
        device_id_type=MESH,
    )
    copy.start()
    return copy


def spread_weights_kernel(inner, with_tokens, *refs):
    here = Place(inner)
    if with_tokens:
        (qkv, out, up, down, tokens, lengths, qkv_all, up_all, low_all, tokens_all, lengths_all,
         send_o, recv_o, send_i, recv_i, local, send_t, recv_t, send_l, recv_l) = refs
    else:
        qkv, out, up, down, qkv_all, up_all, low_all, send_o, recv_o, send_i, recv_i, local = refs
    shard = qkv.shape[0]
    width_qkv, width_up = qkv.shape[1] // SPLIT, up.shape[1] // SPLIT
    width_out, width_down = out.shape[0] // SPLIT, down.shape[0] // SPLIT

    def src(m, part):
        if m == 0:
            return qkv.at[:, pl.ds(part * width_qkv, width_qkv)]
        if m == 1:
            return up.at[:, pl.ds(part * width_up, width_up)]
        if m == 2:
            return out.at[pl.ds(part * width_out, width_out), :]
        return down.at[pl.ds(part * width_down, width_down), :]

    def dst(m, index):
        where = pl.ds(index * shard, shard)
        if m == 0:
            return qkv_all.at[where, :]
        if m == 1:
            return up_all.at[where, :]
        rows = pl.ds(0, width_out) if m == 2 else pl.ds(width_out, width_down)
        return low_all.at[rows, where] if aligned(shard) else low_all.at[index, rows, :]

    peers = [here.outer_peer(s) for s in range(1, SPLIT)]
    peers += [here.inner_peer(r) for r in range(1, inner)]
    if with_tokens:
        peers += [here.far_peer(), here.near_peer()]
    greet(peers)

    waits = []
    token_copies = []
    if with_tokens:
        rows = tokens.shape[0] // QUARTERS

        def piece(part, quarter):
            return tokens_all.at[pl.ds((part * QUARTERS + quarter) * rows, rows), :]

        for s in range(1, SPLIT):
            token_copies.append(
                remote(
                    tokens.at[pl.ds(here.t * rows, rows), :],
                    piece(here.o, here.t),
                    send_t.at[0, s - 1],
                    recv_t.at[0, s - 1],
                    here.outer_peer(s),
                )
            )
        for s in range(1, SPLIT):
            waits.append(
                remote(
                    lengths,
                    lengths_all.at[here.o],
                    send_l.at[s - 1],
                    recv_l.at[s - 1],
                    here.outer_peer(s),
                )
            )
    first = {}
    order = [(m, s) for m in range(4) for s in (2, 1, 3)]

    def send_on(number):
        if number >= len(order):
            return
        m, s = order[number]
        first[m, s] = remote(
            src(m, (here.o + s) % SPLIT),
            dst(m, here.dp),
            send_o.at[m, s - 1],
            recv_o.at[m, s - 1],
            here.outer_peer(s),
        )

    for number in range(0 if with_tokens else AHEAD):
        send_on(number)
    own = []
    for m in range(4):
        own.append(pltpu.make_async_copy(src(m, here.o), dst(m, here.dp), local.at[m]))
    if with_tokens:
        block = tokens.shape[0]
        own.append(
            pltpu.make_async_copy(
                tokens, tokens_all.at[pl.ds(here.o * block, block), :], local.at[4]
            )
        )
        own.append(pltpu.make_async_copy(lengths, lengths_all.at[here.o], local.at[5]))
    for copy in own:
        copy.start()
    for m in range(4):
        for r in range(1, inner):
            waits.append(
                remote(
                    src(m, here.o),
                    dst(m, here.dp),
                    send_i.at[m, 0, r - 1],
                    recv_i.at[m, 0, r - 1],
                    here.inner_peer(r),
                )
            )
    across = {}
    if with_tokens:
        for s in range(1, SPLIT):
            token_copies[s - 1].wait_recv()
            send_on(s - 1)
            part = (here.o + SPLIT - s) % SPLIT
            across[s] = remote(
                piece(part, here.t),
                piece(part, here.t),
                send_t.at[1, s - 1],
                recv_t.at[1, s - 1],
                here.far_peer(),
            )
            waits.append(
                remote(
                    piece(part, here.t),
                    piece(part, here.t),
                    send_t.at[2, s - 1],
                    recv_t.at[2, s - 1],
                    here.near_peer(),
                )
            )
    for number, (m, s) in enumerate(order):
        first[m, s].wait_recv()
        send_on(number + AHEAD)
        index = ((here.o + SPLIT - s) % SPLIT) * inner + here.i
        for r in range(1, inner):
            waits.append(
                remote(
                    dst(m, index),
                    dst(m, index),
                    send_i.at[m, s, r - 1],
                    recv_i.at[m, s, r - 1],
                    here.inner_peer(r),
                )
            )
    if with_tokens:
        for s in range(1, SPLIT):
            across[s].wait_recv()
            part = (here.o + SPLIT - s) % SPLIT
            waits.append(
                remote(
                    piece(part, here.far),
                    piece(part, here.far),
                    send_t.at[3, s - 1],
                    recv_t.at[3, s - 1],
                    here.near_peer(),
                )
            )
        for copy in token_copies:
            copy.wait_send()
        for copy in across.values():
            copy.wait_send()
    for copy in first.values():
        copy.wait_send()
    for copy in own:
        copy.wait()
    for copy in waits:
        copy.wait()


def spread_weights(shards, inner, tokens, lengths, number):
    qkv, out, up, down = shards
    d_model = out.shape[1] * SPLIT * inner
    width = out.shape[0] // SPLIT + down.shape[0] // SPLIT
    shapes = [
        jax.ShapeDtypeStruct((d_model, qkv.shape[1] // SPLIT), BF16),
        jax.ShapeDtypeStruct((d_model, up.shape[1] // SPLIT), BF16),
        jax.ShapeDtypeStruct(
            (width, d_model) if aligned(out.shape[1]) else (SPLIT * inner, width, out.shape[1]),
            BF16,
        ),
    ]
    dma = pltpu.SemaphoreType.DMA
    scratch = [
        dma((4, SPLIT - 1)),
        dma((4, SPLIT - 1)),
        dma((4, SPLIT, max(inner - 1, 1))),
        dma((4, SPLIT, max(inner - 1, 1))),
        dma((6,)),
    ]
    operands = [qkv, out, up, down]
    if tokens is not None:
        operands += [tokens, lengths]
        shapes += [
            jax.ShapeDtypeStruct((tokens.shape[0] * SPLIT, tokens.shape[1]), BF16),
            jax.ShapeDtypeStruct((SPLIT, *lengths.shape), lengths.dtype),
        ]
        scratch += [
            dma((4, SPLIT - 1)),
            dma((4, SPLIT - 1)),
            dma((SPLIT - 1,)),
            dma((SPLIT - 1,)),
        ]
    qkv_all, up_all, low_all, *gathered = pl.pallas_call(
        functools.partial(spread_weights_kernel, inner, tokens is not None),
        out_shape=shapes,
        in_specs=[ANY_SPEC] * len(operands),
        out_specs=[ANY_SPEC] * len(shapes),
        scratch_shapes=scratch,
        compiler_params=pltpu.CompilerParams(collective_id=number, has_side_effects=True),
    )(*operands)
    if low_all.ndim == 3:
        low_all = jnp.swapaxes(low_all, 0, 1).reshape(width, d_model)
    return (qkv_all, up_all, low_all, *gathered)


def f32(value):
    return value.astype(F32)


class RowSum:
    def __init__(self, here, part_ref, total, near_in, far_in, far_out, outer_in, outer_out, *sems):
        self.here, self.part, self.total = here, part_ref, total
        self.near_in, self.far_in, self.far_out = near_in, far_in, far_out
        self.outer_in, self.outer_out = outer_in, outer_out
        self.near_sems, self.far_sems, self.outer_sems = sems[0:2], sems[2:4], sems[4:6]
        self.quarter_sems = sems[6:8]
        self.rows = far_out.shape[1]
        self.near, self.far, self.outer = {}, {}, {}

    def rows_of(self, step, quarter):
        block = (self.here.o + 1 + step) % SPLIT
        return pl.ds((block * QUARTERS + quarter) * self.rows, self.rows)

    def start(self):
        here = self.here
        for step in range(SPLIT):
            for side, quarter in enumerate(((here.near + 2) % QUARTERS, here.near)):
                self.near[step, side] = remote(
                    self.part.at[self.rows_of(step, quarter), :],
                    self.near_in.at[step, side],
                    self.near_sems[0].at[step, side],
                    self.near_sems[1].at[step, side],
                    here.near_peer(),
                )

    def across(self, step):
        here = self.here
        self.near[step, 0].wait_recv()
        self.far_out[step] = (
            f32(self.part[self.rows_of(step, here.far), :]) + f32(self.near_in[step, 0])
        ).astype(BF16)
        self.far[step] = remote(
            self.far_out.at[step],
            self.far_in.at[step],
            self.far_sems[0].at[step],
            self.far_sems[1].at[step],
            here.far_peer(),
        )

    def along(self, step):
        here = self.here
        self.near[step, 1].wait_recv()
        self.far[step].wait_recv()
        value = (
            f32(self.part[self.rows_of(step, here.t), :])
            + f32(self.near_in[step, 1])
            + f32(self.far_in[step])
        )
        if step == SPLIT - 1:
            self.total[...] = value
            return
        self.outer_out[step] = value.astype(BF16)
        self.outer[step] = remote(
            self.outer_out.at[step],
            self.outer_in.at[step],
            self.outer_sems[0].at[step],
            self.outer_sems[1].at[step],
            here.outer_peer(step + 1),
        )

    def value(self):
        value = self.total[...]
        for step in range(SPLIT - 1):
            self.outer[step].wait_recv()
            value = value + f32(self.outer_in[step])
        return value

    def finish(self):
        for copies in (self.near, self.far, self.outer):
            for copy in copies.values():
                copy.wait_send()


def gather_quarters(here, ref, rows, send, recv):
    def piece(quarter):
        return ref.at[pl.ds(quarter * rows, rows), :]

    far = remote(piece(here.t), piece(here.t), send.at[0], recv.at[0], here.far_peer())
    near = remote(piece(here.t), piece(here.t), send.at[1], recv.at[1], here.near_peer())
    far.wait_recv()
    passed = remote(piece(here.far), piece(here.far), send.at[2], recv.at[2], here.near_peer())
    near.wait_recv()
    passed.wait_recv()
    for copy in (far, near, passed):
        copy.wait_send()


def reduce_peers(here):
    return [here.outer_peer(s) for s in range(1, SPLIT)] + [here.far_peer(), here.near_peer()]


def branch_kernel(inner, part_ref, tokens_ref, rows_ref, final_ref, *scratch):
    here = Place(inner)
    sums = RowSum(here, part_ref, *scratch)
    greet(reduce_peers(here))
    mine = pl.ds(here.t * sums.rows, sums.rows)
    sums.start()
    for step in range(SPLIT):
        sums.across(step)
    for step in range(SPLIT):
        sums.along(step)
    branch = sums.value() + rows_ref[0:1, :] + rows_ref[1:2, :]
    final_ref[mine, :] = (f32(tokens_ref[mine, :]) + branch).astype(BF16)
    gather_quarters(here, final_ref, sums.rows, *sums.quarter_sems)
    sums.finish()


def input_change(values, scaled):
    centre = values - jnp.mean(values, axis=1, keepdims=True)
    spread = jnp.mean(centre * centre, axis=1, keepdims=True)
    scale = lax.rsqrt(spread + EPS_NORM)
    normed = centre * scale
    along = jnp.mean(scaled * normed, axis=1, keepdims=True)
    return scale * (scaled - jnp.mean(scaled, axis=1, keepdims=True) - normed * along)


def reduce_scratch(rows, width):
    dma = pltpu.SemaphoreType.DMA
    return [
        pltpu.VMEM((rows, width), F32),
        pltpu.VMEM((SPLIT, 2, rows, width), BF16),
        pltpu.VMEM((SPLIT, rows, width), BF16),
        pltpu.VMEM((SPLIT, rows, width), BF16),
        pltpu.VMEM((SPLIT - 1, rows, width), BF16),
        pltpu.VMEM((SPLIT - 1, rows, width), BF16),
        dma((SPLIT, 2)),
        dma((SPLIT, 2)),
        dma((SPLIT,)),
        dma((SPLIT,)),
        dma((SPLIT - 1,)),
        dma((SPLIT - 1,)),
        dma((3,)),
        dma((3,)),
    ]


def branch_call(inner, part, tokens, extra, number):
    block, width = tokens.shape
    return pl.pallas_call(
        functools.partial(branch_kernel, inner),
        out_shape=jax.ShapeDtypeStruct((block, width), BF16),
        in_specs=[VMEM_SPEC] * 3,
        out_specs=VMEM_SPEC,
        scratch_shapes=reduce_scratch(block // QUARTERS, width),
        compiler_params=pltpu.CompilerParams(
            collective_id=number, has_side_effects=True, vmem_limit_bytes=56 * 1024 * 1024
        ),
    )(part, tokens, extra)


def final_grad_kernel(
    inner, part_ref, quarter_ref, branch_all, near_in, far_in, far_out, low, near_out,
    near_send, near_recv, far_send, far_recv, send, recv, local,
):
    here = Place(inner)
    rows = quarter_ref.shape[0]
    greet(reduce_peers(here))

    def rows_of(quarter):
        return pl.ds(quarter * rows, rows)

    near = []
    for side, quarter in enumerate(((here.near + 2) % QUARTERS, here.near)):
        near_out[side] = part_ref[rows_of(quarter), :].astype(BF16)
        near.append(
            remote(
                near_out.at[side],
                near_in.at[side],
                near_send.at[side],
                near_recv.at[side],
                here.near_peer(),
            )
        )
    near[0].wait_recv()
    far_out[...] = (part_ref[rows_of(here.far), :] + f32(near_in[0])).astype(BF16)
    far = remote(far_out, far_in, far_send, far_recv, here.far_peer())
    near[1].wait_recv()
    far.wait_recv()
    quarter_ref[...] = part_ref[rows_of(here.t), :] + f32(near_in[1]) + f32(far_in[...])
    low[...] = quarter_ref[...].astype(BF16)
    for copy in near + [far]:
        copy.wait_send()

    def piece(part, quarter):
        return branch_all.at[pl.ds((part * QUARTERS + quarter) * rows, rows), :]

    outer = [
        remote(
            low, piece(here.o, here.t), send.at[0, s], recv.at[0, s], here.outer_peer(s)
        )
        for s in range(1, SPLIT)
    ]
    own = pltpu.make_async_copy(low, piece(here.o, here.t), local)
    own.start()
    across, beside = [], []
    for s in range(SPLIT):
        part = (here.o + SPLIT - s) % SPLIT
        if s:
            outer[s - 1].wait_recv()
        source = piece(part, here.t) if s else low
        across.append(
            remote(source, piece(part, here.t), send.at[1, s], recv.at[1, s], here.far_peer())
        )
        beside.append(
            remote(source, piece(part, here.t), send.at[2, s], recv.at[2, s], here.near_peer())
        )
    for s in range(SPLIT):
        part = (here.o + SPLIT - s) % SPLIT
        across[s].wait_recv()
        beside.append(
            remote(
                piece(part, here.far),
                piece(part, here.far),
                send.at[3, s],
                recv.at[3, s],
                here.near_peer(),
            )
        )
    for copy in beside:
        copy.wait_recv()
    for copy in outer + across + beside:
        copy.wait_send()
    own.wait()


def final_grad_call(part, inner, number):
    block, width = part.shape
    rows = block // QUARTERS
    dma = pltpu.SemaphoreType.DMA
    return pl.pallas_call(
        functools.partial(final_grad_kernel, inner),
        out_shape=[
            jax.ShapeDtypeStruct((rows, width), F32),
            jax.ShapeDtypeStruct((SPLIT * block, width), BF16),
        ],
        in_specs=[VMEM_SPEC],
        out_specs=[VMEM_SPEC, ANY_SPEC],
        scratch_shapes=[
            pltpu.VMEM((2, rows, width), BF16),
            pltpu.VMEM((rows, width), BF16),
            pltpu.VMEM((rows, width), BF16),
            pltpu.VMEM((rows, width), BF16),
            pltpu.VMEM((2, rows, width), BF16),
            dma((2,)),
            dma((2,)),
            dma,
            dma,
            dma((4, SPLIT)),
            dma((4, SPLIT)),
            dma,
        ],
        compiler_params=pltpu.CompilerParams(
            collective_id=number, has_side_effects=True, vmem_limit_bytes=48 * 1024 * 1024
        ),
    )(part)


class AllSum:
    def __init__(self, here, mine, near_in, far_in, outer, inner, send, recv):
        self.here, self.mine, self.near_in, self.far_in = here, mine, near_in, far_in
        self.outer, self.inner, self.send, self.recv = outer, inner, send, recv
        self.copies = []

    def pair(self, stage, target, peer):
        copy = remote(
            self.mine.at[stage], target, self.send.at[stage], self.recv.at[stage], peer
        )
        self.copies.append(copy)
        return copy

    def near(self, value):
        self.mine[0] = value
        self.waiting = [self.pair(0, self.near_in, self.here.near_peer())]

    def far(self):
        self.waiting[0].wait_recv()
        self.mine[1] = self.mine[0] + self.near_in[...]
        self.waiting = [self.pair(1, self.far_in, self.here.far_peer())]

    def group(self, buffer, index, first, peers):
        self.waiting = []
        for number, peer in enumerate(peers):
            copy = remote(
                buffer.at[index],
                buffer.at[index],
                self.send.at[first + number],
                self.recv.at[first + number],
                peer,
            )
            self.waiting.append(copy)
            self.copies.append(copy)

    def along_outer(self):
        self.waiting[0].wait_recv()
        here = self.here
        self.outer[here.o] = self.mine[1] + self.far_in[...]
        self.group(self.outer, here.o, 2, [here.outer_peer(s) for s in range(1, SPLIT)])

    def along_inner(self):
        here = self.here
        for copy in self.waiting:
            copy.wait_recv()
        value = self.outer[0]
        for part in range(1, SPLIT):
            value = value + self.outer[part]
        self.inner[here.i] = value
        peers = [here.inner_peer(r) for r in range(1, here.inner)]
        self.group(self.inner, here.i, 1 + SPLIT, peers)

    def value(self):
        for copy in self.waiting:
            copy.wait_recv()
        value = self.inner[0]
        for part in range(1, self.here.inner):
            value = value + self.inner[part]
        for copy in self.copies:
            copy.wait_send()
        return value


def all_sum_scratch(shape, inner):
    dma = pltpu.SemaphoreType.DMA
    return [
        pltpu.VMEM((2, *shape), F32),
        pltpu.VMEM(shape, F32),
        pltpu.VMEM(shape, F32),
        pltpu.VMEM((SPLIT, *shape), F32),
        pltpu.VMEM((inner, *shape), F32),
        dma((SPLIT + inner,)),
        dma((SPLIT + inner,)),
    ]


def whole_sum(value):
    return jnp.sum(jnp.sum(value, axis=1, keepdims=True), axis=0, keepdims=True)


def finish_kernel(
    inner, part_ref, tokens_ref, quarter_ref, qkv, up, low, rows_ref, bias_ref,
    grad_ref, qkv_out, up_out, out_out, down_out, rows_out, bias_out, norm_ref, *scratch,
):
    here = Place(inner)
    sums = RowSum(here, part_ref, *scratch[:14])
    inputs, sends = scratch[14:18], scratch[18:22]
    send_i, recv_i, send_o, recv_o, local = scratch[22:27]
    small = AllSum(here, *scratch[27:34])
    squares = AllSum(here, *scratch[34:41])
    bias_in, bias_send, bias_recv = scratch[41:44]
    outs = (qkv_out, up_out, out_out, down_out)
    shard = qkv_out.shape[0]
    width_out = out_out.shape[0] // SPLIT
    width_down = down_out.shape[0] // SPLIT

    def src(m, index):
        where = pl.ds(index * shard, shard)
        if m == 0:
            return qkv.at[where, :]
        if m == 1:
            return up.at[where, :]
        rows = pl.ds(0, width_out) if m == 2 else pl.ds(width_out, width_down)
        return low.at[rows, where] if aligned(shard) else low.at[index, rows, :]

    def dst(m):
        if m < 2:
            width = outs[m].shape[1] // SPLIT
            return outs[m].at[:, pl.ds(here.o * width, width)]
        width = outs[m].shape[0] // SPLIT
        return outs[m].at[pl.ds(here.o * width, width), :]

    peers = reduce_peers(here) + [here.inner_peer(r) for r in range(1, inner)]
    greet(peers)
    first, last, own = {}, [], []

    order = [(m, s) for m in (2, 3, 1, 0) for s in (2, 1, 3, 0)]

    def trade(number):
        if number >= len(order):
            return
        m, s = order[number]
        part = (here.o + s) % SPLIT
        for r in range(1, inner):
            first[m, s, r] = remote(
                src(m, part * inner + (here.i + r) % inner),
                inputs[m].at[s, r - 1],
                send_i.at[m, s, r - 1],
                recv_i.at[m, s, r - 1],
                here.inner_peer(r),
            )

    def settle(number):
        m, s = order[number]
        part = (here.o + s) % SPLIT
        total = f32(src(m, part * inner + here.i)[...])
        for r in range(1, inner):
            first[m, s, r].wait_recv()
        trade(number + AHEAD)
        for r in range(1, inner):
            total = total + f32(inputs[m][s, r - 1])
        sends[m][s] = total.astype(BF16)
        if s:
            last.append(
                remote(
                    sends[m].at[s],
                    dst(m),
                    send_o.at[m, s - 1],
                    recv_o.at[m, s - 1],
                    here.outer_peer(s),
                )
            )
        else:
            copy = pltpu.make_async_copy(sends[m].at[0], dst(m), local.at[m])
            copy.start()
            own.append(copy)
        return whole_sum(total * total)

    for number in range(AHEAD):
        trade(number)
    sums.start()
    small.near(rows_ref[...])
    bias_in[here.i] = bias_ref[...]
    bias_inner = [
        remote(
            bias_in.at[here.i],
            bias_in.at[here.i],
            bias_send.at[SPLIT + r],
            bias_recv.at[SPLIT + r],
            here.inner_peer(r),
        )
        for r in range(1, inner)
    ]
    square = settle(0)
    square = square + settle(1)
    for step in range(SPLIT):
        sums.across(step)
        square = square + settle(2 + step)
    small.far()
    sums.along(0)
    square = square + settle(6)
    square = square + settle(7)
    small.along_outer()
    for copy in bias_inner:
        copy.wait_recv()
    bias = bias_in[0]
    for part in range(1, inner):
        bias = bias + bias_in[part]
    bias_out[here.o] = bias
    bias_outer = [
        remote(
            bias_out.at[here.o],
            bias_out.at[here.o],
            bias_send.at[s],
            bias_recv.at[s],
            here.outer_peer(s),
        )
        for s in range(1, SPLIT)
    ]
    square = square + whole_sum(bias * bias) / inner
    sums.along(1)
    square = square + settle(8)
    square = square + settle(9)
    small.along_inner()
    sums.along(2)
    square = square + settle(10)
    square = square + settle(11)
    rows_out[...] = small.value()
    sums.along(3)
    for number in range(12, len(order)):
        square = square + settle(number)
    squares.near(jnp.broadcast_to(square, norm_ref.shape))
    squares.far()
    squares.along_outer()
    squares.along_inner()
    norm = squares.value()
    rows = rows_out[...]
    doubled = lax.broadcasted_iota(jnp.int32, rows.shape, 0) == 4
    norm_ref[...] = norm + whole_sum(rows * rows * jnp.where(doubled, 2.0, 1.0))
    mine = pl.ds(here.t * sums.rows, sums.rows)
    change = input_change(f32(tokens_ref[mine, :]), sums.value())
    grad_ref[mine, :] = (quarter_ref[...] + change).astype(BF16)
    gather_quarters(here, grad_ref, sums.rows, *sums.quarter_sems)
    sums.finish()
    for copy in bias_outer:
        copy.wait_recv()
    for copy in bias_inner + bias_outer:
        copy.wait_send()
    for copy in last:
        copy.wait()
    for copy in own:
        copy.wait()
    for copy in first.values():
        copy.wait_send()


def finish_call(part, tokens, quarter, grads, rows, bias, shards, inner, number):
    dma = pltpu.SemaphoreType.DMA
    qkv, out, up, down = shards
    ordered = (qkv, up, out, down)
    if not aligned(out[1]):
        low = grads[2].reshape(grads[2].shape[0], SPLIT * inner, out[1])
        grads = (*grads[:2], jnp.swapaxes(low, 0, 1))
    pieces = [
        (qkv[0], qkv[1] // SPLIT),
        (up[0], up[1] // SPLIT),
        (out[0] // SPLIT, out[1]),
        (down[0] // SPLIT, down[1]),
    ]
    peers = max(inner - 1, 1)
    block, width = tokens.shape
    tile = (8, 128)
    return pl.pallas_call(
        functools.partial(finish_kernel, inner),
        out_shape=[
            jax.ShapeDtypeStruct((block, width), BF16),
            *(jax.ShapeDtypeStruct(shape, BF16) for shape in ordered),
            jax.ShapeDtypeStruct(rows.shape, F32),
            jax.ShapeDtypeStruct((SPLIT, *bias.shape), F32),
            jax.ShapeDtypeStruct(tile, F32),
        ],
        in_specs=[VMEM_SPEC] * 8,
        out_specs=[VMEM_SPEC] + [ANY_SPEC] * 4 + [VMEM_SPEC] * 3,
        scratch_shapes=reduce_scratch(block // QUARTERS, width)
        + [pltpu.VMEM((SPLIT, peers, *piece), BF16) for piece in pieces]
        + [pltpu.VMEM((SPLIT, *piece), BF16) for piece in pieces]
        + [
            dma((4, SPLIT, peers)),
            dma((4, SPLIT, peers)),
            dma((4, SPLIT - 1)),
            dma((4, SPLIT - 1)),
            dma((4,)),
        ]
        + all_sum_scratch(rows.shape, inner)
        + all_sum_scratch(tile, inner)
        + [
            pltpu.VMEM((inner, *bias.shape), F32),
            dma((SPLIT + inner,)),
            dma((SPLIT + inner,)),
        ],
        compiler_params=pltpu.CompilerParams(
            collective_id=number, has_side_effects=True, vmem_limit_bytes=60 * 1024 * 1024
        ),
    )(part, tokens, quarter, *grads, rows, bias)


def reward_kernel(
    inner, stats_ref, member_ref, label_ref, out_ref, stats, outer_in, inner_in,
    send, recv, send_o, recv_o, send_i, recv_i,
):
    here = Place(inner)
    tensor_peers = [(here.dp, (here.t + s) % QUARTERS) for s in range(1, QUARTERS)]
    outer_peers = [here.outer_peer(s) for s in range(1, SPLIT)]
    inner_peers = [here.inner_peer(r) for r in range(1, inner)]
    greet(tensor_peers + outer_peers + inner_peers)

    def share(buffer, index, sends, recvs, peers):
        return [
            remote(buffer.at[index], buffer.at[index], sends.at[n], recvs.at[n], peer)
            for n, peer in enumerate(peers)
        ]

    stats[here.t] = stats_ref[...]
    copies = share(stats, here.t, send, recv, tensor_peers)
    for copy in copies:
        copy.wait_recv()
    quarters = [stats[q] for q in range(QUARTERS)]
    highest = functools.reduce(jnp.maximum, quarters)
    summed = functools.reduce(lambda a, b: a + b, [jnp.exp(q - highest) for q in quarters])
    totals = highest + jnp.log(summed)
    picks = functools.reduce(lambda a, b: a + b, quarters)
    log_probs = picks - totals_to_picks(totals)
    member = member_ref[...]
    policy_docs = jnp.sum(member * log_probs[1:2, :], axis=1, keepdims=True)
    frozen_docs = jnp.sum(member * log_probs[3:4, :], axis=1, keepdims=True)
    reward = policy_docs - frozen_docs
    outer_in[here.o] = jnp.broadcast_to(whole_sum(reward), outer_in.shape[1:])
    more = share(outer_in, here.o, send_o, recv_o, outer_peers)
    for copy in more:
        copy.wait_recv()
    inner_in[here.i] = functools.reduce(lambda a, b: a + b, [outer_in[n] for n in range(SPLIT)])
    rest = share(inner_in, here.i, send_i, recv_i, inner_peers)
    for copy in rest:
        copy.wait_recv()
    total = functools.reduce(lambda a, b: a + b, [inner_in[n] for n in range(inner)])
    seq_count = inner * SPLIT * SEGS
    shift = total[:, 0:1] / seq_count
    sigmoid_value = 1.0 / (1.0 + jnp.exp(-BETA_KTO * (reward - shift)))
    labels = label_ref[:, 0:1]
    doc_grad = BETA_KTO * sigmoid_value * (1.0 - sigmoid_value) * (1.0 - 2.0 * labels) / seq_count
    out_ref[0:1, :] = jnp.sum(member * doc_grad, axis=0, keepdims=True)
    out_ref[1:2, :] = totals[0:1, :]
    for copy in copies + more + rest:
        copy.wait_send()


def totals_to_picks(totals):
    return jnp.concatenate([totals[0:1], totals[0:1], totals[2:3], totals[2:3], totals[4:]], axis=0)


def reward_call(stats, member, labels, inner, number):
    dma = pltpu.SemaphoreType.DMA
    tile = (8, 128)
    peers = max(inner - 1, 1)
    return pl.pallas_call(
        functools.partial(reward_kernel, inner),
        out_shape=jax.ShapeDtypeStruct((2, stats.shape[1]), F32),
        in_specs=[VMEM_SPEC] * 3,
        out_specs=VMEM_SPEC,
        scratch_shapes=[
            pltpu.VMEM((QUARTERS, *stats.shape), F32),
            pltpu.VMEM((SPLIT, *tile), F32),
            pltpu.VMEM((inner, *tile), F32),
            dma((QUARTERS - 1,)),
            dma((QUARTERS - 1,)),
            dma((SPLIT - 1,)),
            dma((SPLIT - 1,)),
            dma((peers,)),
            dma((peers,)),
        ],
        compiler_params=pltpu.CompilerParams(collective_id=number, has_side_effects=True),
    )(stats, member, labels)


def rotate(values, positions, direction):
    half_rot = ROT // 2
    frequency = 10000.0 ** (-2.0 * jnp.arange(half_rot, dtype=F32) / ROT)
    angles = positions.astype(F32)[..., None] * frequency
    cosine = jnp.cos(angles)[..., None, :]
    sine_part = direction * jnp.sin(angles)[..., None, :]
    first_half = values[..., :half_rot]
    second_half = values[..., half_rot:ROT]
    return jnp.concatenate(
        [
            first_half * cosine - second_half * sine_part,
            second_half * cosine + first_half * sine_part,
            values[..., ROT:],
        ],
        axis=-1,
    )


def doc_layout(lengths_row, row_count):
    ends, run = [], 0
    for segment in range(lengths_row.shape[0]):
        run = run + lengths_row[segment]
        ends.append(run)
    doc_ends = jnp.stack(ends)
    starts = doc_ends - lengths_row
    index_rows = jnp.arange(row_count, dtype=jnp.int32)
    member = (index_rows[:, None] >= starts[None, :]) & (index_rows[:, None] < doc_ends[None, :])
    doc_ids = jnp.arange(lengths_row.shape[0], dtype=jnp.int32)
    doc_of = jnp.sum(jnp.where(member, doc_ids[None, :], 0), axis=1)
    positions = index_rows - jnp.sum(jnp.where(member, starts[None, :], 0), axis=1)
    return (member, positions, doc_of)


def allowed_keys(doc_of):
    index_rows = jnp.arange(doc_of.shape[-1], dtype=jnp.int32)
    return (doc_of[..., :, None] == doc_of[..., None, :]) & (
        index_rows[:, None] >= index_rows[None, :]
    )


def contract_rows(left_rows, right_rows):
    return lax.dot_general(
        left_rows, right_rows, (((0,), (0,)), ((), ())), preferred_element_type=F32
    )


def contract_cols(left_rows, right_rows):
    return lax.dot_general(
        left_rows, right_rows, (((1,), (1,)), ((), ())), preferred_element_type=F32
    )


def normed_rows(normed, gain_row, shift_row):
    return (normed * gain_row + shift_row).astype(BF16)


def attention_mlp(one_low, two_low, qkv_bias, up_bias, weight_set, positions, allowed):
    qkv_all, up_all, low_all = weight_set
    blocks, block = positions.shape
    heads_local = qkv_bias.shape[0] // (3 * HD)
    mixed_proj = jnp.dot(one_low, qkv_all, preferred_element_type=F32) + qkv_bias
    mixed_proj = mixed_proj.reshape(blocks, block, heads_local, 3, HD)
    query_low = rotate(mixed_proj[:, :, :, 0], positions, 1.0).astype(BF16)
    key_low = rotate(mixed_proj[:, :, :, 1], positions, 1.0).astype(BF16)
    value_low = mixed_proj[:, :, :, 2].astype(BF16)
    scores = jnp.einsum(
        "bqhd,bkhd->bhqk", query_low, key_low, preferred_element_type=F32
    ) * HD ** (-0.5)
    scores = jnp.where(allowed[:, None], scores, MASKED)
    highest = jnp.max(scores, axis=3, keepdims=True)
    log_total = highest + jnp.log(jnp.sum(jnp.exp(scores - highest), axis=3, keepdims=True))
    probs_low = jnp.exp(scores - log_total).astype(BF16)
    attended = jnp.einsum("bhqk,bkhd->bqhd", probs_low, value_low, preferred_element_type=F32)
    attended = attended.reshape(blocks * block, heads_local * HD).astype(BF16)
    hidden = jnp.dot(two_low, up_all, preferred_element_type=F32) + up_bias
    active = jax.nn.gelu(hidden, approximate=False).astype(BF16)
    joined = jnp.concatenate([attended, active], axis=1)
    branch_part = jnp.dot(joined, low_all, preferred_element_type=F32).astype(BF16)
    kept_values = (query_low, key_low, value_low, log_total, hidden, joined)
    return (branch_part, kept_values)


def layer_backward(branch_low, kept_values, weight_set, positions, allowed):
    qkv_all, up_all, low_all = weight_set
    query_low, key_low, value_low, log_total, hidden, joined = kept_values
    blocks, block, heads_local, _ = query_low.shape
    cut = heads_local * HD
    joined_grad = contract_cols(branch_low, low_all)
    active_grad = joined_grad[:, cut:]
    cumulative = 0.5 * (1.0 + lax.erf(hidden * 0.7071067811865476))
    density = jnp.exp(-0.5 * hidden * hidden) * 0.3989422804014327
    hidden_low = (active_grad * (cumulative + hidden * density)).astype(BF16)
    attended_grad = joined_grad[:, :cut].reshape(blocks, block, heads_local, HD).astype(BF16)
    score_scale = HD ** (-0.5)
    scores = (
        jnp.einsum("bqhd,bkhd->bhqk", query_low, key_low, preferred_element_type=F32) * score_scale
    )
    scores = jnp.where(allowed[:, None], scores, MASKED)
    probs = jnp.exp(scores - log_total)
    prob_grad = jnp.einsum("bqhd,bkhd->bhqk", attended_grad, value_low, preferred_element_type=F32)
    value_grad = jnp.einsum(
        "bhqk,bqhd->bkhd", probs.astype(BF16), attended_grad, preferred_element_type=F32
    )
    score_grad = (probs * (prob_grad - jnp.sum(probs * prob_grad, axis=3, keepdims=True))).astype(
        BF16
    )
    query_grad = (
        jnp.einsum("bhqk,bkhd->bqhd", score_grad, key_low, preferred_element_type=F32) * score_scale
    )
    key_grad = (
        jnp.einsum("bhqk,bqhd->bkhd", score_grad, query_low, preferred_element_type=F32)
        * score_scale
    )
    mixed_grad = jnp.stack(
        [rotate(query_grad, positions, -1.0), rotate(key_grad, positions, -1.0), value_grad], axis=3
    )
    mixed_grad = mixed_grad.reshape(blocks * block, heads_local * 3 * HD).astype(BF16)
    one_part = contract_cols(mixed_grad, qkv_all)
    two_part = contract_cols(hidden_low, up_all)
    return (one_part, two_part, mixed_grad, hidden_low)


def vocab_stats(final_low, head_weight, targets, vocab_start):
    logits = jnp.dot(final_low, head_weight, preferred_element_type=F32)
    highest = jnp.max(logits, axis=1)
    log_total = highest + jnp.log(jnp.sum(jnp.exp(logits - highest[:, None]), axis=1))
    column = vocab_start + lax.broadcasted_iota(jnp.int32, logits.shape, 1)
    chosen = column == targets[:, None]
    picked = jnp.sum(jnp.where(chosen, logits, 0.0), axis=1)
    return (logits, log_total, picked, chosen)


def adam_step(master, mean_old, square_old, gradient, factor, rate, decay_rate):
    clipped = f32(gradient) * factor
    mean_new = BETA_FIRST * mean_old + (1.0 - BETA_FIRST) * clipped
    square_new = BETA_SECOND * square_old + (1.0 - BETA_SECOND) * clipped * clipped
    mean_hat = mean_new / (1.0 - BETA_FIRST**STEP)
    square_hat = square_new / (1.0 - BETA_SECOND**STEP)
    master_new = master - rate * (
        mean_hat / (jnp.sqrt(square_hat) + ADAM_EPS) + decay_rate * master
    )
    return (mean_new, square_new, master_new)


def on_device(
    inputs,
    targets,
    doc_lengths,
    desirable,
    head_weight,
    qkv_master,
    out_master,
    up_master,
    down_master,
    vectors,
    hidden_bias,
    qkv_mean,
    out_mean,
    up_mean,
    down_mean,
    vectors_mean,
    hidden_mean,
    qkv_square,
    out_square,
    up_square,
    down_square,
    vectors_square,
    hidden_square,
    qkv_frozen,
    out_frozen,
    up_frozen,
    down_frozen,
    vectors_frozen,
    hidden_frozen,
):
    dp_size = lax.axis_size("dp")
    tensor_size = lax.axis_size("tensor")
    inner = dp_size // SPLIT
    outer_index = lax.axis_index("dp") // inner
    block = inputs.shape[0]
    lengths_tile = jnp.zeros((8, 128), jnp.int32).at[0, :SEGS].set(doc_lengths[0])
    masters = tuple(w.astype(BF16) for w in (qkv_master, out_master, up_master, down_master))
    *policy_set, tokens_all, lengths_all = spread_weights(masters, inner, inputs, lengths_tile, 0)
    frozen_set = spread_weights(
        (qkv_frozen, out_frozen, up_frozen, down_frozen), inner, None, None, 1
    )
    member, _, _ = doc_layout(doc_lengths[0], block)
    _, positions, doc_of = jax.vmap(lambda row: doc_layout(row, block))(lengths_all[:, 0, :SEGS])
    allowed = allowed_keys(doc_of)

    cut = qkv_master.shape[1]
    width_qkv, width_up = cut // SPLIT, up_master.shape[1] // SPLIT

    def own_bias(bias):
        return (
            lax.dynamic_slice(bias, (outer_index * width_qkv,), (width_qkv,)),
            lax.dynamic_slice(bias, (cut + outer_index * width_up,), (width_up,)),
        )

    values = f32(tokens_all)
    centre = values - jnp.mean(values, axis=1, keepdims=True)
    scale = lax.rsqrt(jnp.mean(centre * centre, axis=1, keepdims=True) + EPS_NORM)
    normed = centre * scale
    one_low = normed_rows(normed, vectors[0], vectors[1])
    two_low = normed_rows(normed, vectors[2], vectors[3])
    policy_part, kept_values = attention_mlp(
        one_low, two_low, *own_bias(hidden_bias), policy_set, positions, allowed
    )
    final_low = branch_call(inner, policy_part, inputs, vectors[4:6], 2)
    frozen_part, _ = attention_mlp(
        normed_rows(normed, vectors_frozen[0], vectors_frozen[1]),
        normed_rows(normed, vectors_frozen[2], vectors_frozen[3]),
        *own_bias(hidden_frozen),
        frozen_set,
        positions,
        allowed,
    )
    frozen_low = branch_call(inner, frozen_part, inputs, vectors_frozen[4:6], 3)
    vocab_start = lax.axis_index("tensor") * head_weight.shape[1]
    policy_logits, policy_total, policy_pick, chosen = vocab_stats(
        final_low, head_weight, targets, vocab_start
    )
    _, frozen_total, frozen_pick, _ = vocab_stats(frozen_low, head_weight, targets, vocab_start)
    none = jnp.zeros_like(policy_total)
    stats = jnp.stack(
        [policy_total, policy_pick, frozen_total, frozen_pick, none, none, none, none]
    )
    doc_rows = jnp.zeros((8, block), F32).at[:SEGS].set(f32(member).T)
    labels = jnp.zeros((8, 128), F32).at[:SEGS].set(f32(desirable[0])[:, None])
    token_grad, policy_total = reward_call(stats, doc_rows, labels, inner, 6)
    logit_grad = (
        token_grad[:, None]
        * (chosen.astype(F32) - jnp.exp(policy_logits - policy_total[:, None]))
    ).astype(BF16)
    final_part = contract_cols(logit_grad, head_weight)
    final_quarter, branch_low = final_grad_call(final_part, inner, 4)
    joined = kept_values[5]
    one_part, two_part, mixed_grad, hidden_low = layer_backward(
        branch_low, kept_values, policy_set, positions, allowed
    )
    scaled_part = (one_part * vectors[0] + two_part * vectors[2]).astype(BF16)
    shards = tuple(w.shape for w in masters)
    grads = (
        contract_rows(one_low, mixed_grad).astype(BF16),
        contract_rows(two_low, hidden_low).astype(BF16),
        contract_rows(joined, branch_low).astype(BF16),
    )
    none = jnp.zeros_like(vectors[0])
    vector_part = jnp.stack(
        [
            jnp.sum(one_part * normed, axis=0),
            jnp.sum(one_part, axis=0),
            jnp.sum(two_part * normed, axis=0),
            jnp.sum(two_part, axis=0),
            jnp.sum(f32(final_quarter.astype(BF16)), axis=0),
            none,
            none,
            none,
        ]
    )
    bias_part = jnp.concatenate(
        [jnp.sum(mixed_grad, axis=0, dtype=F32), jnp.sum(hidden_low, axis=0, dtype=F32)]
    )
    bias_rows = (width_qkv + width_up) // 128
    bias_tile = (
        jnp.zeros((-(-bias_rows // 8) * 8, 128), F32)
        .at[:bias_rows]
        .set(bias_part.reshape(bias_rows, 128))
    )
    input_grad, qkv_grad, up_grad, out_grad, down_grad, vector_sum, bias_sum, square = finish_call(
        scaled_part, inputs, final_quarter, grads, vector_part, bias_tile, shards, inner, 5
    )
    input_grad = f32(input_grad)
    vector_grad = jnp.concatenate([vector_sum[:5], vector_sum[4:5]], axis=0)
    bias_sum = bias_sum[:, :bias_rows].reshape(SPLIT, bias_rows * 128)
    hidden_grad = jnp.concatenate(
        [bias_sum[:, :width_qkv].reshape(-1), bias_sum[:, width_qkv:].reshape(-1)]
    )
    grad_norm = jnp.sqrt(square[0, 0])
    factor = jnp.minimum(1.0, CLIP_NORM / (grad_norm + 1e-06))
    qkv_state = adam_step(
        qkv_master, qkv_mean, qkv_square, qkv_grad, factor, LEARN_RATE, WEIGHT_DECAY
    )
    out_state = adam_step(
        out_master, out_mean, out_square, out_grad, factor, LEARN_RATE, WEIGHT_DECAY
    )
    up_state = adam_step(up_master, up_mean, up_square, up_grad, factor, LEARN_RATE, WEIGHT_DECAY)
    down_state = adam_step(
        down_master, down_mean, down_square, down_grad, factor, LEARN_RATE, WEIGHT_DECAY
    )
    vector_state = adam_step(
        vectors, vectors_mean, vectors_square, vector_grad, factor, VECTOR_RATE, 0.0
    )
    hidden_state = adam_step(
        hidden_bias, hidden_mean, hidden_square, hidden_grad, factor, VECTOR_RATE, 0.0
    )
    return (
        final_low,
        input_grad,
        grad_norm,
        *qkv_state,
        *out_state,
        *up_state,
        *down_state,
        *vector_state,
        *hidden_state,
    )


def solution(mesh):
    rows, cols = P("dp", "tensor"), P("tensor", "dp")
    matrices = (rows, cols, rows, cols)
    placed = (
        P("dp", None),
        P("dp"),
        P("dp", None),
        P("dp", None),
        P(None, "tensor"),
        *matrices,
        P(),
        P("tensor"),
        *matrices,
        P(),
        P("tensor"),
        *matrices,
        P(),
        P("tensor"),
        *matrices,
        P(),
        P("tensor"),
    )
    return jax.shard_map(
        on_device,
        mesh=mesh,
        in_specs=placed,
        out_specs=(
            P("dp", None),
            P("dp", None),
            P(),
            *(spec for spec in matrices for _ in range(3)),
            P(),
            P(),
            P(),
            P("tensor"),
            P("tensor"),
            P("tensor"),
        ),
        check_vma=False,
    )
```

```python
import functools

import jax
import jax.numpy as jnp
from jax import lax
from jax.experimental import pallas as pl
from jax.experimental.pallas import tpu as pltpu
from jax.sharding import PartitionSpec as P

HD = 128
ROT = 32
SEGS = 4
STEP = 3
SPLIT = 4
QUARTERS = 4
AHEAD = 3


EPS_NORM = 1e-05
BETA_KTO = 0.1
CLIP_NORM = 0.01
LEARN_RATE = 0.02
VECTOR_RATE = 0.2
BETA_FIRST = 0.9
BETA_SECOND = 0.999
ADAM_EPS = 1e-08
WEIGHT_DECAY = 0.01
MASKED = -1e30

MESH = pl.DeviceIdType.MESH
BF16 = jnp.bfloat16
F32 = jnp.float32
ANY_SPEC = pl.BlockSpec(memory_space=pltpu.HBM)
VMEM_SPEC = pl.BlockSpec(memory_space=pltpu.VMEM)


class Place:
    def __init__(self, inner):
        self.inner = inner
        self.dp = lax.axis_index("dp")
        self.t = lax.axis_index("tensor")
        self.o = self.dp // inner
        self.i = self.dp % inner
        self.near = self.t + 1 - 2 * (self.t % 2)
        self.far = (self.t + 2) % QUARTERS

    def outer_peer(self, shift):
        return (((self.o + shift) % SPLIT) * self.inner + self.i, self.t)

    def inner_peer(self, shift):
        return (self.o * self.inner + (self.i + shift) % self.inner, self.t)

    def near_peer(self):
        return (self.dp, self.near)

    def far_peer(self):
        return (self.dp, self.far)


def aligned(shard):
    return shard % 128 == 0


def greet(peers):
    barrier = pltpu.get_barrier_semaphore()
    for peer in peers:
        pl.semaphore_signal(barrier, inc=1, device_id=peer, device_id_type=MESH)
    pl.semaphore_wait(barrier, len(peers))


def remote(src, dst, send_sem, recv_sem, peer):
    copy = pltpu.make_async_remote_copy(
        src_ref=src,
        dst_ref=dst,
        send_sem=send_sem,
        recv_sem=recv_sem,
        device_id=peer,
        device_id_type=MESH,
    )
    copy.start()
    return copy


class Spread:
    def __init__(self, here, shards, wholes, send_o, recv_o, send_i, recv_i, local):
        self.here = here
        self.qkv, self.out, self.up, self.down = shards
        self.qkv_all, self.up_all, self.low_all = wholes
        self.send_o, self.recv_o, self.send_i, self.recv_i = send_o, recv_o, send_i, recv_i
        self.local = local
        self.first, self.own, self.passed = {}, [], []
        self.order = [(m, s) for m in range(4) for s in (2, 1, 3)]

    def src(self, m, part):
        shard = (self.qkv, self.up, self.out, self.down)[m]
        width = shard.shape[1 if m < 2 else 0] // SPLIT
        where = pl.ds(part * width, width)
        return shard.at[:, where] if m < 2 else shard.at[where, :]

    def dst(self, m, index):
        shard = self.qkv.shape[0]
        where = pl.ds(index * shard, shard)
        if m < 2:
            return (self.qkv_all, self.up_all)[m].at[where, :]
        width_out, width_down = self.out.shape[0] // SPLIT, self.down.shape[0] // SPLIT
        rows = pl.ds(0, width_out) if m == 2 else pl.ds(width_out, width_down)
        low_all = self.low_all
        return low_all.at[rows, where] if aligned(shard) else low_all.at[index, rows, :]

    def peers(self):
        here = self.here
        peers = [here.outer_peer(s) for s in range(1, SPLIT)]
        return peers + [here.inner_peer(r) for r in range(1, here.inner)]

    def send_on(self, number):
        if number >= len(self.order):
            return
        m, s = self.order[number]
        self.first[m, s] = remote(
            self.src(m, (self.here.o + s) % SPLIT),
            self.dst(m, self.here.dp),
            self.send_o.at[m, s - 1],
            self.recv_o.at[m, s - 1],
            self.here.outer_peer(s),
        )

    def pass_on(self, m, s, source, index):
        here = self.here
        for r in range(1, here.inner):
            self.passed.append(
                remote(
                    source,
                    self.dst(m, index),
                    self.send_i.at[m, s, r - 1],
                    self.recv_i.at[m, s, r - 1],
                    here.inner_peer(r),
                )
            )

    def start_own(self):
        here = self.here
        for m in range(4):
            source = self.src(m, here.o)
            copy = pltpu.make_async_copy(source, self.dst(m, here.dp), self.local.at[m])
            copy.start()
            self.own.append(copy)
            self.pass_on(m, 0, source, here.dp)

    def step(self, number):
        here = self.here
        m, s = self.order[number]
        self.first[m, s].wait_recv()
        self.send_on(number + AHEAD)
        index = ((here.o + SPLIT - s) % SPLIT) * here.inner + here.i
        self.pass_on(m, s, self.dst(m, index), index)

    def finish(self):
        for copy in self.first.values():
            copy.wait_send()
        for copy in self.own:
            copy.wait()
        for copy in self.passed:
            copy.wait()


def spread_weights_kernel(
    inner, qkv, out, up, down, tokens, lengths, qkv_all, up_all, low_all, tokens_all, lengths_all,
    send_o, recv_o, send_i, recv_i, local, send_t, recv_t, send_l, recv_l,
):
    here = Place(inner)
    spread = Spread(
        here, (qkv, out, up, down), (qkv_all, up_all, low_all), send_o, recv_o, send_i, recv_i, local
    )
    greet(spread.peers() + [here.far_peer(), here.near_peer()])
    rows, block = tokens.shape[0] // QUARTERS, tokens.shape[0]

    def piece(part, quarter):
        return tokens_all.at[pl.ds((part * QUARTERS + quarter) * rows, rows), :]

    waits, token_copies, across, own = [], {}, {}, []
    for s in (2, 1, 3):
        token_copies[s] = remote(
            tokens.at[pl.ds(here.t * rows, rows), :],
            piece(here.o, here.t),
            send_t.at[0, s - 1],
            recv_t.at[0, s - 1],
            here.outer_peer(s),
        )
        waits.append(
            remote(
                lengths,
                lengths_all.at[here.o],
                send_l.at[s - 1],
                recv_l.at[s - 1],
                here.outer_peer(s),
            )
        )
    own.append(
        pltpu.make_async_copy(
            tokens, tokens_all.at[pl.ds(here.o * block, block), :], local.at[4]
        )
    )
    own.append(pltpu.make_async_copy(lengths, lengths_all.at[here.o], local.at[5]))
    for copy in own:
        copy.start()
    spread.start_own()
    for number, s in enumerate((2, 1, 3)):
        token_copies[s].wait_recv()
        spread.send_on(number)
        part = (here.o + SPLIT - s) % SPLIT
        for stage, peer in ((1, here.far_peer()), (2, here.near_peer())):
            copy = remote(
                piece(part, here.t),
                piece(part, here.t),
                send_t.at[stage, s - 1],
                recv_t.at[stage, s - 1],
                peer,
            )
            if stage == 1:
                across[s] = copy
            else:
                waits.append(copy)
    for number in range(len(spread.order)):
        spread.step(number)
    for s in (2, 1, 3):
        across[s].wait_recv()
        part = (here.o + SPLIT - s) % SPLIT
        waits.append(
            remote(
                piece(part, here.far),
                piece(part, here.far),
                send_t.at[3, s - 1],
                recv_t.at[3, s - 1],
                here.near_peer(),
            )
        )
    for copy in list(token_copies.values()) + list(across.values()):
        copy.wait_send()
    for copy in own:
        copy.wait()
    spread.finish()
    for copy in waits:
        copy.wait()


def whole_shapes(shards, inner):
    qkv, out, up, down = shards
    d_model = out.shape[1] * SPLIT * inner
    width = out.shape[0] // SPLIT + down.shape[0] // SPLIT
    return [
        jax.ShapeDtypeStruct((d_model, qkv.shape[1] // SPLIT), BF16),
        jax.ShapeDtypeStruct((d_model, up.shape[1] // SPLIT), BF16),
        jax.ShapeDtypeStruct(
            (width, d_model) if aligned(out.shape[1]) else (SPLIT * inner, width, out.shape[1]),
            BF16,
        ),
    ]


def joined_columns(low_all):
    if low_all.ndim == 3:
        low_all = jnp.swapaxes(low_all, 0, 1).reshape(low_all.shape[1], -1)
    return low_all


def spread_scratch(inner):
    dma = pltpu.SemaphoreType.DMA
    return [
        dma((4, SPLIT - 1)),
        dma((4, SPLIT - 1)),
        dma((4, SPLIT, max(inner - 1, 1))),
        dma((4, SPLIT, max(inner - 1, 1))),
        dma((6,)),
    ]


def spread_weights(shards, inner, tokens, lengths, number):
    dma = pltpu.SemaphoreType.DMA
    shapes = whole_shapes(shards, inner) + [
        jax.ShapeDtypeStruct((tokens.shape[0] * SPLIT, tokens.shape[1]), BF16),
        jax.ShapeDtypeStruct((SPLIT, *lengths.shape), lengths.dtype),
    ]
    qkv_all, up_all, low_all, *gathered = pl.pallas_call(
        functools.partial(spread_weights_kernel, inner),
        out_shape=shapes,
        in_specs=[ANY_SPEC] * 6,
        out_specs=[ANY_SPEC] * len(shapes),
        scratch_shapes=spread_scratch(inner)
        + [
            dma((4, SPLIT - 1)),
            dma((4, SPLIT - 1)),
            dma((SPLIT - 1,)),
            dma((SPLIT - 1,)),
        ],
        compiler_params=pltpu.CompilerParams(collective_id=number, has_side_effects=True),
    )(*shards, tokens, lengths)
    return (qkv_all, up_all, joined_columns(low_all), *gathered)


def f32(value):
    return value.astype(F32)


class RowSum:
    def __init__(self, here, part_ref, total, near_in, far_in, far_out, outer_in, outer_out, *sems):
        self.here, self.part, self.total = here, part_ref, total
        self.near_in, self.far_in, self.far_out = near_in, far_in, far_out
        self.outer_in, self.outer_out = outer_in, outer_out
        self.near_sems, self.far_sems, self.outer_sems = sems[0:2], sems[2:4], sems[4:6]
        self.quarter_sems = sems[6:8]
        self.rows = far_out.shape[1]
        self.near, self.far, self.outer = {}, {}, {}

    def rows_of(self, step, quarter):
        block = (self.here.o + 1 + step) % SPLIT
        return pl.ds((block * QUARTERS + quarter) * self.rows, self.rows)

    def start(self, step):
        here = self.here
        for side, quarter in enumerate(((here.near + 2) % QUARTERS, here.near)):
            self.near[step, side] = remote(
                self.part.at[self.rows_of(step, quarter), :],
                self.near_in.at[step, side],
                self.near_sems[0].at[step, side],
                self.near_sems[1].at[step, side],
                here.near_peer(),
            )

    def across(self, step):
        here = self.here
        self.near[step, 0].wait_recv()
        self.far_out[step] = (
            f32(self.part[self.rows_of(step, here.far), :]) + f32(self.near_in[step, 0])
        ).astype(BF16)
        self.far[step] = remote(
            self.far_out.at[step],
            self.far_in.at[step],
            self.far_sems[0].at[step],
            self.far_sems[1].at[step],
            here.far_peer(),
        )

    def along(self, step):
        here = self.here
        self.near[step, 1].wait_recv()
        self.far[step].wait_recv()
        value = (
            f32(self.part[self.rows_of(step, here.t), :])
            + f32(self.near_in[step, 1])
            + f32(self.far_in[step])
        )
        if step == SPLIT - 1:
            self.total[...] = value
            return
        self.outer_out[step] = value.astype(BF16)
        self.outer[step] = remote(
            self.outer_out.at[step],
            self.outer_in.at[step],
            self.outer_sems[0].at[step],
            self.outer_sems[1].at[step],
            here.outer_peer(step + 1),
        )

    def value(self):
        value = self.total[...]
        for step in range(SPLIT - 1):
            self.outer[step].wait_recv()
            value = value + f32(self.outer_in[step])
        return value

    def finish(self):
        for copies in (self.near, self.far, self.outer):
            for copy in copies.values():
                copy.wait_send()


def gather_quarters(here, ref, rows, send, recv):
    def piece(quarter):
        return ref.at[pl.ds(quarter * rows, rows), :]

    far = remote(piece(here.t), piece(here.t), send.at[0], recv.at[0], here.far_peer())
    near = remote(piece(here.t), piece(here.t), send.at[1], recv.at[1], here.near_peer())
    far.wait_recv()
    passed = remote(piece(here.far), piece(here.far), send.at[2], recv.at[2], here.near_peer())
    near.wait_recv()
    passed.wait_recv()
    for copy in (far, near, passed):
        copy.wait_send()


def reduce_peers(here):
    return [here.outer_peer(s) for s in range(1, SPLIT)] + [here.far_peer(), here.near_peer()]


def dot(left, right):
    return jnp.dot(left, right, preferred_element_type=F32)


def dot_cols(left, right):
    return lax.dot_general(left, right, (((1,), (1,)), ((), ())), preferred_element_type=F32)


def error_function(value):
    value = jnp.clip(value, -3.832506856900711, 3.832506856900711)
    square = value * value
    above = jnp.full_like(square, 0.00022905065861350646)
    for term in (0.0034082910107109506, 0.050955695062380861, 0.18520832239976145, 1.128379143519084):
        above = above * square + term
    below = jnp.full_like(square, -1.1791602954361697e-7)
    for term in (
        0.000023547966471313185, 0.0010179625278914885, 0.014070470171167667,
        0.11098505178285362, 0.49746925110067538, 1.0,
    ):
        below = below * square + term
    return value * above / below


def turn(values, tables, where, direction):
    cosine, sine_first, sine_second = (table[where, :] for table in tables)
    ahead = pltpu.roll(values, values.shape[1] - ROT // 2, 1)
    behind = pltpu.roll(values, ROT // 2, 1)
    return values * cosine + direction * (ahead * sine_first + behind * sine_second)


def row_tiles(start, count, tile, body):
    @pl.loop(0, count // tile)
    def _(n):
        body(pl.ds(pl.multiple_of(start + n * tile, tile), tile), pl.ds(pl.multiple_of(n * tile, tile), tile))


def forward_kernel(inner, keep, background, *refs):
    here = Place(inner)
    (tokens_ref, rows_ref, qkv_ref, up_ref, low_ref, qkv_bias, up_bias, cosine, sine_first,
     sine_second, doc_col, doc_row, *refs) = refs
    tables = (cosine, sine_first, sine_second)
    shards = refs[:4] if background else []
    refs = refs[len(shards):]
    final_ref, *refs = refs
    if keep:
        slope_ref, mixed_ref, total_ref, joined_ref, *refs = refs
    wholes = refs[:3] if background else []
    refs = refs[len(wholes):]
    if not keep:
        mixed_ref, joined_ref, *refs = refs
    one_ref, two_ref, hidden_ref, part_ref, *refs = refs
    sums = RowSum(here, part_ref, *refs[:14])
    refs = refs[14:]
    block = one_ref.shape[0]
    heads = qkv_ref.shape[1] // (3 * HD)
    cut = heads * HD
    peers = reduce_peers(here)
    spread = None
    if background:
        spread = Spread(here, shards, wholes, *refs)
        peers = spread.peers() + [here.far_peer(), here.near_peer()]
    greet(peers)
    events = []
    if background:
        for number in range(AHEAD):
            spread.send_on(number)
        spread.start_own()
        events = list(range(len(spread.order)))

    def serve():
        if events:
            spread.step(events.pop(0))

    for step in range(SPLIT):
        start = ((here.o + 1 + step) % SPLIT) * block
        kept = start if keep else 0

        def norm(where, own):
            values = f32(tokens_ref[where, :])
            centre = values - jnp.mean(values, axis=1, keepdims=True)
            spread_of = jnp.mean(centre * centre, axis=1, keepdims=True)
            normed = centre * lax.rsqrt(spread_of + EPS_NORM)
            one_ref[own, :] = (normed * rows_ref[0:1, :] + rows_ref[1:2, :]).astype(BF16)
            two_ref[own, :] = (normed * rows_ref[2:3, :] + rows_ref[3:4, :]).astype(BF16)

        row_tiles(start, block, 16, norm)
        serve()
        if step:
            sums.across(step - 1)
        whole = pl.ds(pl.multiple_of(start, block), block)
        mine = pl.ds(pl.multiple_of(kept, block), block)
        mixed = dot(one_ref[...], qkv_ref[...]) + qkv_bias[...]
        for head in range(heads):
            at = head * 3 * HD
            for offset in (0, HD):
                mixed_ref[mine, at + offset : at + offset + HD] = turn(
                    mixed[:, at + offset : at + offset + HD], tables, whole, 1.0
                ).astype(BF16)
            mixed_ref[mine, at + 2 * HD : at + 3 * HD] = mixed[:, at + 2 * HD : at + 3 * HD].astype(
                BF16
            )
        hidden_ref[...] = dot(two_ref[...], up_ref[...])
        serve()
        for head in range(heads):
            at = head * 3 * HD
            for first in range(0, block, 128):
                queries = pl.ds(pl.multiple_of(kept + first, 128), 128)
                tokens_at = pl.ds(pl.multiple_of(start + first, 128), 128)
                keys = pl.ds(pl.multiple_of(kept, 128), first + 128)
                scores = dot_cols(
                    mixed_ref[queries, at : at + HD], mixed_ref[keys, at + HD : at + 2 * HD]
                ) * HD ** (-0.5)
                own_block = (here.o + 1 + step) % SPLIT
                same = doc_col[tokens_at, :] == doc_row[own_block][:, : first + 128]
                earlier = first + lax.broadcasted_iota(
                    jnp.int32, scores.shape, 0
                ) >= lax.broadcasted_iota(jnp.int32, scores.shape, 1)
                scores = jnp.where(same & earlier, scores, MASKED)
                highest = jnp.max(scores, axis=1, keepdims=True)
                total = highest + jnp.log(
                    jnp.sum(jnp.exp(scores - highest), axis=1, keepdims=True)
                )
                if keep:
                    total_ref[tokens_at, head : head + 1] = total
                probs = jnp.exp(scores - total).astype(BF16)
                joined_ref[queries, head * HD : (head + 1) * HD] = dot(
                    probs, mixed_ref[keys, at + 2 * HD : at + 3 * HD]
                ).astype(BF16)
        if step > 1:
            sums.along(step - 2)

        def activate(where, own):
            hidden = hidden_ref[own, :] + up_bias[...]
            share = 0.5 * (1.0 + error_function(hidden * 0.7071067811865476))
            joined_ref[where, cut:] = (hidden * share).astype(BF16)
            if keep:
                density = jnp.exp(-0.5 * hidden * hidden) * 0.3989422804014327
                slope_ref[where, :] = share + hidden * density

        row_tiles(kept, block, 32, activate)
        serve()
        columns = 512

        @pl.loop(0, part_ref.shape[1] // columns)
        def _(n):
            at = pl.ds(pl.multiple_of(n * columns, columns), columns)
            part_ref[whole, at] = dot(joined_ref[mine, :], low_ref[:, at]).astype(BF16)

        sums.start(step)
    sums.across(SPLIT - 1)
    while events:
        serve()
    sums.along(SPLIT - 2)
    sums.along(SPLIT - 1)
    branch = sums.value() + rows_ref[4:5, :] + rows_ref[5:6, :]
    quarter = pl.ds(pl.multiple_of(here.o * block + here.t * sums.rows, sums.rows), sums.rows)
    final_ref[pl.ds(pl.multiple_of(here.t * sums.rows, sums.rows), sums.rows), :] = (
        f32(tokens_ref[quarter, :]) + branch
    ).astype(BF16)
    gather_quarters(here, final_ref, sums.rows, *sums.quarter_sems)
    sums.finish()
    if background:
        spread.finish()


def forward_call(tokens, rows, weights, biases, layout, block, inner, keep, shards, number):
    total_rows, d_model = tokens.shape
    qkv_all, up_all, low_all = weights
    heads = qkv_all.shape[1] // (3 * HD)
    background = shards is not None
    outs = [jax.ShapeDtypeStruct((block, d_model), BF16)]
    if keep:
        outs += [
            jax.ShapeDtypeStruct((total_rows, up_all.shape[1]), F32),
            jax.ShapeDtypeStruct((total_rows, qkv_all.shape[1]), BF16),
            jax.ShapeDtypeStruct((total_rows, heads), F32),
            jax.ShapeDtypeStruct((total_rows, low_all.shape[0]), BF16),
        ]
    specs = [VMEM_SPEC] * len(outs)
    scratch = []
    if not keep:
        scratch += [
            pltpu.VMEM((block, qkv_all.shape[1]), BF16),
            pltpu.VMEM((block, low_all.shape[0]), BF16),
        ]
    scratch += [
        pltpu.VMEM((block, d_model), BF16),
        pltpu.VMEM((block, d_model), BF16),
        pltpu.VMEM((block, up_all.shape[1]), F32),
        pltpu.VMEM((total_rows, d_model), BF16),
    ]
    scratch += reduce_scratch(block // QUARTERS, d_model)
    operands = [tokens, rows, qkv_all, up_all, low_all, *biases, *layout]
    in_specs = [VMEM_SPEC] * len(operands)
    if background:
        operands += shards
        in_specs += [ANY_SPEC] * 4
        outs += whole_shapes(shards, inner)
        specs += [ANY_SPEC] * 3
        scratch += spread_scratch(inner)
    return pl.pallas_call(
        functools.partial(forward_kernel, inner, keep, background),
        out_shape=outs,
        in_specs=in_specs,
        out_specs=specs,
        scratch_shapes=scratch,
        compiler_params=pltpu.CompilerParams(
            collective_id=number, has_side_effects=True, vmem_limit_bytes=60 * 1024 * 1024
        ),
    )(*operands)


def input_change(values, scaled):
    centre = values - jnp.mean(values, axis=1, keepdims=True)
    spread = jnp.mean(centre * centre, axis=1, keepdims=True)
    scale = lax.rsqrt(spread + EPS_NORM)
    normed = centre * scale
    along = jnp.mean(scaled * normed, axis=1, keepdims=True)
    return scale * (scaled - jnp.mean(scaled, axis=1, keepdims=True) - normed * along)


def reduce_scratch(rows, width):
    dma = pltpu.SemaphoreType.DMA
    return [
        pltpu.VMEM((rows, width), F32),
        pltpu.VMEM((SPLIT, 2, rows, width), BF16),
        pltpu.VMEM((SPLIT, rows, width), BF16),
        pltpu.VMEM((SPLIT, rows, width), BF16),
        pltpu.VMEM((SPLIT - 1, rows, width), BF16),
        pltpu.VMEM((SPLIT - 1, rows, width), BF16),
        dma((SPLIT, 2)),
        dma((SPLIT, 2)),
        dma((SPLIT,)),
        dma((SPLIT,)),
        dma((SPLIT - 1,)),
        dma((SPLIT - 1,)),
        dma((3,)),
        dma((3,)),
    ]


def final_grad_kernel(
    inner, part_ref, quarter_ref, branch_all, near_in, far_in, far_out, low, near_out,
    near_send, near_recv, far_send, far_recv, send, recv, local,
):
    here = Place(inner)
    rows = quarter_ref.shape[0]
    greet(reduce_peers(here))

    def rows_of(quarter):
        return pl.ds(quarter * rows, rows)

    near = []
    for side, quarter in enumerate(((here.near + 2) % QUARTERS, here.near)):
        near_out[side] = part_ref[rows_of(quarter), :].astype(BF16)
        near.append(
            remote(
                near_out.at[side],
                near_in.at[side],
                near_send.at[side],
                near_recv.at[side],
                here.near_peer(),
            )
        )
    near[0].wait_recv()
    far_out[...] = (part_ref[rows_of(here.far), :] + f32(near_in[0])).astype(BF16)
    far = remote(far_out, far_in, far_send, far_recv, here.far_peer())
    near[1].wait_recv()
    far.wait_recv()
    quarter_ref[...] = part_ref[rows_of(here.t), :] + f32(near_in[1]) + f32(far_in[...])
    low[...] = quarter_ref[...].astype(BF16)
    for copy in near + [far]:
        copy.wait_send()

    def piece(part, quarter):
        return branch_all.at[pl.ds((part * QUARTERS + quarter) * rows, rows), :]

    outer = [
        remote(
            low, piece(here.o, here.t), send.at[0, s], recv.at[0, s], here.outer_peer(s)
        )
        for s in range(1, SPLIT)
    ]
    own = pltpu.make_async_copy(low, piece(here.o, here.t), local)
    own.start()
    across, beside = [], []
    for s in range(SPLIT):
        part = (here.o + SPLIT - s) % SPLIT
        if s:
            outer[s - 1].wait_recv()
        source = piece(part, here.t) if s else low
        across.append(
            remote(source, piece(part, here.t), send.at[1, s], recv.at[1, s], here.far_peer())
        )
        beside.append(
            remote(source, piece(part, here.t), send.at[2, s], recv.at[2, s], here.near_peer())
        )
    for s in range(SPLIT):
        part = (here.o + SPLIT - s) % SPLIT
        across[s].wait_recv()
        beside.append(
            remote(
                piece(part, here.far),
                piece(part, here.far),
                send.at[3, s],
                recv.at[3, s],
                here.near_peer(),
            )
        )
    for copy in beside:
        copy.wait_recv()
    for copy in outer + across + beside:
        copy.wait_send()
    own.wait()


def final_grad_call(part, inner, number):
    block, width = part.shape
    rows = block // QUARTERS
    dma = pltpu.SemaphoreType.DMA
    return pl.pallas_call(
        functools.partial(final_grad_kernel, inner),
        out_shape=[
            jax.ShapeDtypeStruct((rows, width), F32),
            jax.ShapeDtypeStruct((SPLIT * block, width), BF16),
        ],
        in_specs=[VMEM_SPEC],
        out_specs=[VMEM_SPEC, ANY_SPEC],
        scratch_shapes=[
            pltpu.VMEM((2, rows, width), BF16),
            pltpu.VMEM((rows, width), BF16),
            pltpu.VMEM((rows, width), BF16),
            pltpu.VMEM((rows, width), BF16),
            pltpu.VMEM((2, rows, width), BF16),
            dma((2,)),
            dma((2,)),
            dma,
            dma,
            dma((4, SPLIT)),
            dma((4, SPLIT)),
            dma,
        ],
        compiler_params=pltpu.CompilerParams(
            collective_id=number, has_side_effects=True, vmem_limit_bytes=48 * 1024 * 1024
        ),
    )(part)


class AllSum:
    def __init__(self, here, mine, near_in, far_in, outer, inner, send, recv):
        self.here, self.mine, self.near_in, self.far_in = here, mine, near_in, far_in
        self.outer, self.inner, self.send, self.recv = outer, inner, send, recv
        self.copies = []

    def pair(self, stage, target, peer):
        copy = remote(
            self.mine.at[stage], target, self.send.at[stage], self.recv.at[stage], peer
        )
        self.copies.append(copy)
        return copy

    def near(self, value):
        self.mine[0] = value
        self.waiting = [self.pair(0, self.near_in, self.here.near_peer())]

    def far(self):
        self.waiting[0].wait_recv()
        self.mine[1] = self.mine[0] + self.near_in[...]
        self.waiting = [self.pair(1, self.far_in, self.here.far_peer())]

    def group(self, buffer, index, first, peers):
        self.waiting = []
        for number, peer in enumerate(peers):
            copy = remote(
                buffer.at[index],
                buffer.at[index],
                self.send.at[first + number],
                self.recv.at[first + number],
                peer,
            )
            self.waiting.append(copy)
            self.copies.append(copy)

    def along_outer(self):
        self.waiting[0].wait_recv()
        here = self.here
        self.outer[here.o] = self.mine[1] + self.far_in[...]
        self.group(self.outer, here.o, 2, [here.outer_peer(s) for s in range(1, SPLIT)])

    def along_inner(self):
        here = self.here
        for copy in self.waiting:
            copy.wait_recv()
        value = self.outer[0]
        for part in range(1, SPLIT):
            value = value + self.outer[part]
        self.inner[here.i] = value
        peers = [here.inner_peer(r) for r in range(1, here.inner)]
        self.group(self.inner, here.i, 1 + SPLIT, peers)

    def value(self):
        for copy in self.waiting:
            copy.wait_recv()
        value = self.inner[0]
        for part in range(1, self.here.inner):
            value = value + self.inner[part]
        for copy in self.copies:
            copy.wait_send()
        return value


def all_sum_scratch(shape, inner):
    dma = pltpu.SemaphoreType.DMA
    return [
        pltpu.VMEM((2, *shape), F32),
        pltpu.VMEM(shape, F32),
        pltpu.VMEM(shape, F32),
        pltpu.VMEM((SPLIT, *shape), F32),
        pltpu.VMEM((inner, *shape), F32),
        dma((SPLIT + inner,)),
        dma((SPLIT + inner,)),
    ]


def whole_sum(value):
    return jnp.sum(jnp.sum(value, axis=1, keepdims=True), axis=0, keepdims=True)


def finish_kernel(
    inner, part_ref, tokens_ref, quarter_ref, qkv, up, low, rows_ref, bias_ref,
    grad_ref, qkv_out, up_out, out_out, down_out, rows_out, bias_out, norm_ref, *scratch,
):
    here = Place(inner)
    sums = RowSum(here, part_ref, *scratch[:14])
    inputs, sends = scratch[14:18], scratch[18:22]
    send_i, recv_i, send_o, recv_o, local = scratch[22:27]
    small = AllSum(here, *scratch[27:34])
    squares = AllSum(here, *scratch[34:41])
    bias_in, bias_send, bias_recv = scratch[41:44]
    outs = (qkv_out, up_out, out_out, down_out)
    shard = qkv_out.shape[0]
    width_out = out_out.shape[0] // SPLIT
    width_down = down_out.shape[0] // SPLIT

    def src(m, index):
        where = pl.ds(index * shard, shard)
        if m == 0:
            return qkv.at[where, :]
        if m == 1:
            return up.at[where, :]
        rows = pl.ds(0, width_out) if m == 2 else pl.ds(width_out, width_down)
        return low.at[rows, where] if aligned(shard) else low.at[index, rows, :]

    def dst(m):
        if m < 2:
            width = outs[m].shape[1] // SPLIT
            return outs[m].at[:, pl.ds(here.o * width, width)]
        width = outs[m].shape[0] // SPLIT
        return outs[m].at[pl.ds(here.o * width, width), :]

    peers = reduce_peers(here) + [here.inner_peer(r) for r in range(1, inner)]
    greet(peers)
    first, last, own = {}, [], []

    order = [(m, s) for m in (2, 3, 1, 0) for s in (2, 1, 3, 0)]

    def trade(number):
        if number >= len(order):
            return
        m, s = order[number]
        part = (here.o + s) % SPLIT
        for r in range(1, inner):
            first[m, s, r] = remote(
                src(m, part * inner + (here.i + r) % inner),
                inputs[m].at[s, r - 1],
                send_i.at[m, s, r - 1],
                recv_i.at[m, s, r - 1],
                here.inner_peer(r),
            )

    def settle(number):
        m, s = order[number]
        part = (here.o + s) % SPLIT
        total = f32(src(m, part * inner + here.i)[...])
        for r in range(1, inner):
            first[m, s, r].wait_recv()
        trade(number + AHEAD)
        for r in range(1, inner):
            total = total + f32(inputs[m][s, r - 1])
        sends[m][s] = total.astype(BF16)
        if s:
            last.append(
                remote(
                    sends[m].at[s],
                    dst(m),
                    send_o.at[m, s - 1],
                    recv_o.at[m, s - 1],
                    here.outer_peer(s),
                )
            )
        else:
            copy = pltpu.make_async_copy(sends[m].at[0], dst(m), local.at[m])
            copy.start()
            own.append(copy)
        return whole_sum(total * total)

    for number in range(AHEAD):
        trade(number)
    for step in range(SPLIT):
        sums.start(step)
    small.near(rows_ref[...])
    bias_in[here.i] = bias_ref[...]
    bias_inner = [
        remote(
            bias_in.at[here.i],
            bias_in.at[here.i],
            bias_send.at[SPLIT + r],
            bias_recv.at[SPLIT + r],
            here.inner_peer(r),
        )
        for r in range(1, inner)
    ]
    square = settle(0)
    square = square + settle(1)
    for step in range(SPLIT):
        sums.across(step)
        square = square + settle(2 + step)
    small.far()
    sums.along(0)
    square = square + settle(6)
    square = square + settle(7)
    small.along_outer()
    for copy in bias_inner:
        copy.wait_recv()
    bias = bias_in[0]
    for part in range(1, inner):
        bias = bias + bias_in[part]
    bias_out[here.o] = bias
    bias_outer = [
        remote(
            bias_out.at[here.o],
            bias_out.at[here.o],
            bias_send.at[s],
            bias_recv.at[s],
            here.outer_peer(s),
        )
        for s in range(1, SPLIT)
    ]
    square = square + whole_sum(bias * bias) / inner
    sums.along(1)
    square = square + settle(8)
    square = square + settle(9)
    small.along_inner()
    sums.along(2)
    square = square + settle(10)
    square = square + settle(11)
    rows_out[...] = small.value()
    sums.along(3)
    for number in range(12, len(order)):
        square = square + settle(number)
    squares.near(jnp.broadcast_to(square, norm_ref.shape))
    squares.far()
    squares.along_outer()
    squares.along_inner()
    norm = squares.value()
    rows = rows_out[...]
    doubled = lax.broadcasted_iota(jnp.int32, rows.shape, 0) == 4
    norm_ref[...] = norm + whole_sum(rows * rows * jnp.where(doubled, 2.0, 1.0))
    mine = pl.ds(here.t * sums.rows, sums.rows)
    change = input_change(f32(tokens_ref[mine, :]), sums.value())
    grad_ref[mine, :] = (quarter_ref[...] + change).astype(BF16)
    gather_quarters(here, grad_ref, sums.rows, *sums.quarter_sems)
    sums.finish()
    for copy in bias_outer:
        copy.wait_recv()
    for copy in bias_inner + bias_outer:
        copy.wait_send()
    for copy in last:
        copy.wait()
    for copy in own:
        copy.wait()
    for copy in first.values():
        copy.wait_send()


def finish_call(part, tokens, quarter, grads, rows, bias, shards, inner, number):
    dma = pltpu.SemaphoreType.DMA
    qkv, out, up, down = shards
    ordered = (qkv, up, out, down)
    if not aligned(out[1]):
        low = grads[2].reshape(grads[2].shape[0], SPLIT * inner, out[1])
        grads = (*grads[:2], jnp.swapaxes(low, 0, 1))
    pieces = [
        (qkv[0], qkv[1] // SPLIT),
        (up[0], up[1] // SPLIT),
        (out[0] // SPLIT, out[1]),
        (down[0] // SPLIT, down[1]),
    ]
    peers = max(inner - 1, 1)
    block, width = tokens.shape
    tile = (8, 128)
    return pl.pallas_call(
        functools.partial(finish_kernel, inner),
        out_shape=[
            jax.ShapeDtypeStruct((block, width), BF16),
            *(jax.ShapeDtypeStruct(shape, BF16) for shape in ordered),
            jax.ShapeDtypeStruct(rows.shape, F32),
            jax.ShapeDtypeStruct((SPLIT, *bias.shape), F32),
            jax.ShapeDtypeStruct(tile, F32),
        ],
        in_specs=[VMEM_SPEC] * 8,
        out_specs=[VMEM_SPEC] + [ANY_SPEC] * 4 + [VMEM_SPEC] * 3,
        scratch_shapes=reduce_scratch(block // QUARTERS, width)
        + [pltpu.VMEM((SPLIT, peers, *piece), BF16) for piece in pieces]
        + [pltpu.VMEM((SPLIT, *piece), BF16) for piece in pieces]
        + [
            dma((4, SPLIT, peers)),
            dma((4, SPLIT, peers)),
            dma((4, SPLIT - 1)),
            dma((4, SPLIT - 1)),
            dma((4,)),
        ]
        + all_sum_scratch(rows.shape, inner)
        + all_sum_scratch(tile, inner)
        + [
            pltpu.VMEM((inner, *bias.shape), F32),
            dma((SPLIT + inner,)),
            dma((SPLIT + inner,)),
        ],
        compiler_params=pltpu.CompilerParams(
            collective_id=number, has_side_effects=True, vmem_limit_bytes=60 * 1024 * 1024
        ),
    )(part, tokens, quarter, *grads, rows, bias)


def reward_kernel(
    inner, stats_ref, member_ref, label_ref, out_ref, stats, outer_in, inner_in,
    send, recv, send_o, recv_o, send_i, recv_i,
):
    here = Place(inner)
    tensor_peers = [(here.dp, (here.t + s) % QUARTERS) for s in range(1, QUARTERS)]
    outer_peers = [here.outer_peer(s) for s in range(1, SPLIT)]
    inner_peers = [here.inner_peer(r) for r in range(1, inner)]
    greet(tensor_peers + outer_peers + inner_peers)

    def share(buffer, index, sends, recvs, peers):
        return [
            remote(buffer.at[index], buffer.at[index], sends.at[n], recvs.at[n], peer)
            for n, peer in enumerate(peers)
        ]

    stats[here.t] = stats_ref[...]
    copies = share(stats, here.t, send, recv, tensor_peers)
    for copy in copies:
        copy.wait_recv()
    quarters = [stats[q] for q in range(QUARTERS)]
    highest = functools.reduce(jnp.maximum, quarters)
    summed = functools.reduce(lambda a, b: a + b, [jnp.exp(q - highest) for q in quarters])
    totals = highest + jnp.log(summed)
    picks = functools.reduce(lambda a, b: a + b, quarters)
    log_probs = picks - totals_to_picks(totals)
    member = member_ref[...]
    policy_docs = jnp.sum(member * log_probs[1:2, :], axis=1, keepdims=True)
    frozen_docs = jnp.sum(member * log_probs[3:4, :], axis=1, keepdims=True)
    reward = policy_docs - frozen_docs
    outer_in[here.o] = jnp.broadcast_to(whole_sum(reward), outer_in.shape[1:])
    more = share(outer_in, here.o, send_o, recv_o, outer_peers)
    for copy in more:
        copy.wait_recv()
    inner_in[here.i] = functools.reduce(lambda a, b: a + b, [outer_in[n] for n in range(SPLIT)])
    rest = share(inner_in, here.i, send_i, recv_i, inner_peers)
    for copy in rest:
        copy.wait_recv()
    total = functools.reduce(lambda a, b: a + b, [inner_in[n] for n in range(inner)])
    seq_count = inner * SPLIT * SEGS
    shift = total[:, 0:1] / seq_count
    sigmoid_value = 1.0 / (1.0 + jnp.exp(-BETA_KTO * (reward - shift)))
    labels = label_ref[:, 0:1]
    doc_grad = BETA_KTO * sigmoid_value * (1.0 - sigmoid_value) * (1.0 - 2.0 * labels) / seq_count
    out_ref[0:1, :] = jnp.sum(member * doc_grad, axis=0, keepdims=True)
    out_ref[1:2, :] = totals[0:1, :]
    for copy in copies + more + rest:
        copy.wait_send()


def totals_to_picks(totals):
    return jnp.concatenate([totals[0:1], totals[0:1], totals[2:3], totals[2:3], totals[4:]], axis=0)


def reward_call(stats, member, labels, inner, number):
    dma = pltpu.SemaphoreType.DMA
    tile = (8, 128)
    peers = max(inner - 1, 1)
    return pl.pallas_call(
        functools.partial(reward_kernel, inner),
        out_shape=jax.ShapeDtypeStruct((2, stats.shape[1]), F32),
        in_specs=[VMEM_SPEC] * 3,
        out_specs=VMEM_SPEC,
        scratch_shapes=[
            pltpu.VMEM((QUARTERS, *stats.shape), F32),
            pltpu.VMEM((SPLIT, *tile), F32),
            pltpu.VMEM((inner, *tile), F32),
            dma((QUARTERS - 1,)),
            dma((QUARTERS - 1,)),
            dma((SPLIT - 1,)),
            dma((SPLIT - 1,)),
            dma((peers,)),
            dma((peers,)),
        ],
        compiler_params=pltpu.CompilerParams(collective_id=number, has_side_effects=True),
    )(stats, member, labels)


def turn_tables(positions):
    half = ROT // 2
    frequency = 10000.0 ** (-2.0 * jnp.arange(half, dtype=F32) / ROT)
    angles = positions.reshape(-1).astype(F32)[:, None] * frequency
    cosine, sine = jnp.cos(angles), jnp.sin(angles)
    none = jnp.zeros((angles.shape[0], HD - ROT), F32)
    empty = jnp.zeros_like(sine)
    return (
        jnp.concatenate([cosine, cosine, none + 1.0], axis=1),
        jnp.concatenate([-sine, empty, none], axis=1),
        jnp.concatenate([empty, sine, none], axis=1),
    )


def rotate_back(values, positions):
    half_rot = ROT // 2
    frequency = 10000.0 ** (-2.0 * jnp.arange(half_rot, dtype=F32) / ROT)
    angles = positions.astype(F32)[..., None] * frequency
    cosine = jnp.cos(angles)[..., None, :]
    sine_part = -jnp.sin(angles)[..., None, :]
    first_half = values[..., :half_rot]
    second_half = values[..., half_rot:ROT]
    return jnp.concatenate(
        [
            first_half * cosine - second_half * sine_part,
            second_half * cosine + first_half * sine_part,
            values[..., ROT:],
        ],
        axis=-1,
    )


def doc_layout(lengths_row, row_count):
    ends, run = [], 0
    for segment in range(lengths_row.shape[0]):
        run = run + lengths_row[segment]
        ends.append(run)
    doc_ends = jnp.stack(ends)
    starts = doc_ends - lengths_row
    index_rows = jnp.arange(row_count, dtype=jnp.int32)
    member = (index_rows[:, None] >= starts[None, :]) & (index_rows[:, None] < doc_ends[None, :])
    doc_ids = jnp.arange(lengths_row.shape[0], dtype=jnp.int32)
    doc_of = jnp.sum(jnp.where(member, doc_ids[None, :], 0), axis=1)
    positions = index_rows - jnp.sum(jnp.where(member, starts[None, :], 0), axis=1)
    return (member, positions, doc_of)


def allowed_keys(doc_of):
    index_rows = jnp.arange(doc_of.shape[-1], dtype=jnp.int32)
    return (doc_of[..., :, None] == doc_of[..., None, :]) & (
        index_rows[:, None] >= index_rows[None, :]
    )


def contract_rows(left_rows, right_rows):
    return lax.dot_general(
        left_rows, right_rows, (((0,), (0,)), ((), ())), preferred_element_type=F32
    )


def contract_cols(left_rows, right_rows):
    return lax.dot_general(
        left_rows, right_rows, (((1,), (1,)), ((), ())), preferred_element_type=F32
    )


def normed_rows(normed, gain_row, shift_row):
    return (normed * gain_row + shift_row).astype(BF16)


def layer_backward(branch_low, kept_values, weight_set, positions, allowed):
    qkv_all, up_all, low_all = weight_set
    slope, mixed_low, log_total, joined = kept_values
    blocks, block = positions.shape
    heads_local = log_total.shape[1]
    mixed_low = mixed_low.reshape(blocks, block, heads_local, 3, HD)
    query_low, key_low, value_low = (mixed_low[:, :, :, n] for n in range(3))
    log_total = log_total.reshape(blocks, block, heads_local).swapaxes(1, 2)[..., None]
    cut = heads_local * HD
    joined_grad = contract_cols(branch_low, low_all)
    hidden_low = (joined_grad[:, cut:] * slope).astype(BF16)
    attended_grad = joined_grad[:, :cut].reshape(blocks, block, heads_local, HD).astype(BF16)
    score_scale = HD ** (-0.5)
    scores = (
        jnp.einsum("bqhd,bkhd->bhqk", query_low, key_low, preferred_element_type=F32) * score_scale
    )
    scores = jnp.where(allowed[:, None], scores, MASKED)
    probs = jnp.exp(scores - log_total)
    prob_grad = jnp.einsum("bqhd,bkhd->bhqk", attended_grad, value_low, preferred_element_type=F32)
    value_grad = jnp.einsum(
        "bhqk,bqhd->bkhd", probs.astype(BF16), attended_grad, preferred_element_type=F32
    )
    score_grad = (probs * (prob_grad - jnp.sum(probs * prob_grad, axis=3, keepdims=True))).astype(
        BF16
    )
    query_grad = (
        jnp.einsum("bhqk,bkhd->bqhd", score_grad, key_low, preferred_element_type=F32) * score_scale
    )
    key_grad = (
        jnp.einsum("bhqk,bqhd->bkhd", score_grad, query_low, preferred_element_type=F32)
        * score_scale
    )
    mixed_grad = jnp.stack(
        [rotate_back(query_grad, positions), rotate_back(key_grad, positions), value_grad], axis=3
    )
    mixed_grad = mixed_grad.reshape(blocks * block, heads_local * 3 * HD).astype(BF16)
    one_part = contract_cols(mixed_grad, qkv_all)
    two_part = contract_cols(hidden_low, up_all)
    return (one_part, two_part, mixed_grad, hidden_low)


def vocab_stats(final_low, head_weight, targets, vocab_start):
    logits = jnp.dot(final_low, head_weight, preferred_element_type=F32)
    highest = jnp.max(logits, axis=1)
    log_total = highest + jnp.log(jnp.sum(jnp.exp(logits - highest[:, None]), axis=1))
    column = vocab_start + lax.broadcasted_iota(jnp.int32, logits.shape, 1)
    chosen = column == targets[:, None]
    picked = jnp.sum(jnp.where(chosen, logits, 0.0), axis=1)
    return (logits, log_total, picked, chosen)


def adam_step(master, mean_old, square_old, gradient, factor, rate, decay_rate):
    clipped = f32(gradient) * factor
    mean_new = BETA_FIRST * mean_old + (1.0 - BETA_FIRST) * clipped
    square_new = BETA_SECOND * square_old + (1.0 - BETA_SECOND) * clipped * clipped
    mean_hat = mean_new / (1.0 - BETA_FIRST**STEP)
    square_hat = square_new / (1.0 - BETA_SECOND**STEP)
    master_new = master - rate * (
        mean_hat / (jnp.sqrt(square_hat) + ADAM_EPS) + decay_rate * master
    )
    return (mean_new, square_new, master_new)


def eight_rows(rows):
    return jnp.zeros((8, rows.shape[1]), F32).at[: rows.shape[0]].set(rows)


def on_device(
    inputs,
    targets,
    doc_lengths,
    desirable,
    head_weight,
    qkv_master,
    out_master,
    up_master,
    down_master,
    vectors,
    hidden_bias,
    qkv_mean,
    out_mean,
    up_mean,
    down_mean,
    vectors_mean,
    hidden_mean,
    qkv_square,
    out_square,
    up_square,
    down_square,
    vectors_square,
    hidden_square,
    qkv_frozen,
    out_frozen,
    up_frozen,
    down_frozen,
    vectors_frozen,
    hidden_frozen,
):
    dp_size = lax.axis_size("dp")
    tensor_size = lax.axis_size("tensor")
    inner = dp_size // SPLIT
    outer_index = lax.axis_index("dp") // inner
    block = inputs.shape[0]
    lengths_tile = jnp.zeros((8, 128), jnp.int32).at[0, :SEGS].set(doc_lengths[0])
    masters = tuple(w.astype(BF16) for w in (qkv_master, out_master, up_master, down_master))
    *policy_set, tokens_all, lengths_all = spread_weights(masters, inner, inputs, lengths_tile, 0)
    frozen_shards = (qkv_frozen, out_frozen, up_frozen, down_frozen)
    member, _, _ = doc_layout(doc_lengths[0], block)
    _, positions, doc_of = jax.vmap(lambda row: doc_layout(row, block))(lengths_all[:, 0, :SEGS])
    allowed = allowed_keys(doc_of)

    cut = qkv_master.shape[1]
    width_qkv, width_up = cut // SPLIT, up_master.shape[1] // SPLIT

    def own_bias(bias):
        return (
            lax.dynamic_slice(bias, (outer_index * width_qkv,), (width_qkv,))[None],
            lax.dynamic_slice(bias, (cut + outer_index * width_up,), (width_up,))[None],
        )

    values = f32(tokens_all)
    centre = values - jnp.mean(values, axis=1, keepdims=True)
    scale = lax.rsqrt(jnp.mean(centre * centre, axis=1, keepdims=True) + EPS_NORM)
    normed = centre * scale
    one_low = normed_rows(normed, vectors[0], vectors[1])
    two_low = normed_rows(normed, vectors[2], vectors[3])
    layout = (
        *turn_tables(positions),
        doc_of.reshape(-1, 1),
        doc_of[:, None, :],
    )
    final_low, *kept = forward_call(
        tokens_all, eight_rows(vectors), policy_set, own_bias(hidden_bias), layout, block, inner,
        True, frozen_shards, 2,
    )
    kept_values = tuple(kept[:4])
    frozen_set = (*kept[4:6], joined_columns(kept[6]))
    (frozen_low,) = forward_call(
        tokens_all, eight_rows(vectors_frozen), frozen_set, own_bias(hidden_frozen), layout, block,
        inner, False, None, 3,
    )
    vocab_start = lax.axis_index("tensor") * head_weight.shape[1]
    policy_logits, policy_total, policy_pick, chosen = vocab_stats(
        final_low, head_weight, targets, vocab_start
    )
    _, frozen_total, frozen_pick, _ = vocab_stats(frozen_low, head_weight, targets, vocab_start)
    none = jnp.zeros_like(policy_total)
    stats = jnp.stack(
        [policy_total, policy_pick, frozen_total, frozen_pick, none, none, none, none]
    )
    doc_rows = jnp.zeros((8, block), F32).at[:SEGS].set(f32(member).T)
    labels = jnp.zeros((8, 128), F32).at[:SEGS].set(f32(desirable[0])[:, None])
    token_grad, policy_total = reward_call(stats, doc_rows, labels, inner, 6)
    logit_grad = (
        token_grad[:, None]
        * (chosen.astype(F32) - jnp.exp(policy_logits - policy_total[:, None]))
    ).astype(BF16)
    final_part = contract_cols(logit_grad, head_weight)
    final_quarter, branch_low = final_grad_call(final_part, inner, 4)
    joined = kept_values[3]
    one_part, two_part, mixed_grad, hidden_low = layer_backward(
        branch_low, kept_values, policy_set, positions, allowed
    )
    scaled_part = (one_part * vectors[0] + two_part * vectors[2]).astype(BF16)
    shards = tuple(w.shape for w in masters)
    grads = (
        contract_rows(one_low, mixed_grad).astype(BF16),
        contract_rows(two_low, hidden_low).astype(BF16),
        contract_rows(joined, branch_low).astype(BF16),
    )
    none = jnp.zeros_like(vectors[0])
    vector_part = jnp.stack(
        [
            jnp.sum(one_part * normed, axis=0),
            jnp.sum(one_part, axis=0),
            jnp.sum(two_part * normed, axis=0),
            jnp.sum(two_part, axis=0),
            jnp.sum(f32(final_quarter.astype(BF16)), axis=0),
            none,
            none,
            none,
        ]
    )
    bias_part = jnp.concatenate(
        [jnp.sum(mixed_grad, axis=0, dtype=F32), jnp.sum(hidden_low, axis=0, dtype=F32)]
    )
    bias_rows = (width_qkv + width_up) // 128
    bias_tile = (
        jnp.zeros((-(-bias_rows // 8) * 8, 128), F32)
        .at[:bias_rows]
        .set(bias_part.reshape(bias_rows, 128))
    )
    input_grad, qkv_grad, up_grad, out_grad, down_grad, vector_sum, bias_sum, square = finish_call(
        scaled_part, inputs, final_quarter, grads, vector_part, bias_tile, shards, inner, 5
    )
    input_grad = f32(input_grad)
    vector_grad = jnp.concatenate([vector_sum[:5], vector_sum[4:5]], axis=0)
    bias_sum = bias_sum[:, :bias_rows].reshape(SPLIT, bias_rows * 128)
    hidden_grad = jnp.concatenate(
        [bias_sum[:, :width_qkv].reshape(-1), bias_sum[:, width_qkv:].reshape(-1)]
    )
    grad_norm = jnp.sqrt(square[0, 0])
    factor = jnp.minimum(1.0, CLIP_NORM / (grad_norm + 1e-06))
    qkv_state = adam_step(
        qkv_master, qkv_mean, qkv_square, qkv_grad, factor, LEARN_RATE, WEIGHT_DECAY
    )
    out_state = adam_step(
        out_master, out_mean, out_square, out_grad, factor, LEARN_RATE, WEIGHT_DECAY
    )
    up_state = adam_step(up_master, up_mean, up_square, up_grad, factor, LEARN_RATE, WEIGHT_DECAY)
    down_state = adam_step(
        down_master, down_mean, down_square, down_grad, factor, LEARN_RATE, WEIGHT_DECAY
    )
    vector_state = adam_step(
        vectors, vectors_mean, vectors_square, vector_grad, factor, VECTOR_RATE, 0.0
    )
    hidden_state = adam_step(
        hidden_bias, hidden_mean, hidden_square, hidden_grad, factor, VECTOR_RATE, 0.0
    )
    return (
        final_low,
        input_grad,
        grad_norm,
        *qkv_state,
        *out_state,
        *up_state,
        *down_state,
        *vector_state,
        *hidden_state,
    )


def solution(mesh):
    rows, cols = P("dp", "tensor"), P("tensor", "dp")
    matrices = (rows, cols, rows, cols)
    placed = (
        P("dp", None),
        P("dp"),
        P("dp", None),
        P("dp", None),
        P(None, "tensor"),
        *matrices,
        P(),
        P("tensor"),
        *matrices,
        P(),
        P("tensor"),
        *matrices,
        P(),
        P("tensor"),
        *matrices,
        P(),
        P("tensor"),
    )
    return jax.shard_map(
        on_device,
        mesh=mesh,
        in_specs=placed,
        out_specs=(
            P("dp", None),
            P("dp", None),
            P(),
            *(spec for spec in matrices for _ in range(3)),
            P(),
            P(),
            P(),
            P("tensor"),
            P("tensor"),
            P("tensor"),
        ),
        check_vma=False,
    )
```

```python
import functools

import jax
import jax.numpy as jnp
from jax import lax
from jax.experimental import pallas as pl
from jax.experimental.pallas import tpu as pltpu
from jax.sharding import PartitionSpec as P

HD = 128
ROT = 32
SEGS = 4
STEP = 3
SPLIT = 4
QUARTERS = 4
MEAN, SCALE, FACTS = 6, 7, 8
AHEAD = 3


EPS_NORM = 1e-05
BETA_KTO = 0.1
CLIP_NORM = 0.01
LEARN_RATE = 0.02
VECTOR_RATE = 0.2
BETA_FIRST = 0.9
BETA_SECOND = 0.999
ADAM_EPS = 1e-08
WEIGHT_DECAY = 0.01
MASKED = -1e30

MESH = pl.DeviceIdType.MESH
BF16 = jnp.bfloat16
F32 = jnp.float32
ANY_SPEC = pl.BlockSpec(memory_space=pltpu.HBM)
VMEM_SPEC = pl.BlockSpec(memory_space=pltpu.VMEM)


class Place:
    def __init__(self, inner):
        self.inner = inner
        self.dp = lax.axis_index("dp")
        self.t = lax.axis_index("tensor")
        self.o = self.dp // inner
        self.i = self.dp % inner
        self.near = self.t + 1 - 2 * (self.t % 2)
        self.far = (self.t + 2) % QUARTERS

    def outer_peer(self, shift):
        return (((self.o + shift) % SPLIT) * self.inner + self.i, self.t)

    def inner_peer(self, shift):
        return (self.o * self.inner + (self.i + shift) % self.inner, self.t)

    def near_peer(self):
        return (self.dp, self.near)

    def far_peer(self):
        return (self.dp, self.far)


def aligned(shard):
    return shard % 128 == 0


def greet(peers):
    barrier = pltpu.get_barrier_semaphore()
    for peer in peers:
        pl.semaphore_signal(barrier, inc=1, device_id=peer, device_id_type=MESH)
    pl.semaphore_wait(barrier, len(peers))


def remote(src, dst, send_sem, recv_sem, peer):
    copy = pltpu.make_async_remote_copy(
        src_ref=src,
        dst_ref=dst,
        send_sem=send_sem,
        recv_sem=recv_sem,
        device_id=peer,
        device_id_type=MESH,
    )
    copy.start()
    return copy


class Spread:
    def __init__(self, here, shards, wholes, send_o, recv_o, send_i, recv_i, local, *held):
        self.here = here
        self.qkv, self.out, self.up, self.down = shards
        self.qkv_all, self.up_all, self.low_all = wholes
        self.send_o, self.recv_o, self.send_i, self.recv_i = send_o, recv_o, send_i, recv_i
        self.local, self.held = local, held
        self.first, self.own, self.passed = {}, [], []
        self.order = [(m, s) for m in range(4) for s in (2, 1, 3)]

    def src(self, m, part):
        shard = (self.qkv, self.up, self.out, self.down)[m]
        width = shard.shape[1 if m < 2 else 0] // SPLIT
        where = pl.ds(part * width, width)
        return shard.at[:, where] if m < 2 else shard.at[where, :]

    def dst(self, m, index):
        shard = self.qkv.shape[0]
        where = pl.ds(index * shard, shard)
        if m < 2:
            return (self.qkv_all, self.up_all)[m].at[where, :]
        width_out, width_down = self.out.shape[0] // SPLIT, self.down.shape[0] // SPLIT
        rows = pl.ds(0, width_out) if m == 2 else pl.ds(width_out, width_down)
        low_all = self.low_all
        return low_all.at[rows, where] if aligned(shard) else low_all.at[index, rows, :]

    def peers(self):
        here = self.here
        peers = [here.outer_peer(s) for s in range(1, SPLIT)]
        return peers + [here.inner_peer(r) for r in range(1, here.inner)]

    def send_on(self, number):
        if number >= len(self.order):
            return
        m, s = self.order[number]
        self.first[m, s] = remote(
            self.src(m, (self.here.o + s) % SPLIT),
            self.dst(m, self.here.dp),
            self.send_o.at[m, s - 1],
            self.recv_o.at[m, s - 1],
            self.here.outer_peer(s),
        )

    def pass_on(self, m, s, source, index):
        here = self.here
        for r in range(1, here.inner):
            self.passed.append(
                remote(
                    source,
                    self.dst(m, index),
                    self.send_i.at[m, s, r - 1],
                    self.recv_i.at[m, s, r - 1],
                    here.inner_peer(r),
                )
            )

    def start_own(self):
        here = self.here
        loads = [
            pltpu.make_async_copy(self.src(m, here.o), self.held[m], self.local.at[m])
            for m in range(4)
        ]
        for load in loads:
            load.start()
        for m, load in enumerate(loads):
            load.wait()
            self.pass_on(m, 0, self.held[m], here.dp)
            copy = pltpu.make_async_copy(self.held[m], self.dst(m, here.dp), self.local.at[4 + m])
            copy.start()
            self.own.append(copy)

    def step(self, number):
        here = self.here
        m, s = self.order[number]
        self.first[m, s].wait_recv()
        self.send_on(number + AHEAD)
        index = ((here.o + SPLIT - s) % SPLIT) * here.inner + here.i
        self.pass_on(m, s, self.dst(m, index), index)

    def finish(self):
        for copy in self.first.values():
            copy.wait_send()
        for copy in self.own:
            copy.wait()
        for copy in self.passed:
            copy.wait()


def spread_weights_kernel(
    inner, qkv, out, up, down, tokens, lengths, qkv_all, up_all, low_all, tokens_all, lengths_all,
    send_o, recv_o, send_i, recv_i, local, held_0, held_1, held_2, held_3,
    send_t, recv_t, send_l, recv_l,
):
    here = Place(inner)
    spread = Spread(
        here, (qkv, out, up, down), (qkv_all, up_all, low_all),
        send_o, recv_o, send_i, recv_i, local, held_0, held_1, held_2, held_3,
    )
    greet(spread.peers() + [here.far_peer(), here.near_peer()])
    rows, block = tokens.shape[0] // QUARTERS, tokens.shape[0]

    def piece(part, quarter):
        return tokens_all.at[pl.ds((part * QUARTERS + quarter) * rows, rows), :]

    waits, token_copies, across, own = [], {}, {}, []
    for s in (2, 1, 3):
        token_copies[s] = remote(
            tokens.at[pl.ds(here.t * rows, rows), :],
            piece(here.o, here.t),
            send_t.at[0, s - 1],
            recv_t.at[0, s - 1],
            here.outer_peer(s),
        )
        waits.append(
            remote(
                lengths,
                lengths_all.at[here.o],
                send_l.at[s - 1],
                recv_l.at[s - 1],
                here.outer_peer(s),
            )
        )
    own.append(
        pltpu.make_async_copy(
            tokens, tokens_all.at[pl.ds(here.o * block, block), :], local.at[8]
        )
    )
    own.append(pltpu.make_async_copy(lengths, lengths_all.at[here.o], local.at[9]))
    for copy in own:
        copy.start()
    spread.start_own()
    for number, s in enumerate((2, 1, 3)):
        token_copies[s].wait_recv()
        spread.send_on(number)
        part = (here.o + SPLIT - s) % SPLIT
        for stage, peer in ((1, here.far_peer()), (2, here.near_peer())):
            copy = remote(
                piece(part, here.t),
                piece(part, here.t),
                send_t.at[stage, s - 1],
                recv_t.at[stage, s - 1],
                peer,
            )
            if stage == 1:
                across[s] = copy
            else:
                waits.append(copy)
    for number in range(len(spread.order)):
        spread.step(number)
    for s in (2, 1, 3):
        across[s].wait_recv()
        part = (here.o + SPLIT - s) % SPLIT
        waits.append(
            remote(
                piece(part, here.far),
                piece(part, here.far),
                send_t.at[3, s - 1],
                recv_t.at[3, s - 1],
                here.near_peer(),
            )
        )
    for copy in list(token_copies.values()) + list(across.values()):
        copy.wait_send()
    for copy in own:
        copy.wait()
    spread.finish()
    for copy in waits:
        copy.wait()


def whole_shapes(shards, inner):
    qkv, out, up, down = shards
    d_model = out.shape[1] * SPLIT * inner
    width = out.shape[0] // SPLIT + down.shape[0] // SPLIT
    return [
        jax.ShapeDtypeStruct((d_model, qkv.shape[1] // SPLIT), BF16),
        jax.ShapeDtypeStruct((d_model, up.shape[1] // SPLIT), BF16),
        jax.ShapeDtypeStruct(
            (width, d_model) if aligned(out.shape[1]) else (SPLIT * inner, width, out.shape[1]),
            BF16,
        ),
    ]


def joined_columns(low_all):
    if low_all.ndim == 3:
        low_all = jnp.swapaxes(low_all, 0, 1).reshape(low_all.shape[1], -1)
    return low_all


def spread_scratch(shards, inner):
    dma = pltpu.SemaphoreType.DMA
    qkv, out, up, down = shards
    pieces = [
        (qkv.shape[0], qkv.shape[1] // SPLIT),
        (up.shape[0], up.shape[1] // SPLIT),
        (out.shape[0] // SPLIT, out.shape[1]),
        (down.shape[0] // SPLIT, down.shape[1]),
    ]
    return [
        dma((4, SPLIT - 1)),
        dma((4, SPLIT - 1)),
        dma((4, SPLIT, max(inner - 1, 1))),
        dma((4, SPLIT, max(inner - 1, 1))),
        dma((10,)),
        *(pltpu.VMEM(piece, BF16) for piece in pieces),
    ]


def spread_weights(shards, inner, tokens, lengths, number):
    dma = pltpu.SemaphoreType.DMA
    shapes = whole_shapes(shards, inner) + [
        jax.ShapeDtypeStruct((tokens.shape[0] * SPLIT, tokens.shape[1]), BF16),
        jax.ShapeDtypeStruct((SPLIT, *lengths.shape), lengths.dtype),
    ]
    qkv_all, up_all, low_all, *gathered = pl.pallas_call(
        functools.partial(spread_weights_kernel, inner),
        out_shape=shapes,
        in_specs=[ANY_SPEC] * 4 + [VMEM_SPEC] * 2,
        out_specs=[ANY_SPEC] * len(shapes),
        scratch_shapes=spread_scratch(shards, inner)
        + [
            dma((4, SPLIT - 1)),
            dma((4, SPLIT - 1)),
            dma((SPLIT - 1,)),
            dma((SPLIT - 1,)),
        ],
        compiler_params=pltpu.CompilerParams(collective_id=number, has_side_effects=True),
    )(*shards, tokens, lengths)
    return (qkv_all, up_all, joined_columns(low_all), *gathered)


def f32(value):
    return value.astype(F32)


class RowSum:
    def __init__(self, here, part_ref, total, near_in, far_in, far_out, outer_in, outer_out, *sems):
        self.here, self.part, self.total = here, part_ref, total
        self.near_in, self.far_in, self.far_out = near_in, far_in, far_out
        self.outer_in, self.outer_out = outer_in, outer_out
        self.near_sems, self.far_sems, self.outer_sems = sems[0:2], sems[2:4], sems[4:6]
        self.quarter_sems = sems[6:8]
        self.rows = far_out.shape[1]
        self.near, self.far, self.outer = {}, {}, {}
        self.slots = None

    def recycle(self, step):
        for side in range(2):
            self.near.pop((step, side)).wait_send()

    def rows_of(self, step, quarter):
        block = self.slots[step] if self.slots else (self.here.o + 1 + step) % SPLIT
        return pl.ds((block * QUARTERS + quarter) * self.rows, self.rows)

    def start(self, step):
        here = self.here
        for side, quarter in enumerate(((here.near + 2) % QUARTERS, here.near)):
            self.near[step, side] = remote(
                self.part.at[self.rows_of(step, quarter), :],
                self.near_in.at[step, side],
                self.near_sems[0].at[step, side],
                self.near_sems[1].at[step, side],
                here.near_peer(),
            )

    def across(self, step):
        here = self.here
        self.near[step, 0].wait_recv()
        self.far_out[step] = (
            f32(self.part[self.rows_of(step, here.far), :]) + f32(self.near_in[step, 0])
        ).astype(BF16)
        self.far[step] = remote(
            self.far_out.at[step],
            self.far_in.at[step],
            self.far_sems[0].at[step],
            self.far_sems[1].at[step],
            here.far_peer(),
        )

    def along(self, step):
        here = self.here
        self.near[step, 1].wait_recv()
        self.far[step].wait_recv()
        value = (
            f32(self.part[self.rows_of(step, here.t), :])
            + f32(self.near_in[step, 1])
            + f32(self.far_in[step])
        )
        if step == SPLIT - 1:
            self.total[...] = value
            return
        self.outer_out[step] = value.astype(BF16)
        self.outer[step] = remote(
            self.outer_out.at[step],
            self.outer_in.at[step],
            self.outer_sems[0].at[step],
            self.outer_sems[1].at[step],
            here.outer_peer(step + 1),
        )

    def value(self):
        value = self.total[...]
        for step in range(SPLIT - 1):
            self.outer[step].wait_recv()
            value = value + f32(self.outer_in[step])
        return value

    def finish(self):
        for copies in (self.near, self.far, self.outer):
            for copy in copies.values():
                copy.wait_send()


def gather_quarters(here, ref, rows, send, recv):
    def piece(quarter):
        return ref.at[pl.ds(quarter * rows, rows), :]

    far = remote(piece(here.t), piece(here.t), send.at[0], recv.at[0], here.far_peer())
    near = remote(piece(here.t), piece(here.t), send.at[1], recv.at[1], here.near_peer())
    far.wait_recv()
    passed = remote(piece(here.far), piece(here.far), send.at[2], recv.at[2], here.near_peer())
    near.wait_recv()
    passed.wait_recv()
    for copy in (far, near, passed):
        copy.wait_send()


def reduce_peers(here):
    return [here.outer_peer(s) for s in range(1, SPLIT)] + [here.far_peer(), here.near_peer()]


def dot(left, right):
    return jnp.dot(left, right, preferred_element_type=F32)


def dot_cols(left, right):
    return lax.dot_general(left, right, (((1,), (1,)), ((), ())), preferred_element_type=F32)


def error_function(value):
    value = jnp.clip(value, -3.832506856900711, 3.832506856900711)
    square = value * value
    above = jnp.full_like(square, 0.00022905065861350646)
    for term in (0.0034082910107109506, 0.050955695062380861, 0.18520832239976145, 1.128379143519084):
        above = above * square + term
    below = jnp.full_like(square, -1.1791602954361697e-7)
    for term in (
        0.000023547966471313185, 0.0010179625278914885, 0.014070470171167667,
        0.11098505178285362, 0.49746925110067538, 1.0,
    ):
        below = below * square + term
    return value * above / below


def turn(values, tables, where, direction):
    cosine, sine = (table[where, :] for table in tables)
    ahead = pltpu.roll(values, values.shape[1] - ROT // 2, 1)
    behind = pltpu.roll(values, ROT // 2, 1)
    first = lax.broadcasted_iota(jnp.int32, values.shape, 1) < ROT // 2
    return values * cosine + direction * (jnp.where(first, ahead, behind) * sine)


def row_tiles(start, count, tile, body):
    @pl.loop(0, count // tile)
    def _(n):
        body(pl.ds(pl.multiple_of(start + n * tile, tile), tile), pl.ds(pl.multiple_of(n * tile, tile), tile))


def forward_kernel(inner, keep, background, *refs):
    here = Place(inner)
    (tokens_ref, rows_ref, qkv_ref, up_ref, low_ref, qkv_bias, up_bias, cosine, sine,
     doc_col, doc_row, *refs) = refs
    if not keep:
        facts_ref, *refs = refs
    tables = (cosine, sine)
    shards = refs[:4] if background else []
    refs = refs[len(shards):]
    final_ref, *refs = refs
    if keep:
        slope_ref, mixed_ref, facts_ref, joined_ref, *refs = refs
    wholes = refs[:3] if background else []
    refs = refs[len(wholes):]
    if not keep:
        mixed_ref, joined_ref, *refs = refs
    one_ref, two_ref, hidden_ref, part_ref, *refs = refs
    sums = RowSum(here, part_ref, *refs[:14])
    refs = refs[14:]
    block = one_ref.shape[0]
    heads = qkv_ref.shape[1] // (3 * HD)
    cut = heads * HD
    peers = reduce_peers(here)
    spread = None
    if background:
        spread = Spread(here, shards, wholes, *refs)
        peers = spread.peers() + [here.far_peer(), here.near_peer()]
    greet(peers)
    events = []
    if background:
        for number in range(AHEAD):
            spread.send_on(number)
        spread.start_own()
        events = list(range(len(spread.order)))

    def serve():
        if events:
            spread.step(events.pop(0))

    for step in range(SPLIT):
        start = ((here.o + 1 + step) % SPLIT) * block
        kept = start if keep else 0

        def norm(where, own):
            values = f32(tokens_ref[where, :])
            if keep:
                mean = jnp.mean(values, axis=1, keepdims=True)
                centre = values - mean
                scale = lax.rsqrt(jnp.mean(centre * centre, axis=1, keepdims=True) + EPS_NORM)
                facts_ref[where, MEAN : MEAN + 1] = mean
                facts_ref[where, SCALE : SCALE + 1] = scale
                normed = centre * scale
            else:
                normed = (values - facts_ref[where, MEAN : MEAN + 1]) * facts_ref[
                    where, SCALE : SCALE + 1
                ]
            one_ref[own, :] = (normed * rows_ref[0:1, :] + rows_ref[1:2, :]).astype(BF16)
            two_ref[own, :] = (normed * rows_ref[2:3, :] + rows_ref[3:4, :]).astype(BF16)

        row_tiles(start, block, 16, norm)
        serve()
        if step:
            sums.across(step - 1)
        whole = pl.ds(pl.multiple_of(start, block), block)
        mine = pl.ds(pl.multiple_of(kept, block), block)
        mixed = dot(one_ref[...], qkv_ref[...]) + qkv_bias[...]
        for head in range(heads):
            at = head * 3 * HD
            for offset in (0, HD):
                mixed_ref[mine, at + offset : at + offset + HD] = turn(
                    mixed[:, at + offset : at + offset + HD], tables, whole, 1.0
                ).astype(BF16)
            mixed_ref[mine, at + 2 * HD : at + 3 * HD] = mixed[:, at + 2 * HD : at + 3 * HD].astype(
                BF16
            )
        hidden_ref[...] = dot(two_ref[...], up_ref[...])
        serve()
        for head in range(heads):
            at = head * 3 * HD
            for first in range(0, block, 128):
                queries = pl.ds(pl.multiple_of(kept + first, 128), 128)
                tokens_at = pl.ds(pl.multiple_of(start + first, 128), 128)
                keys = pl.ds(pl.multiple_of(kept, 128), first + 128)
                scores = dot_cols(
                    mixed_ref[queries, at : at + HD], mixed_ref[keys, at + HD : at + 2 * HD]
                ) * HD ** (-0.5)
                own_block = (here.o + 1 + step) % SPLIT
                same = doc_col[tokens_at, :] == doc_row[own_block][:, : first + 128]
                earlier = first + lax.broadcasted_iota(
                    jnp.int32, scores.shape, 0
                ) >= lax.broadcasted_iota(jnp.int32, scores.shape, 1)
                scores = jnp.where(same & earlier, scores, MASKED)
                highest = jnp.max(scores, axis=1, keepdims=True)
                total = highest + jnp.log(
                    jnp.sum(jnp.exp(scores - highest), axis=1, keepdims=True)
                )
                if keep:
                    facts_ref[tokens_at, head : head + 1] = total
                probs = jnp.exp(scores - total).astype(BF16)
                joined_ref[queries, head * HD : (head + 1) * HD] = dot(
                    probs, mixed_ref[keys, at + 2 * HD : at + 3 * HD]
                ).astype(BF16)
        if step > 1:
            sums.along(step - 2)

        def activate(where, own):
            hidden = hidden_ref[own, :] + up_bias[...]
            share = 0.5 * (1.0 + error_function(hidden * 0.7071067811865476))
            joined_ref[where, cut:] = (hidden * share).astype(BF16)
            if keep:
                density = jnp.exp(-0.5 * hidden * hidden) * 0.3989422804014327
                slope_ref[where, :] = share + hidden * density

        row_tiles(kept, block, 32, activate)
        serve()
        columns = 512

        @pl.loop(0, part_ref.shape[1] // columns)
        def _(n):
            at = pl.ds(pl.multiple_of(n * columns, columns), columns)
            part_ref[whole, at] = dot(joined_ref[mine, :], low_ref[:, at]).astype(BF16)

        sums.start(step)
    sums.across(SPLIT - 1)
    while events:
        serve()
    sums.along(SPLIT - 2)
    sums.along(SPLIT - 1)
    branch = sums.value() + rows_ref[4:5, :] + rows_ref[5:6, :]
    quarter = pl.ds(pl.multiple_of(here.o * block + here.t * sums.rows, sums.rows), sums.rows)
    final_ref[pl.ds(pl.multiple_of(here.t * sums.rows, sums.rows), sums.rows), :] = (
        f32(tokens_ref[quarter, :]) + branch
    ).astype(BF16)
    gather_quarters(here, final_ref, sums.rows, *sums.quarter_sems)
    sums.finish()
    if background:
        spread.finish()


def forward_call(tokens, rows, weights, biases, layout, block, inner, facts, shards, number):
    total_rows, d_model = tokens.shape
    qkv_all, up_all, low_all = weights
    background, keep = shards is not None, facts is None
    outs = [jax.ShapeDtypeStruct((block, d_model), BF16)]
    if keep:
        outs += [
            jax.ShapeDtypeStruct((total_rows, up_all.shape[1]), F32),
            jax.ShapeDtypeStruct((total_rows, qkv_all.shape[1]), BF16),
            jax.ShapeDtypeStruct((total_rows, FACTS), F32),
            jax.ShapeDtypeStruct((total_rows, low_all.shape[0]), BF16),
        ]
    specs = [VMEM_SPEC] * len(outs)
    scratch = []
    if not keep:
        scratch += [
            pltpu.VMEM((block, qkv_all.shape[1]), BF16),
            pltpu.VMEM((block, low_all.shape[0]), BF16),
        ]
    scratch += [
        pltpu.VMEM((block, d_model), BF16),
        pltpu.VMEM((block, d_model), BF16),
        pltpu.VMEM((block, up_all.shape[1]), F32),
        pltpu.VMEM((total_rows, d_model), BF16),
    ]
    scratch += reduce_scratch(block // QUARTERS, d_model)
    operands = [tokens, rows, qkv_all, up_all, low_all, *biases, *layout]
    if not keep:
        operands.append(facts)
    in_specs = [VMEM_SPEC] * len(operands)
    if background:
        operands += shards
        in_specs += [ANY_SPEC] * 4
        outs += whole_shapes(shards, inner)
        specs += [ANY_SPEC] * 3
        scratch += spread_scratch(shards, inner)
    return pl.pallas_call(
        functools.partial(forward_kernel, inner, keep, background),
        out_shape=outs,
        in_specs=in_specs,
        out_specs=specs,
        scratch_shapes=scratch,
        compiler_params=pltpu.CompilerParams(
            collective_id=number, has_side_effects=True, vmem_limit_bytes=60 * 1024 * 1024
        ),
    )(*operands)


def input_change(values, scaled):
    centre = values - jnp.mean(values, axis=1, keepdims=True)
    spread = jnp.mean(centre * centre, axis=1, keepdims=True)
    scale = lax.rsqrt(spread + EPS_NORM)
    normed = centre * scale
    along = jnp.mean(scaled * normed, axis=1, keepdims=True)
    return scale * (scaled - jnp.mean(scaled, axis=1, keepdims=True) - normed * along)


def reduce_scratch(rows, width):
    dma = pltpu.SemaphoreType.DMA
    return [
        pltpu.VMEM((rows, width), F32),
        pltpu.VMEM((SPLIT, 2, rows, width), BF16),
        pltpu.VMEM((SPLIT, rows, width), BF16),
        pltpu.VMEM((SPLIT, rows, width), BF16),
        pltpu.VMEM((SPLIT - 1, rows, width), BF16),
        pltpu.VMEM((SPLIT - 1, rows, width), BF16),
        dma((SPLIT, 2)),
        dma((SPLIT, 2)),
        dma((SPLIT,)),
        dma((SPLIT,)),
        dma((SPLIT - 1,)),
        dma((SPLIT - 1,)),
        dma((3,)),
        dma((3,)),
    ]


def dot_rows(left, right):
    return lax.dot_general(left, right, (((0,), (0,)), ((), ())), preferred_element_type=F32)


def backward_kernel(
    inner, final_part, tokens_hbm, rows_ref, qkv_ref, up_ref, low_ref, slope_ref, mixed_ref,
    facts_ref, cosine, sine, doc_col, doc_row,
    grad_ref, branch_all, mixed_grad, hidden_grad, rows_out, bias_out,
    near_in, far_in, far_out, low, quarter, tokens_ref, own_tokens, joined_ref, key_ref, value_ref,
    part_ref,
    near_send, near_recv, far_send, far_recv, send, recv, local, *scratch,
):
    here = Place(inner)
    tables = (cosine, sine)
    sums = RowSum(here, part_ref, *scratch)
    rows = sums.rows
    block = rows * QUARTERS
    heads = qkv_ref.shape[1] // (3 * HD)
    cut = heads * HD
    greet(reduce_peers(here))

    def rows_of(number):
        return pl.ds(pl.multiple_of(number * rows, rows), rows)

    near = []
    for side, number in enumerate(((here.near + 2) % QUARTERS, here.near)):
        near.append(
            remote(
                final_part.at[rows_of(number), :],
                near_in.at[side],
                near_send.at[side],
                near_recv.at[side],
                here.near_peer(),
            )
        )

    shifts = (1, 3, 2, 0)

    def fetch(position):
        copy = pltpu.make_async_copy(
            tokens_hbm.at[pl.ds(((here.o + SPLIT - shifts[position]) % SPLIT) * block, block), :],
            tokens_ref,
            local.at[0],
        )
        copy.start()
        return copy

    fetched = fetch(0)
    own_copy = pltpu.make_async_copy(
        tokens_hbm.at[rows_of(here.o * QUARTERS + here.t), :], own_tokens, local.at[1]
    )
    own_copy.start()
    near[0].wait_recv()
    far_out[...] = (f32(final_part[rows_of(here.far), :]) + f32(near_in[0])).astype(BF16)
    far = remote(far_out, far_in, far_send, far_recv, here.far_peer())
    near[1].wait_recv()
    far.wait_recv()
    quarter[...] = f32(final_part[rows_of(here.t), :]) + f32(near_in[1]) + f32(far_in[...])
    low[...] = quarter[...].astype(BF16)
    rows_out[...] = jnp.zeros_like(rows_out)
    bias_out[...] = jnp.zeros_like(bias_out)
    rows_out[4:5, :] = jnp.sum(f32(low[...]), axis=0, keepdims=True)

    def piece(s, number):
        part = (here.o + SPLIT - s) % SPLIT
        return branch_all.at[rows_of(part * QUARTERS + number), :]

    outer, across, beside, beyond = {}, {}, {}, {}

    def send_out(s):
        outer[s] = remote(low, piece(0, here.t), send.at[0, s], recv.at[0, s], here.outer_peer(s))

    send_out(1)
    send_out(3)
    own = pltpu.make_async_copy(low, piece(0, here.t), local.at[2])
    own.start()

    def arrived(s):
        if s:
            outer[s].wait_recv()
        if s == 1:
            send_out(2)
        source = piece(s, here.t) if s else low
        across[s] = remote(
            source, piece(s, here.t), send.at[1, s], recv.at[1, s], here.far_peer()
        )
        beside[s] = remote(
            source, piece(s, here.t), send.at[2, s], recv.at[2, s], here.near_peer()
        )

    def crossed(s):
        across[s].wait_recv()
        beyond[s] = remote(
            piece(s, here.far), piece(s, here.far), send.at[3, s], recv.at[3, s], here.near_peer()
        )

    arrived(0)
    crossed(0)
    arrived(1)
    crossed(1)
    own.wait()
    steps = [SPLIT - 1 - s for s in shifts]
    sums.slots = {step: position % 2 for position, step in enumerate(steps)}
    events = [
        (arrived, 3), None, (crossed, 3), (arrived, 2), None, (crossed, 2),
    ]

    def serve():
        event = events.pop(0) if events else None
        if event:
            event[0](event[1])

    for position, s in enumerate(shifts):
        step = steps[position]
        part = (here.o + SPLIT - s) % SPLIT
        start = pl.multiple_of(part * block, block)
        whole = pl.ds(start, block)
        beside[s].wait_recv()
        beyond[s].wait_recv()
        joined_ref[...] = dot_cols(branch_all[whole, :], low_ref[...])

        def activate(where, mine):
            hidden_grad[where, :] = (joined_ref[mine, cut:] * slope_ref[where, :]).astype(BF16)

        row_tiles(start, block, 64, activate)
        serve()
        if position:
            sums.across(steps[position - 1])
        for head in range(heads):
            at = head * 3 * HD
            key_ref[...] = jnp.zeros_like(key_ref)
            value_ref[...] = jnp.zeros_like(value_ref)
            for first in range(0, block, 128):
                queries = pl.ds(pl.multiple_of(start + first, 128), 128)
                width = first + 128
                keys = pl.ds(start, width)
                query = mixed_ref[queries, at : at + HD]
                key = mixed_ref[keys, at + HD : at + 2 * HD]
                scores = dot_cols(query, key) * HD ** (-0.5)
                same = doc_col[queries, :] == doc_row[part][:, :width]
                earlier = first + lax.broadcasted_iota(
                    jnp.int32, scores.shape, 0
                ) >= lax.broadcasted_iota(jnp.int32, scores.shape, 1)
                scores = jnp.where(same & earlier, scores, MASKED)
                probs = jnp.exp(scores - facts_ref[queries, head : head + 1])
                attended_grad = joined_ref[
                    first : first + 128, head * HD : (head + 1) * HD
                ].astype(BF16)
                prob_grad = dot_cols(attended_grad, mixed_ref[keys, at + 2 * HD : at + 3 * HD])
                mean = jnp.sum(probs * prob_grad, axis=1, keepdims=True)
                score_grad = (probs * (prob_grad - mean)).astype(BF16)
                mixed_grad[queries, at : at + HD] = turn(
                    dot(score_grad, key) * HD ** (-0.5), tables, queries, -1.0
                ).astype(BF16)
                key_ref[:width, :] += dot_rows(score_grad, query)
                value_ref[:width, :] += dot_rows(probs.astype(BF16), attended_grad)
            mixed_grad[whole, at + HD : at + 2 * HD] = turn(
                key_ref[...] * HD ** (-0.5), tables, whole, -1.0
            ).astype(BF16)
            mixed_grad[whole, at + 2 * HD : at + 3 * HD] = value_ref[...].astype(BF16)
        bias_out[0:1, : mixed_grad.shape[1]] += jnp.sum(
            f32(mixed_grad[whole, :]), axis=0, keepdims=True
        )
        bias_out[0:1, mixed_grad.shape[1] :] += jnp.sum(
            f32(hidden_grad[whole, :]), axis=0, keepdims=True
        )
        serve()
        if position > 1:
            sums.along(steps[position - 2])
            sums.recycle(steps[position - 2])
        fetched.wait()
        columns = 256
        target = pl.ds((position % 2) * block, block)

        @pl.loop(0, part_ref.shape[1] // columns)
        def _(n):
            at = pl.ds(pl.multiple_of(n * columns, columns), columns)
            one = dot_cols(mixed_grad[whole, :], qkv_ref[at, :])
            two = dot_cols(hidden_grad[whole, :], up_ref[at, :])
            normed = (f32(tokens_ref[:, at]) - facts_ref[whole, MEAN : MEAN + 1]) * facts_ref[
                whole, SCALE : SCALE + 1
            ]
            part_ref[target, at] = (one * rows_ref[0:1, at] + two * rows_ref[2:3, at]).astype(BF16)
            for row, value in enumerate((one * normed, one, two * normed, two)):
                rows_out[row : row + 1, at] += jnp.sum(value, axis=0, keepdims=True)

        sums.start(step)
        if position + 1 < SPLIT:
            fetched = fetch(position + 1)
        serve()
    sums.across(steps[3])
    sums.along(steps[2])
    sums.along(steps[3])
    own_copy.wait()
    change = input_change(f32(own_tokens[...]), sums.value())
    grad_ref[rows_of(here.t), :] = (quarter[...] + change).astype(BF16)
    gather_quarters(here, grad_ref, rows, *sums.quarter_sems)
    sums.finish()
    for copy in near + [far]:
        copy.wait_send()
    for copies in (outer, across, beside, beyond):
        for copy in copies.values():
            copy.wait_send()


def backward_call(part, tokens, rows, weights, kept, layout, inner, number):
    block, width = part.shape
    quarter = block // QUARTERS
    slope, mixed, facts, joined = kept
    dma = pltpu.SemaphoreType.DMA
    return pl.pallas_call(
        functools.partial(backward_kernel, inner),
        out_shape=[
            jax.ShapeDtypeStruct((block, width), BF16),
            jax.ShapeDtypeStruct((SPLIT * block, width), BF16),
            jax.ShapeDtypeStruct(mixed.shape, BF16),
            jax.ShapeDtypeStruct(slope.shape, BF16),
            jax.ShapeDtypeStruct(rows.shape, F32),
            jax.ShapeDtypeStruct((1, mixed.shape[1] + slope.shape[1]), F32),
        ],
        in_specs=[VMEM_SPEC, ANY_SPEC] + [VMEM_SPEC] * 11,
        out_specs=[VMEM_SPEC] * 6,
        scratch_shapes=[
            pltpu.VMEM((2, quarter, width), BF16),
            pltpu.VMEM((quarter, width), BF16),
            pltpu.VMEM((quarter, width), BF16),
            pltpu.VMEM((quarter, width), BF16),
            pltpu.VMEM((quarter, width), F32),
            pltpu.VMEM((block, width), BF16),
            pltpu.VMEM((quarter, width), BF16),
            pltpu.VMEM((block, joined.shape[1]), F32),
            pltpu.VMEM((block, HD), F32),
            pltpu.VMEM((block, HD), F32),
            pltpu.VMEM((2 * block, width), BF16),
            dma((2,)),
            dma((2,)),
            dma,
            dma,
            dma((4, SPLIT)),
            dma((4, SPLIT)),
            dma((3,)),
        ]
        + reduce_scratch(quarter, width),
        compiler_params=pltpu.CompilerParams(
            collective_id=number, has_side_effects=True, vmem_limit_bytes=60 * 1024 * 1024
        ),
    )(part, tokens, rows, *weights, slope, mixed, facts, *layout)


class AllSum:
    def __init__(self, here, mine, near_in, far_in, outer, inner, send, recv):
        self.here, self.mine, self.near_in, self.far_in = here, mine, near_in, far_in
        self.outer, self.inner, self.send, self.recv = outer, inner, send, recv
        self.copies = []

    def pair(self, stage, target, peer):
        copy = remote(
            self.mine.at[stage], target, self.send.at[stage], self.recv.at[stage], peer
        )
        self.copies.append(copy)
        return copy

    def near(self, value):
        self.mine[0] = value
        self.waiting = [self.pair(0, self.near_in, self.here.near_peer())]

    def far(self):
        self.waiting[0].wait_recv()
        self.mine[1] = self.mine[0] + self.near_in[...]
        self.waiting = [self.pair(1, self.far_in, self.here.far_peer())]

    def group(self, buffer, index, first, peers):
        self.waiting = []
        for number, peer in enumerate(peers):
            copy = remote(
                buffer.at[index],
                buffer.at[index],
                self.send.at[first + number],
                self.recv.at[first + number],
                peer,
            )
            self.waiting.append(copy)
            self.copies.append(copy)

    def along_outer(self):
        self.waiting[0].wait_recv()
        here = self.here
        self.outer[here.o] = self.mine[1] + self.far_in[...]
        self.group(self.outer, here.o, 2, [here.outer_peer(s) for s in range(1, SPLIT)])

    def along_inner(self):
        here = self.here
        for copy in self.waiting:
            copy.wait_recv()
        value = self.outer[0]
        for part in range(1, SPLIT):
            value = value + self.outer[part]
        self.inner[here.i] = value
        peers = [here.inner_peer(r) for r in range(1, here.inner)]
        self.group(self.inner, here.i, 1 + SPLIT, peers)

    def value(self):
        for copy in self.waiting:
            copy.wait_recv()
        value = self.inner[0]
        for part in range(1, self.here.inner):
            value = value + self.inner[part]
        for copy in self.copies:
            copy.wait_send()
        return value


def all_sum_scratch(shape, inner):
    dma = pltpu.SemaphoreType.DMA
    return [
        pltpu.VMEM((2, *shape), F32),
        pltpu.VMEM(shape, F32),
        pltpu.VMEM(shape, F32),
        pltpu.VMEM((SPLIT, *shape), F32),
        pltpu.VMEM((inner, *shape), F32),
        dma((SPLIT + inner,)),
        dma((SPLIT + inner,)),
    ]


def whole_sum(value):
    return jnp.sum(jnp.sum(value, axis=1, keepdims=True), axis=0, keepdims=True)


def finish_kernel(
    inner, tokens_ref, branch_ref, gains_ref, joined_ref, mixed_ref, hidden_ref, facts_ref,
    rows_ref, bias_ref, qkv_out, up_out, out_out, down_out, rows_out, bias_out, norm_ref, *scratch,
):
    here = Place(inner)
    sends, inputs, totals = scratch[:3], scratch[3:6], scratch[6:9]
    turned, send_i, recv_i, send_o, recv_o, local, held = scratch[9:16]
    small = AllSum(here, *scratch[16:23])
    squares = AllSum(here, *scratch[23:30])
    bias_in, bias_send, bias_recv = scratch[30:33]
    outs = (qkv_out, up_out, out_out, down_out)
    shard = qkv_out.shape[0]
    width_out = out_out.shape[0] // SPLIT

    def columns_of(ref, index):
        if ref.ndim == 3:
            return ref[index]
        return ref[:, pl.ds(pl.multiple_of(index * shard, shard), shard)]

    def gradient(kind, index):
        if kind == 2:
            return dot(turned[...], columns_of(branch_ref, index))
        if tokens_ref.ndim == 3:
            copy = pltpu.make_async_copy(tokens_ref.at[index], held, local.at[4])
            copy.start()
            copy.wait()
            values = f32(held[...])
        else:
            values = f32(columns_of(tokens_ref, index))
        normed = (values - facts_ref[:, MEAN : MEAN + 1]) * facts_ref[:, SCALE : SCALE + 1]
        rows = columns_of(gains_ref, index)
        at = 2 * kind
        layer_in = (normed * rows[at : at + 1, :] + rows[at + 1 : at + 2, :]).astype(BF16)
        return dot_rows(layer_in, (mixed_ref, hidden_ref)[kind][...])

    def dst(m):
        if m < 2:
            width = outs[m].shape[1] // SPLIT
            return outs[m].at[:, pl.ds(here.o * width, width)]
        width = outs[m].shape[0] // SPLIT
        return outs[m].at[pl.ds(here.o * width, width), :]

    greet(reduce_peers(here) + [here.inner_peer(r) for r in range(1, inner)])
    first, last, own = {}, [], []
    order = [(kind, s) for kind in (2, 1, 0) for s in (2, 1, 3, 0)]
    turned[...] = jnp.transpose(joined_ref[...])

    def trade(number):
        if number >= len(order):
            return
        kind, s = order[number]
        part = (here.o + s) % SPLIT
        for r in range(1, inner):
            sends[kind][s, r - 1] = gradient(kind, part * inner + (here.i + r) % inner).astype(BF16)
            first[kind, s, r] = remote(
                sends[kind].at[s, r - 1],
                inputs[kind].at[s, r - 1],
                send_i.at[kind, s, r - 1],
                recv_i.at[kind, s, r - 1],
                here.inner_peer(r),
            )

    def settle(number):
        kind, s = order[number]
        part = (here.o + s) % SPLIT
        total = gradient(kind, part * inner + here.i)
        for r in range(1, inner):
            first[kind, s, r].wait_recv()
            total = total + f32(inputs[kind][s, r - 1])
        totals[kind][s] = total.astype(BF16)
        source = totals[kind].at[s]
        pieces = [(kind, source)]
        if kind == 2:
            pieces = [
                (2, source.at[pl.ds(0, width_out), :]),
                (3, source.at[pl.ds(width_out, total.shape[0] - width_out), :]),
            ]
        for m, piece in pieces:
            if s:
                last.append(
                    remote(
                        piece, dst(m), send_o.at[m, s - 1], recv_o.at[m, s - 1], here.outer_peer(s)
                    )
                )
            else:
                copy = pltpu.make_async_copy(piece, dst(m), local.at[m])
                copy.start()
                own.append(copy)
        trade(number + AHEAD)
        return whole_sum(total * total)

    for number in range(AHEAD):
        trade(number)
    small.near(rows_ref[...])
    bias_in[here.i] = bias_ref[...]
    bias_inner = [
        remote(
            bias_in.at[here.i],
            bias_in.at[here.i],
            bias_send.at[SPLIT + r],
            bias_recv.at[SPLIT + r],
            here.inner_peer(r),
        )
        for r in range(1, inner)
    ]
    square = settle(0)
    square = square + settle(1)
    small.far()
    for number in range(2, 5):
        square = square + settle(number)
    small.along_outer()
    for copy in bias_inner:
        copy.wait_recv()
    bias = bias_in[0]
    for part in range(1, inner):
        bias = bias + bias_in[part]
    bias_out[here.o] = bias
    bias_outer = [
        remote(
            bias_out.at[here.o],
            bias_out.at[here.o],
            bias_send.at[s],
            bias_recv.at[s],
            here.outer_peer(s),
        )
        for s in range(1, SPLIT)
    ]
    square = square + whole_sum(bias * bias) / inner
    square = square + settle(5)
    square = square + settle(6)
    small.along_inner()
    square = square + settle(7)
    square = square + settle(8)
    rows_out[...] = small.value()
    for number in range(9, len(order)):
        square = square + settle(number)
    squares.near(jnp.broadcast_to(square, norm_ref.shape))
    squares.far()
    squares.along_outer()
    squares.along_inner()
    norm = squares.value()
    rows = rows_out[...]
    doubled = lax.broadcasted_iota(jnp.int32, rows.shape, 0) == 4
    norm_ref[...] = norm + whole_sum(rows * rows * jnp.where(doubled, 2.0, 1.0))
    for copy in bias_outer:
        copy.wait_recv()
    for copy in bias_inner + bias_outer:
        copy.wait_send()
    for copy in last:
        copy.wait()
    for copy in own:
        copy.wait()
    for copy in first.values():
        copy.wait_send()


def finish_call(tokens, branch, rows, kept, grads, sums, bias, shards, inner, number):
    dma = pltpu.SemaphoreType.DMA
    qkv, out, up, down = shards
    ordered = (qkv, up, out, down)
    facts, joined = kept
    shard = out[1]
    wide = [tokens, branch, rows]
    if not aligned(shard):
        wide = [jnp.swapaxes(w.reshape(w.shape[0], -1, shard), 0, 1) for w in wide]
    pieces = [
        (shard, grads[0].shape[1]),
        (shard, grads[1].shape[1]),
        (joined.shape[1], shard),
    ]
    peers = max(inner - 1, 1)
    tile = (8, 128)
    return pl.pallas_call(
        functools.partial(finish_kernel, inner),
        out_shape=[
            *(jax.ShapeDtypeStruct(shape, BF16) for shape in ordered),
            jax.ShapeDtypeStruct(sums.shape, F32),
            jax.ShapeDtypeStruct((SPLIT, *bias.shape), F32),
            jax.ShapeDtypeStruct(tile, F32),
        ],
        in_specs=[VMEM_SPEC if aligned(shard) else ANY_SPEC] + [VMEM_SPEC] * 8,
        out_specs=[ANY_SPEC] * 4 + [VMEM_SPEC] * 3,
        scratch_shapes=[pltpu.VMEM((SPLIT, peers, *piece), BF16) for piece in pieces]
        + [pltpu.VMEM((SPLIT, peers, *piece), BF16) for piece in pieces]
        + [pltpu.VMEM((SPLIT, *piece), BF16) for piece in pieces]
        + [
            pltpu.VMEM(joined.shape[::-1], BF16),
            dma((3, SPLIT, peers)),
            dma((3, SPLIT, peers)),
            dma((4, SPLIT - 1)),
            dma((4, SPLIT - 1)),
            dma((5,)),
            pltpu.VMEM((16, 128) if aligned(shard) else (tokens.shape[0], shard), BF16),
        ]
        + all_sum_scratch(sums.shape, inner)
        + all_sum_scratch(tile, inner)
        + [
            pltpu.VMEM((inner, *bias.shape), F32),
            dma((SPLIT + inner,)),
            dma((SPLIT + inner,)),
        ],
        compiler_params=pltpu.CompilerParams(
            collective_id=number, has_side_effects=True, vmem_limit_bytes=60 * 1024 * 1024
        ),
    )(*wide, joined, *grads, facts, sums, bias)


def reward_kernel(
    inner, stats_ref, member_ref, label_ref, out_ref, stats, outer_in, inner_in,
    send, recv, send_o, recv_o, send_i, recv_i,
):
    here = Place(inner)
    tensor_peers = [(here.dp, (here.t + s) % QUARTERS) for s in range(1, QUARTERS)]
    outer_peers = [here.outer_peer(s) for s in range(1, SPLIT)]
    inner_peers = [here.inner_peer(r) for r in range(1, inner)]
    greet(tensor_peers + outer_peers + inner_peers)

    def share(buffer, index, sends, recvs, peers):
        return [
            remote(buffer.at[index], buffer.at[index], sends.at[n], recvs.at[n], peer)
            for n, peer in enumerate(peers)
        ]

    stats[here.t] = stats_ref[...]
    copies = share(stats, here.t, send, recv, tensor_peers)
    for copy in copies:
        copy.wait_recv()
    quarters = [stats[q] for q in range(QUARTERS)]
    highest = functools.reduce(jnp.maximum, quarters)
    summed = functools.reduce(lambda a, b: a + b, [jnp.exp(q - highest) for q in quarters])
    totals = highest + jnp.log(summed)
    picks = functools.reduce(lambda a, b: a + b, quarters)
    log_probs = picks - totals_to_picks(totals)
    member = member_ref[...]
    policy_docs = jnp.sum(member * log_probs[1:2, :], axis=1, keepdims=True)
    frozen_docs = jnp.sum(member * log_probs[3:4, :], axis=1, keepdims=True)
    reward = policy_docs - frozen_docs
    outer_in[here.o] = jnp.broadcast_to(whole_sum(reward), outer_in.shape[1:])
    more = share(outer_in, here.o, send_o, recv_o, outer_peers)
    for copy in more:
        copy.wait_recv()
    inner_in[here.i] = functools.reduce(lambda a, b: a + b, [outer_in[n] for n in range(SPLIT)])
    rest = share(inner_in, here.i, send_i, recv_i, inner_peers)
    for copy in rest:
        copy.wait_recv()
    total = functools.reduce(lambda a, b: a + b, [inner_in[n] for n in range(inner)])
    seq_count = inner * SPLIT * SEGS
    shift = total[:, 0:1] / seq_count
    sigmoid_value = 1.0 / (1.0 + jnp.exp(-BETA_KTO * (reward - shift)))
    labels = label_ref[:, 0:1]
    doc_grad = BETA_KTO * sigmoid_value * (1.0 - sigmoid_value) * (1.0 - 2.0 * labels) / seq_count
    token_grad = jnp.sum(member * doc_grad, axis=0, keepdims=True)
    out_ref[...] = jnp.transpose(
        jnp.concatenate([token_grad, totals[0:1, :], jnp.zeros((6, totals.shape[1]), F32)], axis=0)
    )
    for copy in copies + more + rest:
        copy.wait_send()


def totals_to_picks(totals):
    return jnp.concatenate([totals[0:1], totals[0:1], totals[2:3], totals[2:3], totals[4:]], axis=0)


def reward_call(stats, member, labels, inner, number):
    dma = pltpu.SemaphoreType.DMA
    tile = (8, 128)
    peers = max(inner - 1, 1)
    return pl.pallas_call(
        functools.partial(reward_kernel, inner),
        out_shape=jax.ShapeDtypeStruct((stats.shape[1], 8), F32),
        in_specs=[VMEM_SPEC] * 3,
        out_specs=VMEM_SPEC,
        scratch_shapes=[
            pltpu.VMEM((QUARTERS, *stats.shape), F32),
            pltpu.VMEM((SPLIT, *tile), F32),
            pltpu.VMEM((inner, *tile), F32),
            dma((QUARTERS - 1,)),
            dma((QUARTERS - 1,)),
            dma((SPLIT - 1,)),
            dma((SPLIT - 1,)),
            dma((peers,)),
            dma((peers,)),
        ],
        compiler_params=pltpu.CompilerParams(collective_id=number, has_side_effects=True),
    )(stats, member, labels)


def turn_tables(positions):
    half = ROT // 2
    frequency = 10000.0 ** (-2.0 * jnp.arange(half, dtype=F32) / ROT)
    angles = positions.reshape(-1).astype(F32)[:, None] * frequency
    cosine, sine = jnp.cos(angles), jnp.sin(angles)
    none = jnp.zeros((angles.shape[0], HD - ROT), F32)
    return (
        jnp.concatenate([cosine, cosine, none + 1.0], axis=1),
        jnp.concatenate([-sine, sine, none], axis=1),
    )


def doc_layout(lengths_row, row_count):
    ends, run = [], 0
    for segment in range(lengths_row.shape[0]):
        run = run + lengths_row[segment]
        ends.append(run)
    doc_ends = jnp.stack(ends)
    starts = doc_ends - lengths_row
    index_rows = jnp.arange(row_count, dtype=jnp.int32)
    member = (index_rows[:, None] >= starts[None, :]) & (index_rows[:, None] < doc_ends[None, :])
    doc_ids = jnp.arange(lengths_row.shape[0], dtype=jnp.int32)
    doc_of = jnp.sum(jnp.where(member, doc_ids[None, :], 0), axis=1)
    positions = index_rows - jnp.sum(jnp.where(member, starts[None, :], 0), axis=1)
    return (member, positions, doc_of)


def chunk_of(width):
    return next(n for n in (1280, 640, 512, 256, 128) if width % n == 0)


def head_kernel(policy_ref, frozen_ref, head_ref, target_ref, logits_ref, stats_ref, other_ref, high_ref, sum_ref, pick_ref):
    chunk = pl.program_id(0)
    rows, columns = logits_ref.shape

    @pl.when(chunk == 0)
    def _():
        high_ref[...] = jnp.full_like(high_ref, MASKED)
        sum_ref[...] = jnp.zeros_like(sum_ref)
        pick_ref[...] = jnp.zeros_like(pick_ref)

    def fold(which, values_ref, begin, width):
        for first in range(0, rows, 64):
            own = pl.ds(first, 64)
            high = high_ref[which, own, :]
            lanes = [values_ref[own, n : n + 128] for n in range(begin, begin + width, 128)]
            highest = functools.reduce(jnp.maximum, lanes, high)
            total = sum_ref[which, own, :] * jnp.exp(high - highest)
            picked = pick_ref[which, own, :]
            target = target_ref[own, :] - (chunk * columns + begin)
            lane = lax.broadcasted_iota(jnp.int32, highest.shape, 1)
            for n, value in enumerate(lanes):
                total = total + jnp.exp(value - highest)
                picked = picked + jnp.where(lane + n * 128 == target, value, 0.0)
            high_ref[which, own, :] = highest
            sum_ref[which, own, :] = total
            pick_ref[which, own, :] = picked

    width = 256 if columns % 256 == 0 else 128
    last = None
    for begin in range(0, columns, width):
        for which, (low_ref, values_ref) in enumerate(
            ((policy_ref, logits_ref), (frozen_ref, other_ref))
        ):
            values_ref[:, begin : begin + width] = dot(
                low_ref[...], head_ref[:, begin : begin + width]
            )
            if last:
                fold(*last)
            last = (which, values_ref, begin, width)
    fold(*last)

    @pl.when(chunk == pl.num_programs(0) - 1)
    def _():
        found = []
        for which in range(2):
            high = jnp.max(high_ref[which], axis=1, keepdims=True)
            total = jnp.sum(
                sum_ref[which] * jnp.exp(high_ref[which] - high), axis=1, keepdims=True
            )
            found.append(high + jnp.log(total))
            found.append(jnp.sum(pick_ref[which], axis=1, keepdims=True))
        lane = lax.broadcasted_iota(jnp.int32, (rows, 128), 1)
        joined = jnp.zeros((rows, 128), F32)
        for n, value in enumerate(found):
            joined = jnp.where(lane == n, value, joined)
        stats_ref[...] = jnp.transpose(joined)[:8, :]


def head_call(policy_low, frozen_low, head_weight, targets):
    rows, depth = policy_low.shape
    width = head_weight.shape[1]
    columns = chunk_of(width)
    return pl.pallas_call(
        head_kernel,
        grid=(width // columns,),
        out_shape=[
            jax.ShapeDtypeStruct((rows, width), F32),
            jax.ShapeDtypeStruct((8, rows), F32),
        ],
        in_specs=[
            pl.BlockSpec((rows, depth), lambda n: (0, 0)),
            pl.BlockSpec((rows, depth), lambda n: (0, 0)),
            pl.BlockSpec((depth, columns), lambda n: (0, n)),
            pl.BlockSpec((rows, 1), lambda n: (0, 0)),
        ],
        out_specs=[
            pl.BlockSpec((rows, columns), lambda n: (0, n)),
            pl.BlockSpec((8, rows), lambda n: (0, 0)),
        ],
        scratch_shapes=[
            pltpu.VMEM((rows, columns), F32),
            pltpu.VMEM((2, rows, 128), F32),
            pltpu.VMEM((2, rows, 128), F32),
            pltpu.VMEM((2, rows, 128), F32),
        ],
        cost_estimate=pl.CostEstimate(
            flops=4 * rows * depth * width,
            bytes_accessed=2 * depth * width + 4 * rows * width,
            transcendentals=2 * rows * width,
        ),
        compiler_params=pltpu.CompilerParams(vmem_limit_bytes=56 * 1024 * 1024),
    )(policy_low, frozen_low, head_weight, targets)


def logit_grad_kernel(logits_ref, head_ref, target_ref, token_ref, part_ref, low_ref, sum_ref):
    chunk = pl.program_id(0)
    rows, columns = logits_ref.shape

    for first in range(0, rows, 32):
        own = pl.ds(first, 32)
        values = logits_ref[own, :]
        target = target_ref[own, :] - chunk * columns
        chosen = lax.broadcasted_iota(jnp.int32, values.shape, 1) == target
        probs = jnp.exp(values - token_ref[own, 1:2])
        low_ref[own, :] = (token_ref[own, 0:1] * (jnp.where(chosen, 1.0, 0.0) - probs)).astype(BF16)
    value = dot_cols(low_ref[...], head_ref[...])

    @pl.when(chunk == 0)
    def _():
        sum_ref[...] = value

    @pl.when(chunk > 0)
    def _():
        sum_ref[...] += value

    @pl.when(chunk == pl.num_programs(0) - 1)
    def _():
        part_ref[...] = sum_ref[...].astype(BF16)


def logit_grad_call(logits, head_weight, targets, tokens):
    rows, width = logits.shape
    depth = head_weight.shape[0]
    columns = chunk_of(width)
    return pl.pallas_call(
        logit_grad_kernel,
        grid=(width // columns,),
        out_shape=jax.ShapeDtypeStruct((rows, depth), BF16),
        in_specs=[
            pl.BlockSpec((rows, columns), lambda n: (0, n)),
            pl.BlockSpec((depth, columns), lambda n: (0, n)),
            pl.BlockSpec((rows, 1), lambda n: (0, 0)),
            pl.BlockSpec((rows, tokens.shape[1]), lambda n: (0, 0)),
        ],
        out_specs=pl.BlockSpec((rows, depth), lambda n: (0, 0)),
        scratch_shapes=[pltpu.VMEM((rows, columns), BF16), pltpu.VMEM((rows, depth), F32)],
        cost_estimate=pl.CostEstimate(
            flops=2 * rows * depth * width,
            bytes_accessed=2 * depth * width + 4 * rows * width,
            transcendentals=rows * width,
        ),
        compiler_params=pltpu.CompilerParams(vmem_limit_bytes=56 * 1024 * 1024),
    )(logits, head_weight, targets, tokens)


def adam_step(master, mean_old, square_old, gradient, factor, rate, decay_rate):
    clipped = f32(gradient) * factor
    mean_new = BETA_FIRST * mean_old + (1.0 - BETA_FIRST) * clipped
    square_new = BETA_SECOND * square_old + (1.0 - BETA_SECOND) * clipped * clipped
    mean_hat = mean_new / (1.0 - BETA_FIRST**STEP)
    square_hat = square_new / (1.0 - BETA_SECOND**STEP)
    master_new = master - rate * (
        mean_hat / (jnp.sqrt(square_hat) + ADAM_EPS) + decay_rate * master
    )
    return (mean_new, square_new, master_new)


def eight_rows(rows):
    return jnp.zeros((8, rows.shape[1]), F32).at[: rows.shape[0]].set(rows)


def on_device(
    inputs,
    targets,
    doc_lengths,
    desirable,
    head_weight,
    qkv_master,
    out_master,
    up_master,
    down_master,
    vectors,
    hidden_bias,
    qkv_mean,
    out_mean,
    up_mean,
    down_mean,
    vectors_mean,
    hidden_mean,
    qkv_square,
    out_square,
    up_square,
    down_square,
    vectors_square,
    hidden_square,
    qkv_frozen,
    out_frozen,
    up_frozen,
    down_frozen,
    vectors_frozen,
    hidden_frozen,
):
    dp_size = lax.axis_size("dp")
    tensor_size = lax.axis_size("tensor")
    inner = dp_size // SPLIT
    outer_index = lax.axis_index("dp") // inner
    block = inputs.shape[0]
    lengths_tile = jnp.zeros((8, 128), jnp.int32).at[0, :SEGS].set(doc_lengths[0])
    masters = tuple(w.astype(BF16) for w in (qkv_master, out_master, up_master, down_master))
    *policy_set, tokens_all, lengths_all = spread_weights(masters, inner, inputs, lengths_tile, 0)
    frozen_shards = (qkv_frozen, out_frozen, up_frozen, down_frozen)
    member, _, _ = doc_layout(doc_lengths[0], block)
    _, positions, doc_of = jax.vmap(lambda row: doc_layout(row, block))(lengths_all[:, 0, :SEGS])

    cut = qkv_master.shape[1]
    width_qkv, width_up = cut // SPLIT, up_master.shape[1] // SPLIT

    def own_bias(bias):
        return (
            lax.dynamic_slice(bias, (outer_index * width_qkv,), (width_qkv,))[None],
            lax.dynamic_slice(bias, (cut + outer_index * width_up,), (width_up,))[None],
        )

    layout = (
        *turn_tables(positions),
        doc_of.reshape(-1, 1),
        doc_of[:, None, :],
    )
    final_low, *kept = forward_call(
        tokens_all, eight_rows(vectors), policy_set, own_bias(hidden_bias), layout, block, inner,
        None, frozen_shards, 2,
    )
    kept_values = tuple(kept[:4])
    frozen_set = (*kept[4:6], joined_columns(kept[6]))
    (frozen_low,) = forward_call(
        tokens_all, eight_rows(vectors_frozen), frozen_set, own_bias(hidden_frozen), layout, block,
        inner, kept_values[2], None, 3,
    )
    vocab_start = lax.axis_index("tensor") * head_weight.shape[1]
    own_targets = (targets - vocab_start)[:, None]
    logits, stats = head_call(final_low, frozen_low, head_weight, own_targets)
    doc_rows = jnp.zeros((8, block), F32).at[:SEGS].set(f32(member).T)
    labels = jnp.zeros((8, 128), F32).at[:SEGS].set(f32(desirable[0])[:, None])
    token_rows = reward_call(stats, doc_rows, labels, inner, 6)
    final_part = logit_grad_call(logits, head_weight, own_targets, token_rows)
    input_grad, branch_low, mixed_grad, hidden_low, vector_part, bias_part = backward_call(
        final_part, tokens_all, eight_rows(vectors), policy_set, kept_values, layout, inner, 4
    )
    shards = tuple(w.shape for w in masters)
    bias_rows = (width_qkv + width_up) // 128
    bias_tile = (
        jnp.zeros((-(-bias_rows // 8) * 8, 128), F32)
        .at[:bias_rows]
        .set(bias_part.reshape(bias_rows, 128))
    )
    qkv_grad, up_grad, out_grad, down_grad, vector_sum, bias_sum, square = finish_call(
        tokens_all, branch_low, eight_rows(vectors), kept_values[2:], (mixed_grad, hidden_low),
        vector_part, bias_tile, shards, inner, 5,
    )
    input_grad = f32(input_grad)
    vector_grad = jnp.concatenate([vector_sum[:5], vector_sum[4:5]], axis=0)
    bias_sum = bias_sum[:, :bias_rows].reshape(SPLIT, bias_rows * 128)
    hidden_grad = jnp.concatenate(
        [bias_sum[:, :width_qkv].reshape(-1), bias_sum[:, width_qkv:].reshape(-1)]
    )
    grad_norm = jnp.sqrt(square[0, 0])
    factor = jnp.minimum(1.0, CLIP_NORM / (grad_norm + 1e-06))
    qkv_state = adam_step(
        qkv_master, qkv_mean, qkv_square, qkv_grad, factor, LEARN_RATE, WEIGHT_DECAY
    )
    out_state = adam_step(
        out_master, out_mean, out_square, out_grad, factor, LEARN_RATE, WEIGHT_DECAY
    )
    up_state = adam_step(up_master, up_mean, up_square, up_grad, factor, LEARN_RATE, WEIGHT_DECAY)
    down_state = adam_step(
        down_master, down_mean, down_square, down_grad, factor, LEARN_RATE, WEIGHT_DECAY
    )
    vector_state = adam_step(
        vectors, vectors_mean, vectors_square, vector_grad, factor, VECTOR_RATE, 0.0
    )
    hidden_state = adam_step(
        hidden_bias, hidden_mean, hidden_square, hidden_grad, factor, VECTOR_RATE, 0.0
    )
    return (
        final_low,
        input_grad,
        grad_norm,
        *qkv_state,
        *out_state,
        *up_state,
        *down_state,
        *vector_state,
        *hidden_state,
    )


def solution(mesh):
    rows, cols = P("dp", "tensor"), P("tensor", "dp")
    matrices = (rows, cols, rows, cols)
    placed = (
        P("dp", None),
        P("dp"),
        P("dp", None),
        P("dp", None),
        P(None, "tensor"),
        *matrices,
        P(),
        P("tensor"),
        *matrices,
        P(),
        P("tensor"),
        *matrices,
        P(),
        P("tensor"),
        *matrices,
        P(),
        P("tensor"),
    )
    return jax.shard_map(
        on_device,
        mesh=mesh,
        in_specs=placed,
        out_specs=(
            P("dp", None),
            P("dp", None),
            P(),
            *(spec for spec in matrices for _ in range(3)),
            P(),
            P(),
            P(),
            P("tensor"),
            P("tensor"),
            P("tensor"),
        ),
        check_vma=False,
    )
```

```python
import functools

import jax
import jax.numpy as jnp
from jax import lax
from jax.experimental import pallas as pl
from jax.experimental.pallas import tpu as pltpu
from jax.sharding import PartitionSpec as P

HD = 128
ROT = 32
SEGS = 4
STEP = 3
SPLIT = 4
QUARTERS = 4
MEAN, SCALE, FACTS = 6, 7, 8
AHEAD = 3


EPS_NORM = 1e-05
BETA_KTO = 0.1
CLIP_NORM = 0.01
LEARN_RATE = 0.02
VECTOR_RATE = 0.2
BETA_FIRST = 0.9
BETA_SECOND = 0.999
ADAM_EPS = 1e-08
WEIGHT_DECAY = 0.01
MASKED = -1e30

MESH = pl.DeviceIdType.MESH
BF16 = jnp.bfloat16
F32 = jnp.float32
ANY_SPEC = pl.BlockSpec(memory_space=pltpu.HBM)
VMEM_SPEC = pl.BlockSpec(memory_space=pltpu.VMEM)


class Place:
    def __init__(self, inner):
        self.inner = inner
        self.dp = lax.axis_index("dp")
        self.t = lax.axis_index("tensor")
        self.o = self.dp // inner
        self.i = self.dp % inner
        self.near = self.t + 1 - 2 * (self.t % 2)
        self.far = (self.t + 2) % QUARTERS

    def outer_peer(self, shift):
        return (((self.o + shift) % SPLIT) * self.inner + self.i, self.t)

    def inner_peer(self, shift):
        return (self.o * self.inner + (self.i + shift) % self.inner, self.t)

    def near_peer(self):
        return (self.dp, self.near)

    def far_peer(self):
        return (self.dp, self.far)


def aligned(shard):
    return shard % 128 == 0


def greet(peers):
    barrier = pltpu.get_barrier_semaphore()
    for peer in peers:
        pl.semaphore_signal(barrier, inc=1, device_id=peer, device_id_type=MESH)
    pl.semaphore_wait(barrier, len(peers))


def remote(src, dst, send_sem, recv_sem, peer):
    copy = pltpu.make_async_remote_copy(
        src_ref=src,
        dst_ref=dst,
        send_sem=send_sem,
        recv_sem=recv_sem,
        device_id=peer,
        device_id_type=MESH,
    )
    copy.start()
    return copy


class Spread:
    def __init__(self, here, shards, wholes, send_o, recv_o, send_i, recv_i, local, *held):
        self.here = here
        self.qkv, self.out, self.up, self.down = shards
        self.qkv_all, self.up_all, self.low_all = wholes
        self.send_o, self.recv_o, self.send_i, self.recv_i = send_o, recv_o, send_i, recv_i
        self.local, self.held = local, held
        self.first, self.own, self.passed = {}, [], []
        self.order = [(m, s) for m in range(4) for s in (2, 1, 3)]

    def src(self, m, part):
        shard = (self.qkv, self.up, self.out, self.down)[m]
        width = shard.shape[1 if m < 2 else 0] // SPLIT
        where = pl.ds(part * width, width)
        return shard.at[:, where] if m < 2 else shard.at[where, :]

    def dst(self, m, index):
        shard = self.qkv.shape[0]
        where = pl.ds(index * shard, shard)
        if m < 2:
            return (self.qkv_all, self.up_all)[m].at[where, :]
        width_out, width_down = self.out.shape[0] // SPLIT, self.down.shape[0] // SPLIT
        rows = pl.ds(0, width_out) if m == 2 else pl.ds(width_out, width_down)
        low_all = self.low_all
        return low_all.at[rows, where] if aligned(shard) else low_all.at[index, rows, :]

    def peers(self):
        here = self.here
        peers = [here.outer_peer(s) for s in range(1, SPLIT)]
        return peers + [here.inner_peer(r) for r in range(1, here.inner)]

    def send_on(self, number):
        if number >= len(self.order):
            return
        m, s = self.order[number]
        self.first[m, s] = remote(
            self.src(m, (self.here.o + s) % SPLIT),
            self.dst(m, self.here.dp),
            self.send_o.at[m, s - 1],
            self.recv_o.at[m, s - 1],
            self.here.outer_peer(s),
        )

    def pass_on(self, m, s, source, index):
        here = self.here
        for r in range(1, here.inner):
            self.passed.append(
                remote(
                    source,
                    self.dst(m, index),
                    self.send_i.at[m, s, r - 1],
                    self.recv_i.at[m, s, r - 1],
                    here.inner_peer(r),
                )
            )

    def start_own(self):
        here = self.here
        loads = [
            pltpu.make_async_copy(self.src(m, here.o), self.held[m], self.local.at[m])
            for m in range(4)
        ]
        for load in loads:
            load.start()
        for m, load in enumerate(loads):
            load.wait()
            self.pass_on(m, 0, self.held[m], here.dp)
            copy = pltpu.make_async_copy(self.held[m], self.dst(m, here.dp), self.local.at[4 + m])
            copy.start()
            self.own.append(copy)

    def step(self, number):
        here = self.here
        m, s = self.order[number]
        self.first[m, s].wait_recv()
        self.send_on(number + AHEAD)
        index = ((here.o + SPLIT - s) % SPLIT) * here.inner + here.i
        self.pass_on(m, s, self.dst(m, index), index)

    def finish(self):
        for copy in self.first.values():
            copy.wait_send()
        for copy in self.own:
            copy.wait()
        for copy in self.passed:
            copy.wait()


def spread_weights_kernel(
    inner, qkv, out, up, down, tokens, lengths, qkv_all, up_all, low_all, tokens_all, lengths_all,
    send_o, recv_o, send_i, recv_i, local, held_0, held_1, held_2, held_3,
    send_t, recv_t, send_l, recv_l,
):
    here = Place(inner)
    spread = Spread(
        here, (qkv, out, up, down), (qkv_all, up_all, low_all),
        send_o, recv_o, send_i, recv_i, local, held_0, held_1, held_2, held_3,
    )
    greet(spread.peers() + [here.far_peer(), here.near_peer()])
    rows, block = tokens.shape[0] // QUARTERS, tokens.shape[0]

    def piece(part, quarter):
        return tokens_all.at[pl.ds((part * QUARTERS + quarter) * rows, rows), :]

    waits, token_copies, across, own = [], {}, {}, []
    for s in (2, 1, 3):
        token_copies[s] = remote(
            tokens.at[pl.ds(here.t * rows, rows), :],
            piece(here.o, here.t),
            send_t.at[0, s - 1],
            recv_t.at[0, s - 1],
            here.outer_peer(s),
        )
        waits.append(
            remote(
                lengths,
                lengths_all.at[here.o],
                send_l.at[s - 1],
                recv_l.at[s - 1],
                here.outer_peer(s),
            )
        )
    own.append(
        pltpu.make_async_copy(
            tokens, tokens_all.at[pl.ds(here.o * block, block), :], local.at[8]
        )
    )
    own.append(pltpu.make_async_copy(lengths, lengths_all.at[here.o], local.at[9]))
    for copy in own:
        copy.start()
    spread.start_own()
    for number, s in enumerate((2, 1, 3)):
        token_copies[s].wait_recv()
        spread.send_on(number)
        part = (here.o + SPLIT - s) % SPLIT
        for stage, peer in ((1, here.far_peer()), (2, here.near_peer())):
            copy = remote(
                piece(part, here.t),
                piece(part, here.t),
                send_t.at[stage, s - 1],
                recv_t.at[stage, s - 1],
                peer,
            )
            if stage == 1:
                across[s] = copy
            else:
                waits.append(copy)
    for number in range(len(spread.order)):
        spread.step(number)
    for s in (2, 1, 3):
        across[s].wait_recv()
        part = (here.o + SPLIT - s) % SPLIT
        waits.append(
            remote(
                piece(part, here.far),
                piece(part, here.far),
                send_t.at[3, s - 1],
                recv_t.at[3, s - 1],
                here.near_peer(),
            )
        )
    for copy in list(token_copies.values()) + list(across.values()):
        copy.wait_send()
    for copy in own:
        copy.wait()
    spread.finish()
    for copy in waits:
        copy.wait()


def whole_shapes(shards, inner):
    qkv, out, up, down = shards
    d_model = out.shape[1] * SPLIT * inner
    width = out.shape[0] // SPLIT + down.shape[0] // SPLIT
    return [
        jax.ShapeDtypeStruct((d_model, qkv.shape[1] // SPLIT), BF16),
        jax.ShapeDtypeStruct((d_model, up.shape[1] // SPLIT), BF16),
        jax.ShapeDtypeStruct(
            (width, d_model) if aligned(out.shape[1]) else (SPLIT * inner, width, out.shape[1]),
            BF16,
        ),
    ]


def joined_columns(low_all):
    if low_all.ndim == 3:
        low_all = jnp.swapaxes(low_all, 0, 1).reshape(low_all.shape[1], -1)
    return low_all


def spread_scratch(shards, inner):
    dma = pltpu.SemaphoreType.DMA
    qkv, out, up, down = shards
    pieces = [
        (qkv.shape[0], qkv.shape[1] // SPLIT),
        (up.shape[0], up.shape[1] // SPLIT),
        (out.shape[0] // SPLIT, out.shape[1]),
        (down.shape[0] // SPLIT, down.shape[1]),
    ]
    return [
        dma((4, SPLIT - 1)),
        dma((4, SPLIT - 1)),
        dma((4, SPLIT, max(inner - 1, 1))),
        dma((4, SPLIT, max(inner - 1, 1))),
        dma((10,)),
        *(pltpu.VMEM(piece, BF16) for piece in pieces),
    ]


def spread_weights(shards, inner, tokens, lengths, number):
    dma = pltpu.SemaphoreType.DMA
    shapes = whole_shapes(shards, inner) + [
        jax.ShapeDtypeStruct((tokens.shape[0] * SPLIT, tokens.shape[1]), BF16),
        jax.ShapeDtypeStruct((SPLIT, *lengths.shape), lengths.dtype),
    ]
    qkv_all, up_all, low_all, *gathered = pl.pallas_call(
        functools.partial(spread_weights_kernel, inner),
        out_shape=shapes,
        in_specs=[ANY_SPEC] * 4 + [VMEM_SPEC] * 2,
        out_specs=[ANY_SPEC] * len(shapes),
        scratch_shapes=spread_scratch(shards, inner)
        + [
            dma((4, SPLIT - 1)),
            dma((4, SPLIT - 1)),
            dma((SPLIT - 1,)),
            dma((SPLIT - 1,)),
        ],
        compiler_params=pltpu.CompilerParams(collective_id=number, has_side_effects=True),
    )(*shards, tokens, lengths)
    return (qkv_all, up_all, joined_columns(low_all), *gathered)


def f32(value):
    return value.astype(F32)


class RowSum:
    def __init__(self, here, part_ref, total, near_in, far_in, far_out, outer_in, outer_out, *sems):
        self.here, self.part, self.total = here, part_ref, total
        self.near_in, self.far_in, self.far_out = near_in, far_in, far_out
        self.outer_in, self.outer_out = outer_in, outer_out
        self.near_sems, self.far_sems, self.outer_sems = sems[0:2], sems[2:4], sems[4:6]
        self.quarter_sems = sems[6:8]
        self.rows = far_out.shape[1]
        self.near, self.far, self.outer, self.coming = {}, {}, {}, {}
        self.slots = None
        self.before = None

    def recycle(self, step):
        for side in range(2):
            self.near.pop((step, side)).wait_send()

    def rows_of(self, step, quarter):
        block = self.slots[step] if self.slots else (self.here.o + 1 + step) % SPLIT
        return pl.ds((block * QUARTERS + quarter) * self.rows, self.rows)

    def start(self, step):
        here = self.here
        for side, quarter in enumerate(((here.near + 2) % QUARTERS, here.near)):
            self.near[step, side] = remote(
                self.part.at[self.rows_of(step, quarter), :],
                self.near_in.at[step, side],
                self.near_sems[0].at[step, side],
                self.near_sems[1].at[step, side],
                here.near_peer(),
            )

    def across(self, step):
        here = self.here
        self.near[step, 0].wait_recv()
        if self.before:
            self.before.far.pop(step).wait_send()
        self.far_out[step] = (
            f32(self.part[self.rows_of(step, here.far), :]) + f32(self.near_in[step, 0])
        ).astype(BF16)
        self.far[step] = remote(
            self.far_out.at[step],
            self.far_in.at[step],
            self.far_sems[0].at[step],
            self.far_sems[1].at[step],
            here.far_peer(),
        )

    def along(self, step):
        here = self.here
        self.near[step, 1].wait_recv()
        self.far[step].wait_recv()
        value = (
            f32(self.part[self.rows_of(step, here.t), :])
            + f32(self.near_in[step, 1])
            + f32(self.far_in[step])
        )
        if step == SPLIT - 1:
            self.total[...] = value
            return
        if self.before:
            self.before.outer.pop(step).wait_send()
        self.outer_out[step] = value.astype(BF16)
        self.outer[step] = self.coming[step] = remote(
            self.outer_out.at[step],
            self.outer_in.at[step],
            self.outer_sems[0].at[step],
            self.outer_sems[1].at[step],
            here.outer_peer(step + 1),
        )

    def value(self):
        value = self.total[...]
        for step in range(SPLIT - 1):
            self.coming[step].wait_recv()
            value = value + f32(self.outer_in[step])
        return value

    def finish(self):
        for copies in (self.near, self.far, self.outer):
            for copy in copies.values():
                copy.wait_send()


class Quarters:
    def __init__(self, here, ref, rows, send, recv):
        self.here, self.ref, self.rows, self.send, self.recv = here, ref, rows, send, recv

    def copy(self, number, quarter, peer):
        piece = self.ref.at[pl.ds(quarter * self.rows, self.rows), :]
        return remote(piece, piece, self.send.at[number], self.recv.at[number], peer)

    def start(self):
        self.far = self.copy(0, self.here.t, self.here.far_peer())
        self.near = self.copy(1, self.here.t, self.here.near_peer())

    def pass_on(self):
        self.far.wait_recv()
        self.passed = self.copy(2, self.here.far, self.here.near_peer())

    def finish(self):
        self.near.wait_recv()
        self.passed.wait_recv()
        for copy in (self.far, self.near, self.passed):
            copy.wait_send()


def gather_quarters(here, ref, rows, send, recv):
    quarters = Quarters(here, ref, rows, send, recv)
    quarters.start()
    quarters.pass_on()
    quarters.finish()


def reduce_peers(here):
    return [here.outer_peer(s) for s in range(1, SPLIT)] + [here.far_peer(), here.near_peer()]


def dot(left, right):
    return jnp.dot(left, right, preferred_element_type=F32)


def dot_cols(left, right):
    return lax.dot_general(left, right, (((1,), (1,)), ((), ())), preferred_element_type=F32)


def error_function(value):
    value = jnp.clip(value, -3.832506856900711, 3.832506856900711)
    square = value * value
    above = jnp.full_like(square, 0.00022905065861350646)
    for term in (0.0034082910107109506, 0.050955695062380861, 0.18520832239976145, 1.128379143519084):
        above = above * square + term
    below = jnp.full_like(square, -1.1791602954361697e-7)
    for term in (
        0.000023547966471313185, 0.0010179625278914885, 0.014070470171167667,
        0.11098505178285362, 0.49746925110067538, 1.0,
    ):
        below = below * square + term
    return value * above / below


def turn(values, tables, where, direction):
    cosine, sine = (table[where, :] for table in tables)
    ahead = pltpu.roll(values, values.shape[1] - ROT // 2, 1)
    behind = pltpu.roll(values, ROT // 2, 1)
    first = lax.broadcasted_iota(jnp.int32, values.shape, 1) < ROT // 2
    return values * cosine + direction * (jnp.where(first, ahead, behind) * sine)


def row_tiles(start, count, tile, body):
    @pl.loop(0, count // tile)
    def _(n):
        body(pl.ds(pl.multiple_of(start + n * tile, tile), tile), pl.ds(pl.multiple_of(n * tile, tile), tile))


def forward_kernel(inner, keeps, background, *refs):
    here = Place(inner)
    refs = list(refs)

    def take(count):
        taken = refs[:count]
        del refs[:count]
        return taken

    tokens_ref, cosine, sine, doc_col, doc_row = take(5)
    tables = (cosine, sine)
    own_rows = [take(3) for _ in keeps]
    given = take(3)
    facts_ref = None if keeps[0] else take(1)[0]
    shards = take(4 if background else 0)
    finals = take(len(keeps))
    slope_ref, kept_mixed, facts_ref, kept_joined = take(4) if keeps[0] else (None, None, facts_ref, None)
    wholes = take(3 if background else 0)
    weights, load = take(3), take(1)[0]
    other_mixed, other_joined = (None, None) if all(keeps) else take(2)
    one_ref, two_ref, hidden_ref, part_ref = take(4)
    block = one_ref.shape[0]
    common = take(14)
    sums = [RowSum(here, part_ref, *common)]
    if len(keeps) > 1:
        total, outer_in, *sems = take(10)
        sums.append(RowSum(here, part_ref, total, *common[1:4], outer_in, common[5], *sems))
        sums[1].before = sums[0]
    for number, layer in enumerate(sums):
        layer.slots = {step: (number * SPLIT + step) % 2 for step in range(SPLIT)}
    rows = sums[0].rows
    qkv_ref, up_ref, low_ref = weights
    heads = qkv_ref.shape[1] // (3 * HD)
    cut = heads * HD
    peers = reduce_peers(here)
    spread = None
    if background:
        spread = Spread(here, shards, wholes, *refs)
        peers = spread.peers() + [here.far_peer(), here.near_peer()]
    greet(peers)
    events = []
    loads = []

    def fetch(sources):
        for number, (source, target) in enumerate(zip(sources, weights)):
            copy = pltpu.make_async_copy(source, target, load.at[number])
            copy.start()
            loads.append(copy)

    fetch(given)
    if background:
        for number in range(AHEAD):
            spread.send_on(number)
        spread.start_own()
        events = list(range(len(spread.order)))

    def serve():
        if events:
            spread.step(events.pop(0))

    def stage(name, position):
        if 0 <= position < len(keeps) * SPLIT:
            getattr(sums[position // SPLIT], name)(position % SPLIT)

    gathers = []

    def settle(number):
        rows_ref = own_rows[number][0]
        branch = sums[number].value() + rows_ref[4:5, :] + rows_ref[5:6, :]
        quarter = pl.ds(pl.multiple_of(here.o * block + here.t * rows, rows), rows)
        mine = pl.ds(pl.multiple_of(here.t * rows, rows), rows)
        finals[number][mine, :] = (f32(tokens_ref[quarter, :]) + branch).astype(BF16)
        gathers.append(Quarters(here, finals[number], rows, *sums[number].quarter_sems))
        gathers[-1].start()

    for position in range(len(keeps) * SPLIT):
        number, step = position // SPLIT, position % SPLIT
        keep = keeps[number]
        rows_ref, qkv_bias, up_bias = own_rows[number]
        mixed_ref, joined_ref = (
            (kept_mixed, kept_joined) if keep else (other_mixed, other_joined)
        )
        own_block = (here.o + 1 + step) % SPLIT
        start = own_block * block
        kept = start if keep else 0

        def norm(where, own):
            values = f32(tokens_ref[where, :])
            if keep:
                mean = jnp.mean(values, axis=1, keepdims=True)
                centre = values - mean
                scale = lax.rsqrt(jnp.mean(centre * centre, axis=1, keepdims=True) + EPS_NORM)
                facts_ref[where, MEAN : MEAN + 1] = mean
                facts_ref[where, SCALE : SCALE + 1] = scale
                normed = centre * scale
            else:
                normed = (values - facts_ref[where, MEAN : MEAN + 1]) * facts_ref[
                    where, SCALE : SCALE + 1
                ]
            one_ref[own, :] = (normed * rows_ref[0:1, :] + rows_ref[1:2, :]).astype(BF16)
            two_ref[own, :] = (normed * rows_ref[2:3, :] + rows_ref[3:4, :]).astype(BF16)

        row_tiles(start, block, 16, norm)
        serve()
        stage("across", position - 1)
        if number and step == 0:
            while events:
                serve()
            spread.finish()
            fetch(wholes)
        while loads:
            loads.pop(0).wait()
        whole = pl.ds(pl.multiple_of(start, block), block)
        mine = pl.ds(kept if keep else 0, block)
        mixed = dot(one_ref[...], qkv_ref[...]) + qkv_bias[...]
        for head in range(heads):
            at = head * 3 * HD
            for offset in (0, HD):
                mixed_ref[mine, at + offset : at + offset + HD] = turn(
                    mixed[:, at + offset : at + offset + HD], tables, whole, 1.0
                ).astype(BF16)
            mixed_ref[mine, at + 2 * HD : at + 3 * HD] = mixed[:, at + 2 * HD : at + 3 * HD].astype(
                BF16
            )
        hidden_ref[...] = dot(two_ref[...], up_ref[...])
        serve()
        for head in range(heads):
            at = head * 3 * HD
            for first in range(0, block, 128):
                queries = pl.ds(pl.multiple_of(kept + first, 128), 128)
                tokens_at = pl.ds(pl.multiple_of(start + first, 128), 128)
                keys = pl.ds(pl.multiple_of(kept, 128), first + 128)
                scores = dot_cols(
                    mixed_ref[queries, at : at + HD], mixed_ref[keys, at + HD : at + 2 * HD]
                ) * HD ** (-0.5)
                same = doc_col[tokens_at, :] == doc_row[own_block][:, : first + 128]
                earlier = first + lax.broadcasted_iota(
                    jnp.int32, scores.shape, 0
                ) >= lax.broadcasted_iota(jnp.int32, scores.shape, 1)
                scores = jnp.where(same & earlier, scores, MASKED)
                highest = jnp.max(scores, axis=1, keepdims=True)
                total = highest + jnp.log(
                    jnp.sum(jnp.exp(scores - highest), axis=1, keepdims=True)
                )
                if keep:
                    facts_ref[tokens_at, head : head + 1] = total
                probs = jnp.exp(scores - total).astype(BF16)
                joined_ref[queries, head * HD : (head + 1) * HD] = dot(
                    probs, mixed_ref[keys, at + 2 * HD : at + 3 * HD]
                ).astype(BF16)
        stage("along", position - 2)
        stage("recycle", position - 2)

        def activate(where, own):
            hidden = hidden_ref[own, :] + up_bias[...]
            share = 0.5 * (1.0 + error_function(hidden * 0.7071067811865476))
            joined_ref[where, cut:] = (hidden * share).astype(BF16)
            if keep:
                density = jnp.exp(-0.5 * hidden * hidden) * 0.3989422804014327
                slope_ref[where, :] = share + hidden * density

        row_tiles(kept, block, 32, activate)
        serve()
        columns = 512
        slot = pl.ds((position % 2) * block, block)

        @pl.loop(0, part_ref.shape[1] // columns)
        def _(n):
            at = pl.ds(pl.multiple_of(n * columns, columns), columns)
            part_ref[slot, at] = dot(joined_ref[mine, :], low_ref[:, at]).astype(BF16)

        stage("start", position)
        if number and step == 2:
            settle(0)
        if number and step == 3:
            gathers[0].pass_on()
    last = len(keeps) - 1
    sums[last].across(SPLIT - 1)
    while events:
        serve()
    sums[last].along(SPLIT - 2)
    sums[last].along(SPLIT - 1)
    settle(last)
    gathers[last].pass_on()
    for gather in gathers:
        gather.finish()
    for layer in sums:
        layer.finish()
    if background and last == 0:
        spread.finish()


def forward_call(tokens, layout, layers, weights, block, inner, facts, shards, number):
    total_rows, d_model = tokens.shape
    qkv_all, up_all, low_all = weights
    background = shards is not None
    keeps = (facts is None,) + (False,) * (len(layers) - 1)
    dma = pltpu.SemaphoreType.DMA
    outs = [jax.ShapeDtypeStruct((block, d_model), BF16) for _ in layers]
    if keeps[0]:
        outs += [
            jax.ShapeDtypeStruct((total_rows, up_all.shape[1]), F32),
            jax.ShapeDtypeStruct((total_rows, qkv_all.shape[1]), BF16),
            jax.ShapeDtypeStruct((total_rows, FACTS), F32),
            jax.ShapeDtypeStruct((total_rows, low_all.shape[0]), BF16),
        ]
    specs = [VMEM_SPEC] * len(outs)
    scratch = [pltpu.VMEM(w.shape, BF16) for w in weights] + [dma((3,))]
    if not all(keeps):
        scratch += [
            pltpu.VMEM((block, qkv_all.shape[1]), BF16),
            pltpu.VMEM((block, low_all.shape[0]), BF16),
        ]
    scratch += [
        pltpu.VMEM((block, d_model), BF16),
        pltpu.VMEM((block, d_model), BF16),
        pltpu.VMEM((block, up_all.shape[1]), F32),
        pltpu.VMEM((2 * block, d_model), BF16),
    ]
    one_sum = reduce_scratch(block // QUARTERS, d_model)
    scratch += one_sum
    if len(layers) > 1:
        scratch += [one_sum[0], one_sum[4], *one_sum[6:]]
    operands = [tokens, *layout]
    for layer in layers:
        operands += layer
    in_specs = [VMEM_SPEC] * len(operands)
    operands += weights
    in_specs += [ANY_SPEC] * 3
    if not keeps[0]:
        operands.append(facts)
        in_specs.append(VMEM_SPEC)
    if background:
        operands += shards
        in_specs += [ANY_SPEC] * 4
        outs += whole_shapes(shards, inner)
        specs += [ANY_SPEC] * 3
        scratch += spread_scratch(shards, inner)
    return pl.pallas_call(
        functools.partial(forward_kernel, inner, keeps, background),
        out_shape=outs,
        in_specs=in_specs,
        out_specs=specs,
        scratch_shapes=scratch,
        compiler_params=pltpu.CompilerParams(
            collective_id=number, has_side_effects=True, vmem_limit_bytes=60 * 1024 * 1024
        ),
    )(*operands)


def input_change(values, scaled):
    centre = values - jnp.mean(values, axis=1, keepdims=True)
    spread = jnp.mean(centre * centre, axis=1, keepdims=True)
    scale = lax.rsqrt(spread + EPS_NORM)
    normed = centre * scale
    along = jnp.mean(scaled * normed, axis=1, keepdims=True)
    return scale * (scaled - jnp.mean(scaled, axis=1, keepdims=True) - normed * along)


def reduce_scratch(rows, width):
    dma = pltpu.SemaphoreType.DMA
    return [
        pltpu.VMEM((rows, width), F32),
        pltpu.VMEM((SPLIT, 2, rows, width), BF16),
        pltpu.VMEM((SPLIT, rows, width), BF16),
        pltpu.VMEM((SPLIT, rows, width), BF16),
        pltpu.VMEM((SPLIT - 1, rows, width), BF16),
        pltpu.VMEM((SPLIT - 1, rows, width), BF16),
        dma((SPLIT, 2)),
        dma((SPLIT, 2)),
        dma((SPLIT,)),
        dma((SPLIT,)),
        dma((SPLIT - 1,)),
        dma((SPLIT - 1,)),
        dma((3,)),
        dma((3,)),
    ]


def dot_rows(left, right):
    return lax.dot_general(left, right, (((0,), (0,)), ((), ())), preferred_element_type=F32)


def backward_kernel(
    inner, final_part, tokens_hbm, rows_ref, qkv_ref, up_ref, low_ref, slope_ref, mixed_ref,
    facts_ref, cosine, sine, doc_col, doc_row,
    grad_ref, branch_all, mixed_grad, hidden_grad, rows_out, bias_out,
    near_in, far_in, far_out, low, quarter, tokens_ref, own_tokens, joined_ref, key_ref, value_ref,
    part_ref,
    near_send, near_recv, far_send, far_recv, send, recv, local, *scratch,
):
    here = Place(inner)
    tables = (cosine, sine)
    sums = RowSum(here, part_ref, *scratch)
    rows = sums.rows
    block = rows * QUARTERS
    heads = qkv_ref.shape[1] // (3 * HD)
    cut = heads * HD
    greet(reduce_peers(here))

    def rows_of(number):
        return pl.ds(pl.multiple_of(number * rows, rows), rows)

    near = []
    for side, number in enumerate(((here.near + 2) % QUARTERS, here.near)):
        near.append(
            remote(
                final_part.at[rows_of(number), :],
                near_in.at[side],
                near_send.at[side],
                near_recv.at[side],
                here.near_peer(),
            )
        )

    shifts = (1, 3, 2, 0)

    def fetch(position):
        copy = pltpu.make_async_copy(
            tokens_hbm.at[pl.ds(((here.o + SPLIT - shifts[position]) % SPLIT) * block, block), :],
            tokens_ref,
            local.at[0],
        )
        copy.start()
        return copy

    fetched = fetch(0)
    own_copy = pltpu.make_async_copy(
        tokens_hbm.at[rows_of(here.o * QUARTERS + here.t), :], own_tokens, local.at[1]
    )
    own_copy.start()
    near[0].wait_recv()
    far_out[...] = (f32(final_part[rows_of(here.far), :]) + f32(near_in[0])).astype(BF16)
    far = remote(far_out, far_in, far_send, far_recv, here.far_peer())
    near[1].wait_recv()
    far.wait_recv()
    quarter[...] = f32(final_part[rows_of(here.t), :]) + f32(near_in[1]) + f32(far_in[...])
    low[...] = quarter[...].astype(BF16)
    rows_out[...] = jnp.zeros_like(rows_out)
    bias_out[...] = jnp.zeros_like(bias_out)
    rows_out[4:5, :] = jnp.sum(f32(low[...]), axis=0, keepdims=True)

    def piece(s, number):
        part = (here.o + SPLIT - s) % SPLIT
        return branch_all.at[rows_of(part * QUARTERS + number), :]

    outer, across, beside, beyond = {}, {}, {}, {}

    def send_out(s):
        outer[s] = remote(low, piece(0, here.t), send.at[0, s], recv.at[0, s], here.outer_peer(s))

    send_out(1)
    send_out(3)
    own = pltpu.make_async_copy(low, piece(0, here.t), local.at[2])
    own.start()

    def arrived(s):
        if s:
            outer[s].wait_recv()
        if s == 1:
            send_out(2)
        source = piece(s, here.t) if s else low
        across[s] = remote(
            source, piece(s, here.t), send.at[1, s], recv.at[1, s], here.far_peer()
        )
        beside[s] = remote(
            source, piece(s, here.t), send.at[2, s], recv.at[2, s], here.near_peer()
        )

    def crossed(s):
        across[s].wait_recv()
        beyond[s] = remote(
            piece(s, here.far), piece(s, here.far), send.at[3, s], recv.at[3, s], here.near_peer()
        )

    arrived(0)
    crossed(0)
    arrived(1)
    crossed(1)
    own.wait()
    steps = [SPLIT - 1 - s for s in shifts]
    sums.slots = {step: position % 2 for position, step in enumerate(steps)}
    events = [
        (arrived, 3), None, (crossed, 3), (arrived, 2), None, (crossed, 2),
    ]

    def serve():
        event = events.pop(0) if events else None
        if event:
            event[0](event[1])

    for position, s in enumerate(shifts):
        step = steps[position]
        part = (here.o + SPLIT - s) % SPLIT
        start = pl.multiple_of(part * block, block)
        whole = pl.ds(start, block)
        beside[s].wait_recv()
        beyond[s].wait_recv()
        joined_ref[...] = dot_cols(branch_all[whole, :], low_ref[...])

        def activate(where, mine):
            hidden_grad[where, :] = (joined_ref[mine, cut:] * slope_ref[where, :]).astype(BF16)

        row_tiles(start, block, 64, activate)
        serve()
        if position:
            sums.across(steps[position - 1])
        for head in range(heads):
            at = head * 3 * HD
            key_ref[...] = jnp.zeros_like(key_ref)
            value_ref[...] = jnp.zeros_like(value_ref)
            for first in range(0, block, 128):
                queries = pl.ds(pl.multiple_of(start + first, 128), 128)
                width = first + 128
                keys = pl.ds(start, width)
                query = mixed_ref[queries, at : at + HD]
                key = mixed_ref[keys, at + HD : at + 2 * HD]
                scores = dot_cols(query, key) * HD ** (-0.5)
                same = doc_col[queries, :] == doc_row[part][:, :width]
                earlier = first + lax.broadcasted_iota(
                    jnp.int32, scores.shape, 0
                ) >= lax.broadcasted_iota(jnp.int32, scores.shape, 1)
                scores = jnp.where(same & earlier, scores, MASKED)
                probs = jnp.exp(scores - facts_ref[queries, head : head + 1])
                attended_grad = joined_ref[
                    first : first + 128, head * HD : (head + 1) * HD
                ].astype(BF16)
                prob_grad = dot_cols(attended_grad, mixed_ref[keys, at + 2 * HD : at + 3 * HD])
                mean = jnp.sum(probs * prob_grad, axis=1, keepdims=True)
                score_grad = (probs * (prob_grad - mean)).astype(BF16)
                mixed_grad[queries, at : at + HD] = turn(
                    dot(score_grad, key) * HD ** (-0.5), tables, queries, -1.0
                ).astype(BF16)
                key_ref[:width, :] += dot_rows(score_grad, query)
                value_ref[:width, :] += dot_rows(probs.astype(BF16), attended_grad)
            mixed_grad[whole, at + HD : at + 2 * HD] = turn(
                key_ref[...] * HD ** (-0.5), tables, whole, -1.0
            ).astype(BF16)
            mixed_grad[whole, at + 2 * HD : at + 3 * HD] = value_ref[...].astype(BF16)
        bias_out[0:1, : mixed_grad.shape[1]] += jnp.sum(
            f32(mixed_grad[whole, :]), axis=0, keepdims=True
        )
        bias_out[0:1, mixed_grad.shape[1] :] += jnp.sum(
            f32(hidden_grad[whole, :]), axis=0, keepdims=True
        )
        serve()
        if position > 1:
            sums.along(steps[position - 2])
            sums.recycle(steps[position - 2])
        fetched.wait()
        columns = 256
        target = pl.ds((position % 2) * block, block)

        @pl.loop(0, part_ref.shape[1] // columns)
        def _(n):
            at = pl.ds(pl.multiple_of(n * columns, columns), columns)
            one = dot_cols(mixed_grad[whole, :], qkv_ref[at, :])
            two = dot_cols(hidden_grad[whole, :], up_ref[at, :])
            normed = (f32(tokens_ref[:, at]) - facts_ref[whole, MEAN : MEAN + 1]) * facts_ref[
                whole, SCALE : SCALE + 1
            ]
            part_ref[target, at] = (one * rows_ref[0:1, at] + two * rows_ref[2:3, at]).astype(BF16)
            for row, value in enumerate((one * normed, one, two * normed, two)):
                rows_out[row : row + 1, at] += jnp.sum(value, axis=0, keepdims=True)

        sums.start(step)
        if position + 1 < SPLIT:
            fetched = fetch(position + 1)
        serve()
    sums.across(steps[3])
    sums.along(steps[2])
    sums.along(steps[3])
    own_copy.wait()
    change = input_change(f32(own_tokens[...]), sums.value())
    grad_ref[rows_of(here.t), :] = (quarter[...] + change).astype(BF16)
    gather_quarters(here, grad_ref, rows, *sums.quarter_sems)
    sums.finish()
    for copy in near + [far]:
        copy.wait_send()
    for copies in (outer, across, beside, beyond):
        for copy in copies.values():
            copy.wait_send()


def backward_call(part, tokens, rows, weights, kept, layout, inner, number):
    block, width = part.shape
    quarter = block // QUARTERS
    slope, mixed, facts, joined = kept
    dma = pltpu.SemaphoreType.DMA
    return pl.pallas_call(
        functools.partial(backward_kernel, inner),
        out_shape=[
            jax.ShapeDtypeStruct((block, width), BF16),
            jax.ShapeDtypeStruct((SPLIT * block, width), BF16),
            jax.ShapeDtypeStruct(mixed.shape, BF16),
            jax.ShapeDtypeStruct(slope.shape, BF16),
            jax.ShapeDtypeStruct(rows.shape, F32),
            jax.ShapeDtypeStruct((1, mixed.shape[1] + slope.shape[1]), F32),
        ],
        in_specs=[VMEM_SPEC, ANY_SPEC] + [VMEM_SPEC] * 11,
        out_specs=[VMEM_SPEC] * 6,
        scratch_shapes=[
            pltpu.VMEM((2, quarter, width), BF16),
            pltpu.VMEM((quarter, width), BF16),
            pltpu.VMEM((quarter, width), BF16),
            pltpu.VMEM((quarter, width), BF16),
            pltpu.VMEM((quarter, width), F32),
            pltpu.VMEM((block, width), BF16),
            pltpu.VMEM((quarter, width), BF16),
            pltpu.VMEM((block, joined.shape[1]), F32),
            pltpu.VMEM((block, HD), F32),
            pltpu.VMEM((block, HD), F32),
            pltpu.VMEM((2 * block, width), BF16),
            dma((2,)),
            dma((2,)),
            dma,
            dma,
            dma((4, SPLIT)),
            dma((4, SPLIT)),
            dma((3,)),
        ]
        + reduce_scratch(quarter, width),
        compiler_params=pltpu.CompilerParams(
            collective_id=number, has_side_effects=True, vmem_limit_bytes=60 * 1024 * 1024
        ),
    )(part, tokens, rows, *weights, slope, mixed, facts, *layout)


class AllSum:
    def __init__(self, here, mine, near_in, far_in, outer, inner, send, recv):
        self.here, self.mine, self.near_in, self.far_in = here, mine, near_in, far_in
        self.outer, self.inner, self.send, self.recv = outer, inner, send, recv
        self.copies = []

    def pair(self, stage, target, peer):
        copy = remote(
            self.mine.at[stage], target, self.send.at[stage], self.recv.at[stage], peer
        )
        self.copies.append(copy)
        return copy

    def near(self, value):
        self.mine[0] = value
        self.waiting = [self.pair(0, self.near_in, self.here.near_peer())]

    def far(self):
        self.waiting[0].wait_recv()
        self.mine[1] = self.mine[0] + self.near_in[...]
        self.waiting = [self.pair(1, self.far_in, self.here.far_peer())]

    def group(self, buffer, index, first, peers):
        self.waiting = []
        for number, peer in enumerate(peers):
            copy = remote(
                buffer.at[index],
                buffer.at[index],
                self.send.at[first + number],
                self.recv.at[first + number],
                peer,
            )
            self.waiting.append(copy)
            self.copies.append(copy)

    def along_outer(self):
        self.waiting[0].wait_recv()
        here = self.here
        self.outer[here.o] = self.mine[1] + self.far_in[...]
        self.group(self.outer, here.o, 2, [here.outer_peer(s) for s in range(1, SPLIT)])

    def along_inner(self):
        here = self.here
        for copy in self.waiting:
            copy.wait_recv()
        value = self.outer[0]
        for part in range(1, SPLIT):
            value = value + self.outer[part]
        self.inner[here.i] = value
        peers = [here.inner_peer(r) for r in range(1, here.inner)]
        self.group(self.inner, here.i, 1 + SPLIT, peers)

    def value(self):
        for copy in self.waiting:
            copy.wait_recv()
        value = self.inner[0]
        for part in range(1, self.here.inner):
            value = value + self.inner[part]
        for copy in self.copies:
            copy.wait_send()
        return value


def all_sum_scratch(shape, inner):
    dma = pltpu.SemaphoreType.DMA
    return [
        pltpu.VMEM((2, *shape), F32),
        pltpu.VMEM(shape, F32),
        pltpu.VMEM(shape, F32),
        pltpu.VMEM((SPLIT, *shape), F32),
        pltpu.VMEM((inner, *shape), F32),
        dma((SPLIT + inner,)),
        dma((SPLIT + inner,)),
    ]


def whole_sum(value):
    return jnp.sum(jnp.sum(value, axis=1, keepdims=True), axis=0, keepdims=True)


def finish_kernel(
    inner, tokens_ref, branch_ref, gains_ref, joined_ref, mixed_ref, hidden_ref, facts_ref,
    rows_ref, bias_ref, qkv_out, up_out, out_out, down_out, rows_out, bias_out, norm_ref, *scratch,
):
    here = Place(inner)
    sends, inputs, totals = scratch[:3], scratch[3:6], scratch[6:9]
    turned, send_i, recv_i, send_o, recv_o, local, held = scratch[9:16]
    small = AllSum(here, *scratch[16:23])
    squares = AllSum(here, *scratch[23:30])
    bias_in, bias_send, bias_recv = scratch[30:33]
    outs = (qkv_out, up_out, out_out, down_out)
    shard = qkv_out.shape[0]
    width_out = out_out.shape[0] // SPLIT

    def columns_of(ref, index):
        if ref.ndim == 3:
            return ref[index]
        return ref[:, pl.ds(pl.multiple_of(index * shard, shard), shard)]

    def gradient(kind, index):
        if kind == 2:
            return dot(turned[...], columns_of(branch_ref, index))
        if tokens_ref.ndim == 3:
            copy = pltpu.make_async_copy(tokens_ref.at[index], held, local.at[4])
            copy.start()
            copy.wait()
            values = f32(held[...])
        else:
            values = f32(columns_of(tokens_ref, index))
        normed = (values - facts_ref[:, MEAN : MEAN + 1]) * facts_ref[:, SCALE : SCALE + 1]
        rows = columns_of(gains_ref, index)
        at = 2 * kind
        layer_in = (normed * rows[at : at + 1, :] + rows[at + 1 : at + 2, :]).astype(BF16)
        return dot_rows(layer_in, (mixed_ref, hidden_ref)[kind][...])

    def dst(m):
        if m < 2:
            width = outs[m].shape[1] // SPLIT
            return outs[m].at[:, pl.ds(here.o * width, width)]
        width = outs[m].shape[0] // SPLIT
        return outs[m].at[pl.ds(here.o * width, width), :]

    greet(reduce_peers(here) + [here.inner_peer(r) for r in range(1, inner)])
    first, last, own = {}, [], []
    order = [(kind, s) for kind in (2, 1, 0) for s in (2, 1, 3, 0)]
    turned[...] = jnp.transpose(joined_ref[...])

    def trade(number):
        if number >= len(order):
            return
        kind, s = order[number]
        part = (here.o + s) % SPLIT
        for r in range(1, inner):
            sends[kind][s, r - 1] = gradient(kind, part * inner + (here.i + r) % inner).astype(BF16)
            first[kind, s, r] = remote(
                sends[kind].at[s, r - 1],
                inputs[kind].at[s, r - 1],
                send_i.at[kind, s, r - 1],
                recv_i.at[kind, s, r - 1],
                here.inner_peer(r),
            )

    def settle(number):
        kind, s = order[number]
        part = (here.o + s) % SPLIT
        total = gradient(kind, part * inner + here.i)
        for r in range(1, inner):
            first[kind, s, r].wait_recv()
            total = total + f32(inputs[kind][s, r - 1])
        totals[kind][s] = total.astype(BF16)
        source = totals[kind].at[s]
        pieces = [(kind, source)]
        if kind == 2:
            pieces = [
                (2, source.at[pl.ds(0, width_out), :]),
                (3, source.at[pl.ds(width_out, total.shape[0] - width_out), :]),
            ]
        for m, piece in pieces:
            if s:
                last.append(
                    remote(
                        piece, dst(m), send_o.at[m, s - 1], recv_o.at[m, s - 1], here.outer_peer(s)
                    )
                )
            else:
                copy = pltpu.make_async_copy(piece, dst(m), local.at[m])
                copy.start()
                own.append(copy)
        trade(number + AHEAD)
        return whole_sum(total * total)

    for number in range(AHEAD):
        trade(number)
    small.near(rows_ref[...])
    bias_in[here.i] = bias_ref[...]
    bias_inner = [
        remote(
            bias_in.at[here.i],
            bias_in.at[here.i],
            bias_send.at[SPLIT + r],
            bias_recv.at[SPLIT + r],
            here.inner_peer(r),
        )
        for r in range(1, inner)
    ]
    square = settle(0)
    square = square + settle(1)
    small.far()
    for number in range(2, 5):
        square = square + settle(number)
    small.along_outer()
    for copy in bias_inner:
        copy.wait_recv()
    bias = bias_in[0]
    for part in range(1, inner):
        bias = bias + bias_in[part]
    bias_out[here.o] = bias
    bias_outer = [
        remote(
            bias_out.at[here.o],
            bias_out.at[here.o],
            bias_send.at[s],
            bias_recv.at[s],
            here.outer_peer(s),
        )
        for s in range(1, SPLIT)
    ]
    square = square + whole_sum(bias * bias) / inner
    square = square + settle(5)
    square = square + settle(6)
    small.along_inner()
    square = square + settle(7)
    square = square + settle(8)
    rows_out[...] = small.value()
    for number in range(9, len(order)):
        square = square + settle(number)
    squares.near(jnp.broadcast_to(square, norm_ref.shape))
    squares.far()
    squares.along_outer()
    squares.along_inner()
    norm = squares.value()
    rows = rows_out[...]
    doubled = lax.broadcasted_iota(jnp.int32, rows.shape, 0) == 4
    norm_ref[...] = norm + whole_sum(rows * rows * jnp.where(doubled, 2.0, 1.0))
    for copy in bias_outer:
        copy.wait_recv()
    for copy in bias_inner + bias_outer:
        copy.wait_send()
    for copy in last:
        copy.wait()
    for copy in own:
        copy.wait()
    for copy in first.values():
        copy.wait_send()


def finish_call(tokens, branch, rows, kept, grads, sums, bias, shards, inner, number):
    dma = pltpu.SemaphoreType.DMA
    qkv, out, up, down = shards
    ordered = (qkv, up, out, down)
    facts, joined = kept
    shard = out[1]
    wide = [tokens, branch, rows]
    if not aligned(shard):
        wide = [jnp.swapaxes(w.reshape(w.shape[0], -1, shard), 0, 1) for w in wide]
    pieces = [
        (shard, grads[0].shape[1]),
        (shard, grads[1].shape[1]),
        (joined.shape[1], shard),
    ]
    peers = max(inner - 1, 1)
    tile = (8, 128)
    return pl.pallas_call(
        functools.partial(finish_kernel, inner),
        out_shape=[
            *(jax.ShapeDtypeStruct(shape, BF16) for shape in ordered),
            jax.ShapeDtypeStruct(sums.shape, F32),
            jax.ShapeDtypeStruct((SPLIT, *bias.shape), F32),
            jax.ShapeDtypeStruct(tile, F32),
        ],
        in_specs=[VMEM_SPEC if aligned(shard) else ANY_SPEC] + [VMEM_SPEC] * 8,
        out_specs=[ANY_SPEC] * 4 + [VMEM_SPEC] * 3,
        scratch_shapes=[pltpu.VMEM((SPLIT, peers, *piece), BF16) for piece in pieces]
        + [pltpu.VMEM((SPLIT, peers, *piece), BF16) for piece in pieces]
        + [pltpu.VMEM((SPLIT, *piece), BF16) for piece in pieces]
        + [
            pltpu.VMEM(joined.shape[::-1], BF16),
            dma((3, SPLIT, peers)),
            dma((3, SPLIT, peers)),
            dma((4, SPLIT - 1)),
            dma((4, SPLIT - 1)),
            dma((5,)),
            pltpu.VMEM((16, 128) if aligned(shard) else (tokens.shape[0], shard), BF16),
        ]
        + all_sum_scratch(sums.shape, inner)
        + all_sum_scratch(tile, inner)
        + [
            pltpu.VMEM((inner, *bias.shape), F32),
            dma((SPLIT + inner,)),
            dma((SPLIT + inner,)),
        ],
        compiler_params=pltpu.CompilerParams(
            collective_id=number, has_side_effects=True, vmem_limit_bytes=60 * 1024 * 1024
        ),
    )(*wide, joined, *grads, facts, sums, bias)


def reward_kernel(
    inner, stats_ref, member_ref, label_ref, out_ref, stats, outer_in, inner_in,
    send, recv, send_o, recv_o, send_i, recv_i,
):
    here = Place(inner)
    tensor_peers = [(here.dp, (here.t + s) % QUARTERS) for s in range(1, QUARTERS)]
    outer_peers = [here.outer_peer(s) for s in range(1, SPLIT)]
    inner_peers = [here.inner_peer(r) for r in range(1, inner)]
    greet(tensor_peers + outer_peers + inner_peers)

    def share(buffer, index, sends, recvs, peers):
        return [
            remote(buffer.at[index], buffer.at[index], sends.at[n], recvs.at[n], peer)
            for n, peer in enumerate(peers)
        ]

    stats[here.t] = stats_ref[...]
    copies = share(stats, here.t, send, recv, tensor_peers)
    for copy in copies:
        copy.wait_recv()
    quarters = [stats[q] for q in range(QUARTERS)]
    highest = functools.reduce(jnp.maximum, quarters)
    summed = functools.reduce(lambda a, b: a + b, [jnp.exp(q - highest) for q in quarters])
    totals = highest + jnp.log(summed)
    picks = functools.reduce(lambda a, b: a + b, quarters)
    log_probs = picks - totals_to_picks(totals)
    member = member_ref[...]
    policy_docs = jnp.sum(member * log_probs[1:2, :], axis=1, keepdims=True)
    frozen_docs = jnp.sum(member * log_probs[3:4, :], axis=1, keepdims=True)
    reward = policy_docs - frozen_docs
    outer_in[here.o] = jnp.broadcast_to(whole_sum(reward), outer_in.shape[1:])
    more = share(outer_in, here.o, send_o, recv_o, outer_peers)
    for copy in more:
        copy.wait_recv()
    inner_in[here.i] = functools.reduce(lambda a, b: a + b, [outer_in[n] for n in range(SPLIT)])
    rest = share(inner_in, here.i, send_i, recv_i, inner_peers)
    for copy in rest:
        copy.wait_recv()
    total = functools.reduce(lambda a, b: a + b, [inner_in[n] for n in range(inner)])
    seq_count = inner * SPLIT * SEGS
    shift = total[:, 0:1] / seq_count
    sigmoid_value = 1.0 / (1.0 + jnp.exp(-BETA_KTO * (reward - shift)))
    labels = label_ref[:, 0:1]
    doc_grad = BETA_KTO * sigmoid_value * (1.0 - sigmoid_value) * (1.0 - 2.0 * labels) / seq_count
    token_grad = jnp.sum(member * doc_grad, axis=0, keepdims=True)
    out_ref[...] = jnp.transpose(
        jnp.concatenate([token_grad, totals[0:1, :], jnp.zeros((6, totals.shape[1]), F32)], axis=0)
    )
    for copy in copies + more + rest:
        copy.wait_send()


def totals_to_picks(totals):
    return jnp.concatenate([totals[0:1], totals[0:1], totals[2:3], totals[2:3], totals[4:]], axis=0)


def reward_call(stats, member, labels, inner, number):
    dma = pltpu.SemaphoreType.DMA
    tile = (8, 128)
    peers = max(inner - 1, 1)
    return pl.pallas_call(
        functools.partial(reward_kernel, inner),
        out_shape=jax.ShapeDtypeStruct((stats.shape[1], 8), F32),
        in_specs=[VMEM_SPEC] * 3,
        out_specs=VMEM_SPEC,
        scratch_shapes=[
            pltpu.VMEM((QUARTERS, *stats.shape), F32),
            pltpu.VMEM((SPLIT, *tile), F32),
            pltpu.VMEM((inner, *tile), F32),
            dma((QUARTERS - 1,)),
            dma((QUARTERS - 1,)),
            dma((SPLIT - 1,)),
            dma((SPLIT - 1,)),
            dma((peers,)),
            dma((peers,)),
        ],
        compiler_params=pltpu.CompilerParams(collective_id=number, has_side_effects=True),
    )(stats, member, labels)


def turn_tables(positions):
    half = ROT // 2
    frequency = 10000.0 ** (-2.0 * jnp.arange(half, dtype=F32) / ROT)
    angles = positions.reshape(-1).astype(F32)[:, None] * frequency
    cosine, sine = jnp.cos(angles), jnp.sin(angles)
    none = jnp.zeros((angles.shape[0], HD - ROT), F32)
    return (
        jnp.concatenate([cosine, cosine, none + 1.0], axis=1),
        jnp.concatenate([-sine, sine, none], axis=1),
    )


def doc_layout(lengths_row, row_count):
    ends, run = [], 0
    for segment in range(lengths_row.shape[0]):
        run = run + lengths_row[segment]
        ends.append(run)
    doc_ends = jnp.stack(ends)
    starts = doc_ends - lengths_row
    index_rows = jnp.arange(row_count, dtype=jnp.int32)
    member = (index_rows[:, None] >= starts[None, :]) & (index_rows[:, None] < doc_ends[None, :])
    doc_ids = jnp.arange(lengths_row.shape[0], dtype=jnp.int32)
    doc_of = jnp.sum(jnp.where(member, doc_ids[None, :], 0), axis=1)
    positions = index_rows - jnp.sum(jnp.where(member, starts[None, :], 0), axis=1)
    return (member, positions, doc_of)


def chunk_of(width):
    return next(n for n in (1280, 640, 512, 256, 128) if width % n == 0)


def head_kernel(policy_ref, frozen_ref, head_ref, target_ref, logits_ref, stats_ref, other_ref, high_ref, sum_ref, pick_ref):
    chunk = pl.program_id(0)
    rows, columns = logits_ref.shape

    @pl.when(chunk == 0)
    def _():
        high_ref[...] = jnp.full_like(high_ref, MASKED)
        sum_ref[...] = jnp.zeros_like(sum_ref)
        pick_ref[...] = jnp.zeros_like(pick_ref)

    def fold(which, values_ref, begin, width):
        for first in range(0, rows, 64):
            own = pl.ds(first, 64)
            high = high_ref[which, own, :]
            lanes = [values_ref[own, n : n + 128] for n in range(begin, begin + width, 128)]
            highest = functools.reduce(jnp.maximum, lanes, high)
            total = sum_ref[which, own, :] * jnp.exp(high - highest)
            picked = pick_ref[which, own, :]
            target = target_ref[own, :] - (chunk * columns + begin)
            lane = lax.broadcasted_iota(jnp.int32, highest.shape, 1)
            for n, value in enumerate(lanes):
                total = total + jnp.exp(value - highest)
                picked = picked + jnp.where(lane + n * 128 == target, value, 0.0)
            high_ref[which, own, :] = highest
            sum_ref[which, own, :] = total
            pick_ref[which, own, :] = picked

    width = 256 if columns % 256 == 0 else 128
    last = None
    for begin in range(0, columns, width):
        for which, (low_ref, values_ref) in enumerate(
            ((policy_ref, logits_ref), (frozen_ref, other_ref))
        ):
            values_ref[:, begin : begin + width] = dot(
                low_ref[...], head_ref[:, begin : begin + width]
            )
            if last:
                fold(*last)
            last = (which, values_ref, begin, width)
    fold(*last)

    @pl.when(chunk == pl.num_programs(0) - 1)
    def _():
        found = []
        for which in range(2):
            high = jnp.max(high_ref[which], axis=1, keepdims=True)
            total = jnp.sum(
                sum_ref[which] * jnp.exp(high_ref[which] - high), axis=1, keepdims=True
            )
            found.append(high + jnp.log(total))
            found.append(jnp.sum(pick_ref[which], axis=1, keepdims=True))
        lane = lax.broadcasted_iota(jnp.int32, (rows, 128), 1)
        joined = jnp.zeros((rows, 128), F32)
        for n, value in enumerate(found):
            joined = jnp.where(lane == n, value, joined)
        stats_ref[...] = jnp.transpose(joined)[:8, :]


def head_call(policy_low, frozen_low, head_weight, targets):
    rows, depth = policy_low.shape
    width = head_weight.shape[1]
    columns = chunk_of(width)
    return pl.pallas_call(
        head_kernel,
        grid=(width // columns,),
        out_shape=[
            jax.ShapeDtypeStruct((rows, width), F32),
            jax.ShapeDtypeStruct((8, rows), F32),
        ],
        in_specs=[
            pl.BlockSpec((rows, depth), lambda n: (0, 0)),
            pl.BlockSpec((rows, depth), lambda n: (0, 0)),
            pl.BlockSpec((depth, columns), lambda n: (0, n)),
            pl.BlockSpec((rows, 1), lambda n: (0, 0)),
        ],
        out_specs=[
            pl.BlockSpec((rows, columns), lambda n: (0, n)),
            pl.BlockSpec((8, rows), lambda n: (0, 0)),
        ],
        scratch_shapes=[
            pltpu.VMEM((rows, columns), F32),
            pltpu.VMEM((2, rows, 128), F32),
            pltpu.VMEM((2, rows, 128), F32),
            pltpu.VMEM((2, rows, 128), F32),
        ],
        cost_estimate=pl.CostEstimate(
            flops=4 * rows * depth * width,
            bytes_accessed=2 * depth * width + 4 * rows * width,
            transcendentals=2 * rows * width,
        ),
        compiler_params=pltpu.CompilerParams(vmem_limit_bytes=56 * 1024 * 1024),
    )(policy_low, frozen_low, head_weight, targets)


def logit_grad_kernel(logits_ref, head_ref, target_ref, token_ref, part_ref, low_ref, sum_ref):
    chunk = pl.program_id(0)
    rows, columns = logits_ref.shape

    for first in range(0, rows, 32):
        own = pl.ds(first, 32)
        values = logits_ref[own, :]
        target = target_ref[own, :] - chunk * columns
        chosen = lax.broadcasted_iota(jnp.int32, values.shape, 1) == target
        probs = jnp.exp(values - token_ref[own, 1:2])
        low_ref[own, :] = (token_ref[own, 0:1] * (jnp.where(chosen, 1.0, 0.0) - probs)).astype(BF16)
    value = dot_cols(low_ref[...], head_ref[...])

    @pl.when(chunk == 0)
    def _():
        sum_ref[...] = value

    @pl.when(chunk > 0)
    def _():
        sum_ref[...] += value

    @pl.when(chunk == pl.num_programs(0) - 1)
    def _():
        part_ref[...] = sum_ref[...].astype(BF16)


def logit_grad_call(logits, head_weight, targets, tokens):
    rows, width = logits.shape
    depth = head_weight.shape[0]
    columns = chunk_of(width)
    return pl.pallas_call(
        logit_grad_kernel,
        grid=(width // columns,),
        out_shape=jax.ShapeDtypeStruct((rows, depth), BF16),
        in_specs=[
            pl.BlockSpec((rows, columns), lambda n: (0, n)),
            pl.BlockSpec((depth, columns), lambda n: (0, n)),
            pl.BlockSpec((rows, 1), lambda n: (0, 0)),
            pl.BlockSpec((rows, tokens.shape[1]), lambda n: (0, 0)),
        ],
        out_specs=pl.BlockSpec((rows, depth), lambda n: (0, 0)),
        scratch_shapes=[pltpu.VMEM((rows, columns), BF16), pltpu.VMEM((rows, depth), F32)],
        cost_estimate=pl.CostEstimate(
            flops=2 * rows * depth * width,
            bytes_accessed=2 * depth * width + 4 * rows * width,
            transcendentals=rows * width,
        ),
        compiler_params=pltpu.CompilerParams(vmem_limit_bytes=56 * 1024 * 1024),
    )(logits, head_weight, targets, tokens)


def adam_step(master, mean_old, square_old, gradient, factor, rate, decay_rate):
    clipped = f32(gradient) * factor
    mean_new = BETA_FIRST * mean_old + (1.0 - BETA_FIRST) * clipped
    square_new = BETA_SECOND * square_old + (1.0 - BETA_SECOND) * clipped * clipped
    mean_hat = mean_new / (1.0 - BETA_FIRST**STEP)
    square_hat = square_new / (1.0 - BETA_SECOND**STEP)
    master_new = master - rate * (
        mean_hat / (jnp.sqrt(square_hat) + ADAM_EPS) + decay_rate * master
    )
    return (mean_new, square_new, master_new)


def eight_rows(rows):
    return jnp.zeros((8, rows.shape[1]), F32).at[: rows.shape[0]].set(rows)


def on_device(
    inputs,
    targets,
    doc_lengths,
    desirable,
    head_weight,
    qkv_master,
    out_master,
    up_master,
    down_master,
    vectors,
    hidden_bias,
    qkv_mean,
    out_mean,
    up_mean,
    down_mean,
    vectors_mean,
    hidden_mean,
    qkv_square,
    out_square,
    up_square,
    down_square,
    vectors_square,
    hidden_square,
    qkv_frozen,
    out_frozen,
    up_frozen,
    down_frozen,
    vectors_frozen,
    hidden_frozen,
):
    dp_size = lax.axis_size("dp")
    tensor_size = lax.axis_size("tensor")
    inner = dp_size // SPLIT
    outer_index = lax.axis_index("dp") // inner
    block = inputs.shape[0]
    lengths_tile = jnp.zeros((8, 128), jnp.int32).at[0, :SEGS].set(doc_lengths[0])
    masters = tuple(w.astype(BF16) for w in (qkv_master, out_master, up_master, down_master))
    *policy_set, tokens_all, lengths_all = spread_weights(masters, inner, inputs, lengths_tile, 0)
    frozen_shards = (qkv_frozen, out_frozen, up_frozen, down_frozen)
    member, _, _ = doc_layout(doc_lengths[0], block)
    _, positions, doc_of = jax.vmap(lambda row: doc_layout(row, block))(lengths_all[:, 0, :SEGS])

    cut = qkv_master.shape[1]
    width_qkv, width_up = cut // SPLIT, up_master.shape[1] // SPLIT

    def own_bias(bias):
        return (
            lax.dynamic_slice(bias, (outer_index * width_qkv,), (width_qkv,))[None],
            lax.dynamic_slice(bias, (cut + outer_index * width_up,), (width_up,))[None],
        )

    layout = (
        *turn_tables(positions),
        doc_of.reshape(-1, 1),
        doc_of[:, None, :],
    )
    policy = (eight_rows(vectors), *own_bias(hidden_bias))
    frozen = (eight_rows(vectors_frozen), *own_bias(hidden_frozen))
    if aligned(out_master.shape[1]):
        final_low, frozen_low, *kept = forward_call(
            tokens_all, layout, (policy, frozen), policy_set, block, inner, None, frozen_shards, 2
        )
        kept_values = tuple(kept[:4])
    else:
        final_low, *kept = forward_call(
            tokens_all, layout, (policy,), policy_set, block, inner, None, frozen_shards, 2
        )
        kept_values = tuple(kept[:4])
        frozen_set = (*kept[4:6], joined_columns(kept[6]))
        (frozen_low,) = forward_call(
            tokens_all, layout, (frozen,), frozen_set, block, inner, kept_values[2], None, 3
        )
    vocab_start = lax.axis_index("tensor") * head_weight.shape[1]
    own_targets = (targets - vocab_start)[:, None]
    logits, stats = head_call(final_low, frozen_low, head_weight, own_targets)
    doc_rows = jnp.zeros((8, block), F32).at[:SEGS].set(f32(member).T)
    labels = jnp.zeros((8, 128), F32).at[:SEGS].set(f32(desirable[0])[:, None])
    token_rows = reward_call(stats, doc_rows, labels, inner, 6)
    final_part = logit_grad_call(logits, head_weight, own_targets, token_rows)
    input_grad, branch_low, mixed_grad, hidden_low, vector_part, bias_part = backward_call(
        final_part, tokens_all, eight_rows(vectors), policy_set, kept_values, layout, inner, 4
    )
    shards = tuple(w.shape for w in masters)
    bias_rows = (width_qkv + width_up) // 128
    bias_tile = (
        jnp.zeros((-(-bias_rows // 8) * 8, 128), F32)
        .at[:bias_rows]
        .set(bias_part.reshape(bias_rows, 128))
    )
    qkv_grad, up_grad, out_grad, down_grad, vector_sum, bias_sum, square = finish_call(
        tokens_all, branch_low, eight_rows(vectors), kept_values[2:], (mixed_grad, hidden_low),
        vector_part, bias_tile, shards, inner, 5,
    )
    input_grad = f32(input_grad)
    vector_grad = jnp.concatenate([vector_sum[:5], vector_sum[4:5]], axis=0)
    bias_sum = bias_sum[:, :bias_rows].reshape(SPLIT, bias_rows * 128)
    hidden_grad = jnp.concatenate(
        [bias_sum[:, :width_qkv].reshape(-1), bias_sum[:, width_qkv:].reshape(-1)]
    )
    grad_norm = jnp.sqrt(square[0, 0])
    factor = jnp.minimum(1.0, CLIP_NORM / (grad_norm + 1e-06))
    qkv_state = adam_step(
        qkv_master, qkv_mean, qkv_square, qkv_grad, factor, LEARN_RATE, WEIGHT_DECAY
    )
    out_state = adam_step(
        out_master, out_mean, out_square, out_grad, factor, LEARN_RATE, WEIGHT_DECAY
    )
    up_state = adam_step(up_master, up_mean, up_square, up_grad, factor, LEARN_RATE, WEIGHT_DECAY)
    down_state = adam_step(
        down_master, down_mean, down_square, down_grad, factor, LEARN_RATE, WEIGHT_DECAY
    )
    vector_state = adam_step(
        vectors, vectors_mean, vectors_square, vector_grad, factor, VECTOR_RATE, 0.0
    )
    hidden_state = adam_step(
        hidden_bias, hidden_mean, hidden_square, hidden_grad, factor, VECTOR_RATE, 0.0
    )
    return (
        final_low,
        input_grad,
        grad_norm,
        *qkv_state,
        *out_state,
        *up_state,
        *down_state,
        *vector_state,
        *hidden_state,
    )


def solution(mesh):
    rows, cols = P("dp", "tensor"), P("tensor", "dp")
    matrices = (rows, cols, rows, cols)
    placed = (
        P("dp", None),
        P("dp"),
        P("dp", None),
        P("dp", None),
        P(None, "tensor"),
        *matrices,
        P(),
        P("tensor"),
        *matrices,
        P(),
        P("tensor"),
        *matrices,
        P(),
        P("tensor"),
        *matrices,
        P(),
        P("tensor"),
    )
    return jax.shard_map(
        on_device,
        mesh=mesh,
        in_specs=placed,
        out_specs=(
            P("dp", None),
            P("dp", None),
            P(),
            *(spec for spec in matrices for _ in range(3)),
            P(),
            P(),
            P(),
            P("tensor"),
            P("tensor"),
            P("tensor"),
        ),
        check_vma=False,
    )
```

```python
import functools

import jax
import jax.numpy as jnp
import numpy as np
from jax import lax
from jax.experimental import pallas as pl
from jax.experimental.pallas import tpu as pltpu
from jax.sharding import PartitionSpec as P

HD = 128
ROT = 32
SEGS = 4
STEP = 3
SPLIT = 4
QUARTERS = 4
MEAN, SCALE, FACTS = 6, 7, 8
AHEAD = 3


EPS_NORM = 1e-05
BETA_KTO = 0.1
CLIP_NORM = 0.01
LEARN_RATE = 0.02
VECTOR_RATE = 0.2
BETA_FIRST = 0.9
BETA_SECOND = 0.999
ADAM_EPS = 1e-08
WEIGHT_DECAY = 0.01
MASKED = -1e30

MESH = pl.DeviceIdType.MESH
BF16 = jnp.bfloat16
F32 = jnp.float32
ANY_SPEC = pl.BlockSpec(memory_space=pltpu.HBM)
VMEM_SPEC = pl.BlockSpec(memory_space=pltpu.VMEM)


class Place:
    def __init__(self, inner):
        self.inner = inner
        self.dp = lax.axis_index("dp")
        self.t = lax.axis_index("tensor")
        self.o = self.dp // inner
        self.i = self.dp % inner
        self.near = self.t + 1 - 2 * (self.t % 2)
        self.far = (self.t + 2) % QUARTERS

    def outer_peer(self, shift):
        return (((self.o + shift) % SPLIT) * self.inner + self.i, self.t)

    def inner_peer(self, shift):
        return (self.o * self.inner + (self.i + shift) % self.inner, self.t)

    def near_peer(self):
        return (self.dp, self.near)

    def far_peer(self):
        return (self.dp, self.far)


def aligned(shard):
    return shard % 128 == 0


def greet(peers):
    barrier = pltpu.get_barrier_semaphore()
    for peer in peers:
        pl.semaphore_signal(barrier, inc=1, device_id=peer, device_id_type=MESH)
    pl.semaphore_wait(barrier, len(peers))


def remote(src, dst, send_sem, recv_sem, peer):
    copy = pltpu.make_async_remote_copy(
        src_ref=src,
        dst_ref=dst,
        send_sem=send_sem,
        recv_sem=recv_sem,
        device_id=peer,
        device_id_type=MESH,
    )
    copy.start()
    return copy


class Spread:
    def __init__(self, here, shards, wholes, send_o, recv_o, send_i, recv_i, local, *held):
        self.here = here
        self.qkv, self.out, self.up, self.down = shards
        self.qkv_all, self.up_all, self.low_all = wholes
        self.send_o, self.recv_o, self.send_i, self.recv_i = send_o, recv_o, send_i, recv_i
        self.local, self.held = local, held
        self.first, self.own, self.passed = {}, [], []
        self.order = [(m, s) for m in range(4) for s in (2, 1, 3)]

    def src(self, m, part):
        shard = (self.qkv, self.up, self.out, self.down)[m]
        width = shard.shape[1 if m < 2 else 0] // SPLIT
        where = pl.ds(part * width, width)
        return shard.at[:, where] if m < 2 else shard.at[where, :]

    def dst(self, m, index):
        shard = self.qkv.shape[0]
        where = pl.ds(index * shard, shard)
        if m < 2:
            return (self.qkv_all, self.up_all)[m].at[where, :]
        width_out, width_down = self.out.shape[0] // SPLIT, self.down.shape[0] // SPLIT
        rows = pl.ds(0, width_out) if m == 2 else pl.ds(width_out, width_down)
        low_all = self.low_all
        return low_all.at[rows, where] if aligned(shard) else low_all.at[index, rows, :]

    def peers(self):
        here = self.here
        peers = [here.outer_peer(s) for s in range(1, SPLIT)]
        return peers + [here.inner_peer(r) for r in range(1, here.inner)]

    def send_on(self, number):
        if number >= len(self.order):
            return
        m, s = self.order[number]
        self.first[m, s] = remote(
            self.src(m, (self.here.o + s) % SPLIT),
            self.dst(m, self.here.dp),
            self.send_o.at[m, s - 1],
            self.recv_o.at[m, s - 1],
            self.here.outer_peer(s),
        )

    def pass_on(self, m, s, source, index):
        here = self.here
        for r in range(1, here.inner):
            self.passed.append(
                remote(
                    source,
                    self.dst(m, index),
                    self.send_i.at[m, s, r - 1],
                    self.recv_i.at[m, s, r - 1],
                    here.inner_peer(r),
                )
            )

    def start_own(self):
        here = self.here
        loads = [
            pltpu.make_async_copy(self.src(m, here.o), self.held[m], self.local.at[m])
            for m in range(4)
        ]
        for load in loads:
            load.start()
        for m, load in enumerate(loads):
            load.wait()
            self.pass_on(m, 0, self.held[m], here.dp)
            copy = pltpu.make_async_copy(self.held[m], self.dst(m, here.dp), self.local.at[4 + m])
            copy.start()
            self.own.append(copy)

    def step(self, number):
        here = self.here
        m, s = self.order[number]
        self.first[m, s].wait_recv()
        self.send_on(number + AHEAD)
        index = ((here.o + SPLIT - s) % SPLIT) * here.inner + here.i
        self.pass_on(m, s, self.dst(m, index), index)

    def finish(self):
        for copy in self.first.values():
            copy.wait_send()
        for copy in self.own:
            copy.wait()
        for copy in self.passed:
            copy.wait()


def spread_weights_kernel(
    inner, qkv, out, up, down, tokens, lengths, qkv_all, up_all, low_all, tokens_all, lengths_all,
    send_o, recv_o, send_i, recv_i, local, held_0, held_1, held_2, held_3,
    send_t, recv_t, send_l, recv_l,
):
    here = Place(inner)
    spread = Spread(
        here, (qkv, out, up, down), (qkv_all, up_all, low_all),
        send_o, recv_o, send_i, recv_i, local, held_0, held_1, held_2, held_3,
    )
    greet(spread.peers() + [here.far_peer(), here.near_peer()])
    rows, block = tokens.shape[0] // QUARTERS, tokens.shape[0]

    def piece(part, quarter):
        return tokens_all.at[pl.ds((part * QUARTERS + quarter) * rows, rows), :]

    waits, token_copies, across, own = [], {}, {}, []
    for s in (2, 1, 3):
        token_copies[s] = remote(
            tokens.at[pl.ds(here.t * rows, rows), :],
            piece(here.o, here.t),
            send_t.at[0, s - 1],
            recv_t.at[0, s - 1],
            here.outer_peer(s),
        )
        waits.append(
            remote(
                lengths,
                lengths_all.at[here.o],
                send_l.at[s - 1],
                recv_l.at[s - 1],
                here.outer_peer(s),
            )
        )
    own.append(
        pltpu.make_async_copy(
            tokens, tokens_all.at[pl.ds(here.o * block, block), :], local.at[8]
        )
    )
    own.append(pltpu.make_async_copy(lengths, lengths_all.at[here.o], local.at[9]))
    for copy in own:
        copy.start()
    spread.start_own()
    for number, s in enumerate((2, 1, 3)):
        token_copies[s].wait_recv()
        spread.send_on(number)
        part = (here.o + SPLIT - s) % SPLIT
        for stage, peer in ((1, here.far_peer()), (2, here.near_peer())):
            copy = remote(
                piece(part, here.t),
                piece(part, here.t),
                send_t.at[stage, s - 1],
                recv_t.at[stage, s - 1],
                peer,
            )
            if stage == 1:
                across[s] = copy
            else:
                waits.append(copy)
    for number in range(len(spread.order)):
        spread.step(number)
    for s in (2, 1, 3):
        across[s].wait_recv()
        part = (here.o + SPLIT - s) % SPLIT
        waits.append(
            remote(
                piece(part, here.far),
                piece(part, here.far),
                send_t.at[3, s - 1],
                recv_t.at[3, s - 1],
                here.near_peer(),
            )
        )
    for copy in list(token_copies.values()) + list(across.values()):
        copy.wait_send()
    for copy in own:
        copy.wait()
    spread.finish()
    for copy in waits:
        copy.wait()


def whole_shapes(shards, inner):
    qkv, out, up, down = shards
    d_model = out.shape[1] * SPLIT * inner
    width = out.shape[0] // SPLIT + down.shape[0] // SPLIT
    return [
        jax.ShapeDtypeStruct((d_model, qkv.shape[1] // SPLIT), BF16),
        jax.ShapeDtypeStruct((d_model, up.shape[1] // SPLIT), BF16),
        jax.ShapeDtypeStruct(
            (width, d_model) if aligned(out.shape[1]) else (SPLIT * inner, width, out.shape[1]),
            BF16,
        ),
    ]


def joined_columns(low_all):
    if low_all.ndim == 3:
        low_all = jnp.swapaxes(low_all, 0, 1).reshape(low_all.shape[1], -1)
    return low_all


def spread_scratch(shards, inner):
    dma = pltpu.SemaphoreType.DMA
    qkv, out, up, down = shards
    pieces = [
        (qkv.shape[0], qkv.shape[1] // SPLIT),
        (up.shape[0], up.shape[1] // SPLIT),
        (out.shape[0] // SPLIT, out.shape[1]),
        (down.shape[0] // SPLIT, down.shape[1]),
    ]
    return [
        dma((4, SPLIT - 1)),
        dma((4, SPLIT - 1)),
        dma((4, SPLIT, max(inner - 1, 1))),
        dma((4, SPLIT, max(inner - 1, 1))),
        dma((10,)),
        *(pltpu.VMEM(piece, BF16) for piece in pieces),
    ]


def spread_weights(shards, inner, tokens, lengths, number):
    dma = pltpu.SemaphoreType.DMA
    shapes = whole_shapes(shards, inner) + [
        jax.ShapeDtypeStruct((tokens.shape[0] * SPLIT, tokens.shape[1]), BF16),
        jax.ShapeDtypeStruct((SPLIT, *lengths.shape), lengths.dtype),
    ]
    qkv_all, up_all, low_all, *gathered = pl.pallas_call(
        functools.partial(spread_weights_kernel, inner),
        out_shape=shapes,
        in_specs=[ANY_SPEC] * 4 + [VMEM_SPEC] * 2,
        out_specs=[ANY_SPEC] * len(shapes),
        scratch_shapes=spread_scratch(shards, inner)
        + [
            dma((4, SPLIT - 1)),
            dma((4, SPLIT - 1)),
            dma((SPLIT - 1,)),
            dma((SPLIT - 1,)),
        ],
        compiler_params=pltpu.CompilerParams(collective_id=number, has_side_effects=True),
    )(*shards, tokens, lengths)
    return (qkv_all, up_all, joined_columns(low_all), *gathered)


def f32(value):
    return value.astype(F32)


class RowSum:
    def __init__(self, here, part_ref, total, near_in, far_in, far_out, outer_in, outer_out, *sems):
        self.here, self.part, self.total = here, part_ref, total
        self.near_in, self.far_in, self.far_out = near_in, far_in, far_out
        self.outer_in, self.outer_out = outer_in, outer_out
        self.near_sems, self.far_sems, self.outer_sems = sems[0:2], sems[2:4], sems[4:6]
        self.quarter_sems = sems[6:8]
        self.rows = far_out.shape[1]
        self.near, self.far, self.outer, self.coming = {}, {}, {}, {}
        self.slots = None
        self.before = None

    def recycle(self, step):
        for side in range(2):
            self.near.pop((step, side)).wait_send()

    def rows_of(self, step, quarter):
        block = self.slots[step] if self.slots else (self.here.o + 1 + step) % SPLIT
        return pl.ds((block * QUARTERS + quarter) * self.rows, self.rows)

    def start(self, step):
        here = self.here
        for side, quarter in enumerate(((here.near + 2) % QUARTERS, here.near)):
            self.near[step, side] = remote(
                self.part.at[self.rows_of(step, quarter), :],
                self.near_in.at[step, side],
                self.near_sems[0].at[step, side],
                self.near_sems[1].at[step, side],
                here.near_peer(),
            )

    def across(self, step):
        here = self.here
        self.near[step, 0].wait_recv()
        if self.before:
            self.before.far.pop(step).wait_send()
        self.far_out[step] = (
            f32(self.part[self.rows_of(step, here.far), :]) + f32(self.near_in[step, 0])
        ).astype(BF16)
        self.far[step] = remote(
            self.far_out.at[step],
            self.far_in.at[step],
            self.far_sems[0].at[step],
            self.far_sems[1].at[step],
            here.far_peer(),
        )

    def along(self, step):
        here = self.here
        self.near[step, 1].wait_recv()
        self.far[step].wait_recv()
        value = (
            f32(self.part[self.rows_of(step, here.t), :])
            + f32(self.near_in[step, 1])
            + f32(self.far_in[step])
        )
        if step == SPLIT - 1:
            self.total[...] = value
            return
        if self.before:
            self.before.outer.pop(step).wait_send()
        self.outer_out[step] = value.astype(BF16)
        self.outer[step] = self.coming[step] = remote(
            self.outer_out.at[step],
            self.outer_in.at[step],
            self.outer_sems[0].at[step],
            self.outer_sems[1].at[step],
            here.outer_peer(step + 1),
        )

    def value(self):
        value = self.total[...]
        for step in range(SPLIT - 1):
            self.coming[step].wait_recv()
            value = value + f32(self.outer_in[step])
        return value

    def finish(self):
        for copies in (self.near, self.far, self.outer):
            for copy in copies.values():
                copy.wait_send()


class Quarters:
    def __init__(self, here, ref, rows, send, recv):
        self.here, self.ref, self.rows, self.send, self.recv = here, ref, rows, send, recv

    def copy(self, number, quarter, peer):
        piece = self.ref.at[pl.ds(quarter * self.rows, self.rows), :]
        return remote(piece, piece, self.send.at[number], self.recv.at[number], peer)

    def start(self):
        self.far = self.copy(0, self.here.t, self.here.far_peer())
        self.near = self.copy(1, self.here.t, self.here.near_peer())

    def pass_on(self):
        self.far.wait_recv()
        self.passed = self.copy(2, self.here.far, self.here.near_peer())

    def finish(self):
        self.near.wait_recv()
        self.passed.wait_recv()
        for copy in (self.far, self.near, self.passed):
            copy.wait_send()


def gather_quarters(here, ref, rows, send, recv):
    quarters = Quarters(here, ref, rows, send, recv)
    quarters.start()
    quarters.pass_on()
    quarters.finish()


def reduce_peers(here):
    return [here.outer_peer(s) for s in range(1, SPLIT)] + [here.far_peer(), here.near_peer()]


def dot(left, right):
    return jnp.dot(left, right, preferred_element_type=F32)


def dot_cols(left, right):
    return lax.dot_general(left, right, (((1,), (1,)), ((), ())), preferred_element_type=F32)


def error_function(value):
    value = jnp.clip(value, -3.832506856900711, 3.832506856900711)
    square = value * value
    above = jnp.full_like(square, 0.00022905065861350646)
    for term in (0.0034082910107109506, 0.050955695062380861, 0.18520832239976145, 1.128379143519084):
        above = above * square + term
    below = jnp.full_like(square, -1.1791602954361697e-7)
    for term in (
        0.000023547966471313185, 0.0010179625278914885, 0.014070470171167667,
        0.11098505178285362, 0.49746925110067538, 1.0,
    ):
        below = below * square + term
    return value * above / below


def turn(values, tables, where, direction):
    cosine, sine = (table[where, :] for table in tables)
    ahead = pltpu.roll(values, values.shape[1] - ROT // 2, 1)
    behind = pltpu.roll(values, ROT // 2, 1)
    first = lax.broadcasted_iota(jnp.int32, values.shape, 1) < ROT // 2
    return values * cosine + direction * (jnp.where(first, ahead, behind) * sine)


def documents(lengths, index):
    end = jnp.zeros((1, 1), jnp.int32)
    found = jnp.zeros(index.shape, jnp.int32)
    for segment in range(SEGS - 1):
        end = end + lengths[0:1, segment : segment + 1]
        found = found + (index >= end).astype(jnp.int32)
    return found


def row_tiles(start, count, tile, body):
    @pl.loop(0, count // tile)
    def _(n):
        body(pl.ds(pl.multiple_of(start + n * tile, tile), tile), pl.ds(pl.multiple_of(n * tile, tile), tile))


def forward_kernel(inner, keeps, background, *refs):
    here = Place(inner)
    refs = list(refs)

    def take(count):
        taken = refs[:count]
        del refs[:count]
        return taken

    tokens_ref, lengths_ref, cosine, sine = take(4)
    tables = (cosine, sine)
    own_rows = [take(2) for _ in keeps]
    given = take(3)
    facts_ref = None if keeps[0] else take(1)[0]
    shards = take(4 if background else 0)
    finals = take(len(keeps))
    slope_ref, kept_mixed, facts_ref, kept_joined = take(4) if keeps[0] else (None, None, facts_ref, None)
    wholes = take(3 if background else 0)
    weights, load = take(3), take(1)[0]
    other_mixed, other_joined = (None, None) if all(keeps) else take(2)
    one_ref, two_ref, hidden_ref, part_ref = take(4)
    block = one_ref.shape[0]
    common = take(14)
    sums = [RowSum(here, part_ref, *common)]
    if len(keeps) > 1:
        total, outer_in, *sems = take(10)
        sums.append(RowSum(here, part_ref, total, *common[1:4], outer_in, common[5], *sems))
        sums[1].before = sums[0]
    for number, layer in enumerate(sums):
        layer.slots = {step: (number * SPLIT + step) % 2 for step in range(SPLIT)}
    rows = sums[0].rows
    qkv_ref, up_ref, low_ref = weights
    heads = qkv_ref.shape[1] // (3 * HD)
    cut = heads * HD
    peers = reduce_peers(here)
    spread = None
    if background:
        spread = Spread(here, shards, wholes, *refs)
        peers = spread.peers() + [here.far_peer(), here.near_peer()]
    greet(peers)
    events = []
    loads = []

    def fetch(sources):
        for number, (source, target) in enumerate(zip(sources, weights)):
            copy = pltpu.make_async_copy(source, target, load.at[number])
            copy.start()
            loads.append(copy)

    fetch(given)
    if background:
        for number in range(AHEAD):
            spread.send_on(number)
        spread.start_own()
        events = list(range(len(spread.order)))

    def serve():
        if events:
            spread.step(events.pop(0))

    def stage(name, position):
        if 0 <= position < len(keeps) * SPLIT:
            getattr(sums[position // SPLIT], name)(position % SPLIT)

    gathers = []

    def settle(number):
        rows_ref = own_rows[number][0]
        branch = sums[number].value() + rows_ref[4:5, :] + rows_ref[5:6, :]
        quarter = pl.ds(pl.multiple_of(here.o * block + here.t * rows, rows), rows)
        mine = pl.ds(pl.multiple_of(here.t * rows, rows), rows)
        finals[number][mine, :] = (f32(tokens_ref[quarter, :]) + branch).astype(BF16)
        gathers.append(Quarters(here, finals[number], rows, *sums[number].quarter_sems))
        gathers[-1].start()

    for position in range(len(keeps) * SPLIT):
        number, step = position // SPLIT, position % SPLIT
        keep = keeps[number]
        rows_ref, bias_ref = own_rows[number]
        mixed_ref, joined_ref = (
            (kept_mixed, kept_joined) if keep else (other_mixed, other_joined)
        )
        own_block = (here.o + 1 + step) % SPLIT
        start = own_block * block
        kept = start if keep else 0

        def norm(where, own):
            values = f32(tokens_ref[where, :])
            if keep:
                mean = jnp.mean(values, axis=1, keepdims=True)
                centre = values - mean
                scale = lax.rsqrt(jnp.mean(centre * centre, axis=1, keepdims=True) + EPS_NORM)
                facts_ref[where, MEAN : MEAN + 1] = mean
                facts_ref[where, SCALE : SCALE + 1] = scale
                normed = centre * scale
            else:
                normed = (values - facts_ref[where, MEAN : MEAN + 1]) * facts_ref[
                    where, SCALE : SCALE + 1
                ]
            one_ref[own, :] = (normed * rows_ref[0:1, :] + rows_ref[1:2, :]).astype(BF16)
            two_ref[own, :] = (normed * rows_ref[2:3, :] + rows_ref[3:4, :]).astype(BF16)

        row_tiles(start, block, 16, norm)
        serve()
        stage("across", position - 1)
        if number and step == 0:
            while events:
                serve()
            spread.finish()
            fetch(wholes)
        while loads:
            loads.pop(0).wait()
        whole = pl.ds(pl.multiple_of(start, block), block)
        mine = pl.ds(kept if keep else 0, block)
        width = qkv_ref.shape[1]
        first_bias = bias_ref[:, pl.ds(pl.multiple_of(here.o * width, 128), width)]
        mixed = dot(one_ref[...], qkv_ref[...]) + first_bias
        for head in range(heads):
            at = head * 3 * HD
            for offset in (0, HD):
                mixed_ref[mine, at + offset : at + offset + HD] = turn(
                    mixed[:, at + offset : at + offset + HD], tables, pl.ds(0, block), 1.0
                ).astype(BF16)
            mixed_ref[mine, at + 2 * HD : at + 3 * HD] = mixed[:, at + 2 * HD : at + 3 * HD].astype(
                BF16
            )
        hidden_ref[...] = dot(two_ref[...], up_ref[...])
        serve()
        lengths = lengths_ref[own_block]
        doc_col = documents(lengths, lax.broadcasted_iota(jnp.int32, (block, 1), 0))
        doc_row = documents(lengths, lax.broadcasted_iota(jnp.int32, (1, block), 1))
        for head in range(heads):
            at = head * 3 * HD
            for first in range(0, block, 128):
                queries = pl.ds(pl.multiple_of(kept + first, 128), 128)
                tokens_at = pl.ds(pl.multiple_of(start + first, 128), 128)
                keys = pl.ds(pl.multiple_of(kept, 128), first + 128)
                scores = dot_cols(
                    mixed_ref[queries, at : at + HD], mixed_ref[keys, at + HD : at + 2 * HD]
                ) * HD ** (-0.5)
                same = doc_col[first : first + 128] == doc_row[:, : first + 128]
                earlier = first + lax.broadcasted_iota(
                    jnp.int32, scores.shape, 0
                ) >= lax.broadcasted_iota(jnp.int32, scores.shape, 1)
                scores = jnp.where(same & earlier, scores, MASKED)
                highest = jnp.max(scores, axis=1, keepdims=True)
                total = highest + jnp.log(
                    jnp.sum(jnp.exp(scores - highest), axis=1, keepdims=True)
                )
                if keep:
                    facts_ref[tokens_at, head : head + 1] = total
                probs = jnp.exp(scores - total).astype(BF16)
                joined_ref[queries, head * HD : (head + 1) * HD] = dot(
                    probs, mixed_ref[keys, at + 2 * HD : at + 3 * HD]
                ).astype(BF16)
        stage("along", position - 2)
        stage("recycle", position - 2)

        def activate(where, own):
            width = up_ref.shape[1]
            begin = SPLIT * qkv_ref.shape[1] + here.o * width
            hidden = hidden_ref[own, :] + bias_ref[:, pl.ds(pl.multiple_of(begin, 128), width)]
            share = 0.5 * (1.0 + error_function(hidden * 0.7071067811865476))
            joined_ref[where, cut:] = (hidden * share).astype(BF16)
            if keep:
                density = jnp.exp(-0.5 * hidden * hidden) * 0.3989422804014327
                slope_ref[where, :] = share + hidden * density

        row_tiles(kept, block, 32, activate)
        serve()
        columns = 512
        slot = pl.ds((position % 2) * block, block)

        @pl.loop(0, part_ref.shape[1] // columns)
        def _(n):
            at = pl.ds(pl.multiple_of(n * columns, columns), columns)
            part_ref[slot, at] = dot(joined_ref[mine, :], low_ref[:, at]).astype(BF16)

        stage("start", position)
        if number and step == 2:
            settle(0)
        if number and step == 3:
            gathers[0].pass_on()
    last = len(keeps) - 1
    sums[last].across(SPLIT - 1)
    while events:
        serve()
    sums[last].along(SPLIT - 2)
    sums[last].along(SPLIT - 1)
    settle(last)
    gathers[last].pass_on()
    for gather in gathers:
        gather.finish()
    for layer in sums:
        layer.finish()
    if background and last == 0:
        spread.finish()


def forward_call(tokens, layout, layers, weights, block, inner, facts, shards, number):
    total_rows, d_model = tokens.shape
    qkv_all, up_all, low_all = weights
    background = shards is not None
    keeps = (facts is None,) + (False,) * (len(layers) - 1)
    dma = pltpu.SemaphoreType.DMA
    outs = [jax.ShapeDtypeStruct((block, d_model), BF16) for _ in layers]
    if keeps[0]:
        outs += [
            jax.ShapeDtypeStruct((total_rows, up_all.shape[1]), F32),
            jax.ShapeDtypeStruct((total_rows, qkv_all.shape[1]), BF16),
            jax.ShapeDtypeStruct((total_rows, FACTS), F32),
            jax.ShapeDtypeStruct((total_rows, low_all.shape[0]), BF16),
        ]
    specs = [VMEM_SPEC] * len(outs)
    scratch = [pltpu.VMEM(w.shape, BF16) for w in weights] + [dma((3,))]
    if not all(keeps):
        scratch += [
            pltpu.VMEM((block, qkv_all.shape[1]), BF16),
            pltpu.VMEM((block, low_all.shape[0]), BF16),
        ]
    scratch += [
        pltpu.VMEM((block, d_model), BF16),
        pltpu.VMEM((block, d_model), BF16),
        pltpu.VMEM((block, up_all.shape[1]), F32),
        pltpu.VMEM((2 * block, d_model), BF16),
    ]
    one_sum = reduce_scratch(block // QUARTERS, d_model)
    scratch += one_sum
    if len(layers) > 1:
        scratch += [one_sum[0], one_sum[4], *one_sum[6:]]
    operands = [tokens, *layout]
    for layer in layers:
        operands += layer
    in_specs = [VMEM_SPEC] * len(operands)
    operands += weights
    in_specs += [ANY_SPEC] * 3
    if not keeps[0]:
        operands.append(facts)
        in_specs.append(VMEM_SPEC)
    if background:
        operands += shards
        in_specs += [ANY_SPEC] * 4
        outs += whole_shapes(shards, inner)
        specs += [ANY_SPEC] * 3
        scratch += spread_scratch(shards, inner)
    return pl.pallas_call(
        functools.partial(forward_kernel, inner, keeps, background),
        out_shape=outs,
        in_specs=in_specs,
        out_specs=specs,
        scratch_shapes=scratch,
        compiler_params=pltpu.CompilerParams(
            collective_id=number, has_side_effects=True, vmem_limit_bytes=60 * 1024 * 1024
        ),
    )(*operands)


def input_change(values, scaled):
    centre = values - jnp.mean(values, axis=1, keepdims=True)
    spread = jnp.mean(centre * centre, axis=1, keepdims=True)
    scale = lax.rsqrt(spread + EPS_NORM)
    normed = centre * scale
    along = jnp.mean(scaled * normed, axis=1, keepdims=True)
    return scale * (scaled - jnp.mean(scaled, axis=1, keepdims=True) - normed * along)


def reduce_scratch(rows, width):
    dma = pltpu.SemaphoreType.DMA
    return [
        pltpu.VMEM((rows, width), F32),
        pltpu.VMEM((SPLIT, 2, rows, width), BF16),
        pltpu.VMEM((SPLIT, rows, width), BF16),
        pltpu.VMEM((SPLIT, rows, width), BF16),
        pltpu.VMEM((SPLIT - 1, rows, width), BF16),
        pltpu.VMEM((SPLIT - 1, rows, width), BF16),
        dma((SPLIT, 2)),
        dma((SPLIT, 2)),
        dma((SPLIT,)),
        dma((SPLIT,)),
        dma((SPLIT - 1,)),
        dma((SPLIT - 1,)),
        dma((3,)),
        dma((3,)),
    ]


def dot_rows(left, right):
    return lax.dot_general(left, right, (((0,), (0,)), ((), ())), preferred_element_type=F32)


def backward_kernel(
    inner, final_part, tokens_hbm, rows_ref, qkv_ref, up_ref, low_ref, slope_ref, mixed_ref,
    facts_ref, lengths_ref, cosine, sine,
    grad_ref, branch_all, mixed_grad, hidden_grad, rows_out, bias_out,
    near_in, far_in, far_out, low, quarter, tokens_ref, own_tokens, joined_ref, key_ref, value_ref,
    part_ref,
    near_send, near_recv, far_send, far_recv, send, recv, local, *scratch,
):
    here = Place(inner)
    tables = (cosine, sine)
    sums = RowSum(here, part_ref, *scratch)
    rows = sums.rows
    block = rows * QUARTERS
    heads = qkv_ref.shape[1] // (3 * HD)
    cut = heads * HD
    greet(reduce_peers(here))

    def rows_of(number):
        return pl.ds(pl.multiple_of(number * rows, rows), rows)

    near = []
    for side, number in enumerate(((here.near + 2) % QUARTERS, here.near)):
        near.append(
            remote(
                final_part.at[rows_of(number), :],
                near_in.at[side],
                near_send.at[side],
                near_recv.at[side],
                here.near_peer(),
            )
        )

    shifts = (1, 3, 2, 0)

    def fetch(position):
        copy = pltpu.make_async_copy(
            tokens_hbm.at[pl.ds(((here.o + SPLIT - shifts[position]) % SPLIT) * block, block), :],
            tokens_ref,
            local.at[0],
        )
        copy.start()
        return copy

    fetched = fetch(0)
    own_copy = pltpu.make_async_copy(
        tokens_hbm.at[rows_of(here.o * QUARTERS + here.t), :], own_tokens, local.at[1]
    )
    own_copy.start()
    near[0].wait_recv()
    far_out[...] = (f32(final_part[rows_of(here.far), :]) + f32(near_in[0])).astype(BF16)
    far = remote(far_out, far_in, far_send, far_recv, here.far_peer())
    near[1].wait_recv()
    far.wait_recv()
    quarter[...] = f32(final_part[rows_of(here.t), :]) + f32(near_in[1]) + f32(far_in[...])
    low[...] = quarter[...].astype(BF16)
    rows_out[...] = jnp.zeros_like(rows_out)
    bias_out[...] = jnp.zeros_like(bias_out)
    rows_out[4:5, :] = jnp.sum(f32(low[...]), axis=0, keepdims=True)

    def piece(s, number):
        part = (here.o + SPLIT - s) % SPLIT
        return branch_all.at[rows_of(part * QUARTERS + number), :]

    outer, across, beside, beyond = {}, {}, {}, {}

    def send_out(s):
        outer[s] = remote(low, piece(0, here.t), send.at[0, s], recv.at[0, s], here.outer_peer(s))

    send_out(1)
    send_out(3)
    own = pltpu.make_async_copy(low, piece(0, here.t), local.at[2])
    own.start()

    def arrived(s):
        if s:
            outer[s].wait_recv()
        if s == 1:
            send_out(2)
        source = piece(s, here.t) if s else low
        across[s] = remote(
            source, piece(s, here.t), send.at[1, s], recv.at[1, s], here.far_peer()
        )
        beside[s] = remote(
            source, piece(s, here.t), send.at[2, s], recv.at[2, s], here.near_peer()
        )

    def crossed(s):
        across[s].wait_recv()
        beyond[s] = remote(
            piece(s, here.far), piece(s, here.far), send.at[3, s], recv.at[3, s], here.near_peer()
        )

    arrived(0)
    crossed(0)
    arrived(1)
    crossed(1)
    own.wait()
    steps = [SPLIT - 1 - s for s in shifts]
    sums.slots = {step: position % 2 for position, step in enumerate(steps)}
    events = [
        (arrived, 3), None, (crossed, 3), (arrived, 2), None, (crossed, 2),
    ]

    def serve():
        event = events.pop(0) if events else None
        if event:
            event[0](event[1])

    for position, s in enumerate(shifts):
        step = steps[position]
        part = (here.o + SPLIT - s) % SPLIT
        start = pl.multiple_of(part * block, block)
        whole = pl.ds(start, block)
        beside[s].wait_recv()
        beyond[s].wait_recv()
        joined_ref[...] = dot_cols(branch_all[whole, :], low_ref[...])

        def activate(where, mine):
            hidden_grad[where, :] = (joined_ref[mine, cut:] * slope_ref[where, :]).astype(BF16)

        row_tiles(start, block, 64, activate)
        serve()
        if position:
            sums.across(steps[position - 1])
        lengths = lengths_ref[part]
        doc_col = documents(lengths, lax.broadcasted_iota(jnp.int32, (block, 1), 0))
        doc_row = documents(lengths, lax.broadcasted_iota(jnp.int32, (1, block), 1))
        for head in range(heads):
            at = head * 3 * HD
            key_ref[...] = jnp.zeros_like(key_ref)
            value_ref[...] = jnp.zeros_like(value_ref)
            for first in range(0, block, 128):
                queries = pl.ds(pl.multiple_of(start + first, 128), 128)
                width = first + 128
                keys = pl.ds(start, width)
                query = mixed_ref[queries, at : at + HD]
                key = mixed_ref[keys, at + HD : at + 2 * HD]
                scores = dot_cols(query, key) * HD ** (-0.5)
                same = doc_col[first : first + 128] == doc_row[:, :width]
                earlier = first + lax.broadcasted_iota(
                    jnp.int32, scores.shape, 0
                ) >= lax.broadcasted_iota(jnp.int32, scores.shape, 1)
                scores = jnp.where(same & earlier, scores, MASKED)
                probs = jnp.exp(scores - facts_ref[queries, head : head + 1])
                attended_grad = joined_ref[
                    first : first + 128, head * HD : (head + 1) * HD
                ].astype(BF16)
                prob_grad = dot_cols(attended_grad, mixed_ref[keys, at + 2 * HD : at + 3 * HD])
                mean = jnp.sum(probs * prob_grad, axis=1, keepdims=True)
                score_grad = (probs * (prob_grad - mean)).astype(BF16)
                mixed_grad[queries, at : at + HD] = turn(
                    dot(score_grad, key) * HD ** (-0.5), tables, pl.ds(first, 128), -1.0
                ).astype(BF16)
                key_ref[:width, :] += dot_rows(score_grad, query)
                value_ref[:width, :] += dot_rows(probs.astype(BF16), attended_grad)
            mixed_grad[whole, at + HD : at + 2 * HD] = turn(
                key_ref[...] * HD ** (-0.5), tables, pl.ds(0, block), -1.0
            ).astype(BF16)
            mixed_grad[whole, at + 2 * HD : at + 3 * HD] = value_ref[...].astype(BF16)
        row = 0
        for ref in (mixed_grad, hidden_grad):
            for n in range(0, ref.shape[1], 128):
                bias_out[row : row + 1, :] += jnp.sum(
                    f32(ref[whole, n : n + 128]), axis=0, keepdims=True
                )
                row += 1
        serve()
        if position > 1:
            sums.along(steps[position - 2])
            sums.recycle(steps[position - 2])
        fetched.wait()
        columns = 256
        target = pl.ds((position % 2) * block, block)

        @pl.loop(0, part_ref.shape[1] // columns)
        def _(n):
            at = pl.ds(pl.multiple_of(n * columns, columns), columns)
            one = dot_cols(mixed_grad[whole, :], qkv_ref[at, :])
            two = dot_cols(hidden_grad[whole, :], up_ref[at, :])
            normed = (f32(tokens_ref[:, at]) - facts_ref[whole, MEAN : MEAN + 1]) * facts_ref[
                whole, SCALE : SCALE + 1
            ]
            part_ref[target, at] = (one * rows_ref[0:1, at] + two * rows_ref[2:3, at]).astype(BF16)
            for row, value in enumerate((one * normed, one, two * normed, two)):
                rows_out[row : row + 1, at] += jnp.sum(value, axis=0, keepdims=True)

        sums.start(step)
        if position + 1 < SPLIT:
            fetched = fetch(position + 1)
        serve()
    sums.across(steps[3])
    sums.along(steps[2])
    sums.along(steps[3])
    own_copy.wait()
    change = input_change(f32(own_tokens[...]), sums.value())
    grad_ref[rows_of(here.t), :] = (quarter[...] + change).astype(BF16)
    gather_quarters(here, grad_ref, rows, *sums.quarter_sems)
    sums.finish()
    for copy in near + [far]:
        copy.wait_send()
    for copies in (outer, across, beside, beyond):
        for copy in copies.values():
            copy.wait_send()


def backward_call(part, tokens, rows, weights, kept, layout, inner, number):
    block, width = part.shape
    quarter = block // QUARTERS
    slope, mixed, facts, joined = kept
    bias_rows = -(-(mixed.shape[1] + slope.shape[1]) // 1024) * 8
    dma = pltpu.SemaphoreType.DMA
    return pl.pallas_call(
        functools.partial(backward_kernel, inner),
        out_shape=[
            jax.ShapeDtypeStruct((block, width), BF16),
            jax.ShapeDtypeStruct((SPLIT * block, width), BF16),
            jax.ShapeDtypeStruct(mixed.shape, BF16),
            jax.ShapeDtypeStruct(slope.shape, BF16),
            jax.ShapeDtypeStruct((8, rows.shape[1]), F32),
            jax.ShapeDtypeStruct((bias_rows, 128), F32),
        ],
        in_specs=[VMEM_SPEC, ANY_SPEC] + [VMEM_SPEC] * (7 + len(layout)),
        out_specs=[VMEM_SPEC] * 6,
        scratch_shapes=[
            pltpu.VMEM((2, quarter, width), BF16),
            pltpu.VMEM((quarter, width), BF16),
            pltpu.VMEM((quarter, width), BF16),
            pltpu.VMEM((quarter, width), BF16),
            pltpu.VMEM((quarter, width), F32),
            pltpu.VMEM((block, width), BF16),
            pltpu.VMEM((quarter, width), BF16),
            pltpu.VMEM((block, joined.shape[1]), F32),
            pltpu.VMEM((block, HD), F32),
            pltpu.VMEM((block, HD), F32),
            pltpu.VMEM((2 * block, width), BF16),
            dma((2,)),
            dma((2,)),
            dma,
            dma,
            dma((4, SPLIT)),
            dma((4, SPLIT)),
            dma((3,)),
        ]
        + reduce_scratch(quarter, width),
        compiler_params=pltpu.CompilerParams(
            collective_id=number, has_side_effects=True, vmem_limit_bytes=60 * 1024 * 1024
        ),
    )(part, tokens, rows, *weights, slope, mixed, facts, *layout)


class AllSum:
    def __init__(self, here, mine, near_in, far_in, outer, inner, send, recv):
        self.here, self.mine, self.near_in, self.far_in = here, mine, near_in, far_in
        self.outer, self.inner, self.send, self.recv = outer, inner, send, recv
        self.copies = []

    def pair(self, stage, target, peer):
        copy = remote(
            self.mine.at[stage], target, self.send.at[stage], self.recv.at[stage], peer
        )
        self.copies.append(copy)
        return copy

    def near(self, value):
        self.mine[0] = value
        self.waiting = [self.pair(0, self.near_in, self.here.near_peer())]

    def far(self):
        self.waiting[0].wait_recv()
        self.mine[1] = self.mine[0] + self.near_in[...]
        self.waiting = [self.pair(1, self.far_in, self.here.far_peer())]

    def group(self, buffer, index, first, peers):
        self.waiting = []
        for number, peer in enumerate(peers):
            copy = remote(
                buffer.at[index],
                buffer.at[index],
                self.send.at[first + number],
                self.recv.at[first + number],
                peer,
            )
            self.waiting.append(copy)
            self.copies.append(copy)

    def along_outer(self):
        self.waiting[0].wait_recv()
        here = self.here
        self.outer[here.o] = self.mine[1] + self.far_in[...]
        self.group(self.outer, here.o, 2, [here.outer_peer(s) for s in range(1, SPLIT)])

    def along_inner(self):
        here = self.here
        for copy in self.waiting:
            copy.wait_recv()
        value = self.outer[0]
        for part in range(1, SPLIT):
            value = value + self.outer[part]
        self.inner[here.i] = value
        peers = [here.inner_peer(r) for r in range(1, here.inner)]
        self.group(self.inner, here.i, 1 + SPLIT, peers)

    def value(self):
        for copy in self.waiting:
            copy.wait_recv()
        value = self.inner[0]
        for part in range(1, self.here.inner):
            value = value + self.inner[part]
        for copy in self.copies:
            copy.wait_send()
        return value


def all_sum_scratch(shape, inner):
    dma = pltpu.SemaphoreType.DMA
    return [
        pltpu.VMEM((2, *shape), F32),
        pltpu.VMEM(shape, F32),
        pltpu.VMEM(shape, F32),
        pltpu.VMEM((SPLIT, *shape), F32),
        pltpu.VMEM((inner, *shape), F32),
        dma((SPLIT + inner,)),
        dma((SPLIT + inner,)),
    ]


def whole_sum(value):
    return jnp.sum(jnp.sum(value, axis=1, keepdims=True), axis=0, keepdims=True)


def finish_kernel(
    inner, tokens_ref, branch_ref, gains_ref, joined_ref, mixed_ref, hidden_ref, facts_ref,
    rows_ref, bias_ref, qkv_out, up_out, out_out, down_out, rows_out, bias_out, norm_ref, *scratch,
):
    here = Place(inner)
    sends, inputs, totals = scratch[:3], scratch[3:6], scratch[6:9]
    turned, send_i, recv_i, send_o, recv_o, local, held = scratch[9:16]
    small = AllSum(here, *scratch[16:23])
    squares = AllSum(here, *scratch[23:30])
    bias_in, bias_send, bias_recv = scratch[30:33]
    outs = (qkv_out, up_out, out_out, down_out)
    shard = qkv_out.shape[0]
    width_out = out_out.shape[0] // SPLIT

    def columns_of(ref, index):
        if ref.ndim == 3:
            return ref[index]
        return ref[:, pl.ds(pl.multiple_of(index * shard, shard), shard)]

    def gradient(kind, index):
        if kind == 2:
            return dot(turned[...], columns_of(branch_ref, index))
        if tokens_ref.ndim == 3:
            copy = pltpu.make_async_copy(tokens_ref.at[index], held, local.at[4])
            copy.start()
            copy.wait()
            values = f32(held[...])
        else:
            values = f32(columns_of(tokens_ref, index))
        normed = (values - facts_ref[:, MEAN : MEAN + 1]) * facts_ref[:, SCALE : SCALE + 1]
        rows = columns_of(gains_ref, index)
        at = 2 * kind
        layer_in = (normed * rows[at : at + 1, :] + rows[at + 1 : at + 2, :]).astype(BF16)
        return dot_rows(layer_in, (mixed_ref, hidden_ref)[kind][...])

    def dst(m):
        if m < 2:
            width = outs[m].shape[1] // SPLIT
            return outs[m].at[:, pl.ds(here.o * width, width)]
        width = outs[m].shape[0] // SPLIT
        return outs[m].at[pl.ds(here.o * width, width), :]

    greet(reduce_peers(here) + [here.inner_peer(r) for r in range(1, inner)])
    first, last, own = {}, [], []
    order = [(kind, s) for kind in (2, 1, 0) for s in (2, 1, 3, 0)]
    turned[...] = jnp.transpose(joined_ref[...])

    def trade(number):
        if number >= len(order):
            return
        kind, s = order[number]
        part = (here.o + s) % SPLIT
        for r in range(1, inner):
            sends[kind][s, r - 1] = gradient(kind, part * inner + (here.i + r) % inner).astype(BF16)
            first[kind, s, r] = remote(
                sends[kind].at[s, r - 1],
                inputs[kind].at[s, r - 1],
                send_i.at[kind, s, r - 1],
                recv_i.at[kind, s, r - 1],
                here.inner_peer(r),
            )

    def settle(number):
        kind, s = order[number]
        part = (here.o + s) % SPLIT
        total = gradient(kind, part * inner + here.i)
        for r in range(1, inner):
            first[kind, s, r].wait_recv()
            total = total + f32(inputs[kind][s, r - 1])
        totals[kind][s] = total.astype(BF16)
        source = totals[kind].at[s]
        pieces = [(kind, source)]
        if kind == 2:
            pieces = [
                (2, source.at[pl.ds(0, width_out), :]),
                (3, source.at[pl.ds(width_out, total.shape[0] - width_out), :]),
            ]
        for m, piece in pieces:
            if s:
                last.append(
                    remote(
                        piece, dst(m), send_o.at[m, s - 1], recv_o.at[m, s - 1], here.outer_peer(s)
                    )
                )
            else:
                copy = pltpu.make_async_copy(piece, dst(m), local.at[m])
                copy.start()
                own.append(copy)
        trade(number + AHEAD)
        return whole_sum(total * total)

    for number in range(AHEAD):
        trade(number)
    small.near(rows_ref[...])
    bias_in[here.i] = bias_ref[...]
    bias_inner = [
        remote(
            bias_in.at[here.i],
            bias_in.at[here.i],
            bias_send.at[SPLIT + r],
            bias_recv.at[SPLIT + r],
            here.inner_peer(r),
        )
        for r in range(1, inner)
    ]
    square = settle(0)
    square = square + settle(1)
    small.far()
    for number in range(2, 5):
        square = square + settle(number)
    small.along_outer()
    for copy in bias_inner:
        copy.wait_recv()
    bias = bias_in[0]
    for part in range(1, inner):
        bias = bias + bias_in[part]
    bias_out[here.o] = bias
    bias_outer = [
        remote(
            bias_out.at[here.o],
            bias_out.at[here.o],
            bias_send.at[s],
            bias_recv.at[s],
            here.outer_peer(s),
        )
        for s in range(1, SPLIT)
    ]
    square = square + whole_sum(bias * bias) / inner
    square = square + settle(5)
    square = square + settle(6)
    small.along_inner()
    square = square + settle(7)
    square = square + settle(8)
    rows_out[...] = small.value()
    for number in range(9, len(order)):
        square = square + settle(number)
    squares.near(jnp.broadcast_to(square, norm_ref.shape))
    squares.far()
    squares.along_outer()
    squares.along_inner()
    norm = squares.value()
    rows = rows_out[...]
    doubled = lax.broadcasted_iota(jnp.int32, rows.shape, 0) == 4
    norm_ref[...] = norm + whole_sum(rows * rows * jnp.where(doubled, 2.0, 1.0))
    for copy in bias_outer:
        copy.wait_recv()
    for copy in bias_inner + bias_outer:
        copy.wait_send()
    for copy in last:
        copy.wait()
    for copy in own:
        copy.wait()
    for copy in first.values():
        copy.wait_send()


def finish_call(tokens, branch, rows, kept, grads, sums, bias, shards, inner, number):
    dma = pltpu.SemaphoreType.DMA
    qkv, out, up, down = shards
    ordered = (qkv, up, out, down)
    facts, joined = kept
    shard = out[1]
    wide = [tokens, branch, rows]
    if not aligned(shard):
        wide = [jnp.swapaxes(w.reshape(w.shape[0], -1, shard), 0, 1) for w in wide]
    pieces = [
        (shard, grads[0].shape[1]),
        (shard, grads[1].shape[1]),
        (joined.shape[1], shard),
    ]
    peers = max(inner - 1, 1)
    tile = (8, 128)
    return pl.pallas_call(
        functools.partial(finish_kernel, inner),
        out_shape=[
            *(jax.ShapeDtypeStruct(shape, BF16) for shape in ordered),
            jax.ShapeDtypeStruct(sums.shape, F32),
            jax.ShapeDtypeStruct((SPLIT, *bias.shape), F32),
            jax.ShapeDtypeStruct(tile, F32),
        ],
        in_specs=[VMEM_SPEC if aligned(shard) else ANY_SPEC] + [VMEM_SPEC] * 8,
        out_specs=[ANY_SPEC] * 4 + [VMEM_SPEC] * 3,
        scratch_shapes=[pltpu.VMEM((SPLIT, peers, *piece), BF16) for piece in pieces]
        + [pltpu.VMEM((SPLIT, peers, *piece), BF16) for piece in pieces]
        + [pltpu.VMEM((SPLIT, *piece), BF16) for piece in pieces]
        + [
            pltpu.VMEM(joined.shape[::-1], BF16),
            dma((3, SPLIT, peers)),
            dma((3, SPLIT, peers)),
            dma((4, SPLIT - 1)),
            dma((4, SPLIT - 1)),
            dma((5,)),
            pltpu.VMEM((16, 128) if aligned(shard) else (tokens.shape[0], shard), BF16),
        ]
        + all_sum_scratch(sums.shape, inner)
        + all_sum_scratch(tile, inner)
        + [
            pltpu.VMEM((inner, *bias.shape), F32),
            dma((SPLIT + inner,)),
            dma((SPLIT + inner,)),
        ],
        compiler_params=pltpu.CompilerParams(
            collective_id=number, has_side_effects=True, vmem_limit_bytes=60 * 1024 * 1024
        ),
    )(*wide, joined, *grads, facts, sums, bias)


def reward_kernel(
    inner, stats_ref, facts_ref, out_ref, stats, outer_in, inner_in,
    send, recv, send_o, recv_o, send_i, recv_i,
):
    here = Place(inner)
    tensor_peers = [(here.dp, (here.t + s) % QUARTERS) for s in range(1, QUARTERS)]
    outer_peers = [here.outer_peer(s) for s in range(1, SPLIT)]
    inner_peers = [here.inner_peer(r) for r in range(1, inner)]
    greet(tensor_peers + outer_peers + inner_peers)

    def share(buffer, index, sends, recvs, peers):
        return [
            remote(buffer.at[index], buffer.at[index], sends.at[n], recvs.at[n], peer)
            for n, peer in enumerate(peers)
        ]

    stats[here.t] = stats_ref[...]
    copies = share(stats, here.t, send, recv, tensor_peers)
    for copy in copies:
        copy.wait_recv()
    quarters = [stats[q] for q in range(QUARTERS)]
    highest = functools.reduce(jnp.maximum, quarters)
    summed = functools.reduce(lambda a, b: a + b, [jnp.exp(q - highest) for q in quarters])
    totals = highest + jnp.log(summed)
    picks = functools.reduce(lambda a, b: a + b, quarters)
    log_probs = picks - totals_to_picks(totals)
    doc = lax.broadcasted_iota(jnp.int32, (8, 1), 0)
    start = end = labels = jnp.zeros((8, 1), jnp.int32)
    for segment in range(SEGS):
        length = facts_ref[0:1, segment : segment + 1]
        start = start + jnp.where(doc > segment, length, 0)
        end = end + jnp.where(doc >= segment, length, 0)
        labels = labels + jnp.where(doc == segment, facts_ref[1:2, segment : segment + 1], 0)
    token = lax.broadcasted_iota(jnp.int32, (8, stats_ref.shape[1]), 1)
    member = jnp.where((token >= start) & (token < end), 1.0, 0.0)
    policy_docs = jnp.sum(member * log_probs[1:2, :], axis=1, keepdims=True)
    frozen_docs = jnp.sum(member * log_probs[3:4, :], axis=1, keepdims=True)
    reward = policy_docs - frozen_docs
    outer_in[here.o] = jnp.broadcast_to(whole_sum(reward), outer_in.shape[1:])
    more = share(outer_in, here.o, send_o, recv_o, outer_peers)
    for copy in more:
        copy.wait_recv()
    inner_in[here.i] = functools.reduce(lambda a, b: a + b, [outer_in[n] for n in range(SPLIT)])
    rest = share(inner_in, here.i, send_i, recv_i, inner_peers)
    for copy in rest:
        copy.wait_recv()
    total = functools.reduce(lambda a, b: a + b, [inner_in[n] for n in range(inner)])
    seq_count = inner * SPLIT * SEGS
    shift = total[:, 0:1] / seq_count
    sigmoid_value = 1.0 / (1.0 + jnp.exp(-BETA_KTO * (reward - shift)))
    labels = f32(labels)
    doc_grad = BETA_KTO * sigmoid_value * (1.0 - sigmoid_value) * (1.0 - 2.0 * labels) / seq_count
    token_grad = jnp.sum(member * doc_grad, axis=0, keepdims=True)
    out_ref[...] = jnp.transpose(
        jnp.concatenate([token_grad, totals[0:1, :], jnp.zeros((6, totals.shape[1]), F32)], axis=0)
    )
    for copy in copies + more + rest:
        copy.wait_send()


def totals_to_picks(totals):
    return jnp.concatenate([totals[0:1], totals[0:1], totals[2:3], totals[2:3], totals[4:]], axis=0)


def reward_call(stats, facts, inner, number):
    dma = pltpu.SemaphoreType.DMA
    tile = (8, 128)
    peers = max(inner - 1, 1)
    return pl.pallas_call(
        functools.partial(reward_kernel, inner),
        out_shape=jax.ShapeDtypeStruct((stats.shape[1], 8), F32),
        in_specs=[VMEM_SPEC] * 2,
        out_specs=VMEM_SPEC,
        scratch_shapes=[
            pltpu.VMEM((QUARTERS, *stats.shape), F32),
            pltpu.VMEM((SPLIT, *tile), F32),
            pltpu.VMEM((inner, *tile), F32),
            dma((QUARTERS - 1,)),
            dma((QUARTERS - 1,)),
            dma((SPLIT - 1,)),
            dma((SPLIT - 1,)),
            dma((peers,)),
            dma((peers,)),
        ],
        compiler_params=pltpu.CompilerParams(collective_id=number, has_side_effects=True),
    )(stats, facts)


def turn_tables(count):
    half = ROT // 2
    frequency = np.float32(10000.0) ** (np.float32(-2.0) * np.arange(half, dtype=np.float32) / ROT)
    angles = np.arange(count, dtype=np.float32)[:, None] * frequency.astype(np.float32)
    cosine, sine = np.cos(angles), np.sin(angles)
    none = np.zeros((count, HD - ROT), np.float32)
    return (
        jnp.asarray(np.concatenate([cosine, cosine, none + 1.0], axis=1), F32),
        jnp.asarray(np.concatenate([-sine, sine, none], axis=1), F32),
    )


def chunk_of(width):
    return next(n for n in (1280, 640, 512, 256, 128) if width % n == 0)


def head_kernel(policy_ref, frozen_ref, head_ref, target_ref, logits_ref, stats_ref, other_ref, high_ref, sum_ref, pick_ref):
    chunk = pl.program_id(0)
    rows, columns = logits_ref.shape

    @pl.when(chunk == 0)
    def _():
        high_ref[...] = jnp.full_like(high_ref, MASKED)
        sum_ref[...] = jnp.zeros_like(sum_ref)
        pick_ref[...] = jnp.zeros_like(pick_ref)

    def fold(which, values_ref, begin, width):
        for first in range(0, rows, 64):
            own = pl.ds(first, 64)
            high = high_ref[which, own, :]
            lanes = [values_ref[own, n : n + 128] for n in range(begin, begin + width, 128)]
            highest = functools.reduce(jnp.maximum, lanes, high)
            total = sum_ref[which, own, :] * jnp.exp(high - highest)
            picked = pick_ref[which, own, :]
            target = target_ref[own, :] - (chunk * columns + begin)
            lane = lax.broadcasted_iota(jnp.int32, highest.shape, 1)
            for n, value in enumerate(lanes):
                total = total + jnp.exp(value - highest)
                picked = picked + jnp.where(lane + n * 128 == target, value, 0.0)
            high_ref[which, own, :] = highest
            sum_ref[which, own, :] = total
            pick_ref[which, own, :] = picked

    width = 256 if columns % 256 == 0 else 128
    last = None
    for begin in range(0, columns, width):
        for which, (low_ref, values_ref) in enumerate(
            ((policy_ref, logits_ref), (frozen_ref, other_ref))
        ):
            values_ref[:, begin : begin + width] = dot(
                low_ref[...], head_ref[:, begin : begin + width]
            )
            if last:
                fold(*last)
            last = (which, values_ref, begin, width)
    fold(*last)

    @pl.when(chunk == pl.num_programs(0) - 1)
    def _():
        found = []
        for which in range(2):
            high = jnp.max(high_ref[which], axis=1, keepdims=True)
            total = jnp.sum(
                sum_ref[which] * jnp.exp(high_ref[which] - high), axis=1, keepdims=True
            )
            found.append(high + jnp.log(total))
            found.append(jnp.sum(pick_ref[which], axis=1, keepdims=True))
        lane = lax.broadcasted_iota(jnp.int32, (rows, 128), 1)
        joined = jnp.zeros((rows, 128), F32)
        for n, value in enumerate(found):
            joined = jnp.where(lane == n, value, joined)
        stats_ref[...] = jnp.transpose(joined)[:8, :]


def head_call(policy_low, frozen_low, head_weight, targets):
    rows, depth = policy_low.shape
    width = head_weight.shape[1]
    columns = chunk_of(width)
    return pl.pallas_call(
        head_kernel,
        grid=(width // columns,),
        out_shape=[
            jax.ShapeDtypeStruct((rows, width), F32),
            jax.ShapeDtypeStruct((8, rows), F32),
        ],
        in_specs=[
            pl.BlockSpec((rows, depth), lambda n: (0, 0)),
            pl.BlockSpec((rows, depth), lambda n: (0, 0)),
            pl.BlockSpec((depth, columns), lambda n: (0, n)),
            pl.BlockSpec((rows, 1), lambda n: (0, 0)),
        ],
        out_specs=[
            pl.BlockSpec((rows, columns), lambda n: (0, n)),
            pl.BlockSpec((8, rows), lambda n: (0, 0)),
        ],
        scratch_shapes=[
            pltpu.VMEM((rows, columns), F32),
            pltpu.VMEM((2, rows, 128), F32),
            pltpu.VMEM((2, rows, 128), F32),
            pltpu.VMEM((2, rows, 128), F32),
        ],
        cost_estimate=pl.CostEstimate(
            flops=4 * rows * depth * width,
            bytes_accessed=2 * depth * width + 4 * rows * width,
            transcendentals=2 * rows * width,
        ),
        compiler_params=pltpu.CompilerParams(vmem_limit_bytes=56 * 1024 * 1024),
    )(policy_low, frozen_low, head_weight, targets)


def logit_grad_kernel(logits_ref, head_ref, target_ref, token_ref, part_ref, low_ref, sum_ref):
    chunk = pl.program_id(0)
    rows, columns = logits_ref.shape

    for first in range(0, rows, 32):
        own = pl.ds(first, 32)
        values = logits_ref[own, :]
        target = target_ref[own, :] - chunk * columns
        chosen = lax.broadcasted_iota(jnp.int32, values.shape, 1) == target
        probs = jnp.exp(values - token_ref[own, 1:2])
        low_ref[own, :] = (token_ref[own, 0:1] * (jnp.where(chosen, 1.0, 0.0) - probs)).astype(BF16)
    value = dot_cols(low_ref[...], head_ref[...])

    @pl.when(chunk == 0)
    def _():
        sum_ref[...] = value

    @pl.when(chunk > 0)
    def _():
        sum_ref[...] += value

    @pl.when(chunk == pl.num_programs(0) - 1)
    def _():
        part_ref[...] = sum_ref[...].astype(BF16)


def logit_grad_call(logits, head_weight, targets, tokens):
    rows, width = logits.shape
    depth = head_weight.shape[0]
    columns = chunk_of(width)
    return pl.pallas_call(
        logit_grad_kernel,
        grid=(width // columns,),
        out_shape=jax.ShapeDtypeStruct((rows, depth), BF16),
        in_specs=[
            pl.BlockSpec((rows, columns), lambda n: (0, n)),
            pl.BlockSpec((depth, columns), lambda n: (0, n)),
            pl.BlockSpec((rows, 1), lambda n: (0, 0)),
            pl.BlockSpec((rows, tokens.shape[1]), lambda n: (0, 0)),
        ],
        out_specs=pl.BlockSpec((rows, depth), lambda n: (0, 0)),
        scratch_shapes=[pltpu.VMEM((rows, columns), BF16), pltpu.VMEM((rows, depth), F32)],
        cost_estimate=pl.CostEstimate(
            flops=2 * rows * depth * width,
            bytes_accessed=2 * depth * width + 4 * rows * width,
            transcendentals=rows * width,
        ),
        compiler_params=pltpu.CompilerParams(vmem_limit_bytes=56 * 1024 * 1024),
    )(logits, head_weight, targets, tokens)


def adam_step(master, mean_old, square_old, gradient, factor, rate, decay_rate):
    clipped = f32(gradient) * factor
    mean_new = BETA_FIRST * mean_old + (1.0 - BETA_FIRST) * clipped
    square_new = BETA_SECOND * square_old + (1.0 - BETA_SECOND) * clipped * clipped
    mean_hat = mean_new / (1.0 - BETA_FIRST**STEP)
    square_hat = square_new / (1.0 - BETA_SECOND**STEP)
    master_new = master - rate * (
        mean_hat / (jnp.sqrt(square_hat) + ADAM_EPS) + decay_rate * master
    )
    return (mean_new, square_new, master_new)


def on_device(
    inputs,
    targets,
    doc_lengths,
    desirable,
    head_weight,
    qkv_master,
    out_master,
    up_master,
    down_master,
    vectors,
    hidden_bias,
    qkv_mean,
    out_mean,
    up_mean,
    down_mean,
    vectors_mean,
    hidden_mean,
    qkv_square,
    out_square,
    up_square,
    down_square,
    vectors_square,
    hidden_square,
    qkv_frozen,
    out_frozen,
    up_frozen,
    down_frozen,
    vectors_frozen,
    hidden_frozen,
):
    dp_size = lax.axis_size("dp")
    tensor_size = lax.axis_size("tensor")
    inner = dp_size // SPLIT
    outer_index = lax.axis_index("dp") // inner
    block = inputs.shape[0]
    small = jnp.concatenate([doc_lengths, desirable], axis=0).astype(jnp.int32)
    lengths_tile = jnp.pad(small, ((0, 8 - small.shape[0]), (0, 128 - SEGS)))
    masters = tuple(w.astype(BF16) for w in (qkv_master, out_master, up_master, down_master))
    *policy_set, tokens_all, lengths_all = spread_weights(masters, inner, inputs, lengths_tile, 0)
    frozen_shards = (qkv_frozen, out_frozen, up_frozen, down_frozen)
    cut = qkv_master.shape[1]
    width_qkv, width_up = cut // SPLIT, up_master.shape[1] // SPLIT

    layout = (lengths_all, *turn_tables(block))
    policy = (vectors, hidden_bias[None])
    frozen = (vectors_frozen, hidden_frozen[None])
    if aligned(out_master.shape[1]):
        final_low, frozen_low, *kept = forward_call(
            tokens_all, layout, (policy, frozen), policy_set, block, inner, None, frozen_shards, 2
        )
        kept_values = tuple(kept[:4])
    else:
        final_low, *kept = forward_call(
            tokens_all, layout, (policy,), policy_set, block, inner, None, frozen_shards, 2
        )
        kept_values = tuple(kept[:4])
        frozen_set = (*kept[4:6], joined_columns(kept[6]))
        (frozen_low,) = forward_call(
            tokens_all, layout, (frozen,), frozen_set, block, inner, kept_values[2], None, 3
        )
    vocab_start = lax.axis_index("tensor") * head_weight.shape[1]
    own_targets = (targets - vocab_start)[:, None]
    logits, stats = head_call(final_low, frozen_low, head_weight, own_targets)
    token_rows = reward_call(stats, lengths_tile, inner, 6)
    final_part = logit_grad_call(logits, head_weight, own_targets, token_rows)
    input_grad, branch_low, mixed_grad, hidden_low, vector_part, bias_tile = backward_call(
        final_part, tokens_all, vectors, policy_set, kept_values, layout, inner, 4
    )
    shards = tuple(w.shape for w in masters)
    bias_rows = (width_qkv + width_up) // 128
    input_grad = f32(input_grad)
    qkv_grad, up_grad, out_grad, down_grad, vector_sum, bias_sum, square = finish_call(
        tokens_all, branch_low, vectors, kept_values[2:], (mixed_grad, hidden_low),
        vector_part, bias_tile, shards, inner, 5,
    )
    vector_grad = jnp.concatenate([vector_sum[:5], vector_sum[4:5]], axis=0)
    bias_sum = bias_sum[:, :bias_rows].reshape(SPLIT, bias_rows * 128)
    hidden_grad = jnp.concatenate(
        [bias_sum[:, :width_qkv].reshape(-1), bias_sum[:, width_qkv:].reshape(-1)]
    )
    grad_norm = jnp.sqrt(square[0, 0])
    factor = jnp.minimum(1.0, CLIP_NORM / (grad_norm + 1e-06))
    qkv_state = adam_step(
        qkv_master, qkv_mean, qkv_square, qkv_grad, factor, LEARN_RATE, WEIGHT_DECAY
    )
    out_state = adam_step(
        out_master, out_mean, out_square, out_grad, factor, LEARN_RATE, WEIGHT_DECAY
    )
    up_state = adam_step(up_master, up_mean, up_square, up_grad, factor, LEARN_RATE, WEIGHT_DECAY)
    down_state = adam_step(
        down_master, down_mean, down_square, down_grad, factor, LEARN_RATE, WEIGHT_DECAY
    )
    vector_state = adam_step(
        vectors, vectors_mean, vectors_square, vector_grad, factor, VECTOR_RATE, 0.0
    )
    hidden_state = adam_step(
        hidden_bias, hidden_mean, hidden_square, hidden_grad, factor, VECTOR_RATE, 0.0
    )
    return (
        final_low,
        input_grad,
        grad_norm,
        *qkv_state,
        *out_state,
        *up_state,
        *down_state,
        *vector_state,
        *hidden_state,
    )


def solution(mesh):
    rows, cols = P("dp", "tensor"), P("tensor", "dp")
    matrices = (rows, cols, rows, cols)
    placed = (
        P("dp", None),
        P("dp"),
        P("dp", None),
        P("dp", None),
        P(None, "tensor"),
        *matrices,
        P(),
        P("tensor"),
        *matrices,
        P(),
        P("tensor"),
        *matrices,
        P(),
        P("tensor"),
        *matrices,
        P(),
        P("tensor"),
    )
    return jax.shard_map(
        on_device,
        mesh=mesh,
        in_specs=placed,
        out_specs=(
            P("dp", None),
            P("dp", None),
            P(),
            *(spec for spec in matrices for _ in range(3)),
            P(),
            P(),
            P(),
            P("tensor"),
            P("tensor"),
            P("tensor"),
        ),
        check_vma=False,
    )
```

```python
import functools

import jax
import jax.numpy as jnp
import numpy as np
from jax import lax
from jax.experimental import pallas as pl
from jax.experimental.pallas import tpu as pltpu
from jax.sharding import PartitionSpec as P

HD = 128
ROT = 32
SEGS = 4
STEP = 3
SPLIT = 4
QUARTERS = 4
MEAN, SCALE, FACTS = 6, 7, 8
AHEAD = 3


EPS_NORM = 1e-05
BETA_KTO = 0.1
CLIP_NORM = 0.01
LEARN_RATE = 0.02
VECTOR_RATE = 0.2
BETA_FIRST = 0.9
BETA_SECOND = 0.999
ADAM_EPS = 1e-08
WEIGHT_DECAY = 0.01
MASKED = -1e30

MESH = pl.DeviceIdType.MESH
BF16 = jnp.bfloat16
F32 = jnp.float32
ANY_SPEC = pl.BlockSpec(memory_space=pltpu.HBM)
VMEM_SPEC = pl.BlockSpec(memory_space=pltpu.VMEM)


class Place:
    def __init__(self, inner):
        self.inner = inner
        self.dp = lax.axis_index("dp")
        self.t = lax.axis_index("tensor")
        self.o = self.dp // inner
        self.i = self.dp % inner
        self.near = self.t + 1 - 2 * (self.t % 2)
        self.far = (self.t + 2) % QUARTERS

    def outer_peer(self, shift):
        return (((self.o + shift) % SPLIT) * self.inner + self.i, self.t)

    def inner_peer(self, shift):
        return (self.o * self.inner + (self.i + shift) % self.inner, self.t)

    def tensor_peers(self):
        return [(self.dp, (self.t + s) % QUARTERS) for s in range(1, QUARTERS)]

    def dp_peers(self):
        count = SPLIT * self.inner
        return [((self.dp + s) % count, self.t) for s in range(1, count)]

    def near_peer(self):
        return (self.dp, self.near)

    def far_peer(self):
        return (self.dp, self.far)


def aligned(shard):
    return shard % 128 == 0


def greet(peers):
    barrier = pltpu.get_barrier_semaphore()
    for peer in peers:
        pl.semaphore_signal(barrier, inc=1, device_id=peer, device_id_type=MESH)
    pl.semaphore_wait(barrier, len(peers))


def remote(src, dst, send_sem, recv_sem, peer):
    copy = pltpu.make_async_remote_copy(
        src_ref=src,
        dst_ref=dst,
        send_sem=send_sem,
        recv_sem=recv_sem,
        device_id=peer,
        device_id_type=MESH,
    )
    copy.start()
    return copy


class Spread:
    def __init__(self, here, shards, wholes, send_o, recv_o, send_i, recv_i, local, *held):
        self.here = here
        self.qkv, self.out, self.up, self.down = shards
        self.qkv_all, self.up_all, self.low_all = wholes
        self.send_o, self.recv_o, self.send_i, self.recv_i = send_o, recv_o, send_i, recv_i
        self.local, self.held = local, held
        self.first, self.own, self.passed = {}, [], []
        self.order = [(m, s) for m in range(4) for s in (2, 1, 3)]

    def src(self, m, part):
        shard = (self.qkv, self.up, self.out, self.down)[m]
        width = shard.shape[1 if m < 2 else 0] // SPLIT
        where = pl.ds(part * width, width)
        return shard.at[:, where] if m < 2 else shard.at[where, :]

    def dst(self, m, index):
        shard = self.qkv.shape[0]
        where = pl.ds(index * shard, shard)
        if m < 2:
            return (self.qkv_all, self.up_all)[m].at[where, :]
        width_out, width_down = self.out.shape[0] // SPLIT, self.down.shape[0] // SPLIT
        rows = pl.ds(0, width_out) if m == 2 else pl.ds(width_out, width_down)
        low_all = self.low_all
        return low_all.at[rows, where] if aligned(shard) else low_all.at[index, rows, :]

    def peers(self):
        here = self.here
        peers = [here.outer_peer(s) for s in range(1, SPLIT)]
        return peers + [here.inner_peer(r) for r in range(1, here.inner)]

    def send_on(self, number):
        if number >= len(self.order):
            return
        m, s = self.order[number]
        self.first[m, s] = remote(
            self.src(m, (self.here.o + s) % SPLIT),
            self.dst(m, self.here.dp),
            self.send_o.at[m, s - 1],
            self.recv_o.at[m, s - 1],
            self.here.outer_peer(s),
        )

    def pass_on(self, m, s, source, index):
        here = self.here
        for r in range(1, here.inner):
            self.passed.append(
                remote(
                    source,
                    self.dst(m, index),
                    self.send_i.at[m, s, r - 1],
                    self.recv_i.at[m, s, r - 1],
                    here.inner_peer(r),
                )
            )

    def start_own(self):
        here = self.here
        loads = [
            pltpu.make_async_copy(self.src(m, here.o), self.held[m], self.local.at[m])
            for m in range(4)
        ]
        for load in loads:
            load.start()
        for m, load in enumerate(loads):
            load.wait()
            self.pass_on(m, 0, self.held[m], here.dp)
            copy = pltpu.make_async_copy(self.held[m], self.dst(m, here.dp), self.local.at[4 + m])
            copy.start()
            self.own.append(copy)

    def step(self, number):
        here = self.here
        m, s = self.order[number]
        self.first[m, s].wait_recv()
        self.send_on(number + AHEAD)
        index = ((here.o + SPLIT - s) % SPLIT) * here.inner + here.i
        self.pass_on(m, s, self.dst(m, index), index)

    def finish(self):
        for copy in self.first.values():
            copy.wait_send()
        for copy in self.own:
            copy.wait()
        for copy in self.passed:
            copy.wait()


def spread_weights_kernel(
    inner, qkv, out, up, down, tokens, lengths, qkv_all, up_all, low_all, tokens_all, lengths_all,
    send_o, recv_o, send_i, recv_i, local, held_0, held_1, held_2, held_3,
    send_t, recv_t, send_l, recv_l,
):
    here = Place(inner)
    spread = Spread(
        here, (qkv, out, up, down), (qkv_all, up_all, low_all),
        send_o, recv_o, send_i, recv_i, local, held_0, held_1, held_2, held_3,
    )
    greet(spread.peers() + [here.far_peer(), here.near_peer()])
    rows, block = tokens.shape[0] // QUARTERS, tokens.shape[0]

    def piece(part, quarter):
        return tokens_all.at[pl.ds((part * QUARTERS + quarter) * rows, rows), :]

    waits, token_copies, across, own = [], {}, {}, []
    for s in (2, 1, 3):
        token_copies[s] = remote(
            tokens.at[pl.ds(here.t * rows, rows), :],
            piece(here.o, here.t),
            send_t.at[0, s - 1],
            recv_t.at[0, s - 1],
            here.outer_peer(s),
        )
        waits.append(
            remote(
                lengths,
                lengths_all.at[here.o],
                send_l.at[s - 1],
                recv_l.at[s - 1],
                here.outer_peer(s),
            )
        )
    own.append(
        pltpu.make_async_copy(
            tokens, tokens_all.at[pl.ds(here.o * block, block), :], local.at[8]
        )
    )
    own.append(pltpu.make_async_copy(lengths, lengths_all.at[here.o], local.at[9]))
    for copy in own:
        copy.start()
    spread.start_own()
    for number, s in enumerate((2, 1, 3)):
        token_copies[s].wait_recv()
        spread.send_on(number)
        part = (here.o + SPLIT - s) % SPLIT
        for stage, peer in ((1, here.far_peer()), (2, here.near_peer())):
            copy = remote(
                piece(part, here.t),
                piece(part, here.t),
                send_t.at[stage, s - 1],
                recv_t.at[stage, s - 1],
                peer,
            )
            if stage == 1:
                across[s] = copy
            else:
                waits.append(copy)
    for number in range(len(spread.order)):
        spread.step(number)
    for s in (2, 1, 3):
        across[s].wait_recv()
        part = (here.o + SPLIT - s) % SPLIT
        waits.append(
            remote(
                piece(part, here.far),
                piece(part, here.far),
                send_t.at[3, s - 1],
                recv_t.at[3, s - 1],
                here.near_peer(),
            )
        )
    for copy in list(token_copies.values()) + list(across.values()):
        copy.wait_send()
    for copy in own:
        copy.wait()
    spread.finish()
    for copy in waits:
        copy.wait()


def whole_shapes(shards, inner):
    qkv, out, up, down = shards
    d_model = out.shape[1] * SPLIT * inner
    width = out.shape[0] // SPLIT + down.shape[0] // SPLIT
    return [
        jax.ShapeDtypeStruct((d_model, qkv.shape[1] // SPLIT), BF16),
        jax.ShapeDtypeStruct((d_model, up.shape[1] // SPLIT), BF16),
        jax.ShapeDtypeStruct(
            (width, d_model) if aligned(out.shape[1]) else (SPLIT * inner, width, out.shape[1]),
            BF16,
        ),
    ]


def joined_columns(low_all):
    if low_all.ndim == 3:
        low_all = jnp.swapaxes(low_all, 0, 1).reshape(low_all.shape[1], -1)
    return low_all


def spread_scratch(shards, inner):
    dma = pltpu.SemaphoreType.DMA
    qkv, out, up, down = shards
    pieces = [
        (qkv.shape[0], qkv.shape[1] // SPLIT),
        (up.shape[0], up.shape[1] // SPLIT),
        (out.shape[0] // SPLIT, out.shape[1]),
        (down.shape[0] // SPLIT, down.shape[1]),
    ]
    return [
        dma((4, SPLIT - 1)),
        dma((4, SPLIT - 1)),
        dma((4, SPLIT, max(inner - 1, 1))),
        dma((4, SPLIT, max(inner - 1, 1))),
        dma((10,)),
        *(pltpu.VMEM(piece, BF16) for piece in pieces),
    ]


def spread_weights(shards, inner, tokens, lengths, number):
    dma = pltpu.SemaphoreType.DMA
    shapes = whole_shapes(shards, inner) + [
        jax.ShapeDtypeStruct((tokens.shape[0] * SPLIT, tokens.shape[1]), BF16),
        jax.ShapeDtypeStruct((SPLIT, *lengths.shape), lengths.dtype),
    ]
    qkv_all, up_all, low_all, *gathered = pl.pallas_call(
        functools.partial(spread_weights_kernel, inner),
        out_shape=shapes,
        in_specs=[ANY_SPEC] * 4 + [VMEM_SPEC] * 2,
        out_specs=[ANY_SPEC] * len(shapes),
        scratch_shapes=spread_scratch(shards, inner)
        + [
            dma((4, SPLIT - 1)),
            dma((4, SPLIT - 1)),
            dma((SPLIT - 1,)),
            dma((SPLIT - 1,)),
        ],
        compiler_params=pltpu.CompilerParams(collective_id=number, has_side_effects=True),
    )(*shards, tokens, lengths)
    return (qkv_all, up_all, joined_columns(low_all), *gathered)


def f32(value):
    return value.astype(F32)


class RowSum:
    def __init__(self, here, part_ref, total, near_in, far_in, far_out, outer_in, outer_out, *sems):
        self.here, self.part, self.total = here, part_ref, total
        self.near_in, self.far_in, self.far_out = near_in, far_in, far_out
        self.outer_in, self.outer_out = outer_in, outer_out
        self.near_sems, self.far_sems, self.outer_sems = sems[0:2], sems[2:4], sems[4:6]
        self.quarter_sems = sems[6:8]
        self.rows = far_out.shape[1]
        self.near, self.far, self.outer, self.coming = {}, {}, {}, {}
        self.slots = None
        self.before = None

    def recycle(self, step):
        for side in range(2):
            self.near.pop((step, side)).wait_send()

    def rows_of(self, step, quarter):
        block = self.slots[step] if self.slots else (self.here.o + 1 + step) % SPLIT
        return pl.ds((block * QUARTERS + quarter) * self.rows, self.rows)

    def start(self, step):
        here = self.here
        for side, quarter in enumerate(((here.near + 2) % QUARTERS, here.near)):
            self.near[step, side] = remote(
                self.part.at[self.rows_of(step, quarter), :],
                self.near_in.at[step, side],
                self.near_sems[0].at[step, side],
                self.near_sems[1].at[step, side],
                here.near_peer(),
            )

    def across(self, step):
        here = self.here
        self.near[step, 0].wait_recv()
        if self.before:
            self.before.far.pop(step).wait_send()
        self.far_out[step] = (
            f32(self.part[self.rows_of(step, here.far), :]) + f32(self.near_in[step, 0])
        ).astype(BF16)
        self.far[step] = remote(
            self.far_out.at[step],
            self.far_in.at[step],
            self.far_sems[0].at[step],
            self.far_sems[1].at[step],
            here.far_peer(),
        )

    def along(self, step):
        here = self.here
        self.near[step, 1].wait_recv()
        self.far[step].wait_recv()
        value = (
            f32(self.part[self.rows_of(step, here.t), :])
            + f32(self.near_in[step, 1])
            + f32(self.far_in[step])
        )
        if step == SPLIT - 1:
            self.total[...] = value
            return
        if self.before:
            self.before.outer.pop(step).wait_send()
        self.outer_out[step] = value.astype(BF16)
        self.outer[step] = self.coming[step] = remote(
            self.outer_out.at[step],
            self.outer_in.at[step],
            self.outer_sems[0].at[step],
            self.outer_sems[1].at[step],
            here.outer_peer(step + 1),
        )

    def value(self):
        value = self.total[...]
        for step in range(SPLIT - 1):
            self.coming[step].wait_recv()
            value = value + f32(self.outer_in[step])
        return value

    def finish(self):
        for copies in (self.near, self.far, self.outer):
            for copy in copies.values():
                copy.wait_send()


class Quarters:
    def __init__(self, here, ref, rows, send, recv):
        self.here, self.ref, self.rows, self.send, self.recv = here, ref, rows, send, recv

    def copy(self, number, quarter, peer):
        piece = self.ref.at[pl.ds(quarter * self.rows, self.rows), :]
        return remote(piece, piece, self.send.at[number], self.recv.at[number], peer)

    def start(self):
        self.far = self.copy(0, self.here.t, self.here.far_peer())
        self.near = self.copy(1, self.here.t, self.here.near_peer())

    def pass_on(self):
        self.far.wait_recv()
        self.passed = self.copy(2, self.here.far, self.here.near_peer())

    def finish(self):
        self.near.wait_recv()
        self.passed.wait_recv()
        for copy in (self.far, self.near, self.passed):
            copy.wait_send()


def gather_quarters(here, ref, rows, send, recv):
    quarters = Quarters(here, ref, rows, send, recv)
    quarters.start()
    quarters.pass_on()
    quarters.finish()


def reduce_peers(here):
    return [here.outer_peer(s) for s in range(1, SPLIT)] + [here.far_peer(), here.near_peer()]


def dot(left, right):
    return jnp.dot(left, right, preferred_element_type=F32)


def dot_cols(left, right):
    return lax.dot_general(left, right, (((1,), (1,)), ((), ())), preferred_element_type=F32)


def error_function(value):
    value = jnp.clip(value, -3.832506856900711, 3.832506856900711)
    square = value * value
    above = jnp.full_like(square, 0.00022905065861350646)
    for term in (0.0034082910107109506, 0.050955695062380861, 0.18520832239976145, 1.128379143519084):
        above = above * square + term
    below = jnp.full_like(square, -1.1791602954361697e-7)
    for term in (
        0.000023547966471313185, 0.0010179625278914885, 0.014070470171167667,
        0.11098505178285362, 0.49746925110067538, 1.0,
    ):
        below = below * square + term
    return value * above / below


def turn(values, tables, where, direction):
    cosine, sine = (table[where, :] for table in tables)
    ahead = pltpu.roll(values, values.shape[1] - ROT // 2, 1)
    behind = pltpu.roll(values, ROT // 2, 1)
    first = lax.broadcasted_iota(jnp.int32, values.shape, 1) < ROT // 2
    return values * cosine + direction * (jnp.where(first, ahead, behind) * sine)


def documents(lengths, index):
    end = jnp.zeros((1, 1), jnp.int32)
    found = jnp.zeros(index.shape, jnp.int32)
    for segment in range(SEGS - 1):
        end = end + lengths[0:1, segment : segment + 1]
        found = found + (index >= end).astype(jnp.int32)
    return found


def row_tiles(start, count, tile, body):
    @pl.loop(0, count // tile)
    def _(n):
        body(pl.ds(pl.multiple_of(start + n * tile, tile), tile), pl.ds(pl.multiple_of(n * tile, tile), tile))


def forward_kernel(inner, keeps, background, *refs):
    here = Place(inner)
    refs = list(refs)

    def take(count):
        taken = refs[:count]
        del refs[:count]
        return taken

    tokens_ref, lengths_ref, cosine, sine = take(4)
    tables = (cosine, sine)
    own_rows = [take(2) for _ in keeps]
    given = take(3)
    facts_ref = None if keeps[0] else take(1)[0]
    shards = take(4 if background else 0)
    finals = take(len(keeps))
    slope_ref, kept_mixed, facts_ref, kept_joined = take(4) if keeps[0] else (None, None, facts_ref, None)
    wholes = take(3 if background else 0)
    weights, load = take(3), take(1)[0]
    other_mixed, other_joined = (None, None) if all(keeps) else take(2)
    one_ref, two_ref, hidden_ref, part_ref = take(4)
    block = one_ref.shape[0]
    common = take(14)
    sums = [RowSum(here, part_ref, *common)]
    if len(keeps) > 1:
        total, outer_in, *sems = take(10)
        sums.append(RowSum(here, part_ref, total, *common[1:4], outer_in, common[5], *sems))
        sums[1].before = sums[0]
    for number, layer in enumerate(sums):
        layer.slots = {step: (number * SPLIT + step) % 2 for step in range(SPLIT)}
    rows = sums[0].rows
    qkv_ref, up_ref, low_ref = weights
    heads = qkv_ref.shape[1] // (3 * HD)
    cut = heads * HD
    peers = reduce_peers(here)
    spread = None
    if background:
        spread = Spread(here, shards, wholes, *refs)
        peers = spread.peers() + [here.far_peer(), here.near_peer()]
    greet(peers)
    events = []
    loads = []

    def fetch(sources):
        for number, (source, target) in enumerate(zip(sources, weights)):
            copy = pltpu.make_async_copy(source, target, load.at[number])
            copy.start()
            loads.append(copy)

    fetch(given)
    if background:
        for number in range(AHEAD):
            spread.send_on(number)
        spread.start_own()
        events = list(range(len(spread.order)))

    def serve():
        if events:
            spread.step(events.pop(0))

    def stage(name, position):
        if 0 <= position < len(keeps) * SPLIT:
            getattr(sums[position // SPLIT], name)(position % SPLIT)

    gathers = []

    def settle(number):
        rows_ref = own_rows[number][0]
        branch = sums[number].value() + rows_ref[4:5, :] + rows_ref[5:6, :]
        quarter = pl.ds(pl.multiple_of(here.o * block + here.t * rows, rows), rows)
        mine = pl.ds(pl.multiple_of(here.t * rows, rows), rows)
        finals[number][mine, :] = (f32(tokens_ref[quarter, :]) + branch).astype(BF16)
        gathers.append(Quarters(here, finals[number], rows, *sums[number].quarter_sems))
        gathers[-1].start()

    for position in range(len(keeps) * SPLIT):
        number, step = position // SPLIT, position % SPLIT
        keep = keeps[number]
        rows_ref, bias_ref = own_rows[number]
        mixed_ref, joined_ref = (
            (kept_mixed, kept_joined) if keep else (other_mixed, other_joined)
        )
        own_block = (here.o + 1 + step) % SPLIT
        start = own_block * block
        kept = start if keep else 0

        def norm(where, own):
            values = f32(tokens_ref[where, :])
            if keep:
                mean = jnp.mean(values, axis=1, keepdims=True)
                centre = values - mean
                scale = lax.rsqrt(jnp.mean(centre * centre, axis=1, keepdims=True) + EPS_NORM)
                facts_ref[where, MEAN : MEAN + 1] = mean
                facts_ref[where, SCALE : SCALE + 1] = scale
                normed = centre * scale
            else:
                normed = (values - facts_ref[where, MEAN : MEAN + 1]) * facts_ref[
                    where, SCALE : SCALE + 1
                ]
            one_ref[own, :] = (normed * rows_ref[0:1, :] + rows_ref[1:2, :]).astype(BF16)
            two_ref[own, :] = (normed * rows_ref[2:3, :] + rows_ref[3:4, :]).astype(BF16)

        row_tiles(start, block, 16, norm)
        serve()
        stage("across", position - 1)
        if number and step == 0:
            while events:
                serve()
            spread.finish()
            fetch(wholes)
        while loads:
            loads.pop(0).wait()
        whole = pl.ds(pl.multiple_of(start, block), block)
        mine = pl.ds(kept if keep else 0, block)
        width = qkv_ref.shape[1]
        first_bias = bias_ref[:, pl.ds(pl.multiple_of(here.o * width, 128), width)]
        mixed = dot(one_ref[...], qkv_ref[...]) + first_bias
        for head in range(heads):
            at = head * 3 * HD
            for offset in (0, HD):
                mixed_ref[mine, at + offset : at + offset + HD] = turn(
                    mixed[:, at + offset : at + offset + HD], tables, pl.ds(0, block), 1.0
                ).astype(BF16)
            mixed_ref[mine, at + 2 * HD : at + 3 * HD] = mixed[:, at + 2 * HD : at + 3 * HD].astype(
                BF16
            )
        hidden_ref[...] = dot(two_ref[...], up_ref[...])
        serve()
        lengths = lengths_ref[own_block]
        doc_col = documents(lengths, lax.broadcasted_iota(jnp.int32, (block, 1), 0))
        doc_row = documents(lengths, lax.broadcasted_iota(jnp.int32, (1, block), 1))
        for head in range(heads):
            at = head * 3 * HD
            for first in range(0, block, 128):
                queries = pl.ds(pl.multiple_of(kept + first, 128), 128)
                tokens_at = pl.ds(pl.multiple_of(start + first, 128), 128)
                keys = pl.ds(pl.multiple_of(kept, 128), first + 128)
                scores = dot_cols(
                    mixed_ref[queries, at : at + HD], mixed_ref[keys, at + HD : at + 2 * HD]
                ) * HD ** (-0.5)
                same = doc_col[first : first + 128] == doc_row[:, : first + 128]
                earlier = first + lax.broadcasted_iota(
                    jnp.int32, scores.shape, 0
                ) >= lax.broadcasted_iota(jnp.int32, scores.shape, 1)
                scores = jnp.where(same & earlier, scores, MASKED)
                highest = jnp.max(scores, axis=1, keepdims=True)
                total = highest + jnp.log(
                    jnp.sum(jnp.exp(scores - highest), axis=1, keepdims=True)
                )
                if keep:
                    facts_ref[tokens_at, head : head + 1] = total
                probs = jnp.exp(scores - total).astype(BF16)
                joined_ref[queries, head * HD : (head + 1) * HD] = dot(
                    probs, mixed_ref[keys, at + 2 * HD : at + 3 * HD]
                ).astype(BF16)
        stage("along", position - 2)
        stage("recycle", position - 2)

        def activate(where, own):
            width = up_ref.shape[1]
            begin = SPLIT * qkv_ref.shape[1] + here.o * width
            hidden = hidden_ref[own, :] + bias_ref[:, pl.ds(pl.multiple_of(begin, 128), width)]
            share = 0.5 * (1.0 + error_function(hidden * 0.7071067811865476))
            joined_ref[where, cut:] = (hidden * share).astype(BF16)
            if keep:
                density = jnp.exp(-0.5 * hidden * hidden) * 0.3989422804014327
                slope_ref[where, :] = share + hidden * density

        row_tiles(kept, block, 32, activate)
        serve()
        columns = 512
        slot = pl.ds((position % 2) * block, block)

        @pl.loop(0, part_ref.shape[1] // columns)
        def _(n):
            at = pl.ds(pl.multiple_of(n * columns, columns), columns)
            part_ref[slot, at] = dot(joined_ref[mine, :], low_ref[:, at]).astype(BF16)

        stage("start", position)
        if number and step == 2:
            settle(0)
        if number and step == 3:
            gathers[0].pass_on()
    last = len(keeps) - 1
    sums[last].across(SPLIT - 1)
    while events:
        serve()
    sums[last].along(SPLIT - 2)
    sums[last].along(SPLIT - 1)
    settle(last)
    gathers[last].pass_on()
    for gather in gathers:
        gather.finish()
    for layer in sums:
        layer.finish()
    if background and last == 0:
        spread.finish()


def forward_call(tokens, layout, layers, weights, block, inner, facts, shards, number):
    total_rows, d_model = tokens.shape
    qkv_all, up_all, low_all = weights
    background = shards is not None
    keeps = (facts is None,) + (False,) * (len(layers) - 1)
    dma = pltpu.SemaphoreType.DMA
    outs = [jax.ShapeDtypeStruct((block, d_model), BF16) for _ in layers]
    if keeps[0]:
        outs += [
            jax.ShapeDtypeStruct((total_rows, up_all.shape[1]), F32),
            jax.ShapeDtypeStruct((total_rows, qkv_all.shape[1]), BF16),
            jax.ShapeDtypeStruct((total_rows, FACTS), F32),
            jax.ShapeDtypeStruct((total_rows, low_all.shape[0]), BF16),
        ]
    specs = [VMEM_SPEC] * len(outs)
    scratch = [pltpu.VMEM(w.shape, BF16) for w in weights] + [dma((3,))]
    if not all(keeps):
        scratch += [
            pltpu.VMEM((block, qkv_all.shape[1]), BF16),
            pltpu.VMEM((block, low_all.shape[0]), BF16),
        ]
    scratch += [
        pltpu.VMEM((block, d_model), BF16),
        pltpu.VMEM((block, d_model), BF16),
        pltpu.VMEM((block, up_all.shape[1]), F32),
        pltpu.VMEM((2 * block, d_model), BF16),
    ]
    one_sum = reduce_scratch(block // QUARTERS, d_model)
    scratch += one_sum
    if len(layers) > 1:
        scratch += [one_sum[0], one_sum[4], *one_sum[6:]]
    operands = [tokens, *layout]
    for layer in layers:
        operands += layer
    in_specs = [VMEM_SPEC] * len(operands)
    operands += weights
    in_specs += [ANY_SPEC] * 3
    if not keeps[0]:
        operands.append(facts)
        in_specs.append(VMEM_SPEC)
    if background:
        operands += shards
        in_specs += [ANY_SPEC] * 4
        outs += whole_shapes(shards, inner)
        specs += [ANY_SPEC] * 3
        scratch += spread_scratch(shards, inner)
    return pl.pallas_call(
        functools.partial(forward_kernel, inner, keeps, background),
        out_shape=outs,
        in_specs=in_specs,
        out_specs=specs,
        scratch_shapes=scratch,
        compiler_params=pltpu.CompilerParams(
            collective_id=number, has_side_effects=True, vmem_limit_bytes=60 * 1024 * 1024
        ),
    )(*operands)


def input_change(values, scaled):
    centre = values - jnp.mean(values, axis=1, keepdims=True)
    spread = jnp.mean(centre * centre, axis=1, keepdims=True)
    scale = lax.rsqrt(spread + EPS_NORM)
    normed = centre * scale
    along = jnp.mean(scaled * normed, axis=1, keepdims=True)
    return scale * (scaled - jnp.mean(scaled, axis=1, keepdims=True) - normed * along)


def reduce_scratch(rows, width):
    dma = pltpu.SemaphoreType.DMA
    return [
        pltpu.VMEM((rows, width), F32),
        pltpu.VMEM((SPLIT, 2, rows, width), BF16),
        pltpu.VMEM((SPLIT, rows, width), BF16),
        pltpu.VMEM((SPLIT, rows, width), BF16),
        pltpu.VMEM((SPLIT - 1, rows, width), BF16),
        pltpu.VMEM((SPLIT - 1, rows, width), BF16),
        dma((SPLIT, 2)),
        dma((SPLIT, 2)),
        dma((SPLIT,)),
        dma((SPLIT,)),
        dma((SPLIT - 1,)),
        dma((SPLIT - 1,)),
        dma((3,)),
        dma((3,)),
    ]


def dot_rows(left, right):
    return lax.dot_general(left, right, (((0,), (0,)), ((), ())), preferred_element_type=F32)


def backward_kernel(
    inner, final_part, tokens_hbm, rows_ref, qkv_ref, up_ref, low_ref, slope_ref, mixed_ref,
    facts_ref, lengths_ref, cosine, sine,
    grad_ref, branch_all, mixed_grad, hidden_grad, rows_out, bias_out,
    near_in, far_in, far_out, low, quarter, tokens_ref, own_tokens, joined_ref, key_ref, value_ref,
    part_ref,
    near_send, near_recv, far_send, far_recv, send, recv, local, *scratch,
):
    here = Place(inner)
    tables = (cosine, sine)
    sums = RowSum(here, part_ref, *scratch)
    rows = sums.rows
    block = rows * QUARTERS
    heads = qkv_ref.shape[1] // (3 * HD)
    cut = heads * HD
    greet(reduce_peers(here))

    def rows_of(number):
        return pl.ds(pl.multiple_of(number * rows, rows), rows)

    near = []
    for side, number in enumerate(((here.near + 2) % QUARTERS, here.near)):
        near.append(
            remote(
                final_part.at[rows_of(number), :],
                near_in.at[side],
                near_send.at[side],
                near_recv.at[side],
                here.near_peer(),
            )
        )

    shifts = (1, 3, 2, 0)

    def fetch(position):
        copy = pltpu.make_async_copy(
            tokens_hbm.at[pl.ds(((here.o + SPLIT - shifts[position]) % SPLIT) * block, block), :],
            tokens_ref,
            local.at[0],
        )
        copy.start()
        return copy

    fetched = fetch(0)
    own_copy = pltpu.make_async_copy(
        tokens_hbm.at[rows_of(here.o * QUARTERS + here.t), :], own_tokens, local.at[1]
    )
    own_copy.start()
    near[0].wait_recv()
    far_out[...] = (f32(final_part[rows_of(here.far), :]) + f32(near_in[0])).astype(BF16)
    far = remote(far_out, far_in, far_send, far_recv, here.far_peer())
    near[1].wait_recv()
    far.wait_recv()
    quarter[...] = f32(final_part[rows_of(here.t), :]) + f32(near_in[1]) + f32(far_in[...])
    low[...] = quarter[...].astype(BF16)
    rows_out[...] = jnp.zeros_like(rows_out)
    bias_out[...] = jnp.zeros_like(bias_out)
    rows_out[4:5, :] = jnp.sum(f32(low[...]), axis=0, keepdims=True)

    def piece(s, number):
        part = (here.o + SPLIT - s) % SPLIT
        return branch_all.at[rows_of(part * QUARTERS + number), :]

    outer, across, beside, beyond = {}, {}, {}, {}

    def send_out(s):
        outer[s] = remote(low, piece(0, here.t), send.at[0, s], recv.at[0, s], here.outer_peer(s))

    send_out(1)
    send_out(3)
    own = pltpu.make_async_copy(low, piece(0, here.t), local.at[2])
    own.start()

    def arrived(s):
        if s:
            outer[s].wait_recv()
        if s == 1:
            send_out(2)
        source = piece(s, here.t) if s else low
        across[s] = remote(
            source, piece(s, here.t), send.at[1, s], recv.at[1, s], here.far_peer()
        )
        beside[s] = remote(
            source, piece(s, here.t), send.at[2, s], recv.at[2, s], here.near_peer()
        )

    def crossed(s):
        across[s].wait_recv()
        beyond[s] = remote(
            piece(s, here.far), piece(s, here.far), send.at[3, s], recv.at[3, s], here.near_peer()
        )

    arrived(0)
    crossed(0)
    arrived(1)
    crossed(1)
    own.wait()
    steps = [SPLIT - 1 - s for s in shifts]
    sums.slots = {step: position % 2 for position, step in enumerate(steps)}
    events = [
        (arrived, 3), None, (crossed, 3), (arrived, 2), None, (crossed, 2),
    ]

    def serve():
        event = events.pop(0) if events else None
        if event:
            event[0](event[1])

    for position, s in enumerate(shifts):
        step = steps[position]
        part = (here.o + SPLIT - s) % SPLIT
        start = pl.multiple_of(part * block, block)
        whole = pl.ds(start, block)
        beside[s].wait_recv()
        beyond[s].wait_recv()
        joined_ref[...] = dot_cols(branch_all[whole, :], low_ref[...])

        def activate(where, mine):
            hidden_grad[where, :] = (joined_ref[mine, cut:] * slope_ref[where, :]).astype(BF16)

        row_tiles(start, block, 64, activate)
        serve()
        if position:
            sums.across(steps[position - 1])
        lengths = lengths_ref[part]
        doc_col = documents(lengths, lax.broadcasted_iota(jnp.int32, (block, 1), 0))
        doc_row = documents(lengths, lax.broadcasted_iota(jnp.int32, (1, block), 1))
        for head in range(heads):
            at = head * 3 * HD
            key_ref[...] = jnp.zeros_like(key_ref)
            value_ref[...] = jnp.zeros_like(value_ref)
            for first in range(0, block, 128):
                queries = pl.ds(pl.multiple_of(start + first, 128), 128)
                width = first + 128
                keys = pl.ds(start, width)
                query = mixed_ref[queries, at : at + HD]
                key = mixed_ref[keys, at + HD : at + 2 * HD]
                scores = dot_cols(query, key) * HD ** (-0.5)
                same = doc_col[first : first + 128] == doc_row[:, :width]
                earlier = first + lax.broadcasted_iota(
                    jnp.int32, scores.shape, 0
                ) >= lax.broadcasted_iota(jnp.int32, scores.shape, 1)
                scores = jnp.where(same & earlier, scores, MASKED)
                probs = jnp.exp(scores - facts_ref[queries, head : head + 1])
                attended_grad = joined_ref[
                    first : first + 128, head * HD : (head + 1) * HD
                ].astype(BF16)
                prob_grad = dot_cols(attended_grad, mixed_ref[keys, at + 2 * HD : at + 3 * HD])
                mean = jnp.sum(probs * prob_grad, axis=1, keepdims=True)
                score_grad = (probs * (prob_grad - mean)).astype(BF16)
                mixed_grad[queries, at : at + HD] = turn(
                    dot(score_grad, key) * HD ** (-0.5), tables, pl.ds(first, 128), -1.0
                ).astype(BF16)
                key_ref[:width, :] += dot_rows(score_grad, query)
                value_ref[:width, :] += dot_rows(probs.astype(BF16), attended_grad)
            mixed_grad[whole, at + HD : at + 2 * HD] = turn(
                key_ref[...] * HD ** (-0.5), tables, pl.ds(0, block), -1.0
            ).astype(BF16)
            mixed_grad[whole, at + 2 * HD : at + 3 * HD] = value_ref[...].astype(BF16)
        row = 0
        for ref in (mixed_grad, hidden_grad):
            for n in range(0, ref.shape[1], 128):
                bias_out[row : row + 1, :] += jnp.sum(
                    f32(ref[whole, n : n + 128]), axis=0, keepdims=True
                )
                row += 1
        serve()
        if position > 1:
            sums.along(steps[position - 2])
            sums.recycle(steps[position - 2])
        fetched.wait()
        columns = 256
        target = pl.ds((position % 2) * block, block)

        @pl.loop(0, part_ref.shape[1] // columns)
        def _(n):
            at = pl.ds(pl.multiple_of(n * columns, columns), columns)
            one = dot_cols(mixed_grad[whole, :], qkv_ref[at, :])
            two = dot_cols(hidden_grad[whole, :], up_ref[at, :])
            normed = (f32(tokens_ref[:, at]) - facts_ref[whole, MEAN : MEAN + 1]) * facts_ref[
                whole, SCALE : SCALE + 1
            ]
            part_ref[target, at] = (one * rows_ref[0:1, at] + two * rows_ref[2:3, at]).astype(BF16)
            for row, value in enumerate((one * normed, one, two * normed, two)):
                rows_out[row : row + 1, at] += jnp.sum(value, axis=0, keepdims=True)

        sums.start(step)
        if position + 1 < SPLIT:
            fetched = fetch(position + 1)
        serve()
    sums.across(steps[3])
    sums.along(steps[2])
    sums.along(steps[3])
    own_copy.wait()
    change = input_change(f32(own_tokens[...]), sums.value())
    grad_ref[rows_of(here.t), :] = (quarter[...] + change).astype(BF16)
    gather_quarters(here, grad_ref, rows, *sums.quarter_sems)
    sums.finish()
    for copy in near + [far]:
        copy.wait_send()
    for copies in (outer, across, beside, beyond):
        for copy in copies.values():
            copy.wait_send()


def backward_call(part, tokens, rows, weights, kept, layout, inner, number):
    block, width = part.shape
    quarter = block // QUARTERS
    slope, mixed, facts, joined = kept
    bias_rows = -(-(mixed.shape[1] + slope.shape[1]) // 1024) * 8
    dma = pltpu.SemaphoreType.DMA
    return pl.pallas_call(
        functools.partial(backward_kernel, inner),
        out_shape=[
            jax.ShapeDtypeStruct((block, width), BF16),
            jax.ShapeDtypeStruct((SPLIT * block, width), BF16),
            jax.ShapeDtypeStruct(mixed.shape, BF16),
            jax.ShapeDtypeStruct(slope.shape, BF16),
            jax.ShapeDtypeStruct((8, rows.shape[1]), F32),
            jax.ShapeDtypeStruct((bias_rows, 128), F32),
        ],
        in_specs=[VMEM_SPEC, ANY_SPEC] + [VMEM_SPEC] * (7 + len(layout)),
        out_specs=[VMEM_SPEC] * 6,
        scratch_shapes=[
            pltpu.VMEM((2, quarter, width), BF16),
            pltpu.VMEM((quarter, width), BF16),
            pltpu.VMEM((quarter, width), BF16),
            pltpu.VMEM((quarter, width), BF16),
            pltpu.VMEM((quarter, width), F32),
            pltpu.VMEM((block, width), BF16),
            pltpu.VMEM((quarter, width), BF16),
            pltpu.VMEM((block, joined.shape[1]), F32),
            pltpu.VMEM((block, HD), F32),
            pltpu.VMEM((block, HD), F32),
            pltpu.VMEM((2 * block, width), BF16),
            dma((2,)),
            dma((2,)),
            dma,
            dma,
            dma((4, SPLIT)),
            dma((4, SPLIT)),
            dma((3,)),
        ]
        + reduce_scratch(quarter, width),
        compiler_params=pltpu.CompilerParams(
            collective_id=number, has_side_effects=True, vmem_limit_bytes=60 * 1024 * 1024
        ),
    )(part, tokens, rows, *weights, slope, mixed, facts, *layout)


class AllSum:
    def __init__(self, here, mine, near_in, far_in, outer, inner, send, recv):
        self.here, self.mine, self.near_in, self.far_in = here, mine, near_in, far_in
        self.outer, self.inner, self.send, self.recv = outer, inner, send, recv
        self.copies = []

    def pair(self, stage, target, peer):
        copy = remote(
            self.mine.at[stage], target, self.send.at[stage], self.recv.at[stage], peer
        )
        self.copies.append(copy)
        return copy

    def near(self, value):
        self.mine[0] = value
        self.waiting = [self.pair(0, self.near_in, self.here.near_peer())]

    def far(self):
        self.waiting[0].wait_recv()
        self.mine[1] = self.mine[0] + self.near_in[...]
        self.waiting = [self.pair(1, self.far_in, self.here.far_peer())]

    def group(self, buffer, index, first, peers):
        self.waiting = []
        for number, peer in enumerate(peers):
            copy = remote(
                buffer.at[index],
                buffer.at[index],
                self.send.at[first + number],
                self.recv.at[first + number],
                peer,
            )
            self.waiting.append(copy)
            self.copies.append(copy)

    def along_outer(self):
        self.waiting[0].wait_recv()
        here = self.here
        self.outer[here.o] = self.mine[1] + self.far_in[...]
        self.group(self.outer, here.o, 2, [here.outer_peer(s) for s in range(1, SPLIT)])

    def along_inner(self):
        here = self.here
        for copy in self.waiting:
            copy.wait_recv()
        value = self.outer[0]
        for part in range(1, SPLIT):
            value = value + self.outer[part]
        self.inner[here.i] = value
        peers = [here.inner_peer(r) for r in range(1, here.inner)]
        self.group(self.inner, here.i, 1 + SPLIT, peers)

    def value(self):
        for copy in self.waiting:
            copy.wait_recv()
        value = self.inner[0]
        for part in range(1, self.here.inner):
            value = value + self.inner[part]
        for copy in self.copies:
            copy.wait_send()
        return value


class ShortSum:
    def __init__(self, here, quarters, parts, send, recv, send_dp, recv_dp):
        self.here, self.quarters, self.parts = here, quarters, parts
        self.sems, self.dp_sems = (send, recv), (send_dp, recv_dp)
        self.copies = []

    def share(self, buffer, index, sems, peers):
        waiting = [
            remote(buffer.at[index], buffer.at[index], sems[0].at[n], sems[1].at[n], peer)
            for n, peer in enumerate(peers)
        ]
        self.copies += waiting
        for copy in waiting:
            copy.wait_recv()
        return functools.reduce(lambda a, b: a + b, [buffer[n] for n in range(buffer.shape[0])])

    def along_tensor(self, value):
        self.quarters[self.here.t] = value
        return self.share(self.quarters, self.here.t, self.sems, self.here.tensor_peers())

    def along_dp(self, value):
        self.parts[self.here.dp] = value
        return self.share(self.parts, self.here.dp, self.dp_sems, self.here.dp_peers())

    def finish(self):
        for copy in self.copies:
            copy.wait_send()


def short_sum_scratch(inner):
    dma = pltpu.SemaphoreType.DMA
    count = SPLIT * inner
    return [
        pltpu.VMEM((QUARTERS, 8, 128), F32),
        pltpu.VMEM((count, 8, 128), F32),
        dma((QUARTERS - 1,)),
        dma((QUARTERS - 1,)),
        dma((count - 1,)),
        dma((count - 1,)),
    ]


def all_sum_scratch(shape, inner):
    dma = pltpu.SemaphoreType.DMA
    return [
        pltpu.VMEM((2, *shape), F32),
        pltpu.VMEM(shape, F32),
        pltpu.VMEM(shape, F32),
        pltpu.VMEM((SPLIT, *shape), F32),
        pltpu.VMEM((inner, *shape), F32),
        dma((SPLIT + inner,)),
        dma((SPLIT + inner,)),
    ]


def whole_sum(value):
    return jnp.sum(jnp.sum(value, axis=1, keepdims=True), axis=0, keepdims=True)


def finish_kernel(
    inner, tokens_ref, branch_ref, gains_ref, joined_ref, mixed_ref, hidden_ref, facts_ref,
    rows_ref, bias_ref, qkv_out, up_out, out_out, down_out, rows_out, bias_out, norm_ref, *scratch,
):
    here = Place(inner)
    sends, inputs, totals = scratch[:3], scratch[3:6], scratch[6:9]
    turned, send_i, recv_i, send_o, recv_o, local, held = scratch[9:16]
    small = AllSum(here, *scratch[16:23])
    squares = ShortSum(here, *scratch[23:29])
    bias_in, bias_send, bias_recv = scratch[29:32]
    outs = (qkv_out, up_out, out_out, down_out)
    shard = qkv_out.shape[0]
    width_out = out_out.shape[0] // SPLIT

    def columns_of(ref, index):
        if ref.ndim == 3:
            return ref[index]
        return ref[:, pl.ds(pl.multiple_of(index * shard, shard), shard)]

    def gradient(kind, index):
        if kind == 2:
            return dot(turned[...], columns_of(branch_ref, index))
        if tokens_ref.ndim == 3:
            copy = pltpu.make_async_copy(tokens_ref.at[index], held, local.at[4])
            copy.start()
            copy.wait()
            values = f32(held[...])
        else:
            values = f32(columns_of(tokens_ref, index))
        normed = (values - facts_ref[:, MEAN : MEAN + 1]) * facts_ref[:, SCALE : SCALE + 1]
        rows = columns_of(gains_ref, index)
        at = 2 * kind
        layer_in = (normed * rows[at : at + 1, :] + rows[at + 1 : at + 2, :]).astype(BF16)
        return dot_rows(layer_in, (mixed_ref, hidden_ref)[kind][...])

    def dst(m):
        if m < 2:
            width = outs[m].shape[1] // SPLIT
            return outs[m].at[:, pl.ds(here.o * width, width)]
        width = outs[m].shape[0] // SPLIT
        return outs[m].at[pl.ds(here.o * width, width), :]

    greet(here.tensor_peers() + here.dp_peers())
    first, last, own = {}, [], []
    order = [(kind, s) for kind in (2, 1, 0) for s in (2, 1, 3, 0)]
    turned[...] = jnp.transpose(joined_ref[...])

    def trade(number):
        if number >= len(order):
            return
        kind, s = order[number]
        part = (here.o + s) % SPLIT
        for r in range(1, inner):
            sends[kind][s, r - 1] = gradient(kind, part * inner + (here.i + r) % inner).astype(BF16)
            first[kind, s, r] = remote(
                sends[kind].at[s, r - 1],
                inputs[kind].at[s, r - 1],
                send_i.at[kind, s, r - 1],
                recv_i.at[kind, s, r - 1],
                here.inner_peer(r),
            )

    def settle(number):
        kind, s = order[number]
        part = (here.o + s) % SPLIT
        total = gradient(kind, part * inner + here.i)
        for r in range(1, inner):
            first[kind, s, r].wait_recv()
            total = total + f32(inputs[kind][s, r - 1])
        totals[kind][s] = total.astype(BF16)
        source = totals[kind].at[s]
        pieces = [(kind, source)]
        if kind == 2:
            pieces = [
                (2, source.at[pl.ds(0, width_out), :]),
                (3, source.at[pl.ds(width_out, total.shape[0] - width_out), :]),
            ]
        for m, piece in pieces:
            if s:
                last.append(
                    remote(
                        piece, dst(m), send_o.at[m, s - 1], recv_o.at[m, s - 1], here.outer_peer(s)
                    )
                )
            else:
                copy = pltpu.make_async_copy(piece, dst(m), local.at[m])
                copy.start()
                own.append(copy)
        trade(number + AHEAD)
        return whole_sum(total * total)

    for number in range(AHEAD):
        trade(number)
    small.near(rows_ref[...])
    bias_in[here.i] = bias_ref[...]
    bias_inner = [
        remote(
            bias_in.at[here.i],
            bias_in.at[here.i],
            bias_send.at[SPLIT + r],
            bias_recv.at[SPLIT + r],
            here.inner_peer(r),
        )
        for r in range(1, inner)
    ]
    square = settle(0)
    square = square + settle(1)
    small.far()
    for number in range(2, 5):
        square = square + settle(number)
    small.along_outer()
    for copy in bias_inner:
        copy.wait_recv()
    bias = bias_in[0]
    for part in range(1, inner):
        bias = bias + bias_in[part]
    bias_out[here.o] = bias
    bias_outer = [
        remote(
            bias_out.at[here.o],
            bias_out.at[here.o],
            bias_send.at[s],
            bias_recv.at[s],
            here.outer_peer(s),
        )
        for s in range(1, SPLIT)
    ]
    square = square + whole_sum(bias * bias) / inner
    square = square + settle(5)
    square = square + settle(6)
    small.along_inner()
    square = square + settle(7)
    square = square + settle(8)
    rows_out[...] = small.value()
    for number in range(9, len(order)):
        square = square + settle(number)
    norm = squares.along_dp(squares.along_tensor(jnp.broadcast_to(square, norm_ref.shape)))
    squares.finish()
    rows = rows_out[...]
    doubled = lax.broadcasted_iota(jnp.int32, rows.shape, 0) == 4
    norm_ref[...] = norm + whole_sum(rows * rows * jnp.where(doubled, 2.0, 1.0))
    for copy in bias_outer:
        copy.wait_recv()
    for copy in bias_inner + bias_outer:
        copy.wait_send()
    for copy in last:
        copy.wait()
    for copy in own:
        copy.wait()
    for copy in first.values():
        copy.wait_send()


def finish_call(tokens, branch, rows, kept, grads, sums, bias, shards, inner, number):
    dma = pltpu.SemaphoreType.DMA
    qkv, out, up, down = shards
    ordered = (qkv, up, out, down)
    facts, joined = kept
    shard = out[1]
    wide = [tokens, branch, rows]
    if not aligned(shard):
        wide = [jnp.swapaxes(w.reshape(w.shape[0], -1, shard), 0, 1) for w in wide]
    pieces = [
        (shard, grads[0].shape[1]),
        (shard, grads[1].shape[1]),
        (joined.shape[1], shard),
    ]
    peers = max(inner - 1, 1)
    tile = (8, 128)
    return pl.pallas_call(
        functools.partial(finish_kernel, inner),
        out_shape=[
            *(jax.ShapeDtypeStruct(shape, BF16) for shape in ordered),
            jax.ShapeDtypeStruct(sums.shape, F32),
            jax.ShapeDtypeStruct((SPLIT, *bias.shape), F32),
            jax.ShapeDtypeStruct(tile, F32),
        ],
        in_specs=[VMEM_SPEC if aligned(shard) else ANY_SPEC] + [VMEM_SPEC] * 8,
        out_specs=[ANY_SPEC] * 4 + [VMEM_SPEC] * 3,
        scratch_shapes=[pltpu.VMEM((SPLIT, peers, *piece), BF16) for piece in pieces]
        + [pltpu.VMEM((SPLIT, peers, *piece), BF16) for piece in pieces]
        + [pltpu.VMEM((SPLIT, *piece), BF16) for piece in pieces]
        + [
            pltpu.VMEM(joined.shape[::-1], BF16),
            dma((3, SPLIT, peers)),
            dma((3, SPLIT, peers)),
            dma((4, SPLIT - 1)),
            dma((4, SPLIT - 1)),
            dma((5,)),
            pltpu.VMEM((16, 128) if aligned(shard) else (tokens.shape[0], shard), BF16),
        ]
        + all_sum_scratch(sums.shape, inner)
        + short_sum_scratch(inner)
        + [
            pltpu.VMEM((inner, *bias.shape), F32),
            dma((SPLIT + inner,)),
            dma((SPLIT + inner,)),
        ],
        compiler_params=pltpu.CompilerParams(
            collective_id=number, has_side_effects=True, vmem_limit_bytes=60 * 1024 * 1024
        ),
    )(*wide, joined, *grads, facts, sums, bias)


def reward_kernel(
    inner, stats_ref, facts_ref, out_ref, stats, send, recv, *scratch,
):
    here = Place(inner)
    sums = ShortSum(here, *scratch)
    greet(here.tensor_peers() + here.dp_peers())

    def share(buffer, index, sends, recvs, peers):
        return [
            remote(buffer.at[index], buffer.at[index], sends.at[n], recvs.at[n], peer)
            for n, peer in enumerate(peers)
        ]

    stats[here.t] = stats_ref[...]
    copies = share(stats, here.t, send, recv, here.tensor_peers())
    for copy in copies:
        copy.wait_recv()
    quarters = [stats[q] for q in range(QUARTERS)]
    highest = functools.reduce(jnp.maximum, quarters)
    summed = functools.reduce(lambda a, b: a + b, [jnp.exp(q - highest) for q in quarters])
    totals = highest + jnp.log(summed)
    picks = functools.reduce(lambda a, b: a + b, quarters)
    log_probs = picks - totals_to_picks(totals)
    doc = lax.broadcasted_iota(jnp.int32, (8, 1), 0)
    start = end = labels = jnp.zeros((8, 1), jnp.int32)
    for segment in range(SEGS):
        length = facts_ref[0:1, segment : segment + 1]
        start = start + jnp.where(doc > segment, length, 0)
        end = end + jnp.where(doc >= segment, length, 0)
        labels = labels + jnp.where(doc == segment, facts_ref[1:2, segment : segment + 1], 0)
    token = lax.broadcasted_iota(jnp.int32, (8, stats_ref.shape[1]), 1)
    member = jnp.where((token >= start) & (token < end), 1.0, 0.0)
    policy_docs = jnp.sum(member * log_probs[1:2, :], axis=1, keepdims=True)
    frozen_docs = jnp.sum(member * log_probs[3:4, :], axis=1, keepdims=True)
    reward = policy_docs - frozen_docs
    total = sums.along_dp(jnp.broadcast_to(whole_sum(reward), (8, 128)))
    seq_count = inner * SPLIT * SEGS
    shift = total[:, 0:1] / seq_count
    sigmoid_value = 1.0 / (1.0 + jnp.exp(-BETA_KTO * (reward - shift)))
    labels = f32(labels)
    doc_grad = BETA_KTO * sigmoid_value * (1.0 - sigmoid_value) * (1.0 - 2.0 * labels) / seq_count
    token_grad = jnp.sum(member * doc_grad, axis=0, keepdims=True)
    out_ref[...] = jnp.transpose(
        jnp.concatenate([token_grad, totals[0:1, :], jnp.zeros((6, totals.shape[1]), F32)], axis=0)
    )
    for copy in copies:
        copy.wait_send()
    sums.finish()


def totals_to_picks(totals):
    return jnp.concatenate([totals[0:1], totals[0:1], totals[2:3], totals[2:3], totals[4:]], axis=0)


def reward_call(stats, facts, inner, number):
    dma = pltpu.SemaphoreType.DMA
    return pl.pallas_call(
        functools.partial(reward_kernel, inner),
        out_shape=jax.ShapeDtypeStruct((stats.shape[1], 8), F32),
        in_specs=[VMEM_SPEC] * 2,
        out_specs=VMEM_SPEC,
        scratch_shapes=[
            pltpu.VMEM((QUARTERS, *stats.shape), F32),
            dma((QUARTERS - 1,)),
            dma((QUARTERS - 1,)),
            *short_sum_scratch(inner),
        ],
        compiler_params=pltpu.CompilerParams(collective_id=number, has_side_effects=True),
    )(stats, facts)


def turn_tables(count):
    half = ROT // 2
    frequency = np.float32(10000.0) ** (np.float32(-2.0) * np.arange(half, dtype=np.float32) / ROT)
    angles = np.arange(count, dtype=np.float32)[:, None] * frequency.astype(np.float32)
    cosine, sine = np.cos(angles), np.sin(angles)
    none = np.zeros((count, HD - ROT), np.float32)
    return (
        jnp.asarray(np.concatenate([cosine, cosine, none + 1.0], axis=1), F32),
        jnp.asarray(np.concatenate([-sine, sine, none], axis=1), F32),
    )


def chunk_of(width):
    return next(n for n in (1280, 640, 512, 256, 128) if width % n == 0)


def head_kernel(policy_ref, frozen_ref, head_ref, target_ref, logits_ref, stats_ref, other_ref, high_ref, sum_ref, pick_ref):
    chunk = pl.program_id(0)
    rows, columns = logits_ref.shape

    @pl.when(chunk == 0)
    def _():
        high_ref[...] = jnp.full_like(high_ref, MASKED)
        sum_ref[...] = jnp.zeros_like(sum_ref)
        pick_ref[...] = jnp.zeros_like(pick_ref)

    def fold(which, values_ref, begin, width):
        for first in range(0, rows, 64):
            own = pl.ds(first, 64)
            high = high_ref[which, own, :]
            lanes = [values_ref[own, n : n + 128] for n in range(begin, begin + width, 128)]
            highest = functools.reduce(jnp.maximum, lanes, high)
            total = sum_ref[which, own, :] * jnp.exp(high - highest)
            picked = pick_ref[which, own, :]
            target = target_ref[own, :] - (chunk * columns + begin)
            lane = lax.broadcasted_iota(jnp.int32, highest.shape, 1)
            for n, value in enumerate(lanes):
                total = total + jnp.exp(value - highest)
                picked = picked + jnp.where(lane + n * 128 == target, value, 0.0)
            high_ref[which, own, :] = highest
            sum_ref[which, own, :] = total
            pick_ref[which, own, :] = picked

    width = 256 if columns % 256 == 0 else 128
    last = None
    for begin in range(0, columns, width):
        for which, (low_ref, values_ref) in enumerate(
            ((policy_ref, logits_ref), (frozen_ref, other_ref))
        ):
            values_ref[:, begin : begin + width] = dot(
                low_ref[...], head_ref[:, begin : begin + width]
            )
            if last:
                fold(*last)
            last = (which, values_ref, begin, width)
    fold(*last)

    @pl.when(chunk == pl.num_programs(0) - 1)
    def _():
        found = []
        for which in range(2):
            high = jnp.max(high_ref[which], axis=1, keepdims=True)
            total = jnp.sum(
                sum_ref[which] * jnp.exp(high_ref[which] - high), axis=1, keepdims=True
            )
            found.append(high + jnp.log(total))
            found.append(jnp.sum(pick_ref[which], axis=1, keepdims=True))
        lane = lax.broadcasted_iota(jnp.int32, (rows, 128), 1)
        joined = jnp.zeros((rows, 128), F32)
        for n, value in enumerate(found):
            joined = jnp.where(lane == n, value, joined)
        stats_ref[...] = jnp.transpose(joined)[:8, :]


def head_call(policy_low, frozen_low, head_weight, targets):
    rows, depth = policy_low.shape
    width = head_weight.shape[1]
    columns = chunk_of(width)
    return pl.pallas_call(
        head_kernel,
        grid=(width // columns,),
        out_shape=[
            jax.ShapeDtypeStruct((rows, width), F32),
            jax.ShapeDtypeStruct((8, rows), F32),
        ],
        in_specs=[
            pl.BlockSpec((rows, depth), lambda n: (0, 0)),
            pl.BlockSpec((rows, depth), lambda n: (0, 0)),
            pl.BlockSpec((depth, columns), lambda n: (0, n)),
            pl.BlockSpec((rows, 1), lambda n: (0, 0)),
        ],
        out_specs=[
            pl.BlockSpec((rows, columns), lambda n: (0, n)),
            pl.BlockSpec((8, rows), lambda n: (0, 0)),
        ],
        scratch_shapes=[
            pltpu.VMEM((rows, columns), F32),
            pltpu.VMEM((2, rows, 128), F32),
            pltpu.VMEM((2, rows, 128), F32),
            pltpu.VMEM((2, rows, 128), F32),
        ],
        cost_estimate=pl.CostEstimate(
            flops=4 * rows * depth * width,
            bytes_accessed=2 * depth * width + 4 * rows * width,
            transcendentals=2 * rows * width,
        ),
        compiler_params=pltpu.CompilerParams(vmem_limit_bytes=56 * 1024 * 1024),
    )(policy_low, frozen_low, head_weight, targets)


def logit_grad_kernel(logits_ref, head_ref, target_ref, token_ref, part_ref, low_ref, sum_ref):
    chunk = pl.program_id(0)
    rows, columns = logits_ref.shape

    for first in range(0, rows, 32):
        own = pl.ds(first, 32)
        values = logits_ref[own, :]
        target = target_ref[own, :] - chunk * columns
        chosen = lax.broadcasted_iota(jnp.int32, values.shape, 1) == target
        probs = jnp.exp(values - token_ref[own, 1:2])
        low_ref[own, :] = (token_ref[own, 0:1] * (jnp.where(chosen, 1.0, 0.0) - probs)).astype(BF16)
    value = dot_cols(low_ref[...], head_ref[...])

    @pl.when(chunk == 0)
    def _():
        sum_ref[...] = value

    @pl.when(chunk > 0)
    def _():
        sum_ref[...] += value

    @pl.when(chunk == pl.num_programs(0) - 1)
    def _():
        part_ref[...] = sum_ref[...].astype(BF16)


def logit_grad_call(logits, head_weight, targets, tokens):
    rows, width = logits.shape
    depth = head_weight.shape[0]
    columns = chunk_of(width)
    return pl.pallas_call(
        logit_grad_kernel,
        grid=(width // columns,),
        out_shape=jax.ShapeDtypeStruct((rows, depth), BF16),
        in_specs=[
            pl.BlockSpec((rows, columns), lambda n: (0, n)),
            pl.BlockSpec((depth, columns), lambda n: (0, n)),
            pl.BlockSpec((rows, 1), lambda n: (0, 0)),
            pl.BlockSpec((rows, tokens.shape[1]), lambda n: (0, 0)),
        ],
        out_specs=pl.BlockSpec((rows, depth), lambda n: (0, 0)),
        scratch_shapes=[pltpu.VMEM((rows, columns), BF16), pltpu.VMEM((rows, depth), F32)],
        cost_estimate=pl.CostEstimate(
            flops=2 * rows * depth * width,
            bytes_accessed=2 * depth * width + 4 * rows * width,
            transcendentals=rows * width,
        ),
        compiler_params=pltpu.CompilerParams(vmem_limit_bytes=56 * 1024 * 1024),
    )(logits, head_weight, targets, tokens)


def adam_step(master, mean_old, square_old, gradient, factor, rate, decay_rate):
    clipped = f32(gradient) * factor
    mean_new = BETA_FIRST * mean_old + (1.0 - BETA_FIRST) * clipped
    square_new = BETA_SECOND * square_old + (1.0 - BETA_SECOND) * clipped * clipped
    mean_hat = mean_new / (1.0 - BETA_FIRST**STEP)
    square_hat = square_new / (1.0 - BETA_SECOND**STEP)
    master_new = master - rate * (
        mean_hat / (jnp.sqrt(square_hat) + ADAM_EPS) + decay_rate * master
    )
    return (mean_new, square_new, master_new)


def on_device(
    inputs,
    targets,
    doc_lengths,
    desirable,
    head_weight,
    qkv_master,
    out_master,
    up_master,
    down_master,
    vectors,
    hidden_bias,
    qkv_mean,
    out_mean,
    up_mean,
    down_mean,
    vectors_mean,
    hidden_mean,
    qkv_square,
    out_square,
    up_square,
    down_square,
    vectors_square,
    hidden_square,
    qkv_frozen,
    out_frozen,
    up_frozen,
    down_frozen,
    vectors_frozen,
    hidden_frozen,
):
    dp_size = lax.axis_size("dp")
    tensor_size = lax.axis_size("tensor")
    inner = dp_size // SPLIT
    outer_index = lax.axis_index("dp") // inner
    block = inputs.shape[0]
    small = jnp.concatenate([doc_lengths, desirable], axis=0).astype(jnp.int32)
    lengths_tile = jnp.pad(small, ((0, 8 - small.shape[0]), (0, 128 - SEGS)))
    masters = tuple(w.astype(BF16) for w in (qkv_master, out_master, up_master, down_master))
    *policy_set, tokens_all, lengths_all = spread_weights(masters, inner, inputs, lengths_tile, 0)
    frozen_shards = (qkv_frozen, out_frozen, up_frozen, down_frozen)
    cut = qkv_master.shape[1]
    width_qkv, width_up = cut // SPLIT, up_master.shape[1] // SPLIT

    layout = (lengths_all, *turn_tables(block))
    policy = (vectors, hidden_bias[None])
    frozen = (vectors_frozen, hidden_frozen[None])
    if aligned(out_master.shape[1]):
        final_low, frozen_low, *kept = forward_call(
            tokens_all, layout, (policy, frozen), policy_set, block, inner, None, frozen_shards, 2
        )
        kept_values = tuple(kept[:4])
    else:
        final_low, *kept = forward_call(
            tokens_all, layout, (policy,), policy_set, block, inner, None, frozen_shards, 2
        )
        kept_values = tuple(kept[:4])
        frozen_set = (*kept[4:6], joined_columns(kept[6]))
        (frozen_low,) = forward_call(
            tokens_all, layout, (frozen,), frozen_set, block, inner, kept_values[2], None, 3
        )
    vocab_start = lax.axis_index("tensor") * head_weight.shape[1]
    own_targets = (targets - vocab_start)[:, None]
    logits, stats = head_call(final_low, frozen_low, head_weight, own_targets)
    token_rows = reward_call(stats, lengths_tile, inner, 6)
    final_part = logit_grad_call(logits, head_weight, own_targets, token_rows)
    input_grad, branch_low, mixed_grad, hidden_low, vector_part, bias_tile = backward_call(
        final_part, tokens_all, vectors, policy_set, kept_values, layout, inner, 4
    )
    shards = tuple(w.shape for w in masters)
    bias_rows = (width_qkv + width_up) // 128
    input_grad = f32(input_grad)
    qkv_grad, up_grad, out_grad, down_grad, vector_sum, bias_sum, square = finish_call(
        tokens_all, branch_low, vectors, kept_values[2:], (mixed_grad, hidden_low),
        vector_part, bias_tile, shards, inner, 5,
    )
    vector_grad = jnp.concatenate([vector_sum[:5], vector_sum[4:5]], axis=0)
    bias_sum = bias_sum[:, :bias_rows].reshape(SPLIT, bias_rows * 128)
    hidden_grad = jnp.concatenate(
        [bias_sum[:, :width_qkv].reshape(-1), bias_sum[:, width_qkv:].reshape(-1)]
    )
    grad_norm = jnp.sqrt(square[0, 0])
    factor = jnp.minimum(1.0, CLIP_NORM / (grad_norm + 1e-06))
    qkv_state = adam_step(
        qkv_master, qkv_mean, qkv_square, qkv_grad, factor, LEARN_RATE, WEIGHT_DECAY
    )
    out_state = adam_step(
        out_master, out_mean, out_square, out_grad, factor, LEARN_RATE, WEIGHT_DECAY
    )
    up_state = adam_step(up_master, up_mean, up_square, up_grad, factor, LEARN_RATE, WEIGHT_DECAY)
    down_state = adam_step(
        down_master, down_mean, down_square, down_grad, factor, LEARN_RATE, WEIGHT_DECAY
    )
    vector_state = adam_step(
        vectors, vectors_mean, vectors_square, vector_grad, factor, VECTOR_RATE, 0.0
    )
    hidden_state = adam_step(
        hidden_bias, hidden_mean, hidden_square, hidden_grad, factor, VECTOR_RATE, 0.0
    )
    return (
        final_low,
        input_grad,
        grad_norm,
        *qkv_state,
        *out_state,
        *up_state,
        *down_state,
        *vector_state,
        *hidden_state,
    )


def solution(mesh):
    rows, cols = P("dp", "tensor"), P("tensor", "dp")
    matrices = (rows, cols, rows, cols)
    placed = (
        P("dp", None),
        P("dp"),
        P("dp", None),
        P("dp", None),
        P(None, "tensor"),
        *matrices,
        P(),
        P("tensor"),
        *matrices,
        P(),
        P("tensor"),
        *matrices,
        P(),
        P("tensor"),
        *matrices,
        P(),
        P("tensor"),
    )
    return jax.shard_map(
        on_device,
        mesh=mesh,
        in_specs=placed,
        out_specs=(
            P("dp", None),
            P("dp", None),
            P(),
            *(spec for spec in matrices for _ in range(3)),
            P(),
            P(),
            P(),
            P("tensor"),
            P("tensor"),
            P("tensor"),
        ),
        check_vma=False,
    )
```
